32 devices in a mesh: section: 2 (over y), dp: 16 (over z, x, core).
Axes of the slice: x: 2, y: 2, z: 4, core: 2. Of those that a mesh axis runs over, the one named last changes fastest.
Arguments:
- mel_input: bfloat16 [32, 80, 2048], P('dp'), may hold values from -6 to 6
- time_start: int32 [32], P('dp'), may hold values from 0 to 2047
- time_width: int32 [32], P('dp'), may hold values from 0 to 100
- freq_start: int32 [32], P('dp'), may hold values from 0 to 79
- freq_width: int32 [32], P('dp'), may hold values from 0 to 27
- text_len: int32 [32], P('dp'), may hold values from 5 to 448, as said below
- text_embed: bfloat16 [32, 448, 512], P('dp'), may hold values from -6 to 6
- cotangent: bfloat16 [32, 448, 512], P('dp'), may hold values from -6 to 6
- positions: bfloat16 [1024, 512], replicated, may hold values from -1 to 1
- conv_first: bfloat16 [3, 80, 512], P(None, None, 'section'), may hold values from -0.375 to 0.375
- conv_first_bias: bfloat16 [512], P('section'), may hold values from -3 to 3
- conv_second: bfloat16 [3, 512, 512], P(None, None, 'section'), may hold values from -0.15625 to 0.15625
- norm_gain: bfloat16 [2, 3, 512], P('section'), may hold values from 0.5 to 1.5
- norm_shift: bfloat16 [2, 3, 512], P('section'), may hold values from -1.5 to 1.5
- attn_in: bfloat16 [2, 512, 1536], P('section'), may hold values from -0.25 to 0.25
- attn_out: bfloat16 [2, 512, 512], P('section'), may hold values from -1.5 to 1.5
- mlp_up: bfloat16 [2, 512, 2048], P('section'), may hold values from -0.25 to 0.25
- mlp_down: bfloat16 [2, 2048, 512], P('section'), may hold values from -0.125 to 0.125
- up_bias: bfloat16 [2, 2048], P('section'), may hold values from -1 to 1
- small_bias: bfloat16 [2, 6, 512], P('section'), may hold values from -0.5 to 0.5
- cross_first: bfloat16 [2, 512, 512], P('section'), may hold values from -0.25 to 0.25
- cross_second: bfloat16 [2, 512, 512], P('section'), may hold values from -1 to 1
Outputs:
- decoded: float32 [32, 448, 512], P('dp', None, 'section')
- text_grad: float32 [32, 448, 512], P('dp', None, 'section')
- mel_grad: float32 [32, 80, 2048], P('dp', None, 'section')
- conv_first_grad: float32 [3, 80, 512], P(None, None, 'section')
- conv_first_bias_grad: float32 [512], P('section')
- conv_second_grad: float32 [3, 512, 512], P(None, None, 'section')
- norm_gain_grad: float32 [2, 3, 512], P('section')
- norm_shift_grad: float32 [2, 3, 512], P('section')
- attn_in_grad: float32 [2, 512, 1536], P('section')
- attn_out_grad: float32 [2, 512, 512], P('section')
- mlp_up_grad: float32 [2, 512, 2048], P('section')
- mlp_down_grad: float32 [2, 2048, 512], P('section')
- up_bias_grad: float32 [2, 2048], P('section')
- small_bias_grad: float32 [2, 6, 512], P('section')
- cross_first_grad: float32 [2, 512, 512], P('section')
- cross_second_grad: float32 [2, 512, 512], P('section')
- cross_bias_grad: float32 [512], P('section')
The draws below stay inside these ranges and needn't reach their ends.
Inputs may be any that keep to these rules, and one draw needn't show every extreme that they name: `text_len`: in every draw some clip has exactly 448 text positions and some exactly 5.
All inputs are finite; a program needn't handle non-finite values.
Results may differ from the reference program's by a relative error of at most 0.025.
Values may be sent and summed in bfloat16 or wider, within the bound.
A program may use at most 384 MiB of HBM per device.

```python
import jax
import jax.numpy as jnp
from jax import lax

D = 512
HEADS = 8
HEAD = 64
FF = 2048
MELS = 80
TEXT = 448
FRAMES = 1024
TMASK = 100
FMASK = 27
MEL_FRAMES = 2048
CLIPS = 32
N_SECTION = 2


def draw_text_len(key, part):
    lengths = jax.random.randint(jax.random.fold_in(key, 11), (CLIPS,), 5, TEXT + 1)
    spots = jax.random.permutation(jax.random.fold_in(key, 12), CLIPS)
    lengths = lengths.at[spots[0]].set(TEXT)
    lengths = lengths.at[spots[1]].set(5)
    return lengths.astype(jnp.int32)


def plant(drawn, key, smallest, largest):
    spot = [jax.random.randint(jax.random.fold_in(key, axis), (), 0, length) for axis, length in enumerate(drawn.shape)]
    widest = drawn.shape.index(max(drawn.shape))
    beside = spot[:widest] + [(spot[widest] + 1) % drawn.shape[widest]] + spot[widest + 1:]
    return drawn.at[tuple(spot)].set(smallest).at[tuple(beside)].set(largest)


def level_of(key, dims, cuts, least, largest):
    def one(dim, blocks):
        steps = jax.random.uniform(jax.random.fold_in(jax.random.fold_in(key, 6), dim), (blocks,), jnp.float32, least / len(cuts), largest / len(cuts))
        return jnp.repeat(jnp.exp(steps), dims[dim] // blocks).reshape((-1,) + (1,) * (len(dims) - dim - 1))

    factor_of = one(*cuts[0])
    for cut in cuts[1:]:
        factor_of = factor_of * one(*cut)
    return factor_of


def noise(key, shape, spread, reach, cuts=(), kind=jnp.bfloat16):
    drawn = jax.random.normal(key, shape, jnp.float32) * spread
    if len(cuts) > 0:
        drawn = level_of(key, shape, cuts, -0.22, 0.18) * drawn
    return jnp.clip(drawn, min=-reach, max=reach).astype(kind)


def setup_inputs(seed: int = 0) -> dict:
    keys = jax.random.split(jax.random.key(seed), 23)
    mel_input = noise(keys[0], (CLIPS, MELS, MEL_FRAMES), 1.0, 6.0, ((0, 16),))
    time_start = plant(jax.random.randint(keys[1], (CLIPS,), 0, MEL_FRAMES), jax.random.fold_in(keys[1], 1), 0, MEL_FRAMES - 1).astype(jnp.int32)
    time_width = plant(jax.random.randint(keys[2], (CLIPS,), 0, TMASK + 1), jax.random.fold_in(keys[2], 1), 0, TMASK).astype(jnp.int32)
    freq_start = plant(jax.random.randint(keys[3], (CLIPS,), 0, MELS), jax.random.fold_in(keys[3], 1), 0, MELS - 1).astype(jnp.int32)
    freq_width = plant(jax.random.randint(keys[4], (CLIPS,), 0, FMASK + 1), jax.random.fold_in(keys[4], 1), 0, FMASK).astype(jnp.int32)
    text_len = draw_text_len(jax.random.fold_in(keys[22], 71), 0)
    text_embed = noise(keys[6], (CLIPS, TEXT, D), 1.0, 6.0, ((0, 16),))
    cotangent = noise(keys[7], (CLIPS, TEXT, D), 1.0, 6.0, ((0, 16),))
    positions = jnp.clip(jax.random.uniform(keys[8], (FRAMES, D), jnp.float32, -1.0, 1.0), -1.0, 1.0).astype(jnp.bfloat16)
    conv_first = noise(keys[9], (3, MELS, D), (3 * MELS) ** -0.5, 0.375, ((2, 2),))
    conv_first_bias = noise(keys[10], (D,), 0.5, 3.0, ((0, 2),))
    conv_second = noise(keys[11], (3, D, D), (3 * D) ** -0.5, 0.15625, ((2, 2),))
    norm_gain = jnp.clip(1.0 + 0.1 * jax.random.normal(keys[12], (N_SECTION, 3, D), jnp.float32), 0.5, 1.5).astype(jnp.bfloat16)
    norm_shift = noise(keys[13], (N_SECTION, 3, D), 0.3, 1.5, ((0, 2),))
    attn_in = noise(keys[14], (N_SECTION, D, 3 * D), D ** -0.5, 0.25, ((0, 2),))
    attn_out = noise(keys[15], (N_SECTION, D, D), 16 ** -0.5, 1.5, ((0, 2),))
    mlp_up = noise(keys[16], (N_SECTION, D, FF), D ** -0.5, 0.25, ((0, 2),))
    mlp_down = noise(keys[17], (N_SECTION, FF, D), FF ** -0.5, 0.125, ((0, 2),))
    up_bias = noise(keys[18], (N_SECTION, FF), 0.2, 1.0, ((0, 2),))
    small_bias = noise(keys[19], (N_SECTION, 6, D), 0.1, 0.5, ((0, 2),))
    cross_first = noise(keys[20], (N_SECTION, D, D), D ** -0.5, 0.25, ((0, 2),))
    cross_second = noise(keys[21], (N_SECTION, D, D), 32 ** -0.5, 1.0, ((0, 2),))
    return {"mel_input": mel_input, "time_start": time_start, "time_width": time_width, "freq_start": freq_start, "freq_width": freq_width, "text_len": text_len, "text_embed": text_embed, "cotangent": cotangent, "positions": positions, "conv_first": conv_first, "conv_first_bias": conv_first_bias, "conv_second": conv_second, "norm_gain": norm_gain, "norm_shift": norm_shift, "attn_in": attn_in, "attn_out": attn_out, "mlp_up": mlp_up, "mlp_down": mlp_down, "up_bias": up_bias, "small_bias": small_bias, "cross_first": cross_first, "cross_second": cross_second}


epsilon = 1e-05
root_half = 0.7071067811865476

@jax.custom_vjp
def low(v):
    return lax.optimization_barrier(v.astype(jnp.bfloat16)).astype(jnp.float32)

@jax.custom_vjp
def low_back(v):
    return v

def low_keep(v):
    return (low(v), None)

def low_pass(kept, grad):
    return (grad,)

def back_keep(v):
    return (v, None)

def back_low(kept, grad):
    return (low(grad),)
low.defvjp(low_keep, low_pass)
low_back.defvjp(back_keep, back_low)

def product(left, right):
    return jnp.dot(left, right, precision=lax.Precision.HIGHEST, preferred_element_type=jnp.float32)

def gelu_value(inputs):
    return 0.5 * inputs * (1.0 + lax.erf(inputs * root_half))

def norm_rows(inputs, gain, shift):
    centred = inputs - lax.optimization_barrier(jnp.mean(inputs, axis=-1, keepdims=True))
    inverse = lax.rsqrt(lax.optimization_barrier(jnp.mean(centred * centred, axis=-1, keepdims=True)) + epsilon)
    return centred * inverse * gain + shift

def attention(queries, memory_keys, memory_values, causal):
    row_count = queries.shape[0]
    key_count = memory_keys.shape[0]
    query_heads = queries.reshape(row_count, HEADS, HEAD)
    key_heads = memory_keys.reshape(key_count, HEADS, HEAD)
    value_heads = memory_values.reshape(key_count, HEADS, HEAD)
    scores = jnp.einsum('qhd,khd->hqk', query_heads, key_heads, precision=lax.Precision.HIGHEST)
    scores = low_back(scores * float(HEAD) ** (-0.5))
    if causal:
        allowed = jnp.arange(key_count)[None, None, :] <= jnp.arange(row_count)[None, :, None]
        scores = jnp.where(allowed, scores, -1e+30)
    row_max = lax.optimization_barrier(jnp.max(scores, axis=-1, keepdims=True))
    exponent = jnp.exp(scores - row_max)
    probability = low(exponent / lax.optimization_barrier(jnp.sum(exponent, axis=-1, keepdims=True)))
    mixed_heads = jnp.einsum('hqk,khd->qhd', probability, value_heads, precision=lax.Precision.HIGHEST)
    return low(low_back(mixed_heads.reshape(row_count, -1)))

def self_block(inputs, gain, shift, weight_in, weight_out, bias_query, bias_value, bias_out, causal):
    model_width = inputs.shape[1]
    normed = low(norm_rows(inputs, gain, shift))
    joint = low_back(product(normed, weight_in))
    queries = low(joint[:, :model_width] + bias_query)
    memory_keys = low(joint[:, model_width:2 * model_width])
    memory_values = low(joint[:, 2 * model_width:] + bias_value)
    mixed = attention(queries, memory_keys, memory_values, causal)
    return inputs + low_back(product(mixed, weight_out)) + bias_out

def feed_block(inputs, gain, shift, weight_up, bias_up, weight_down, bias_down):
    normed = low(norm_rows(inputs, gain, shift))
    hidden = low(gelu_value(low_back(product(normed, weight_up)) + bias_up))
    return inputs + low_back(product(hidden, weight_down)) + bias_down

def clip_forward(masked, text_rows, weight_set, place_rows, text_length):
    conv_first, conv_first_bias, conv_second, norm_gain, norm_shift, attn_in, attn_out, mlp_up, mlp_down, up_bias, small_bias, cross_first, cross_second = weight_set
    frame_count = masked.shape[1]
    padded = jnp.pad(low(masked), ((0, 0), (1, 1)))
    conv_sum = jnp.einsum('mt,mc->tc', padded[:, 0:frame_count], conv_first[0], precision=lax.Precision.HIGHEST)
    conv_sum = conv_sum + jnp.einsum('mt,mc->tc', padded[:, 1:frame_count + 1], conv_first[1], precision=lax.Precision.HIGHEST)
    conv_sum = conv_sum + jnp.einsum('mt,mc->tc', padded[:, 2:frame_count + 2], conv_first[2], precision=lax.Precision.HIGHEST)
    first_pre = low_back(conv_sum) + conv_first_bias
    hidden = low(gelu_value(first_pre))
    pairs = hidden.reshape(frame_count // 2, 2, hidden.shape[1])
    even_rows = pairs[:, 0]
    odd_rows = pairs[:, 1]
    prior_rows = jnp.pad(odd_rows, ((1, 0), (0, 0)))[:-1]
    conv_out = product(prior_rows, conv_second[0]) + product(even_rows, conv_second[1]) + product(odd_rows, conv_second[2])
    encoded = gelu_value(low_back(conv_out) + small_bias[0, 4]) + place_rows
    encoded = self_block(encoded, norm_gain[0, 0], norm_shift[0, 0], attn_in[0], attn_out[0], small_bias[0, 0], small_bias[0, 1], small_bias[0, 2], False)
    encoded = feed_block(encoded, norm_gain[0, 1], norm_shift[0, 1], mlp_up[0], up_bias[0], mlp_down[0], small_bias[0, 3])
    memory = low(norm_rows(encoded, norm_gain[0, 2], norm_shift[0, 2]))
    memory_keys = low(low_back(product(memory, cross_first[0])))
    memory_values = low(low_back(product(memory, cross_second[0]) + small_bias[0, 5]))
    state = self_block(text_rows, norm_gain[1, 0], norm_shift[1, 0], attn_in[1], attn_out[1], small_bias[1, 0], small_bias[1, 1], small_bias[1, 2], True)
    cross_in = low(norm_rows(state, norm_gain[1, 1], norm_shift[1, 1]))
    queries = low(low_back(product(cross_in, cross_first[1])) + small_bias[1, 4])
    mixed = attention(queries, memory_keys, memory_values, False)
    state = state + low_back(product(mixed, cross_second[1])) + small_bias[1, 5]
    state = feed_block(state, norm_gain[1, 2], norm_shift[1, 2], mlp_up[1], up_bias[1], mlp_down[1], small_bias[1, 3])
    valid = jnp.arange(text_rows.shape[0], dtype=jnp.int32) < text_length
    return jnp.where(valid[:, None], state, 0.0)

def reference(mel_input, time_start, time_width, freq_start, freq_width, text_len, text_embed, cotangent, positions, conv_first, conv_first_bias, conv_second, norm_gain, norm_shift, attn_in, attn_out, mlp_up, mlp_down, up_bias, small_bias, cross_first, cross_second):
    weight_set = tuple((weight.astype(jnp.float32) for weight in (conv_first, conv_first_bias, conv_second, norm_gain, norm_shift, attn_in, attn_out, mlp_up, mlp_down, up_bias, small_bias, cross_first, cross_second)))
    place_rows = positions.astype(jnp.float32)
    band_at = jnp.arange(mel_input.shape[1], dtype=jnp.int32)
    frame_at = jnp.arange(mel_input.shape[2], dtype=jnp.int32)

    def clip_step(totals, item):
        mel_clip, time_begin, time_span, band_begin, band_span, text_length, text_clip, cot_clip = item
        keep_time = jnp.logical_or(frame_at < time_begin, frame_at >= time_begin + time_span)
        keep_band = jnp.logical_or(band_at < band_begin, band_at >= band_begin + band_span)
        keep = jnp.logical_and(keep_band[:, None], keep_time[None, :])

        def forward(mel_rows, text_rows, weights_now):
            return clip_forward(jnp.where(keep, mel_rows, 0.0), text_rows, weights_now, place_rows, text_length)
        decoded, pull_back = jax.vjp(forward, mel_clip.astype(jnp.float32), text_clip.astype(jnp.float32), weight_set)
        grad_mel, grad_text, grad_weights = pull_back(cot_clip.astype(jnp.float32))
        totals = jax.tree.map(jnp.add, totals, grad_weights)
        return (totals, (decoded, grad_text, grad_mel))
    start_totals = tuple((jnp.zeros_like(weight) for weight in weight_set))
    totals, (decoded, grad_text, grad_mel) = lax.scan(clip_step, start_totals, (mel_input, time_start, time_width, freq_start, freq_width, text_len, text_embed, cotangent))
    return (decoded, grad_text, grad_mel, totals[0], totals[1], totals[2], totals[3], totals[4], totals[5], totals[6], totals[7], totals[8], totals[9], totals[10], totals[11], totals[12], totals[10][1, 5])
```

```python
import jax
import jax.numpy as jnp
from jax import lax
from jax.sharding import PartitionSpec as P

HEADS = 8


epsilon = 1e-05
root_half = 0.7071067811865476
gauss_norm = 0.3989422804014327


def shifted(shard, axis, by):
    size = lax.axis_size(axis)
    pairs = [(i, i + by) for i in range(size) if 0 <= i + by < size]
    return lax.ppermute(shard, axis, pairs)


def gelu_value(inputs):
    return 0.5 * inputs * (1.0 + lax.erf(inputs * root_half))


def gelu_slope(inputs):
    return 0.5 * (1.0 + lax.erf(inputs * root_half)) + inputs * gauss_norm * jnp.exp(
        -0.5 * inputs * inputs
    )


def matmul(left, right):
    return jnp.dot(left, right, preferred_element_type=jnp.float32)


def weight_grad(inputs, grad_low):
    return lax.dot_general(
        inputs, grad_low, (((0,), (0,)), ((), ())), preferred_element_type=jnp.float32
    )


def input_grad(grad_low, weight):
    return lax.dot_general(
        grad_low, weight, (((1,), (1,)), ((), ())), preferred_element_type=jnp.float32
    )


def norm_rows(inputs, gain, shift):
    centred = inputs - jnp.mean(inputs, axis=-1, keepdims=True)
    inverse = lax.rsqrt(jnp.mean(centred * centred, axis=-1, keepdims=True) + epsilon)
    normed = centred * inverse
    return (normed * gain.astype(jnp.float32) + shift.astype(jnp.float32), normed, inverse)


def norm_rows_back(grad, gain, normed, inverse):
    scaled = grad * gain.astype(jnp.float32)
    grad_inputs = inverse * (
        scaled
        - jnp.mean(scaled, axis=-1, keepdims=True)
        - normed * jnp.mean(scaled * normed, axis=-1, keepdims=True)
    )
    return (grad_inputs, jnp.sum(grad * normed, axis=0), jnp.sum(grad, axis=0))


def spec_keep(time_begin, time_span, band_begin, band_span, band_count, frame_count):
    frame_at = jnp.arange(frame_count, dtype=jnp.int32)
    band_at = jnp.arange(band_count, dtype=jnp.int32)
    keep_time = jnp.logical_or(frame_at < time_begin, frame_at >= time_begin + time_span)
    keep_band = jnp.logical_or(band_at < band_begin, band_at >= band_begin + band_span)
    return jnp.logical_and(keep_band[:, None], keep_time[None, :])


def conv_tap(padded, weight, tap_index, frame_count):
    return jnp.einsum(
        "mt,mc->tc",
        padded[:, tap_index : tap_index + frame_count],
        weight[tap_index],
        preferred_element_type=jnp.float32,
    )


def stem_first(masked, weight, bias):
    frame_count = masked.shape[1]
    padded = jnp.pad(masked, ((0, 0), (1, 1)))
    conv_sum = (
        conv_tap(padded, weight, 0, frame_count)
        + conv_tap(padded, weight, 1, frame_count)
        + conv_tap(padded, weight, 2, frame_count)
    )
    pre_act = conv_sum + bias.astype(jnp.float32)
    return (pre_act, gelu_value(pre_act).astype(jnp.bfloat16))


def stem_first_back(masked, weight, pre_act, grad_hidden):
    frame_count = masked.shape[1]
    padded = jnp.pad(masked, ((0, 0), (1, 1)))
    grad_pre = grad_hidden * gelu_slope(pre_act)
    grad_low = grad_pre.astype(jnp.bfloat16)
    grad_weight = jnp.stack(
        [
            jnp.einsum(
                "mt,tc->mc",
                padded[:, tap_index : tap_index + frame_count],
                grad_low,
                preferred_element_type=jnp.float32,
            )
            for tap_index in range(3)
        ]
    )
    parts = [
        jnp.einsum("tc,mc->mt", grad_low, weight[tap_index], preferred_element_type=jnp.float32)
        for tap_index in range(3)
    ]
    grad_masked = (
        parts[1]
        + jnp.pad(parts[0][:, 1:], ((0, 0), (0, 1)))
        + jnp.pad(parts[2][:, :-1], ((0, 0), (1, 0)))
    )
    return (grad_weight, jnp.sum(grad_pre, axis=0), grad_masked)


def odd_even(hidden):
    pairs = hidden.reshape(hidden.shape[0] // 2, 2, hidden.shape[1])
    even_rows = pairs[:, 0]
    odd_rows = pairs[:, 1]
    prior_rows = jnp.pad(odd_rows, ((1, 0), (0, 0)))[:-1]
    return (prior_rows, even_rows, odd_rows)


def stem_second(hidden, weight):
    prior_rows, even_rows, odd_rows = odd_even(hidden)
    return (
        matmul(prior_rows, weight[0]) + matmul(even_rows, weight[1]) + matmul(odd_rows, weight[2])
    )


def stem_second_back(hidden, weight, grad_low):
    prior_rows, even_rows, odd_rows = odd_even(hidden)
    grad_weight = jnp.stack(
        [
            weight_grad(prior_rows, grad_low),
            weight_grad(even_rows, grad_low),
            weight_grad(odd_rows, grad_low),
        ]
    )
    grad_prior = input_grad(grad_low, weight[0])
    grad_even = input_grad(grad_low, weight[1])
    grad_odd = input_grad(grad_low, weight[2]) + jnp.pad(grad_prior[1:], ((0, 1), (0, 0)))
    grad_hidden = jnp.stack([grad_even, grad_odd], axis=1).reshape(hidden.shape[0], -1)
    return (grad_weight, grad_hidden)


def head_split(inputs):
    return inputs.reshape(inputs.shape[0], HEADS, inputs.shape[1] // HEADS)


def block_scores(query_block, key_heads, block_start, causal):
    score_scale = float(key_heads.shape[2]) ** (-0.5)
    scores = (
        jnp.einsum("qhd,khd->hqk", query_block, key_heads, preferred_element_type=jnp.float32)
        * score_scale
    )
    if causal:
        rows_at = block_start + jnp.arange(query_block.shape[0], dtype=jnp.int32)
        keys_at = jnp.arange(key_heads.shape[0], dtype=jnp.int32)
        scores = jnp.where(keys_at[None, None, :] <= rows_at[None, :, None], scores, -1e30)
    return scores


def attend(queries, memory_keys, memory_values, causal):
    row_count = queries.shape[0]
    block_rows = min(row_count, 512)
    block_count = row_count // block_rows
    key_heads = head_split(memory_keys)
    value_heads = head_split(memory_values)
    query_blocks = queries.reshape(block_count, block_rows, HEADS, -1)
    block_starts = jnp.arange(block_count, dtype=jnp.int32) * block_rows

    def one_block(block_item):
        query_block, block_start = block_item
        scores = block_scores(query_block, key_heads, block_start, causal)
        row_max = jnp.max(scores, axis=-1, keepdims=True)
        exponent = jnp.exp(scores - row_max)
        row_total = jnp.sum(exponent, axis=-1, keepdims=True)
        probability = (exponent / row_total).astype(jnp.bfloat16)
        mixed_heads = jnp.einsum(
            "hqk,khd->qhd", probability, value_heads, preferred_element_type=jnp.float32
        )
        return (
            mixed_heads.reshape(block_rows, -1).astype(jnp.bfloat16),
            (row_max + jnp.log(row_total))[..., 0],
        )

    mixed_heads, log_total = lax.map(one_block, (query_blocks, block_starts))
    return (mixed_heads.reshape(row_count, -1), log_total)


def attend_back(queries, memory_keys, memory_values, log_total, grad_mixed, causal):
    row_count = queries.shape[0]
    block_rows = min(row_count, 512)
    block_count = row_count // block_rows
    score_scale = float(queries.shape[1] // HEADS) ** (-0.5)
    key_heads = head_split(memory_keys)
    value_heads = head_split(memory_values)
    query_blocks = queries.reshape(block_count, block_rows, HEADS, -1)
    grad_blocks = grad_mixed.reshape(block_count, block_rows, HEADS, -1)
    block_starts = jnp.arange(block_count, dtype=jnp.int32) * block_rows

    def one_block(running, block_item):
        grad_keys, grad_values = running
        query_block, grad_block, total_block, block_start = block_item
        probability = jnp.exp(
            block_scores(query_block, key_heads, block_start, causal) - total_block[..., None]
        )
        grad_prob = jnp.einsum(
            "qhd,khd->hqk", grad_block, value_heads, preferred_element_type=jnp.float32
        )
        grad_values = grad_values + jnp.einsum(
            "hqk,qhd->khd",
            probability.astype(jnp.bfloat16),
            grad_block,
            preferred_element_type=jnp.float32,
        )
        grad_scores = (
            probability * (grad_prob - jnp.sum(probability * grad_prob, axis=-1, keepdims=True))
        ).astype(jnp.bfloat16)
        grad_query = (
            jnp.einsum("hqk,khd->qhd", grad_scores, key_heads, preferred_element_type=jnp.float32)
            * score_scale
        )
        grad_keys = (
            grad_keys
            + jnp.einsum(
                "hqk,qhd->khd", grad_scores, query_block, preferred_element_type=jnp.float32
            )
            * score_scale
        )
        return ((grad_keys, grad_values), grad_query.reshape(block_rows, -1))

    zero_keys = jnp.zeros(key_heads.shape, jnp.float32)
    (grad_keys, grad_values), grad_queries = lax.scan(
        one_block, (zero_keys, zero_keys), (query_blocks, grad_blocks, log_total, block_starts)
    )
    key_count = memory_keys.shape[0]
    return (
        grad_queries.reshape(row_count, -1),
        grad_keys.reshape(key_count, -1),
        grad_values.reshape(key_count, -1),
    )


def self_block(
    inputs, gain, shift, weight_in, weight_out, bias_query, bias_value, bias_out, causal
):
    model_width = inputs.shape[1]
    normed_in, normed, inverse = norm_rows(inputs, gain, shift)
    normed_low = normed_in.astype(jnp.bfloat16)
    joint = matmul(normed_low, weight_in)
    queries = (joint[:, :model_width] + bias_query.astype(jnp.float32)).astype(jnp.bfloat16)
    memory_keys = joint[:, model_width : 2 * model_width].astype(jnp.bfloat16)
    memory_values = (joint[:, 2 * model_width :] + bias_value.astype(jnp.float32)).astype(
        jnp.bfloat16
    )
    mixed_heads, log_total = attend(queries, memory_keys, memory_values, causal)
    result = inputs + matmul(mixed_heads, weight_out) + bias_out.astype(jnp.float32)
    return (
        result,
        (normed, inverse, normed_low, queries, memory_keys, memory_values, mixed_heads, log_total),
    )


def self_block_back(grad, kept, gain, weight_in, weight_out, causal):
    normed, inverse, normed_low, queries, memory_keys, memory_values, mixed_heads, log_total = kept
    grad_low = grad.astype(jnp.bfloat16)
    grad_weight_out = weight_grad(mixed_heads, grad_low)
    grad_mixed = input_grad(grad_low, weight_out).astype(jnp.bfloat16)
    grad_query, grad_key, grad_value = attend_back(
        queries, memory_keys, memory_values, log_total, grad_mixed, causal
    )
    joint_low = jnp.concatenate([grad_query, grad_key, grad_value], axis=1).astype(jnp.bfloat16)
    grad_weight_in = weight_grad(normed_low, joint_low)
    grad_normed = input_grad(joint_low, weight_in)
    grad_inputs, grad_gain, grad_shift = norm_rows_back(grad_normed, gain, normed, inverse)
    return (
        grad + grad_inputs,
        (
            grad_gain,
            grad_shift,
            grad_weight_in,
            grad_weight_out,
            jnp.sum(grad_query, axis=0),
            jnp.sum(grad_value, axis=0),
            jnp.sum(grad, axis=0),
        ),
    )


def feed_block(inputs, gain, shift, weight_up, bias_up, weight_down, bias_down):
    normed_in, normed, inverse = norm_rows(inputs, gain, shift)
    normed_low = normed_in.astype(jnp.bfloat16)
    hidden_pre = matmul(normed_low, weight_up) + bias_up.astype(jnp.float32)
    hidden = gelu_value(hidden_pre).astype(jnp.bfloat16)
    result = inputs + matmul(hidden, weight_down) + bias_down.astype(jnp.float32)
    return (result, (normed, inverse, normed_low, hidden_pre, hidden))


def feed_block_back(grad, kept, gain, weight_up, weight_down):
    normed, inverse, normed_low, hidden_pre, hidden = kept
    grad_low = grad.astype(jnp.bfloat16)
    grad_weight_down = weight_grad(hidden, grad_low)
    grad_pre = input_grad(grad_low, weight_down) * gelu_slope(hidden_pre)
    pre_low = grad_pre.astype(jnp.bfloat16)
    grad_weight_up = weight_grad(normed_low, pre_low)
    grad_normed = input_grad(pre_low, weight_up)
    grad_inputs, grad_gain, grad_shift = norm_rows_back(grad_normed, gain, normed, inverse)
    return (
        grad + grad_inputs,
        (
            grad_gain,
            grad_shift,
            grad_weight_up,
            grad_weight_down,
            jnp.sum(grad_pre, axis=0),
            jnp.sum(grad, axis=0),
        ),
    )


def encode(conv_out, positions, weights):
    (
        gains,
        shifts,
        weight_in,
        weight_out,
        weight_up,
        weight_down,
        bias_up,
        small,
        cross_a,
        cross_b,
    ) = weights
    second_pre = conv_out + small[4].astype(jnp.float32)
    encoded = gelu_value(second_pre) + positions.astype(jnp.float32)
    middle, kept_attn = self_block(
        encoded, gains[0], shifts[0], weight_in, weight_out, small[0], small[1], small[2], False
    )
    ending, kept_feed = feed_block(
        middle, gains[1], shifts[1], weight_up, bias_up, weight_down, small[3]
    )
    memory_in, normed, inverse = norm_rows(ending, gains[2], shifts[2])
    memory = memory_in.astype(jnp.bfloat16)
    memory_keys = matmul(memory, cross_a).astype(jnp.bfloat16)
    memory_values = (matmul(memory, cross_b) + small[5].astype(jnp.float32)).astype(jnp.bfloat16)
    return (memory_keys, memory_values, (second_pre, kept_attn, kept_feed, normed, inverse, memory))


def blank_encode(frame_count, model_width, hidden_width):
    block_rows = min(frame_count, 512)
    block_count = frame_count // block_rows
    wide_f32 = jnp.zeros((frame_count, model_width), jnp.float32)
    wide_low = jnp.zeros((frame_count, model_width), jnp.bfloat16)
    column = jnp.zeros((frame_count, 1), jnp.float32)
    log_blank = jnp.zeros((block_count, HEADS, block_rows), jnp.float32)
    kept_attn = (wide_f32, column, wide_low, wide_low, wide_low, wide_low, wide_low, log_blank)
    kept_feed = (
        wide_f32,
        column,
        wide_low,
        jnp.zeros((frame_count, hidden_width), jnp.float32),
        jnp.zeros((frame_count, hidden_width), jnp.bfloat16),
    )
    return (wide_low, wide_low, (wide_f32, kept_attn, kept_feed, wide_f32, column, wide_low))


def encode_back(keys_back, values_back, kept, weights):
    (
        gains,
        shifts,
        weight_in,
        weight_out,
        weight_up,
        weight_down,
        bias_up,
        small,
        cross_a,
        cross_b,
    ) = weights
    second_pre, kept_attn, kept_feed, normed, inverse, memory = kept
    grad_cross_a = weight_grad(memory, keys_back)
    grad_cross_b = weight_grad(memory, values_back)
    grad_memory = input_grad(keys_back, cross_a) + input_grad(values_back, cross_b)
    grad_ending, gain_post, shift_post = norm_rows_back(grad_memory, gains[2], normed, inverse)
    grad_middle, feed_grads = feed_block_back(
        grad_ending, kept_feed, gains[1], weight_up, weight_down
    )
    grad_encoded, attn_grads = self_block_back(
        grad_middle, kept_attn, gains[0], weight_in, weight_out, False
    )
    grad_second = grad_encoded * gelu_slope(second_pre)
    grad_gains = jnp.stack([attn_grads[0], feed_grads[0], gain_post])
    grad_shifts = jnp.stack([attn_grads[1], feed_grads[1], shift_post])
    grad_small = jnp.stack(
        [
            attn_grads[4],
            attn_grads[5],
            attn_grads[6],
            feed_grads[5],
            jnp.sum(grad_second, axis=0),
            jnp.sum(values_back.astype(jnp.float32), axis=0),
        ]
    )
    grads = (
        grad_gains,
        grad_shifts,
        attn_grads[2],
        attn_grads[3],
        feed_grads[2],
        feed_grads[3],
        feed_grads[4],
        grad_small,
        grad_cross_a,
        grad_cross_b,
    )
    return (grads, grad_second)


def decode(text_clip, cot_clip, text_length, memory_keys, memory_values, weights):
    (
        gains,
        shifts,
        weight_in,
        weight_out,
        weight_up,
        weight_down,
        bias_up,
        small,
        cross_a,
        cross_b,
    ) = weights
    middle, kept_attn = self_block(
        text_clip.astype(jnp.float32),
        gains[0],
        shifts[0],
        weight_in,
        weight_out,
        small[0],
        small[1],
        small[2],
        True,
    )
    cross_in, cross_normed, cross_inverse = norm_rows(middle, gains[1], shifts[1])
    cross_low = cross_in.astype(jnp.bfloat16)
    queries = (matmul(cross_low, cross_a) + small[4].astype(jnp.float32)).astype(jnp.bfloat16)
    mixed_heads, log_total = attend(queries, memory_keys, memory_values, False)
    after = middle + matmul(mixed_heads, cross_b) + small[5].astype(jnp.float32)
    ending, kept_feed = feed_block(
        after, gains[2], shifts[2], weight_up, bias_up, weight_down, small[3]
    )
    valid = (jnp.arange(text_clip.shape[0], dtype=jnp.int32) < text_length)[:, None]
    decoded = jnp.where(valid, ending, 0.0)
    grad_ending = jnp.where(valid, cot_clip.astype(jnp.float32), 0.0)
    grad_after, feed_grads = feed_block_back(
        grad_ending, kept_feed, gains[2], weight_up, weight_down
    )
    after_low = grad_after.astype(jnp.bfloat16)
    grad_cross_b = weight_grad(mixed_heads, after_low)
    grad_mixed = input_grad(after_low, cross_b).astype(jnp.bfloat16)
    grad_query, grad_key, grad_value = attend_back(
        queries, memory_keys, memory_values, log_total, grad_mixed, False
    )
    query_low = grad_query.astype(jnp.bfloat16)
    grad_cross_a = weight_grad(cross_low, query_low)
    grad_cross_in = input_grad(query_low, cross_a)
    grad_cross_x, gain_cross, shift_cross = norm_rows_back(
        grad_cross_in, gains[1], cross_normed, cross_inverse
    )
    grad_text, attn_grads = self_block_back(
        grad_after + grad_cross_x, kept_attn, gains[0], weight_in, weight_out, True
    )
    grad_gains = jnp.stack([attn_grads[0], gain_cross, feed_grads[0]])
    grad_shifts = jnp.stack([attn_grads[1], shift_cross, feed_grads[1]])
    grad_small = jnp.stack(
        [
            attn_grads[4],
            attn_grads[5],
            attn_grads[6],
            feed_grads[5],
            jnp.sum(grad_query, axis=0),
            jnp.sum(grad_after, axis=0),
        ]
    )
    grads = (
        grad_gains,
        grad_shifts,
        attn_grads[2],
        attn_grads[3],
        feed_grads[2],
        feed_grads[3],
        feed_grads[4],
        grad_small,
        grad_cross_a,
        grad_cross_b,
    )
    return (
        decoded,
        grad_text,
        grad_key.astype(jnp.bfloat16),
        grad_value.astype(jnp.bfloat16),
        grads,
    )


def shards(
    mel_input,
    time_start,
    time_width,
    freq_start,
    freq_width,
    text_len,
    text_embed,
    cotangent,
    positions,
    conv_first,
    conv_first_bias,
    conv_second,
    norm_gain,
    norm_shift,
    attn_in,
    attn_out,
    mlp_up,
    mlp_down,
    up_bias,
    small_bias,
    cross_first,
    cross_second,
):
    is_first = lax.axis_index("section") == 0
    weights = (
        norm_gain[0],
        norm_shift[0],
        attn_in[0],
        attn_out[0],
        mlp_up[0],
        mlp_down[0],
        up_bias[0],
        small_bias[0],
        cross_first[0],
        cross_second[0],
    )
    section_at = lax.axis_index("section")

    def both(weight):
        return lax.all_gather(weight, "section", axis=0, tiled=False)

    gathered = tuple(both(weight) for weight in weights)
    audio_weights = tuple(weight[0] for weight in gathered)
    text_weights = tuple(weight[1] for weight in gathered)
    first_all = lax.all_gather(conv_first, "section", axis=2, tiled=True)
    bias_all = lax.all_gather(conv_first_bias, "section", axis=0, tiled=True)
    second_all = lax.all_gather(conv_second, "section", axis=2, tiled=True)

    def own(array):
        return lax.dynamic_index_in_dim(array, section_at, 0, keepdims=False)

    mel_clip, text_clip, cot_clip = own(mel_input), own(text_embed), own(cotangent)
    mel_frames = mel_input.shape[2]
    keep = spec_keep(
        own(time_start), own(time_width), own(freq_start), own(freq_width), mel_input.shape[1], mel_frames
    )
    masked = jnp.where(keep, mel_clip, jnp.zeros_like(mel_clip))
    pre_act, hidden = stem_first(masked, first_all, bias_all)
    conv_out = stem_second(hidden, second_all)
    memory_keys, memory_values, kept = encode(conv_out, positions, audio_weights)
    decoded, text_grad, keys_back, values_back, text_grads = decode(
        text_clip, cot_clip, own(text_len), memory_keys, memory_values, text_weights
    )
    audio_grads, grad_second = encode_back(keys_back, values_back, kept, audio_weights)
    second_low = grad_second.astype(jnp.bfloat16)
    grad_conv_second, grad_hidden = stem_second_back(hidden, second_all, second_low)
    grad_conv_first, grad_conv_bias, grad_masked = stem_first_back(
        masked, first_all, pre_act, grad_hidden
    )
    mel_grad = jnp.where(keep, grad_masked, 0.0)

    half = first_all.shape[2] // 2

    def halves(array):
        return jnp.stack([array[..., :half], array[..., half:]])

    big = [
        jnp.stack([audio_grads[n], text_grads[n]]) for n in (2, 3, 4, 5, 8, 9)
    ] + [halves(grad_conv_first), halves(grad_conv_second)]
    small = [jnp.stack([audio_grads[n], text_grads[n]]) for n in (0, 1, 6, 7)] + [
        halves(grad_conv_bias)
    ]
    flat = jnp.concatenate(
        [array.reshape(2, -1, 512).astype(jnp.bfloat16) for array in big], axis=1
    )
    pad = -flat.shape[1] % (16 * lax.axis_size("dp"))
    flat = jnp.pad(flat, ((0, 0), (0, pad), (0, 0)))
    flat_shard = lax.psum_scatter(
        flat, "section", scatter_dimension=0, tiled=False
    )
    flat_all = lax.psum(flat_shard, "dp").astype(jnp.float32)
    small_flat = jnp.concatenate([array.reshape(2, -1) for array in small], axis=1)
    small_all = lax.psum(
        lax.psum_scatter(small_flat, "section", scatter_dimension=0, tiled=False), "dp"
    )
    outs, at = [], 0
    for array in big:
        rows = array.size // 1024
        outs.append(flat_all[at : at + rows].reshape(array.shape[1:]))
        at += rows
    smalls, at = [], 0
    for array in small:
        count = array.size // 2
        smalls.append(small_all[at : at + count].reshape(array.shape[1:]))
        at += count

    def swap(array, axis):
        size = array.shape[axis] // 2
        first = lax.slice_in_dim(array, 0, size, axis=axis)
        second = lax.slice_in_dim(array, size, 2 * size, axis=axis)
        is_first = section_at == 0
        keep_part = jnp.where(is_first, first, second)
        send_part = jnp.where(is_first, second, first).astype(jnp.bfloat16)
        got = lax.ppermute(send_part, "section", [(0, 1), (1, 0)]).astype(jnp.float32)
        return jnp.where(
            is_first, jnp.stack([keep_part, got]), jnp.stack([got, keep_part])
        )

    cross_all = lax.ppermute(smalls[3][5].astype(jnp.bfloat16), "section", [(1, 0)])
    cross_row = jnp.where(section_at == 0, cross_all.astype(jnp.float32), smalls[3][5])
    cross_half = cross_row.shape[0] // 2
    cross_bias = jnp.where(section_at == 0, cross_row[:cross_half], cross_row[cross_half:])
    return (
        swap(decoded, 1),
        swap(text_grad, 1),
        swap(mel_grad, 1),
        outs[6],
        smalls[4],
        outs[7],
        smalls[0][None],
        smalls[1][None],
        outs[0][None],
        outs[1][None],
        outs[2][None],
        outs[3][None],
        smalls[2][None],
        smalls[3][None],
        outs[4][None],
        outs[5][None],
        cross_bias,
    )


def solution(mesh):
    return jax.shard_map(
        shards,
        mesh=mesh,
        in_specs=(
            P("dp", None, None),
            P("dp"),
            P("dp"),
            P("dp"),
            P("dp"),
            P("dp"),
            P("dp", None, None),
            P("dp", None, None),
            P(),
            P(None, None, "section"),
            P("section"),
            P(None, None, "section"),
            P("section", None, None),
            P("section", None, None),
            P("section", None, None),
            P("section", None, None),
            P("section", None, None),
            P("section", None, None),
            P("section", None),
            P("section", None, None),
            P("section", None, None),
            P("section", None, None),
        ),
        out_specs=(
            P("dp", None, "section"),
            P("dp", None, "section"),
            P("dp", None, "section"),
            P(None, None, "section"),
            P("section"),
            P(None, None, "section"),
            P("section", None, None),
            P("section", None, None),
            P("section", None, None),
            P("section", None, None),
            P("section", None, None),
            P("section", None, None),
            P("section", None),
            P("section", None, None),
            P("section", None, None),
            P("section", None, None),
            P("section"),
        ),
        check_vma=False,
    )
```

```python
import functools

import jax
import jax.numpy as jnp
from jax import lax
from jax.experimental import pallas as pl
from jax.experimental.pallas import tpu as pltpu
from jax.sharding import PartitionSpec as P

HEADS = 8
epsilon = 1e-05
root_half = 0.7071067811865476
gauss_norm = 0.3989422804014327
log2_e = 1.4426950408889634
VMEM_BYTES = 56 << 20

f32 = jnp.float32
low = jnp.bfloat16


def dot(left, right):
    return lax.dot_general(left, right, (((1,), (0,)), ((), ())), preferred_element_type=f32)


def dot_t(left, right):
    return lax.dot_general(left, right, (((1,), (1,)), ((), ())), preferred_element_type=f32)


def dot_tt(left, right):
    return lax.dot_general(left, right, (((0,), (0,)), ((), ())), preferred_element_type=f32)


def gelu_both(inputs):
    ratio = 1.0 / (1.0 + (0.3275911 * root_half) * jnp.abs(inputs))
    bell = jnp.exp2((-0.5 * log2_e) * inputs * inputs)
    tail = ratio * (
        0.127414796
        + ratio * (-0.142248368 + ratio * (0.7107068705 + ratio * (-0.7265760135 + ratio * 0.5307027145)))
    )
    tail = tail * bell
    below = jnp.where(inputs >= 0.0, 1.0 - tail, tail)
    return inputs * below, below + inputs * bell * gauss_norm


def norm_rows(inputs):
    centred = inputs - jnp.mean(inputs, axis=-1, keepdims=True)
    inverse = lax.rsqrt(jnp.mean(centred * centred, axis=-1, keepdims=True) + epsilon)
    return centred * inverse, inverse


def norm_back(grad, gain, normed, inverse):
    scaled = grad * gain
    return inverse * (
        scaled
        - jnp.mean(scaled, axis=-1, keepdims=True)
        - normed * jnp.mean(scaled * normed, axis=-1, keepdims=True)
    )


def col_sum(inputs):
    return jnp.sum(inputs, axis=0, keepdims=True)


class Side:
    def __init__(self, side, own, other):
        self.side, self.own, self.other = side, own, other


def call(body, name, steps, block, ins, outs, scratch=(), reverse=False, flops=0, grid=None):
    arrays, specs, kinds, weight_scratch = [], [], [], []
    at = (lambda i: steps - 1 - i) if reverse else (lambda i: i)
    for array, kind in ins:
        if kind == "side":
            arrays += [array.own, array.other]
            specs += [pl.BlockSpec(memory_space=pl.ANY)] * 2
            weight_scratch.append(pltpu.VMEM(array.own.shape[1:], array.own.dtype))
        elif kind == "rows":
            arrays.append(array)
            specs.append(pl.BlockSpec((block, array.shape[1]), lambda i: (at(i), 0)))
        elif kind == "smem":
            arrays.append(array)
            specs.append(pl.BlockSpec(memory_space=pltpu.SMEM))
        else:
            arrays.append(array)
            specs.append(
                pl.BlockSpec(
                    array.shape,
                    lambda i, n=array.ndim: (0,) * n,
                    pipeline_mode=pl.Buffered(1),
                )
            )
        kinds.append((kind, array.side if kind == "side" else None))
    out_specs = [
        pl.BlockSpec((block, shape[1]), lambda i: (at(i), 0))
        if kind == "rows"
        else pl.BlockSpec(shape, lambda i, n=len(shape): (0,) * n)
        for shape, dtype, kind in outs
    ]
    n_in, n_out, n_weight = len(arrays), len(outs), len(weight_scratch)

    def kernel(*refs):
        in_refs, out_refs = refs[:n_in], refs[n_in : n_in + n_out]
        weights = refs[n_in + n_out : n_in + n_out + n_weight]
        extra = refs[n_in + n_out + n_weight :]
        given, r, w, loads = [], 0, 0, []
        for kind, side in kinds:
            if kind == "side":
                loads.append((side, in_refs[r], in_refs[r + 1], weights[w]))
                given.append(weights[w])
                r, w = r + 2, w + 1
            else:
                given.append(in_refs[r])
                r += 1
        step = pl.program_id(0)
        if loads:
            sem = extra[-1]
            extra = extra[:-1]

            @pl.when(step == 0)
            def _():
                mine = lax.axis_index("section")
                for n, (side, own, other, held) in enumerate(loads):

                    @pl.when(mine == side)
                    def _(own=own, held=held, n=n):
                        pltpu.make_async_copy(own.at[0], held, sem.at[n]).start()

                    @pl.when(mine != side)
                    def _(other=other, held=held, n=n):
                        pltpu.make_async_copy(other.at[0], held, sem.at[n]).start()

                for n, (side, own, other, held) in enumerate(loads):
                    pltpu.make_async_copy(own.at[0], held, sem.at[n]).wait()

        for ref, (shape, dtype, kind) in zip(out_refs, outs):
            if kind == "sums":

                @pl.when(step == 0)
                def _(ref=ref):
                    ref[...] = jnp.zeros(ref.shape, ref.dtype)

        body(step, given, out_refs, extra)

    scratch_shapes = weight_scratch + list(scratch)
    if weight_scratch:
        scratch_shapes.append(pltpu.SemaphoreType.DMA((n_weight,)))
    total = sum(a.size * a.dtype.itemsize for a in arrays) + sum(
        2 * s[0] * s[1] for s, d, k in outs
    )
    return pl.pallas_call(
        kernel,
        name=name,
        grid=(steps,),
        in_specs=specs,
        out_specs=out_specs,
        out_shape=[jax.ShapeDtypeStruct(shape, dtype) for shape, dtype, kind in outs],
        scratch_shapes=scratch_shapes,
        compiler_params=pltpu.CompilerParams(
            dimension_semantics=("arbitrary",), vmem_limit_bytes=VMEM_BYTES
        ),
        cost_estimate=pl.CostEstimate(flops=int(flops), bytes_accessed=int(total), transcendentals=0),
    )(*arrays)


def row(ref, n):
    return ref[n : n + 1, :].astype(f32)


def stem(taps, weight, bias, second, smalls, positions):
    rows, width = positions.shape
    block = 256

    def body(step, given, outs, extra):
        taps, weight, bias, second, smalls, positions = given
        encoded, even_out, odd_out, even_slope, odd_slope, slope_out = outs
        (carry,) = extra

        @pl.when(step == 0)
        def _():
            carry[...] = jnp.zeros(carry.shape, f32)

        pre = dot(taps[:, 0:384], weight[...]) + bias[...].astype(f32)
        value, slope = gelu_both(pre)
        even = value.astype(low)
        even_out[...] = even
        even_slope[...] = slope.astype(low)
        pre = dot(taps[:, 128:512], weight[...]) + bias[...].astype(f32)
        value, slope = gelu_both(pre)
        odd = value.astype(low)
        odd_out[...] = odd
        odd_slope[...] = slope.astype(low)
        prior = dot(odd, second[0])
        moved = pltpu.roll(prior, 1, 0)
        at_row = lax.broadcasted_iota(jnp.int32, (block, width), 0)
        moved = jnp.where(at_row == 0, carry[0:1, :], moved)
        carry[0:1, :] = prior[block - 1 : block, :]
        pre = moved + dot(even, second[1]) + dot(odd, second[2]) + row(smalls, 10)
        value, slope = gelu_both(pre)
        slope_out[...] = slope.astype(low)
        encoded[...] = value + positions[...].astype(f32)

    shape = (rows, width)
    return call(
        body, "stem", rows // block, block,
        [(taps, "rows"), (weight, "full"), (bias, "full"), (second, "full"), (smalls, "full"), (positions, "rows")],
        [(shape, f32, "rows")] + [(shape, low, "rows")] * 5,
        scratch=[pltpu.VMEM((8, width), f32)],
        flops=2 * rows * width * (768 + 3 * width),
    )


def project(inputs, weight, smalls, block):
    rows, width = inputs.shape

    def body(step, given, outs, extra):
        inputs, weight, smalls = given
        low_out, joint_out = outs
        normed, inverse = norm_rows(inputs[...].astype(f32))
        rounded = (normed * row(smalls, 0) + row(smalls, 3)).astype(low)
        low_out[...] = rounded
        part = dot(rounded, weight[:, :width])
        joint_out[:, :width] = (part + row(smalls, 6)).astype(low) * 0.125
        joint_out[:, width : 2 * width] = dot(rounded, weight[:, width : 2 * width]).astype(low)
        part = dot(rounded, weight[:, 2 * width :])
        joint_out[:, 2 * width :] = (part + row(smalls, 7)).astype(low)

    return call(
        body, "project", rows // block, block,
        [(inputs, "rows"), (weight, "side"), (smalls, "full")],
        [((rows, width), low, "rows"), ((rows, 3 * width), low, "rows")],
        flops=6 * rows * width * width,
    )


def attend(queries, keys, values, cols, causal, block):
    rows, key_rows = queries.shape[0], keys.shape[0]
    pairs, steps = HEADS // 2, rows // block

    def kernel(query_ref, key_ref, value_ref, mixed_ref, log_ref):
        lane = lax.broadcasted_iota(jnp.int32, (1, 128), 1)
        query, key, value = query_ref[...], key_ref[...], value_ref[...]
        mixed, logs = [], []
        for head in range(2):
            part = jnp.where(lane // 64 == head, query, jnp.zeros_like(query))
            scores = dot_t(part, key)
            if causal:
                key_at = lax.broadcasted_iota(jnp.int32, scores.shape, 1)
                query_at = lax.broadcasted_iota(jnp.int32, scores.shape, 0) + pl.program_id(1) * block
                scores = jnp.where(key_at <= query_at, scores, -1e30)
            top = jnp.max(scores, axis=1, keepdims=True) * log2_e
            exponent = jnp.exp2(scores * log2_e - top)
            total = jnp.sum(exponent, axis=1, keepdims=True)
            mixed.append(dot(exponent.astype(low), value) * (1.0 / total))
            logs.append(top + jnp.log2(total))
        mixed_ref[...] = jnp.where(lane < 64, mixed[0], mixed[1]).astype(low)
        both = jnp.where(lane == 0, logs[0], logs[1])
        log_ref[...] = both.T[0:8, :]

    q_at, k_at, v_at = cols
    return pl.pallas_call(
        kernel,
        name="attend",
        grid=(pairs, steps),
        in_specs=[
            pl.BlockSpec((block, 128), lambda h, i: (i, q_at + h)),
            pl.BlockSpec((key_rows, 128), lambda h, i: (0, k_at + h)),
            pl.BlockSpec((key_rows, 128), lambda h, i: (0, v_at + h)),
        ],
        out_specs=[
            pl.BlockSpec((block, 128), lambda h, i: (i, h)),
            pl.BlockSpec((8, block), lambda h, i: (h, i)),
        ],
        out_shape=[
            jax.ShapeDtypeStruct((rows, 128 * pairs), low),
            jax.ShapeDtypeStruct((8 * pairs, rows), f32),
        ],
        compiler_params=pltpu.CompilerParams(
            dimension_semantics=("arbitrary", "arbitrary"), vmem_limit_bytes=VMEM_BYTES
        ),
        cost_estimate=pl.CostEstimate(
            flops=16 * rows * key_rows * 512, bytes_accessed=2 * 512 * (2 * rows + 2 * key_rows), transcendentals=0
        ),
    )(queries, keys, values)


def attend_back(queries, keys, values, cols, logs, grad, causal, round_sums, block):
    rows, key_rows = queries.shape[0], keys.shape[0]
    pairs, steps = HEADS // 2, rows // block

    def kernel(
        query_ref, key_ref, value_ref, log_ref, grad_ref,
        query_out, key_out, value_out, sum_out, key_acc, value_acc, key_turned,
    ):
        step = pl.program_id(1)
        lane = lax.broadcasted_iota(jnp.int32, (1, 128), 1)

        @pl.when(step == 0)
        def _():
            key_acc[...] = jnp.zeros(key_acc.shape, f32)
            value_acc[...] = jnp.zeros(value_acc.shape, f32)
            sum_out[...] = jnp.zeros(sum_out.shape, f32)
            key_turned[...] = key_ref[...].astype(f32).T.astype(low)

        query, key, value, grad = query_ref[...], key_ref[...], value_ref[...], grad_ref[...]
        turned = key_turned[...]
        sub = lax.broadcasted_iota(jnp.int32, (128, 1), 0)
        query_turned = jnp.zeros((128, block), f32)
        for head in range(2):
            part = jnp.where(lane // 64 == head, query, jnp.zeros_like(query))
            grad_part = jnp.where(lane // 64 == head, grad, jnp.zeros_like(grad))
            scores = dot_t(key, part)
            chance = jnp.exp2(scores * log2_e - log_ref[head : head + 1, :])
            if causal:
                key_at = lax.broadcasted_iota(jnp.int32, scores.shape, 0)
                query_at = lax.broadcasted_iota(jnp.int32, scores.shape, 1) + step * block
                chance = jnp.where(key_at <= query_at, chance, 0.0)
            grad_chance = dot_t(value, grad_part)
            product = chance * grad_chance
            grad_scores = (product - chance * jnp.sum(product, axis=0, keepdims=True)).astype(low)
            value_acc[...] += dot(chance.astype(low), grad_part)
            key_acc[...] += dot(grad_scores, part)
            query_turned += dot(jnp.where(sub // 64 == head, turned, jnp.zeros_like(turned)), grad_scores)
        grad_query = query_turned.T * 0.125
        query_out[...] = grad_query.astype(low)
        sum_out[0:1, :] += col_sum(grad_query)

        @pl.when(step == steps - 1)
        def _():
            key_out[...] = key_acc[...].astype(low)
            rounded = value_acc[...].astype(low)
            value_out[...] = rounded
            sum_out[1:2, :] = col_sum(rounded.astype(f32) if round_sums else value_acc[...])

    q_at, k_at, v_at = cols
    row_spec = pl.BlockSpec((block, 128), lambda h, i: (i, h))
    key_spec = pl.BlockSpec((key_rows, 128), lambda h, i: (0, h))
    return pl.pallas_call(
        kernel,
        name="attend_back",
        grid=(pairs, steps),
        in_specs=[
            pl.BlockSpec((block, 128), lambda h, i: (i, q_at + h)),
            pl.BlockSpec((key_rows, 128), lambda h, i: (0, k_at + h)),
            pl.BlockSpec((key_rows, 128), lambda h, i: (0, v_at + h)),
            pl.BlockSpec((8, block), lambda h, i: (h, i)),
            row_spec,
        ],
        out_specs=[row_spec, key_spec, key_spec, pl.BlockSpec((8, 128), lambda h, i: (0, h))],
        out_shape=[
            jax.ShapeDtypeStruct((rows, 128 * pairs), low),
            jax.ShapeDtypeStruct((key_rows, 128 * pairs), low),
            jax.ShapeDtypeStruct((key_rows, 128 * pairs), low),
            jax.ShapeDtypeStruct((8, 128 * pairs), f32),
        ],
        scratch_shapes=[
            pltpu.VMEM((key_rows, 128), f32),
            pltpu.VMEM((key_rows, 128), f32),
            pltpu.VMEM((128, key_rows), low),
        ],
        compiler_params=pltpu.CompilerParams(
            dimension_semantics=("arbitrary", "arbitrary"), vmem_limit_bytes=VMEM_BYTES
        ),
        cost_estimate=pl.CostEstimate(
            flops=40 * rows * key_rows * 512, bytes_accessed=2 * 512 * (4 * rows + 4 * key_rows), transcendentals=0
        ),
    )(queries, keys, values, logs, grad)


def audio_feed(inputs, mixed, weight_out, smalls, ups, weight_up, weight_down, cross_a, cross_b, block):
    rows, width = inputs.shape
    hidden = ups.shape[1]

    def body(step, given, outs, extra):
        inputs, mixed, weight_out, smalls, ups, weight_up, weight_down, cross_a, cross_b = given
        middle_out, norm_out, hidden_out, slope_out, ending_out, memory_out, key_out, value_out = outs
        middle = inputs[...] + dot(mixed[...], weight_out[...]) + row(smalls, 8)
        middle_out[...] = middle
        normed, inverse = norm_rows(middle)
        rounded = (normed * row(smalls, 1) + row(smalls, 4)).astype(low)
        norm_out[...] = rounded
        ending = middle + row(smalls, 9)
        for part in range(hidden // 512):
            cols = slice(part * 512, part * 512 + 512)
            pre = dot(rounded, weight_up[:, cols]) + ups[:, cols].astype(f32)
            value, slope = gelu_both(pre)
            act = value.astype(low)
            hidden_out[:, cols] = act
            slope_out[:, cols] = slope.astype(low)
            ending += dot(act, weight_down[cols, :])
        ending_out[...] = ending
        normed, inverse = norm_rows(ending)
        memory = (normed * row(smalls, 2) + row(smalls, 5)).astype(low)
        memory_out[...] = memory
        key_out[...] = dot(memory, cross_a[...]).astype(low)
        value_out[...] = (dot(memory, cross_b[...]) + row(smalls, 11)).astype(low)

    wide, shape = (rows, hidden), (rows, width)
    return call(
        body, "audio_feed", rows // block, block,
        [(inputs, "rows"), (mixed, "rows"), (weight_out, "side"), (smalls, "full"), (ups, "full"),
         (weight_up, "side"), (weight_down, "side"), (cross_a, "side"), (cross_b, "side")],
        [(shape, f32, "rows"), (shape, low, "rows"), (wide, low, "rows"), (wide, low, "rows"),
         (shape, f32, "rows"), (shape, low, "rows"), (shape, low, "rows"), (shape, low, "rows")],
        flops=2 * rows * width * (3 * width + 2 * hidden),
    )


def text_middle(inputs, mixed, weight_out, smalls, cross_a, block):
    rows, width = inputs.shape

    def body(step, given, outs, extra):
        inputs, mixed, weight_out, smalls, cross_a = given
        middle_out, low_out, query_out = outs
        middle = inputs[...].astype(f32) + dot(mixed[...], weight_out[...]) + row(smalls, 8)
        middle_out[...] = middle
        normed, inverse = norm_rows(middle)
        rounded = (normed * row(smalls, 1) + row(smalls, 4)).astype(low)
        low_out[...] = rounded
        query_out[...] = (dot(rounded, cross_a[...]) + row(smalls, 10)).astype(low) * 0.125

    shape = (rows, width)
    return call(
        body, "text_middle", rows // block, block,
        [(inputs, "rows"), (mixed, "rows"), (weight_out, "side"), (smalls, "full"), (cross_a, "side")],
        [(shape, f32, "rows"), (shape, low, "rows"), (shape, low, "rows")],
        flops=4 * rows * width * width,
    )


def text_feed(length, middle, mixed, cotangent, cross_b, smalls, ups, weight_up, weight_down, block):
    rows, width = middle.shape
    hidden = ups.shape[1]

    def body(step, given, outs, extra):
        length, middle, mixed, cotangent, cross_b, smalls, ups, weight_up, weight_down = given
        decoded_out, norm_out, hidden_out, pre_out, cot_out, grad_out, grad_low, mixed_out, sums, wide_sums = outs
        after = middle[...] + dot(mixed[...], cross_b[...]) + row(smalls, 11)
        normed, inverse = norm_rows(after)
        rounded = (normed * row(smalls, 2) + row(smalls, 5)).astype(low)
        norm_out[...] = rounded
        at_row = lax.broadcasted_iota(jnp.int32, (block, 1), 0) + step * block
        valid = at_row < length[0]
        grad = jnp.where(valid, cotangent[...].astype(f32), 0.0)
        cot = grad.astype(low)
        cot_out[...] = cot
        ending = after + row(smalls, 9)
        back = jnp.zeros((block, width), f32)
        for part in range(hidden // 512):
            cols = slice(part * 512, part * 512 + 512)
            pre = dot(rounded, weight_up[:, cols]) + ups[:, cols].astype(f32)
            value, slope = gelu_both(pre)
            act = value.astype(low)
            hidden_out[:, cols] = act
            ending += dot(act, weight_down[cols, :])
            grad_pre = dot_t(cot, weight_down[cols, :]) * slope
            wide_sums[0:1, cols] += col_sum(grad_pre)
            pre_low = grad_pre.astype(low)
            pre_out[:, cols] = pre_low
            back += dot_t(pre_low, weight_up[:, cols])
        decoded_out[...] = jnp.where(valid, ending, 0.0)
        sums[0:1, :] += col_sum(back * normed)
        sums[1:2, :] += col_sum(back)
        sums[2:3, :] += col_sum(grad)
        grad = grad + norm_back(back, row(smalls, 2), normed, inverse)
        sums[3:4, :] += col_sum(grad)
        grad_out[...] = grad
        rounded = grad.astype(low)
        grad_low[...] = rounded
        mixed_out[...] = dot_t(rounded, cross_b[...]).astype(low)

    wide, shape = (rows, hidden), (rows, width)
    return call(
        body, "text_feed", rows // block, block,
        [(length, "smem"), (middle, "rows"), (mixed, "rows"), (cotangent, "rows"), (cross_b, "side"),
         (smalls, "full"), (ups, "full"), (weight_up, "side"), (weight_down, "side")],
        [(shape, f32, "rows"), (shape, low, "rows"), (wide, low, "rows"), (wide, low, "rows"), (shape, low, "rows"),
         (shape, f32, "rows"), (shape, low, "rows"), (shape, low, "rows"),
         ((8, width), f32, "sums"), ((8, hidden), f32, "sums")],
        flops=2 * rows * width * (2 * width + 4 * hidden),
    )


def text_cross_back(query_grad, middle, grad, smalls, cross_a, weight_out, block):
    rows, width = middle.shape

    def body(step, given, outs, extra):
        query_grad, middle, grad, smalls, cross_a, weight_out = given
        grad_out, low_out, mixed_out, sums = outs
        back = dot_t(query_grad[...], cross_a[...])
        normed, inverse = norm_rows(middle[...])
        sums[0:1, :] += col_sum(back * normed)
        sums[1:2, :] += col_sum(back)
        total = grad[...] + norm_back(back, row(smalls, 1), normed, inverse)
        sums[2:3, :] += col_sum(total)
        grad_out[...] = total
        rounded = total.astype(low)
        low_out[...] = rounded
        mixed_out[...] = dot_t(rounded, weight_out[...]).astype(low)

    shape = (rows, width)
    return call(
        body, "text_cross_back", rows // block, block,
        [(query_grad, "rows"), (middle, "rows"), (grad, "rows"), (smalls, "full"), (cross_a, "side"), (weight_out, "side")],
        [(shape, f32, "rows"), (shape, low, "rows"), (shape, low, "rows"), ((8, width), f32, "sums")],
        flops=4 * rows * width * width,
    )


def project_back(query_grad, key_grad, value_grad, inputs, grad, smalls, weight, block):
    rows, width = inputs.shape

    def body(step, given, outs, extra):
        query_grad, key_grad, value_grad, inputs, grad, smalls, weight = given
        grad_out, sums = outs
        back = (
            dot_t(query_grad[...], weight[:, :width])
            + dot_t(key_grad[...], weight[:, width : 2 * width])
            + dot_t(value_grad[...], weight[:, 2 * width :])
        )
        normed, inverse = norm_rows(inputs[...].astype(f32))
        sums[0:1, :] += col_sum(back * normed)
        sums[1:2, :] += col_sum(back)
        grad_out[...] = grad[...] + norm_back(back, row(smalls, 0), normed, inverse)

    return call(
        body, "project_back", rows // block, block,
        [(query_grad, "rows"), (key_grad, "rows"), (value_grad, "rows"), (inputs, "rows"), (grad, "rows"),
         (smalls, "full"), (weight, "side")],
        [((rows, width), f32, "rows"), ((8, width), f32, "sums")],
        flops=6 * rows * width * width,
    )


def audio_feed_back(key_grad, value_grad, ending, middle, slope, smalls, cross_a, cross_b, weight_up, weight_down, weight_out, block):
    rows, width = ending.shape
    hidden = slope.shape[1]

    def body(step, given, outs, extra):
        key_grad, value_grad, ending, middle, slope, smalls, cross_a, cross_b, weight_up, weight_down, weight_out = given
        end_low, pre_out, grad_out, grad_low, mixed_out, sums, wide_sums = outs
        back = dot_t(key_grad[...], cross_a[...]) + dot_t(value_grad[...], cross_b[...])
        normed, inverse = norm_rows(ending[...])
        sums[0:1, :] += col_sum(back * normed)
        sums[1:2, :] += col_sum(back)
        grad = norm_back(back, row(smalls, 2), normed, inverse)
        sums[2:3, :] += col_sum(grad)
        rounded = grad.astype(low)
        end_low[...] = rounded
        back = jnp.zeros((block, width), f32)
        for part in range(hidden // 512):
            cols = slice(part * 512, part * 512 + 512)
            grad_pre = dot_t(rounded, weight_down[cols, :]) * slope[:, cols].astype(f32)
            wide_sums[0:1, cols] += col_sum(grad_pre)
            pre_low = grad_pre.astype(low)
            pre_out[:, cols] = pre_low
            back += dot_t(pre_low, weight_up[:, cols])
        normed, inverse = norm_rows(middle[...])
        sums[3:4, :] += col_sum(back * normed)
        sums[4:5, :] += col_sum(back)
        grad = grad + norm_back(back, row(smalls, 1), normed, inverse)
        sums[5:6, :] += col_sum(grad)
        grad_out[...] = grad
        rounded = grad.astype(low)
        grad_low[...] = rounded
        mixed_out[...] = dot_t(rounded, weight_out[...]).astype(low)

    wide, shape = (rows, hidden), (rows, width)
    return call(
        body, "audio_feed_back", rows // block, block,
        [(key_grad, "rows"), (value_grad, "rows"), (ending, "rows"), (middle, "rows"), (slope, "rows"), (smalls, "full"),
         (cross_a, "side"), (cross_b, "side"), (weight_up, "side"), (weight_down, "side"), (weight_out, "side")],
        [(shape, low, "rows"), (wide, low, "rows"), (shape, f32, "rows"), (shape, low, "rows"), (shape, low, "rows"),
         ((8, width), f32, "sums"), ((8, hidden), f32, "sums")],
        flops=2 * rows * width * (3 * width + 2 * hidden),
    )


def stem_back(query_grad, key_grad, value_grad, encoded, grad, smalls, weight, slope_second, second, even_slope, odd_slope, first, block):
    rows, width = encoded.shape

    def body(step, given, outs, extra):
        query_grad, key_grad, value_grad, encoded, grad, smalls, weight, slope_second, second, even_slope, odd_slope, first = given
        second_low, next_low, even_low, odd_low, taps_out, sums = outs
        (carry,) = extra

        @pl.when(step == 0)
        def _():
            carry[...] = jnp.zeros(carry.shape, f32)

        back = (
            dot_t(query_grad[...], weight[:, :width])
            + dot_t(key_grad[...], weight[:, width : 2 * width])
            + dot_t(value_grad[...], weight[:, 2 * width :])
        )
        normed, inverse = norm_rows(encoded[...])
        sums[0:1, :] += col_sum(back * normed)
        sums[1:2, :] += col_sum(back)
        total = grad[...] + norm_back(back, row(smalls, 0), normed, inverse)
        total = total * slope_second[...].astype(f32)
        sums[2:3, :] += col_sum(total)
        rounded = total.astype(low)
        second_low[...] = rounded
        at_row = lax.broadcasted_iota(jnp.int32, (block, width), 0)
        wide = rounded.astype(f32)
        moved = jnp.where(at_row == block - 1, carry[0:1, :], pltpu.roll(wide, block - 1, 0))
        carry[0:1, :] = wide[0:1, :]
        moved = moved.astype(low)
        next_low[...] = moved
        moved = dot_t(moved, second[0])
        grad_even = dot_t(rounded, second[1]) * even_slope[...].astype(f32)
        grad_odd = (dot_t(rounded, second[2]) + moved) * odd_slope[...].astype(f32)
        sums[3:4, :] += col_sum(grad_even) + col_sum(grad_odd)
        grad_even = grad_even.astype(low)
        grad_odd = grad_odd.astype(low)
        even_low[...] = grad_even
        odd_low[...] = grad_odd
        taps_even = dot_t(grad_even, first[...])
        taps_odd = dot_t(grad_odd, first[...])
        taps_out[:, 0:128] = taps_even[:, 0:128]
        taps_out[:, 128:256] = taps_even[:, 128:256] + taps_odd[:, 0:128]
        taps_out[:, 256:384] = taps_even[:, 256:384] + taps_odd[:, 128:256]
        taps_out[:, 384:512] = taps_odd[:, 256:384]

    shape = (rows, width)
    return call(
        body, "stem_back", rows // block, block,
        [(query_grad, "rows"), (key_grad, "rows"), (value_grad, "rows"), (encoded, "rows"), (grad, "rows"), (smalls, "full"),
         (weight, "side"), (slope_second, "rows"), (second, "full"), (even_slope, "rows"), (odd_slope, "rows"), (first, "full")],
        [(shape, low, "rows")] * 4 + [((rows, 512), f32, "rows"), ((8, width), f32, "sums")],
        scratch=[pltpu.VMEM((8, width), f32)],
        reverse=True,
        flops=2 * rows * width * (6 * width + 768),
    )


def weight_grads(audio, text, taps, even_low, odd_low, conv, small, flat_rows):
    width = 512
    frames, text_rows = taps.shape[0], text[0][0].shape[0]
    jobs_audio = audio + conv
    arrays, places = [], {}

    def place(array):
        if id(array) not in places:
            places[id(array)] = len(arrays)
            arrays.append(array)
        return places[id(array)]

    lists = [
        [(place(x), xc, place(y), yc) for x, xc, y, yc in jobs] for jobs in (jobs_audio, text)
    ]
    at_taps, at_even, at_odd, at_small = place(taps), place(even_low), place(odd_low), place(small)
    base = len(audio) * width
    half = width // 2
    first_base, small_base = base + 3 * half, base + 3 * half + 192

    def kernel(*refs):
        given, flat = refs[: len(arrays)], refs[len(arrays)]
        x_audio, y_audio, x_text, y_text, out_buf, first_buf, in_sem, out_sem, first_sem, small_sem = refs[len(arrays) + 1 :]

        def small_copies():
            here = pl.ds(small_base, small.shape[1])
            return [pltpu.make_async_copy(given[at_small].at[s], flat.at[s, here], small_sem.at[s]) for s in range(2)]

        for copy in small_copies():
            copy.start()

        def run(side, jobs, x_buf, y_buf, plain):
            count = len(jobs)

            def copies(job, slot):
                x, xc, y, yc = job
                return (
                    pltpu.make_async_copy(given[x].at[:, xc * width : (xc + 1) * width], x_buf.at[slot], in_sem.at[0, slot]),
                    pltpu.make_async_copy(given[y].at[:, yc * width : (yc + 1) * width], y_buf.at[slot], in_sem.at[1, slot]),
                )

            def fetch(i, slot):
                for n, job in enumerate(jobs):

                    @pl.when(i == n)
                    def _(job=job):
                        for copy in copies(job, slot):
                            copy.start()

            def out_wait(slot):
                pltpu.make_async_copy(out_buf.at[slot], flat.at[0, 0:width], out_sem.at[slot]).wait()

            fetch(0, 0)

            @pl.loop(0, count)
            def _(i):
                slot = i % 2

                @pl.when(i + 1 < count)
                def _():
                    fetch(i + 1, 1 - slot)

                for copy in copies(jobs[0], slot):
                    copy.wait()

                @pl.when(i >= 2)
                def _():
                    out_wait(slot)

                out_buf[slot] = dot_tt(x_buf[slot], y_buf[slot]).astype(low)

                @pl.when(i < plain)
                def _():
                    pltpu.make_async_copy(
                        out_buf.at[slot], flat.at[side, pl.ds(pl.multiple_of(i * width, width), width)], out_sem.at[slot]
                    ).start()

                for tap in range(count - plain):

                    @pl.when(i == plain + tap)
                    def _(tap=tap):
                        for s in range(2):
                            cols = slice(s * half, s * half + half)
                            start = tap * width
                            for block in range(2):
                                r = start + block * half
                                left = r < 3 * half
                                to = base + (r if left else r - 3 * half)
                                pltpu.make_async_copy(
                                    out_buf.at[slot, block * half : block * half + half, cols],
                                    flat.at[s, to : to + half, 0:half] if left else flat.at[s, to : to + half, half:width],
                                    out_sem.at[slot],
                                ).start()

            for i in range(count - 2, count):
                out_wait(i % 2)

        run(0, lists[0], x_audio, y_audio, len(audio))
        run(1, lists[1], x_text, y_text, len(text))

        copies = [
            pltpu.make_async_copy(given[at_taps].at[:, 0:384], x_audio.at[0, :, 0:384], in_sem.at[0, 0]),
            pltpu.make_async_copy(given[at_even], y_audio.at[0], in_sem.at[1, 0]),
            pltpu.make_async_copy(given[at_taps].at[:, 128:512], x_audio.at[1, :, 0:384], in_sem.at[0, 1]),
            pltpu.make_async_copy(given[at_odd], y_audio.at[1], in_sem.at[1, 1]),
        ]
        for copy in copies:
            copy.start()
        for copy in copies:
            copy.wait()
        total = dot_tt(x_audio[0, :, 0:384], y_audio[0]) + dot_tt(x_audio[1, :, 0:384], y_audio[1])
        first_buf[...] = total.astype(low)
        copies = [
            pltpu.make_async_copy(
                first_buf.at[b * 192 : b * 192 + 192, s * half : s * half + half],
                flat.at[s, first_base : first_base + 192, b * half : b * half + half],
                first_sem.at[s, b],
            )
            for s in range(2)
            for b in range(2)
        ]
        for copy in copies:
            copy.start()
        for copy in copies + small_copies():
            copy.wait()

    return pl.pallas_call(
        kernel,
        name="weight_grads",
        in_specs=[pl.BlockSpec(memory_space=pl.ANY)] * len(arrays),
        out_specs=pl.BlockSpec(memory_space=pl.ANY),
        out_shape=jax.ShapeDtypeStruct((2, flat_rows, width), low),
        scratch_shapes=[
            pltpu.VMEM((2, frames, width), low),
            pltpu.VMEM((2, frames, width), low),
            pltpu.VMEM((2, text_rows, width), low),
            pltpu.VMEM((2, text_rows, width), low),
            pltpu.VMEM((2, width, width), low),
            pltpu.VMEM((384, width), low),
            pltpu.SemaphoreType.DMA((2, 2)),
            pltpu.SemaphoreType.DMA((2,)),
            pltpu.SemaphoreType.DMA((2, 2)),
            pltpu.SemaphoreType.DMA((2,)),
        ],
        compiler_params=pltpu.CompilerParams(vmem_limit_bytes=VMEM_BYTES),
        cost_estimate=pl.CostEstimate(
            flops=2 * width * width * (frames * (len(jobs_audio) + 2) + text_rows * len(text)),
            bytes_accessed=sum(2 * a.size for a in arrays), transcendentals=0,
        ),
    )(*arrays)


def factors_of(size):
    found, rest = [], size // 2
    while rest > 1:
        radix = 2 if rest in (2, 8) or rest % 4 else 4
        found.append(radix)
        rest //= radix
    return found


def reduce_all(flat):
    rows, width = flat.shape[1:]
    replicas = lax.axis_size("dp")
    factors = factors_of(replicas)
    chunk = max(512, 16 * replicas)
    count = rows // chunk
    half = chunk // 2
    sizes = []
    for radix in factors:
        sizes.append((sizes[-1] if sizes else half) // radix)
    levels = len(factors)

    def kernel(flat_ref, out_ref, acc, core_recv, side_recv, work, final, *refs):
        recvs = refs[:levels]
        local_sem, out_sem, core_sem, side_sem, back_sem = refs[levels : levels + 5]
        rs_sems = refs[levels + 5 : 2 * levels + 5]
        ag_sems = refs[2 * levels + 5 :]
        section, replica = lax.axis_index("section"), lax.axis_index("dp")
        core = replica % 2
        digits, strides, rest, stride = [], [], replica // 2, 2
        for radix in factors:
            digits.append(rest % radix)
            strides.append(stride)
            rest, stride = rest // radix, stride * radix
        core_peer = {"dp": replica + 1 - 2 * core}
        side_peer = {"section": 1 - section}

        def peer(level, distance):
            digit = (digits[level] + distance) % factors[level]
            return digit, {"dp": replica + (digit - digits[level]) * strides[level]}

        def remote(source, target, sems, at, device):
            return pltpu.make_async_remote_copy(
                src_ref=source, dst_ref=target, send_sem=sems.at[(0,) + at], recv_sem=sems.at[(1,) + at],
                device_id=device, device_id_type=pl.DeviceIdType.MESH,
            )

        def start_of(k, level):
            row_at = k * chunk + core * half
            for n in range(level):
                row_at = row_at + digits[n] * sizes[n]
            return row_at

        def place_of(k, level):
            return start_of(k, level) - k * chunk - core * half + k * half

        def rows_at(start, size):
            return pl.ds(pl.multiple_of(start, 16), size)

        def load(k):
            return pltpu.make_async_copy(
                flat_ref.at[:, rows_at(k * chunk + core * half, half)], acc.at[:, rows_at(k * half, half)], local_sem.at[k]
            )

        def core_copy(k):
            return remote(
                flat_ref.at[:, rows_at(k * chunk + (1 - core) * half, half)],
                core_recv.at[:, rows_at(k * half, half)], core_sem, (k,), core_peer,
            )

        def side_copy(k):
            return remote(acc.at[1 - section, rows_at(k * half, half)], side_recv.at[rows_at(k * half, half)], side_sem, (k,), side_peer)

        def scatter_copy(k, level, distance):
            digit, device = peer(level, distance)
            size = sizes[level]
            return remote(
                work.at[rows_at(place_of(k, level) + digit * size, size)],
                recvs[level].at[distance - 1, rows_at(k * size, size)], rs_sems[level], (distance - 1, k), device,
            )

        def gather_copy(k, level, distance):
            digit, device = peer(level, distance)
            here = final.at[rows_at(start_of(k, level + 1), sizes[level])]
            return remote(here, here, ag_sems[level], (distance - 1, k), device)

        def back_copy(k):
            here = final.at[rows_at(k * chunk + core * half, half)]
            return remote(here, here, back_sem, (k,), core_peer)

        def store(k):
            here = rows_at(k * chunk, chunk)
            return pltpu.make_async_copy(final.at[here], out_ref.at[here], out_sem.at[k])

        def stage_core(k):
            load(k).wait()
            core_copy(k).wait_recv()
            here = rows_at(k * half, half)
            acc[:, here] = (acc[:, here].astype(f32) + core_recv[:, here].astype(f32)).astype(low)
            side_copy(k).start()

        def stage_side(k):
            side_copy(k).wait_recv()
            here = rows_at(k * half, half)
            work[here] = (
                acc[section, here].astype(f32) + side_recv[here].astype(f32)
            ).astype(low)
            for distance in range(1, factors[0]):
                scatter_copy(k, 0, distance).start()

        def stage_scatter(k, level):
            size = sizes[level]
            for distance in range(1, factors[level]):
                scatter_copy(k, level, distance).wait_recv()
            here = rows_at(place_of(k, level + 1), size)
            total = work[here].astype(f32)
            for distance in range(1, factors[level]):
                total += recvs[level][distance - 1, rows_at(k * size, size)].astype(f32)
            if level + 1 < levels:
                work[here] = total.astype(low)
                for distance in range(1, factors[level + 1]):
                    scatter_copy(k, level + 1, distance).start()
            else:
                final[rows_at(start_of(k, level + 1), size)] = total.astype(low)
                for distance in range(1, factors[level]):
                    gather_copy(k, level, distance).start()

        def stage_gather(k, level):
            for distance in range(1, factors[level]):
                gather_copy(k, level, distance).wait_recv()
            if level > 0:
                for distance in range(1, factors[level - 1]):
                    gather_copy(k, level - 1, distance).start()
            else:
                back_copy(k).start()

        def stage_back(k):
            back_copy(k).wait_recv()
            store(k).start()

        stages = [stage_core, stage_side]
        stages += [functools.partial(stage_scatter, level=n) for n in range(levels)]
        stages += [functools.partial(stage_gather, level=n) for n in reversed(range(levels))]
        stages.append(stage_back)

        barrier = pltpu.get_barrier_semaphore()
        peers = [core_peer, side_peer]
        peers += [peer(n, d)[1] for n in range(levels) for d in range(1, factors[n])]
        for device in peers:
            pl.semaphore_signal(barrier, inc=1, device_id=device, device_id_type=pl.DeviceIdType.MESH)
        pl.semaphore_wait(barrier, len(peers))

        @pl.loop(0, count)
        def _(k):
            load(k).start()
            core_copy(k).start()

        @pl.loop(0, count + len(stages) - 1)
        def _(tick):
            for n, stage in enumerate(stages):

                @pl.when(jnp.logical_and(tick >= n, tick < count + n))
                def _(n=n, stage=stage):
                    stage(tick - n)

        @pl.loop(0, count)
        def _(k):
            core_copy(k).wait_send()
            side_copy(k).wait_send()
            for level in range(levels):
                for distance in range(1, factors[level]):
                    scatter_copy(k, level, distance).wait_send()
                    gather_copy(k, level, distance).wait_send()
            back_copy(k).wait_send()
            store(k).wait()

    def sems(*shape):
        return pltpu.SemaphoreType.DMA(shape)

    return pl.pallas_call(
        kernel,
        name="reduce_all",
        in_specs=[pl.BlockSpec(memory_space=pl.ANY)],
        out_specs=pl.BlockSpec(memory_space=pl.ANY),
        out_shape=jax.ShapeDtypeStruct((rows, width), low),
        scratch_shapes=[
            pltpu.VMEM((2, rows // 2, width), low),
            pltpu.VMEM((2, rows // 2, width), low),
            pltpu.VMEM((rows // 2, width), low),
            pltpu.VMEM((rows // 2, width), low),
            pltpu.VMEM((rows, width), low),
            *[pltpu.VMEM((r - 1, count * s, width), low) for r, s in zip(factors, sizes)],
            sems(count), sems(count), sems(2, count), sems(2, count), sems(2, count),
            *[sems(2, r - 1, count) for r in factors],
            *[sems(2, r - 1, count) for r in factors],
        ],
        compiler_params=pltpu.CompilerParams(
            collective_id=0, has_side_effects=True, vmem_limit_bytes=VMEM_BYTES
        ),
        cost_estimate=pl.CostEstimate(flops=0, bytes_accessed=100 * flat.size, transcendentals=0),
    )(flat)


def shards(
    mel_input,
    time_start,
    time_width,
    freq_start,
    freq_width,
    text_len,
    text_embed,
    cotangent,
    positions,
    conv_first,
    conv_first_bias,
    conv_second,
    norm_gain,
    norm_shift,
    attn_in,
    attn_out,
    mlp_up,
    mlp_down,
    up_bias,
    small_bias,
    cross_first,
    cross_second,
):
    mine = lax.axis_index("section")
    is_first = mine == 0
    frames, width = positions.shape
    bands, mel_frames = mel_input.shape[1], mel_input.shape[2]
    text_rows = text_embed.shape[1]
    audio_block = 256
    text_block = 224
    swap_pairs = [(0, 1), (1, 0)]

    def own(array):
        return lax.dynamic_index_in_dim(array, mine, 0, keepdims=False)

    def partner(array):
        return lax.ppermute(array, "section", swap_pairs)

    packed = jnp.concatenate(
        [norm_gain[0], norm_shift[0], small_bias[0], up_bias[0].reshape(-1, width)], axis=0
    )
    conv_own = jnp.concatenate([conv_first.reshape(-1, width // 2), conv_first_bias[None]], axis=0)
    conv_other = partner(conv_own)
    second_other = partner(conv_second)
    packed_other = partner(packed)
    others = [partner(w) for w in (attn_in, attn_out, mlp_up, mlp_down, cross_first, cross_second)]
    owns = (attn_in, attn_out, mlp_up, mlp_down, cross_first, cross_second)
    a_in, a_out, a_up, a_down, a_cross_a, a_cross_b = [Side(0, o, p) for o, p in zip(owns, others)]
    t_in, t_out, t_up, t_down, t_cross_a, t_cross_b = [Side(1, o, p) for o, p in zip(owns, others)]

    def ordered(first, second):
        return jnp.where(
            is_first,
            jnp.concatenate([first, second], axis=-1),
            jnp.concatenate([second, first], axis=-1),
        )

    conv_all = ordered(conv_own, conv_other)
    second_all = ordered(conv_second, second_other)
    first_all = jnp.pad(
        conv_all[: 3 * bands].reshape(3, bands, width), ((0, 0), (0, 128 - bands), (0, 0))
    ).reshape(384, width)
    first_bias = conv_all[3 * bands :].astype(f32)
    a_packed = jnp.where(is_first, packed, packed_other).astype(f32)
    t_packed = jnp.where(is_first, packed_other, packed).astype(f32)
    a_small, a_ups = a_packed[:12], a_packed[12:].reshape(1, -1)
    t_small, t_ups = t_packed[:12], t_packed[12:].reshape(1, -1)

    frame_at = jnp.arange(mel_frames, dtype=jnp.int32)
    band_at = jnp.arange(bands, dtype=jnp.int32)
    begin, band = own(time_start), own(freq_start)
    keep = jnp.logical_and(
        jnp.logical_or(band_at < band, band_at >= band + own(freq_width))[:, None],
        jnp.logical_or(frame_at < begin, frame_at >= begin + own(time_width))[None, :],
    )
    mel_clip = own(mel_input)
    masked = jnp.where(keep, mel_clip, jnp.zeros_like(mel_clip)).T.reshape(frames, 2, bands)
    masked = jnp.pad(masked, ((0, 0), (0, 0), (0, 128 - bands)))
    even, odd = masked[:, 0], masked[:, 1]
    taps = jnp.concatenate(
        [jnp.pad(odd, ((1, 0), (0, 0)))[:-1], even, odd, jnp.pad(even, ((0, 1), (0, 0)))[1:]], axis=1
    )

    encoded, even_act, odd_act, even_slope, odd_slope, slope_second = stem(
        taps, first_all, first_bias, second_all, a_small, positions
    )
    a_norm, a_joint = project(encoded, a_in, a_small, audio_block)
    a_mixed, a_logs = attend(a_joint, a_joint, a_joint, (0, 4, 8), False, audio_block)
    a_middle, a_feed_norm, a_hidden, a_slope, a_ending, memory, memory_keys, memory_values = audio_feed(
        encoded, a_mixed, a_out, a_small, a_ups, a_up, a_down, a_cross_a, a_cross_b, audio_block
    )

    text_clip, cot_clip = own(text_embed), own(cotangent)
    t_norm, t_joint = project(text_clip, t_in, t_small, text_block)
    t_mixed, t_logs = attend(t_joint, t_joint, t_joint, (0, 4, 8), True, text_rows)
    t_middle, cross_low, cross_query = text_middle(text_clip, t_mixed, t_out, t_small, t_cross_a, text_block)
    c_mixed, c_logs = attend(cross_query, memory_keys, memory_values, (0, 0, 0), False, text_rows)
    (
        decoded, t_feed_norm, t_hidden, t_pre, cot_low, after_grad, after_low, c_mixed_grad, feed_sums, feed_wide,
    ) = text_feed(
        own(text_len)[None], t_middle, c_mixed, cot_clip, t_cross_b, t_small, t_ups, t_up, t_down, text_block
    )
    query_grad, key_grad, value_grad, c_sums = attend_back(
        cross_query, memory_keys, memory_values, (0, 0, 0), c_logs, c_mixed_grad, False, True, text_rows
    )
    middle_grad, middle_low, t_mixed_grad, cross_sums = text_cross_back(
        query_grad, t_middle, after_grad, t_small, t_cross_a, t_out, text_block
    )
    tq_grad, tk_grad, tv_grad, t_sums = attend_back(
        t_joint, t_joint, t_joint, (0, 4, 8), t_logs, t_mixed_grad, True, False, text_rows
    )
    text_grad, text_sums = project_back(
        tq_grad, tk_grad, tv_grad, text_clip, middle_grad, t_small, t_in, text_block
    )

    end_low, a_pre, a_grad, a_grad_low, a_mixed_grad, a_feed_sums, a_feed_wide = audio_feed_back(
        key_grad, value_grad, a_ending, a_middle, a_slope, a_small, a_cross_a, a_cross_b, a_up, a_down, a_out, audio_block
    )
    aq_grad, ak_grad, av_grad, a_sums = attend_back(
        a_joint, a_joint, a_joint, (0, 4, 8), a_logs, a_mixed_grad, False, False, audio_block
    )
    second_low, next_low, even_low, odd_low, taps_grad, stem_sums = stem_back(
        aq_grad, ak_grad, av_grad, encoded, a_grad, a_small, a_in, slope_second, second_all,
        even_slope, odd_slope, first_all, audio_block,
    )
    odd_grad = taps_grad[:, 256 : 256 + bands] + jnp.pad(taps_grad[1:, 0:bands], ((0, 1), (0, 0)))
    even_grad = taps_grad[:, 128 : 128 + bands] + jnp.pad(taps_grad[:-1, 384 : 384 + bands], ((1, 0), (0, 0)))
    mel_grad = jnp.stack([even_grad, odd_grad], axis=1).reshape(mel_frames, bands).T
    mel_grad = jnp.where(keep, mel_grad, 0.0)

    half = width // 2

    a_rows = jnp.stack(
        [
            stem_sums[0], a_feed_sums[3], a_feed_sums[0], stem_sums[1], a_feed_sums[4], a_feed_sums[1],
            a_sums[0], a_sums[1], a_feed_sums[5], a_feed_sums[2], stem_sums[2], c_sums[1],
        ]
    )
    t_rows = jnp.stack(
        [
            text_sums[0], cross_sums[0], feed_sums[0], text_sums[1], cross_sums[1], feed_sums[1],
            t_sums[0], t_sums[1], cross_sums[2], feed_sums[2], c_sums[0], feed_sums[3],
        ]
    )
    bias_row = jnp.pad(stem_sums[3].reshape(2, 1, half), ((0, 0), (0, 0), (0, half)))
    wide_rows = jnp.stack([a_feed_wide[0].reshape(-1, width), feed_wide[0].reshape(-1, width)])
    small = jnp.concatenate([jnp.stack([a_rows, t_rows]), wide_rows, bias_row], axis=1).astype(low)
    small = jnp.pad(small, ((0, 0), (0, 32 - small.shape[1]), (0, 0)))
    audio = [(a_norm, 0, part, 0) for part in (aq_grad, ak_grad, av_grad)] + [(a_mixed, 0, a_grad_low, 0)]
    audio += [(a_feed_norm, 0, a_pre, n) for n in range(4)] + [(a_hidden, n, end_low, 0) for n in range(4)]
    audio += [(memory, 0, key_grad, 0), (memory, 0, value_grad, 0)]
    text = [(t_norm, 0, part, 0) for part in (tq_grad, tk_grad, tv_grad)] + [(t_mixed, 0, middle_low, 0)]
    text += [(t_feed_norm, 0, t_pre, n) for n in range(4)] + [(t_hidden, n, cot_low, 0) for n in range(4)]
    text += [(cross_low, 0, query_grad, 0), (c_mixed, 0, after_low, 0)]
    conv = [(odd_act, 0, next_low, 0), (even_act, 0, second_low, 0), (odd_act, 0, second_low, 0)]
    flat = weight_grads(audio, text, taps, even_low, odd_low, conv, small, 16 * 512)
    total = reduce_all(flat).astype(f32)

    def tiles(first, count):
        return [total[n * 512 : n * 512 + 512] for n in range(first, first + count)]

    def unfold(start, count):
        part = total[start : start + count]
        return jnp.concatenate([part[:, :half], part[:, half:]], axis=0)

    conv_at = 14 * 512
    small_at = conv_at + 768 + 192
    rows_out = total[small_at : small_at + 12]
    first_grad = unfold(conv_at + 768, 192).reshape(3, 128, half)[:, :bands]

    def swap(array, axis):
        size = array.shape[axis] // 2
        first = lax.slice_in_dim(array, 0, size, axis=axis)
        second = lax.slice_in_dim(array, size, 2 * size, axis=axis)
        keep_part = jnp.where(is_first, first, second)
        got = partner(jnp.where(is_first, second, first).astype(low)).astype(f32)
        return jnp.where(is_first, jnp.stack([keep_part, got]), jnp.stack([got, keep_part]))

    cross_row = lax.ppermute(rows_out[11].astype(low), "section", [(1, 0)]).astype(f32)
    cross_bias = jnp.where(is_first, cross_row[:half], rows_out[11][half:])
    return (
        swap(decoded, 1),
        swap(text_grad, 1),
        swap(mel_grad, 1),
        first_grad,
        total[small_at + 16, :half],
        unfold(conv_at, 768).reshape(3, 512, half),
        rows_out[None, 0:3],
        rows_out[None, 3:6],
        jnp.concatenate(tiles(0, 3), axis=1)[None],
        total[None, 1536:2048],
        jnp.concatenate(tiles(4, 4), axis=1)[None],
        total[None, 4096:6144],
        total[small_at + 12 : small_at + 16].reshape(1, -1),
        rows_out[None, 6:12],
        total[None, 6144:6656],
        total[None, 6656:7168],
        cross_bias,
    )


def solution(mesh):
    return jax.shard_map(
        shards,
        mesh=mesh,
        in_specs=(
            P("dp", None, None),
            P("dp"),
            P("dp"),
            P("dp"),
            P("dp"),
            P("dp"),
            P("dp", None, None),
            P("dp", None, None),
            P(),
            P(None, None, "section"),
            P("section"),
            P(None, None, "section"),
            P("section", None, None),
            P("section", None, None),
            P("section", None, None),
            P("section", None, None),
            P("section", None, None),
            P("section", None, None),
            P("section", None),
            P("section", None, None),
            P("section", None, None),
            P("section", None, None),
        ),
        out_specs=(
            P("dp", None, "section"),
            P("dp", None, "section"),
            P("dp", None, "section"),
            P(None, None, "section"),
            P("section"),
            P(None, None, "section"),
            P("section", None, None),
            P("section", None, None),
            P("section", None, None),
            P("section", None, None),
            P("section", None, None),
            P("section", None, None),
            P("section", None),
            P("section", None, None),
            P("section", None, None),
            P("section", None, None),
            P("section"),
        ),
        check_vma=False,
    )
```

```python
import functools

import jax
import jax.numpy as jnp
from jax import lax
from jax.experimental import pallas as pl
from jax.experimental.pallas import tpu as pltpu
from jax.sharding import PartitionSpec as P

HEADS = 8
epsilon = 1e-05
root_half = 0.7071067811865476
gauss_norm = 0.3989422804014327
log2_e = 1.4426950408889634
VMEM_BYTES = 56 << 20

f32 = jnp.float32
low = jnp.bfloat16


def dot(left, right):
    return lax.dot_general(left, right, (((1,), (0,)), ((), ())), preferred_element_type=f32)


def dot_t(left, right):
    return lax.dot_general(left, right, (((1,), (1,)), ((), ())), preferred_element_type=f32)


def dot_tt(left, right):
    return lax.dot_general(left, right, (((0,), (0,)), ((), ())), preferred_element_type=f32)


def gelu_both(inputs):
    ratio = 1.0 / (1.0 + (0.3275911 * root_half) * jnp.abs(inputs))
    bell = jnp.exp2((-0.5 * log2_e) * inputs * inputs)
    tail = ratio * (
        0.127414796
        + ratio * (-0.142248368 + ratio * (0.7107068705 + ratio * (-0.7265760135 + ratio * 0.5307027145)))
    )
    tail = tail * bell
    below = jnp.where(inputs >= 0.0, 1.0 - tail, tail)
    return inputs * below, below + inputs * bell * gauss_norm


def norm_rows(inputs):
    centred = inputs - jnp.mean(inputs, axis=-1, keepdims=True)
    inverse = lax.rsqrt(jnp.mean(centred * centred, axis=-1, keepdims=True) + epsilon)
    return centred * inverse, inverse


def norm_back(grad, gain, normed, inverse):
    scaled = grad * gain
    return inverse * (
        scaled
        - jnp.mean(scaled, axis=-1, keepdims=True)
        - normed * jnp.mean(scaled * normed, axis=-1, keepdims=True)
    )


def col_sum(inputs):
    return jnp.sum(inputs, axis=0, keepdims=True)


class Side:
    def __init__(self, side, own, other):
        self.side, self.own, self.other, self.shape = side, own, other, own.shape

    def copies(self, mine, own, other, held, sem):
        return [pltpu.make_async_copy(own if mine == self.side else other, held, sem)]


class Split:
    def __init__(self, own, other, groups, apart):
        self.own, self.other, self.groups, self.apart = own, other, groups, apart
        self.shape = (groups * apart, 2 * own.shape[1])

    def copies(self, mine, own, other, held, sem):
        size, half = self.own.shape[0] // self.groups, self.own.shape[1]
        found = []
        for which, ref in ((mine, own), (1 - mine, other)):
            cols = slice(which * half, which * half + half)
            for n in range(self.groups):
                found.append(
                    pltpu.make_async_copy(
                        ref.at[n * size : n * size + size], held.at[n * self.apart : n * self.apart + size, cols], sem
                    )
                )
        return found


def call(body, name, steps, block, ins, outs, scratch=(), reverse=False, flops=0, grid=None):
    arrays, specs, kinds, weight_scratch = [], [], [], []
    at = (lambda i: steps - 1 - i) if reverse else (lambda i: i)
    for array, kind in ins:
        if kind in ("side", "split"):
            arrays += [array.own, array.other]
            specs += [pl.BlockSpec(memory_space=pl.ANY)] * 2
            weight_scratch.append(pltpu.VMEM(array.shape, array.own.dtype))
        elif kind == "rows":
            arrays.append(array)
            specs.append(pl.BlockSpec((block, array.shape[1]), lambda i: (at(i), 0)))
        elif kind == "smem":
            arrays.append(array)
            specs.append(pl.BlockSpec(memory_space=pltpu.SMEM))
        else:
            arrays.append(array)
            specs.append(
                pl.BlockSpec(
                    array.shape,
                    lambda i, n=array.ndim: (0,) * n,
                    pipeline_mode=pl.Buffered(1),
                )
            )
        kinds.append((kind, array if kind in ("side", "split") else None))
    out_specs = [
        pl.BlockSpec((block, shape[1]), lambda i: (at(i), 0))
        if kind == "rows"
        else pl.BlockSpec(shape, lambda i, n=len(shape): (0,) * n)
        for shape, dtype, kind in outs
    ]
    n_in, n_out, n_weight = len(arrays), len(outs), len(weight_scratch)

    def kernel(*refs):
        in_refs, out_refs = refs[:n_in], refs[n_in : n_in + n_out]
        weights = refs[n_in + n_out : n_in + n_out + n_weight]
        extra = refs[n_in + n_out + n_weight :]
        given, r, w, loads = [], 0, 0, []
        for kind, array in kinds:
            if kind in ("side", "split"):
                loads.append((array, in_refs[r], in_refs[r + 1], weights[w]))
                given.append(weights[w])
                r, w = r + 2, w + 1
            else:
                given.append(in_refs[r])
                r += 1
        step = pl.program_id(0)
        if loads:
            sem = extra[-1]
            extra = extra[:-1]

            @pl.when(step == 0)
            def _():
                mine = lax.axis_index("section")
                for n, load in enumerate(loads):
                    for which in range(2):

                        @pl.when(mine == which)
                        def _(load=load, n=n, which=which):
                            array, own, other, held = load
                            for copy in array.copies(which, own, other, held, sem.at[n]):
                                copy.start()

                for n, (array, own, other, held) in enumerate(loads):
                    for copy in array.copies(0, own, other, held, sem.at[n]):
                        copy.wait()

        for ref, (shape, dtype, kind) in zip(out_refs, outs):
            if kind == "sums":

                @pl.when(step == 0)
                def _(ref=ref):
                    ref[...] = jnp.zeros(ref.shape, ref.dtype)

        body(step, given, out_refs, extra)

    scratch_shapes = weight_scratch + list(scratch)
    if weight_scratch:
        scratch_shapes.append(pltpu.SemaphoreType.DMA((n_weight,)))
    total = sum(a.size * a.dtype.itemsize for a in arrays) + sum(
        2 * s[0] * s[1] for s, d, k in outs
    )
    return pl.pallas_call(
        kernel,
        name=name,
        grid=(steps,),
        in_specs=specs,
        out_specs=out_specs,
        out_shape=[jax.ShapeDtypeStruct(shape, dtype) for shape, dtype, kind in outs],
        scratch_shapes=scratch_shapes,
        compiler_params=pltpu.CompilerParams(
            dimension_semantics=("arbitrary",), vmem_limit_bytes=VMEM_BYTES
        ),
        cost_estimate=pl.CostEstimate(flops=int(flops), bytes_accessed=int(total), transcendentals=0),
    )(*arrays)


def row(ref, n):
    return ref[n : n + 1, :].astype(f32)


def clear_pads(weight, bands):
    for n in range(3):
        weight[n * 128 + bands : n * 128 + 128, :] = jnp.zeros((128 - bands, weight.shape[1]), weight.dtype)


def stem(taps, weight, bias, second, smalls, positions, bands):
    rows, width = positions.shape
    block = 256

    def body(step, given, outs, extra):
        taps, weight, bias, second, smalls, positions = given
        encoded, even_out, odd_out, even_slope, odd_slope, slope_out = outs
        (carry,) = extra

        @pl.when(step == 0)
        def _():
            carry[...] = jnp.zeros(carry.shape, f32)
            clear_pads(weight, bands)

        pre = dot(taps[:, 0:384], weight[...]) + bias[...].astype(f32)
        value, slope = gelu_both(pre)
        even = value.astype(low)
        even_out[...] = even
        even_slope[...] = slope.astype(low)
        pre = dot(taps[:, 128:512], weight[...]) + bias[...].astype(f32)
        value, slope = gelu_both(pre)
        odd = value.astype(low)
        odd_out[...] = odd
        odd_slope[...] = slope.astype(low)
        prior = dot(odd, second[0:width])
        moved = pltpu.roll(prior, 1, 0)
        at_row = lax.broadcasted_iota(jnp.int32, (block, width), 0)
        moved = jnp.where(at_row == 0, carry[0:1, :], moved)
        carry[0:1, :] = prior[block - 1 : block, :]
        pre = moved + dot(even, second[width : 2 * width]) + dot(odd, second[2 * width :]) + row(smalls, 10)
        value, slope = gelu_both(pre)
        slope_out[...] = slope.astype(low)
        encoded[...] = value + positions[...].astype(f32)

    shape = (rows, width)
    return call(
        body, "stem", rows // block, block,
        [(taps, "rows"), (weight, "split"), (bias, "full"), (second, "split"), (smalls, "full"), (positions, "rows")],
        [(shape, f32, "rows")] + [(shape, low, "rows")] * 5,
        scratch=[pltpu.VMEM((8, width), f32)],
        flops=2 * rows * width * (768 + 3 * width),
    )


def write_halves(values, keep, send):
    half = values.shape[1] // 2
    mine = lax.axis_index("section")
    first, second = values[:, :half], values[:, half:]

    @pl.when(mine == 0)
    def _():
        keep[...] = first
        send[...] = second.astype(low)

    @pl.when(mine != 0)
    def _():
        keep[...] = second
        send[...] = first.astype(low)


def project(inputs, weight, smalls, block):
    rows, width = inputs.shape

    def body(step, given, outs, extra):
        inputs, weight, smalls = given
        low_out, joint_out = outs
        normed, inverse = norm_rows(inputs[...].astype(f32))
        rounded = (normed * row(smalls, 0) + row(smalls, 3)).astype(low)
        low_out[...] = rounded
        part = dot(rounded, weight[:, :width])
        joint_out[:, :width] = (part + row(smalls, 6)).astype(low) * 0.125
        joint_out[:, width : 2 * width] = dot(rounded, weight[:, width : 2 * width]).astype(low)
        part = dot(rounded, weight[:, 2 * width :])
        joint_out[:, 2 * width :] = (part + row(smalls, 7)).astype(low)

    return call(
        body, "project", rows // block, block,
        [(inputs, "rows"), (weight, "side"), (smalls, "full")],
        [((rows, width), low, "rows"), ((rows, 3 * width), low, "rows")],
        flops=6 * rows * width * width,
    )


def attend(queries, keys, values, cols, causal, block):
    rows, key_rows = queries.shape[0], keys.shape[0]
    pairs, steps = HEADS // 2, rows // block

    def kernel(query_ref, key_ref, value_ref, mixed_ref, log_ref):
        lane = lax.broadcasted_iota(jnp.int32, (1, 128), 1)
        query, key, value = query_ref[...], key_ref[...], value_ref[...]
        mixed, logs = [], []
        for head in range(2):
            part = jnp.where(lane // 64 == head, query, jnp.zeros_like(query))
            scores = dot_t(part, key)
            if causal:
                key_at = lax.broadcasted_iota(jnp.int32, scores.shape, 1)
                query_at = lax.broadcasted_iota(jnp.int32, scores.shape, 0) + pl.program_id(1) * block
                scores = jnp.where(key_at <= query_at, scores, -1e30)
            top = jnp.max(scores, axis=1, keepdims=True) * log2_e
            exponent = jnp.exp2(scores * log2_e - top)
            total = jnp.sum(exponent, axis=1, keepdims=True)
            mixed.append(dot(exponent.astype(low), value) * (1.0 / total))
            logs.append(top + jnp.log2(total))
        mixed_ref[...] = jnp.where(lane < 64, mixed[0], mixed[1]).astype(low)
        both = jnp.where(lane == 0, logs[0], logs[1])
        log_ref[...] = both.T[0:8, :]

    q_at, k_at, v_at = cols
    return pl.pallas_call(
        kernel,
        name="attend",
        grid=(pairs, steps),
        in_specs=[
            pl.BlockSpec((block, 128), lambda h, i: (i, q_at + h)),
            pl.BlockSpec((key_rows, 128), lambda h, i: (0, k_at + h)),
            pl.BlockSpec((key_rows, 128), lambda h, i: (0, v_at + h)),
        ],
        out_specs=[
            pl.BlockSpec((block, 128), lambda h, i: (i, h)),
            pl.BlockSpec((8, block), lambda h, i: (h, i)),
        ],
        out_shape=[
            jax.ShapeDtypeStruct((rows, 128 * pairs), low),
            jax.ShapeDtypeStruct((8 * pairs, rows), f32),
        ],
        compiler_params=pltpu.CompilerParams(
            dimension_semantics=("arbitrary", "arbitrary"), vmem_limit_bytes=VMEM_BYTES
        ),
        cost_estimate=pl.CostEstimate(
            flops=16 * rows * key_rows * 512, bytes_accessed=2 * 512 * (2 * rows + 2 * key_rows), transcendentals=0
        ),
    )(queries, keys, values)


def attend_back(queries, keys, values, cols, logs, grad, causal, round_sums, block):
    rows, key_rows = queries.shape[0], keys.shape[0]
    pairs, steps = HEADS // 2, rows // block

    def kernel(
        query_ref, key_ref, value_ref, log_ref, grad_ref,
        query_out, key_out, value_out, sum_out, key_acc, value_acc, key_turned,
    ):
        step = pl.program_id(1)
        lane = lax.broadcasted_iota(jnp.int32, (1, 128), 1)

        @pl.when(step == 0)
        def _():
            key_acc[...] = jnp.zeros(key_acc.shape, f32)
            value_acc[...] = jnp.zeros(value_acc.shape, f32)
            sum_out[...] = jnp.zeros(sum_out.shape, f32)
            key_turned[...] = key_ref[...].astype(f32).T.astype(low)

        query, key, value, grad = query_ref[...], key_ref[...], value_ref[...], grad_ref[...]
        turned = key_turned[...]
        sub = lax.broadcasted_iota(jnp.int32, (128, 1), 0)
        query_turned = jnp.zeros((128, block), f32)
        for head in range(2):
            part = jnp.where(lane // 64 == head, query, jnp.zeros_like(query))
            grad_part = jnp.where(lane // 64 == head, grad, jnp.zeros_like(grad))
            scores = dot_t(key, part)
            chance = jnp.exp2(scores * log2_e - log_ref[head : head + 1, :])
            if causal:
                key_at = lax.broadcasted_iota(jnp.int32, scores.shape, 0)
                query_at = lax.broadcasted_iota(jnp.int32, scores.shape, 1) + step * block
                chance = jnp.where(key_at <= query_at, chance, 0.0)
            grad_chance = dot_t(value, grad_part)
            product = chance * grad_chance
            grad_scores = (product - chance * jnp.sum(product, axis=0, keepdims=True)).astype(low)
            value_acc[...] += dot(chance.astype(low), grad_part)
            key_acc[...] += dot(grad_scores, part)
            query_turned += dot(jnp.where(sub // 64 == head, turned, jnp.zeros_like(turned)), grad_scores)
        grad_query = query_turned.T * 0.125
        query_out[...] = grad_query.astype(low)
        sum_out[0:1, :] += col_sum(grad_query)

        @pl.when(step == steps - 1)
        def _():
            key_out[...] = key_acc[...].astype(low)
            rounded = value_acc[...].astype(low)
            value_out[...] = rounded
            sum_out[1:2, :] = col_sum(rounded.astype(f32) if round_sums else value_acc[...])

    q_at, k_at, v_at = cols
    row_spec = pl.BlockSpec((block, 128), lambda h, i: (i, h))
    key_spec = pl.BlockSpec((key_rows, 128), lambda h, i: (0, h))
    return pl.pallas_call(
        kernel,
        name="attend_back",
        grid=(pairs, steps),
        in_specs=[
            pl.BlockSpec((block, 128), lambda h, i: (i, q_at + h)),
            pl.BlockSpec((key_rows, 128), lambda h, i: (0, k_at + h)),
            pl.BlockSpec((key_rows, 128), lambda h, i: (0, v_at + h)),
            pl.BlockSpec((8, block), lambda h, i: (h, i)),
            row_spec,
        ],
        out_specs=[row_spec, key_spec, key_spec, pl.BlockSpec((8, 128), lambda h, i: (0, h))],
        out_shape=[
            jax.ShapeDtypeStruct((rows, 128 * pairs), low),
            jax.ShapeDtypeStruct((key_rows, 128 * pairs), low),
            jax.ShapeDtypeStruct((key_rows, 128 * pairs), low),
            jax.ShapeDtypeStruct((8, 128 * pairs), f32),
        ],
        scratch_shapes=[
            pltpu.VMEM((key_rows, 128), f32),
            pltpu.VMEM((key_rows, 128), f32),
            pltpu.VMEM((128, key_rows), low),
        ],
        compiler_params=pltpu.CompilerParams(
            dimension_semantics=("arbitrary", "arbitrary"), vmem_limit_bytes=VMEM_BYTES
        ),
        cost_estimate=pl.CostEstimate(
            flops=40 * rows * key_rows * 512, bytes_accessed=2 * 512 * (4 * rows + 4 * key_rows), transcendentals=0
        ),
    )(queries, keys, values, logs, grad)


def audio_feed(inputs, mixed, weight_out, smalls, ups, weight_up, weight_down, cross_a, cross_b, block):
    rows, width = inputs.shape
    hidden = ups.shape[1]

    def body(step, given, outs, extra):
        inputs, mixed, weight_out, smalls, ups, weight_up, weight_down, cross_a, cross_b = given
        middle_out, norm_out, hidden_out, slope_out, ending_out, memory_out, key_out, value_out = outs
        middle = inputs[...] + dot(mixed[...], weight_out[...]) + row(smalls, 8)
        middle_out[...] = middle
        normed, inverse = norm_rows(middle)
        rounded = (normed * row(smalls, 1) + row(smalls, 4)).astype(low)
        norm_out[...] = rounded
        ending = middle + row(smalls, 9)
        for part in range(hidden // 512):
            cols = slice(part * 512, part * 512 + 512)
            pre = dot(rounded, weight_up[:, cols]) + ups[:, cols].astype(f32)
            value, slope = gelu_both(pre)
            act = value.astype(low)
            hidden_out[:, cols] = act
            slope_out[:, cols] = slope.astype(low)
            ending += dot(act, weight_down[cols, :])
        ending_out[...] = ending
        normed, inverse = norm_rows(ending)
        memory = (normed * row(smalls, 2) + row(smalls, 5)).astype(low)
        memory_out[...] = memory
        key_out[...] = dot(memory, cross_a[...]).astype(low)
        value_out[...] = (dot(memory, cross_b[...]) + row(smalls, 11)).astype(low)

    wide, shape = (rows, hidden), (rows, width)
    return call(
        body, "audio_feed", rows // block, block,
        [(inputs, "rows"), (mixed, "rows"), (weight_out, "side"), (smalls, "full"), (ups, "full"),
         (weight_up, "side"), (weight_down, "side"), (cross_a, "side"), (cross_b, "side")],
        [(shape, f32, "rows"), (shape, low, "rows"), (wide, low, "rows"), (wide, low, "rows"),
         (shape, f32, "rows"), (shape, low, "rows"), (shape, low, "rows"), (shape, low, "rows")],
        flops=2 * rows * width * (3 * width + 2 * hidden),
    )


def text_middle(inputs, mixed, weight_out, smalls, cross_a, block):
    rows, width = inputs.shape

    def body(step, given, outs, extra):
        inputs, mixed, weight_out, smalls, cross_a = given
        middle_out, low_out, query_out = outs
        middle = inputs[...].astype(f32) + dot(mixed[...], weight_out[...]) + row(smalls, 8)
        middle_out[...] = middle
        normed, inverse = norm_rows(middle)
        rounded = (normed * row(smalls, 1) + row(smalls, 4)).astype(low)
        low_out[...] = rounded
        query_out[...] = (dot(rounded, cross_a[...]) + row(smalls, 10)).astype(low) * 0.125

    shape = (rows, width)
    return call(
        body, "text_middle", rows // block, block,
        [(inputs, "rows"), (mixed, "rows"), (weight_out, "side"), (smalls, "full"), (cross_a, "side")],
        [(shape, f32, "rows"), (shape, low, "rows"), (shape, low, "rows")],
        flops=4 * rows * width * width,
    )


def text_feed(length, middle, mixed, cotangent, cross_b, smalls, ups, weight_up, weight_down, block):
    rows, width = middle.shape
    hidden = ups.shape[1]

    def body(step, given, outs, extra):
        length, middle, mixed, cotangent, cross_b, smalls, ups, weight_up, weight_down = given
        decoded_keep, decoded_send, norm_out, hidden_out, pre_out, cot_out, grad_out, grad_low, mixed_out, sums, wide_sums = outs
        after = middle[...] + dot(mixed[...], cross_b[...]) + row(smalls, 11)
        normed, inverse = norm_rows(after)
        rounded = (normed * row(smalls, 2) + row(smalls, 5)).astype(low)
        norm_out[...] = rounded
        at_row = lax.broadcasted_iota(jnp.int32, (block, 1), 0) + step * block
        valid = at_row < length[0]
        grad = jnp.where(valid, cotangent[...].astype(f32), 0.0)
        cot = grad.astype(low)
        cot_out[...] = cot
        ending = after + row(smalls, 9)
        back = jnp.zeros((block, width), f32)
        for part in range(hidden // 512):
            cols = slice(part * 512, part * 512 + 512)
            pre = dot(rounded, weight_up[:, cols]) + ups[:, cols].astype(f32)
            value, slope = gelu_both(pre)
            act = value.astype(low)
            hidden_out[:, cols] = act
            ending += dot(act, weight_down[cols, :])
            grad_pre = dot_t(cot, weight_down[cols, :]) * slope
            wide_sums[0:1, cols] += col_sum(grad_pre)
            pre_low = grad_pre.astype(low)
            pre_out[:, cols] = pre_low
            back += dot_t(pre_low, weight_up[:, cols])
        write_halves(jnp.where(valid, ending, 0.0), decoded_keep, decoded_send)
        sums[0:1, :] += col_sum(back * normed)
        sums[1:2, :] += col_sum(back)
        sums[2:3, :] += col_sum(grad)
        grad = grad + norm_back(back, row(smalls, 2), normed, inverse)
        sums[3:4, :] += col_sum(grad)
        grad_out[...] = grad
        rounded = grad.astype(low)
        grad_low[...] = rounded
        mixed_out[...] = dot_t(rounded, cross_b[...]).astype(low)

    wide, shape = (rows, hidden), (rows, width)
    return call(
        body, "text_feed", rows // block, block,
        [(length, "smem"), (middle, "rows"), (mixed, "rows"), (cotangent, "rows"), (cross_b, "side"),
         (smalls, "full"), (ups, "full"), (weight_up, "side"), (weight_down, "side")],
        [((rows, width // 2), f32, "rows"), ((rows, width // 2), low, "rows"), (shape, low, "rows"), (wide, low, "rows"),
         (wide, low, "rows"), (shape, low, "rows"), (shape, f32, "rows"), (shape, low, "rows"), (shape, low, "rows"),
         ((8, width), f32, "sums"), ((8, hidden), f32, "sums")],
        flops=2 * rows * width * (2 * width + 4 * hidden),
    )


def text_cross_back(query_grad, middle, grad, smalls, cross_a, weight_out, block):
    rows, width = middle.shape

    def body(step, given, outs, extra):
        query_grad, middle, grad, smalls, cross_a, weight_out = given
        grad_out, low_out, mixed_out, sums = outs
        back = dot_t(query_grad[...], cross_a[...])
        normed, inverse = norm_rows(middle[...])
        sums[0:1, :] += col_sum(back * normed)
        sums[1:2, :] += col_sum(back)
        total = grad[...] + norm_back(back, row(smalls, 1), normed, inverse)
        sums[2:3, :] += col_sum(total)
        grad_out[...] = total
        rounded = total.astype(low)
        low_out[...] = rounded
        mixed_out[...] = dot_t(rounded, weight_out[...]).astype(low)

    shape = (rows, width)
    return call(
        body, "text_cross_back", rows // block, block,
        [(query_grad, "rows"), (middle, "rows"), (grad, "rows"), (smalls, "full"), (cross_a, "side"), (weight_out, "side")],
        [(shape, f32, "rows"), (shape, low, "rows"), (shape, low, "rows"), ((8, width), f32, "sums")],
        flops=4 * rows * width * width,
    )


def project_back(query_grad, key_grad, value_grad, inputs, grad, smalls, weight, block):
    rows, width = inputs.shape

    def body(step, given, outs, extra):
        query_grad, key_grad, value_grad, inputs, grad, smalls, weight = given
        grad_keep, grad_send, sums = outs
        back = (
            dot_t(query_grad[...], weight[:, :width])
            + dot_t(key_grad[...], weight[:, width : 2 * width])
            + dot_t(value_grad[...], weight[:, 2 * width :])
        )
        normed, inverse = norm_rows(inputs[...].astype(f32))
        sums[0:1, :] += col_sum(back * normed)
        sums[1:2, :] += col_sum(back)
        write_halves(grad[...] + norm_back(back, row(smalls, 0), normed, inverse), grad_keep, grad_send)

    return call(
        body, "project_back", rows // block, block,
        [(query_grad, "rows"), (key_grad, "rows"), (value_grad, "rows"), (inputs, "rows"), (grad, "rows"),
         (smalls, "full"), (weight, "side")],
        [((rows, width // 2), f32, "rows"), ((rows, width // 2), low, "rows"), ((8, width), f32, "sums")],
        flops=6 * rows * width * width,
    )


def audio_feed_back(key_grad, value_grad, ending, middle, slope, smalls, cross_a, cross_b, weight_up, weight_down, weight_out, block):
    rows, width = ending.shape
    hidden = slope.shape[1]

    def body(step, given, outs, extra):
        key_grad, value_grad, ending, middle, slope, smalls, cross_a, cross_b, weight_up, weight_down, weight_out = given
        end_low, pre_out, grad_out, grad_low, mixed_out, sums, wide_sums = outs
        back = dot_t(key_grad[...], cross_a[...]) + dot_t(value_grad[...], cross_b[...])
        normed, inverse = norm_rows(ending[...])
        sums[0:1, :] += col_sum(back * normed)
        sums[1:2, :] += col_sum(back)
        grad = norm_back(back, row(smalls, 2), normed, inverse)
        sums[2:3, :] += col_sum(grad)
        rounded = grad.astype(low)
        end_low[...] = rounded
        back = jnp.zeros((block, width), f32)
        for part in range(hidden // 512):
            cols = slice(part * 512, part * 512 + 512)
            grad_pre = dot_t(rounded, weight_down[cols, :]) * slope[:, cols].astype(f32)
            wide_sums[0:1, cols] += col_sum(grad_pre)
            pre_low = grad_pre.astype(low)
            pre_out[:, cols] = pre_low
            back += dot_t(pre_low, weight_up[:, cols])
        normed, inverse = norm_rows(middle[...])
        sums[3:4, :] += col_sum(back * normed)
        sums[4:5, :] += col_sum(back)
        grad = grad + norm_back(back, row(smalls, 1), normed, inverse)
        sums[5:6, :] += col_sum(grad)
        grad_out[...] = grad
        rounded = grad.astype(low)
        grad_low[...] = rounded
        mixed_out[...] = dot_t(rounded, weight_out[...]).astype(low)

    wide, shape = (rows, hidden), (rows, width)
    return call(
        body, "audio_feed_back", rows // block, block,
        [(key_grad, "rows"), (value_grad, "rows"), (ending, "rows"), (middle, "rows"), (slope, "rows"), (smalls, "full"),
         (cross_a, "side"), (cross_b, "side"), (weight_up, "side"), (weight_down, "side"), (weight_out, "side")],
        [(shape, low, "rows"), (wide, low, "rows"), (shape, f32, "rows"), (shape, low, "rows"), (shape, low, "rows"),
         ((8, width), f32, "sums"), ((8, hidden), f32, "sums")],
        flops=2 * rows * width * (3 * width + 2 * hidden),
    )


def stem_back(query_grad, key_grad, value_grad, encoded, grad, smalls, weight, slope_second, second, even_slope, odd_slope, first, block, bands):
    rows, width = encoded.shape

    def body(step, given, outs, extra):
        query_grad, key_grad, value_grad, encoded, grad, smalls, weight, slope_second, second, even_slope, odd_slope, first = given
        second_low, next_low, even_low, odd_low, taps_out, sums = outs
        (carry,) = extra

        @pl.when(step == 0)
        def _():
            carry[...] = jnp.zeros(carry.shape, f32)
            clear_pads(first, bands)

        back = (
            dot_t(query_grad[...], weight[:, :width])
            + dot_t(key_grad[...], weight[:, width : 2 * width])
            + dot_t(value_grad[...], weight[:, 2 * width :])
        )
        normed, inverse = norm_rows(encoded[...])
        sums[0:1, :] += col_sum(back * normed)
        sums[1:2, :] += col_sum(back)
        total = grad[...] + norm_back(back, row(smalls, 0), normed, inverse)
        total = total * slope_second[...].astype(f32)
        sums[2:3, :] += col_sum(total)
        rounded = total.astype(low)
        second_low[...] = rounded
        at_row = lax.broadcasted_iota(jnp.int32, (block, width), 0)
        wide = rounded.astype(f32)
        moved = jnp.where(at_row == block - 1, carry[0:1, :], pltpu.roll(wide, block - 1, 0))
        carry[0:1, :] = wide[0:1, :]
        moved = moved.astype(low)
        next_low[...] = moved
        moved = dot_t(moved, second[0:width])
        grad_even = dot_t(rounded, second[width : 2 * width]) * even_slope[...].astype(f32)
        grad_odd = (dot_t(rounded, second[2 * width :]) + moved) * odd_slope[...].astype(f32)
        sums[3:4, :] += col_sum(grad_even) + col_sum(grad_odd)
        grad_even = grad_even.astype(low)
        grad_odd = grad_odd.astype(low)
        even_low[...] = grad_even
        odd_low[...] = grad_odd
        taps_even = dot_t(grad_even, first[...])
        taps_odd = dot_t(grad_odd, first[...])
        taps_out[:, 0:128] = taps_even[:, 0:128]
        taps_out[:, 128:256] = taps_even[:, 128:256] + taps_odd[:, 0:128]
        taps_out[:, 256:384] = taps_even[:, 256:384] + taps_odd[:, 128:256]
        taps_out[:, 384:512] = taps_odd[:, 256:384]

    shape = (rows, width)
    return call(
        body, "stem_back", rows // block, block,
        [(query_grad, "rows"), (key_grad, "rows"), (value_grad, "rows"), (encoded, "rows"), (grad, "rows"), (smalls, "full"),
         (weight, "side"), (slope_second, "rows"), (second, "split"), (even_slope, "rows"), (odd_slope, "rows"), (first, "split")],
        [(shape, low, "rows")] * 4 + [((rows, 512), f32, "rows"), ((8, width), f32, "sums")],
        scratch=[pltpu.VMEM((8, width), f32)],
        reverse=True,
        flops=2 * rows * width * (6 * width + 768),
    )


def exchange(split, whole, collective_id):
    n_split, n_all = len(split), len(split) + len(whole)
    arrays = split + whole

    def kernel(*refs):
        sources, targets = refs[:n_all], refs[n_all : 2 * n_all]
        side_sem, near_sem, core_sem = refs[2 * n_all :]
        section, replica = lax.axis_index("section"), lax.axis_index("dp")
        quarter = replica % 4
        near_quarter = (quarter + 2) % 4
        side_peer = {"section": 1 - section}
        near_peer = {"dp": replica + near_quarter - quarter}
        core_peer = {"dp": replica + 1 - 2 * (replica % 2)}

        def remote(source, target, sems, at, device):
            return pltpu.make_async_remote_copy(
                src_ref=source, dst_ref=target, send_sem=sems.at[(0,) + at], recv_sem=sems.at[(1,) + at],
                device_id=device, device_id_type=pl.DeviceIdType.MESH,
            )

        def part(n, q):
            size = arrays[n].shape[0] // 4
            return pl.ds(pl.multiple_of(q * size, size), size)

        def side_copy(n):
            if n >= n_split:
                return remote(sources[n], targets[n], side_sem, (n,), side_peer)
            here = part(n, quarter)
            return remote(sources[n].at[here], targets[n].at[here], side_sem, (n,), side_peer)

        def near_copy(n):
            here = targets[n].at[part(n, quarter)]
            return remote(here, here, near_sem, (n,), near_peer)

        def core_copy(n, b):
            here = targets[n].at[part(n, near_quarter if b else quarter)]
            return remote(here, here, core_sem, (b, n), core_peer)

        barrier = pltpu.get_barrier_semaphore()
        peers = (side_peer, near_peer, core_peer)
        for device in peers:
            pl.semaphore_signal(barrier, inc=1, device_id=device, device_id_type=pl.DeviceIdType.MESH)
        pl.semaphore_wait(barrier, len(peers))
        order = list(range(n_split, n_all)) + list(range(n_split))
        for n in order:
            side_copy(n).start()
        for n in range(n_split + 1):
            if n < n_split:
                side_copy(n).wait_recv()
                near_copy(n).start()
                core_copy(n, 0).start()
            if n > 0:
                near_copy(n - 1).wait_recv()
                core_copy(n - 1, 1).start()
        for n in range(n_split, n_all):
            side_copy(n).wait_recv()
        for n in range(n_all):
            side_copy(n).wait_send()
        for n in range(n_split):
            near_copy(n).wait_send()
            for b in range(2):
                core_copy(n, b).wait()

    def sems(*shape):
        return pltpu.SemaphoreType.DMA(shape)

    return pl.pallas_call(
        kernel,
        name="exchange",
        in_specs=[pl.BlockSpec(memory_space=pl.ANY)] * n_all,
        out_specs=[pl.BlockSpec(memory_space=pl.ANY)] * n_all,
        out_shape=[jax.ShapeDtypeStruct(a.shape, a.dtype) for a in arrays],
        scratch_shapes=[sems(2, n_all), sems(2, n_all), sems(2, 2, n_all)],
        compiler_params=pltpu.CompilerParams(collective_id=collective_id, has_side_effects=True),
        cost_estimate=pl.CostEstimate(
            flops=0, bytes_accessed=80 * sum(a.size for a in arrays), transcendentals=0
        ),
    )(*arrays)


def unpack(total, bands):
    width, half = total.shape[1], total.shape[1] // 2

    def kernel(tile, joint, out, up, down, cross_a, cross_b, first, bias, second, gain, shift, wide, small, cross):
        step = pl.program_id(0)

        def when(cond, ref, value):
            @pl.when(cond)
            def _():
                ref[...] = value().reshape(ref.shape).astype(f32)

        full = lambda: tile[...]
        when(step < 4, up, full)
        when(jnp.logical_and(step >= 4, step < 8), down, full)
        when(step == 8, cross_a, full)
        when(step == 9, cross_b, full)
        when(step == 10, out, full)
        when(jnp.logical_and(step >= 11, step < 14), joint, full)

        @pl.when(step == 14)
        def _():
            second[0] = tile[:, 0:half].astype(f32)
            second[1, half:width] = tile[0:half, half:width].astype(f32)
            second[2, 0:half] = tile[half:width, half:width].astype(f32)

        @pl.when(step == 15)
        def _():
            second[1, 0:half] = tile[0:half, 0:half].astype(f32)
            second[2, half:width] = tile[0:half, half:width].astype(f32)
            first[0] = tile[half : half + bands, 0:half].astype(f32)
            first[1, 0:64] = tile[half + 128 : half + 192, 0:half].astype(f32)
            first[1, 64:bands] = tile[half : half + bands - 64, half:width].astype(f32)
            first[2] = tile[half + 64 : half + 64 + bands, half:width].astype(f32)
            rows = tile[half + 192 : half + 224, :].astype(f32)
            gain[0] = rows[0:3]
            shift[0] = rows[3:6]
            small[0] = rows[6:12]
            for n in range(4):
                wide[:, n * width : (n + 1) * width] = rows[12 + n : 13 + n]
            bias[...] = rows[16:17, 0:half]
            cross[...] = rows[17:18]

    def fixed(*shape):
        return pl.BlockSpec(shape, lambda i, n=len(shape): (0,) * n)

    shapes = [
        (1, width, 3 * width), (1, width, width), (1, width, 4 * width), (1, 4 * width, width), (1, width, width), (1, width, width),
        (3, bands, half), (1, half), (3, width, half), (1, 3, width), (1, 3, width), (1, 4 * width), (1, 6, width), (1, width),
    ]
    square = (1, width, width)
    return pl.pallas_call(
        kernel,
        name="unpack",
        grid=(16,),
        in_specs=[pl.BlockSpec((width, width), lambda i: (i, 0))],
        out_specs=[
            pl.BlockSpec(square, lambda i: (0, 0, jnp.clip(i - 11, 0, 2))),
            fixed(*square),
            pl.BlockSpec(square, lambda i: (0, 0, jnp.clip(i, 0, 3))),
            pl.BlockSpec(square, lambda i: (0, jnp.clip(i - 4, 0, 3), 0)),
            fixed(*square), fixed(*square),
            *[fixed(*shape) for shape in shapes[6:]],
        ],
        out_shape=[jax.ShapeDtypeStruct(shape, f32) for shape in shapes],
        compiler_params=pltpu.CompilerParams(
            dimension_semantics=("arbitrary",), vmem_limit_bytes=VMEM_BYTES
        ),
        cost_estimate=pl.CostEstimate(flops=0, bytes_accessed=6 * total.size, transcendentals=0),
    )(total)


def finish(parts):
    def kernel(*refs):
        mine = lax.axis_index("section")
        for n in range(len(parts)):
            out = refs[2 * len(parts) + n]
            out[mine] = refs[2 * n][...]
            out[1 - mine] = refs[2 * n + 1][...].astype(f32)

    flat = [array for pair in parts for array in pair]
    return pl.pallas_call(
        kernel,
        name="finish",
        out_shape=[jax.ShapeDtypeStruct((2,) + keep.shape, f32) for keep, got in parts],
        compiler_params=pltpu.CompilerParams(vmem_limit_bytes=VMEM_BYTES),
        cost_estimate=pl.CostEstimate(flops=0, bytes_accessed=sum(8 * a.size for a in flat), transcendentals=0),
    )(*flat)


def begin(mel_input, spans, gain, shift, biases, up_bias, first_bias, first, second, joint_weight, weights, positions):
    frames, width = positions.shape
    bands, mel_frames = mel_input.shape[1:]
    lanes = width // 2
    hidden = up_bias.shape[1]
    block = 256
    blocks = frames // block
    sent = [second, joint_weight] + weights
    n_sent = len(sent)
    pieces = []
    for n, array in enumerate(sent):
        cuts = 2 if array.size >= 700000 else 1
        size = array.shape[0] // cuts
        pieces += [(n, c * size, size) for c in range(cuts)]
    n_pieces = len(pieces)
    flying = 2
    first_held = Split(first, first, 3, 128)
    second_held = Split(second, second, 3, width)
    n_any = n_sent + 3

    def kernel(*refs):
        mel_ref, positions_ref, first_ref = refs[:3]
        own = refs[3:n_any]
        times, time_spans, bands_from, band_spans = refs[n_any : n_any + 4]
        gain, shift, biases, up_bias, first_bias = refs[n_any + 4 : n_any + 9]
        outs = refs[n_any + 9 :]
        first_other = outs[0]
        other = outs[1 : 1 + n_sent]
        a_small, t_small, a_ups, t_ups = outs[1 + n_sent : 5 + n_sent]
        results = outs[5 + n_sent : 16 + n_sent]
        (
            taps, encoded, even_act, odd_act, even_slope, odd_slope, slope_second, norm, joint, mixed, logs,
            mel, turned, place, conv_first, conv_second, weight, carry, pack, pack_other,
            load_sem, weight_sem, out_sem, side_sem, near_sem, core_sem,
        ) = outs[16 + n_sent :]
        held = (taps, encoded, even_act, odd_act, even_slope, odd_slope, slope_second, norm, joint, mixed, logs)

        section, replica = lax.axis_index("section"), lax.axis_index("dp")
        side_peer = {"section": 1 - section}

        def flipped(value, bit):
            return value + bit - 2 * bit * ((value // bit) % 2)

        def peer(bit):
            return {"dp": flipped(replica, bit)}

        def remote(source, target, sems, at, device):
            return pltpu.make_async_remote_copy(
                src_ref=source, dst_ref=target, send_sem=sems.at[(0,) + at], recv_sem=sems.at[(1,) + at],
                device_id=device, device_id_type=pl.DeviceIdType.MESH,
            )

        def part(p, q):
            n, start, size = pieces[p]
            return pl.ds(pl.multiple_of(start + q * (size // 4), 16), size // 4)

        def near(p):
            bit = 4 if p % 2 else 2
            quarter = replica % 2 + 2 * ((replica // bit) % 2)
            return bit, (quarter, flipped(quarter, 2))

        def side_copy(p):
            n = pieces[p][0]
            here = part(p, near(p)[1][0])
            return remote(own[n].at[here], other[n].at[here], side_sem, (p,), side_peer)

        def pass_on(p, q, sems, at, bit):
            here = other[pieces[p][0]].at[part(p, q)]
            return remote(here, here, sems, at, peer(bit))

        def near_copies(p):
            bit, quarters = near(p)
            return [pass_on(p, quarters[0], near_sem, (p,), bit)]

        def core_copies(p):
            return [pass_on(p, q, core_sem, (b, p), 1) for b, q in enumerate(near(p)[1])]

        hops = (lambda p: [side_copy(p)], near_copies, core_copies)

        def advance(p, n):
            for copy in hops[n](p):
                copy.wait_recv()
            if n == 0 and p + flying < n_pieces:
                side_copy(p + flying).start()
            if n + 1 < len(hops):
                for copy in hops[n + 1](p):
                    copy.start()

        def tick(at):
            if at < 4:
                turn = [[(1, 0)], [(2, 0), (1, 1)], [(3, 0), (2, 1), (1, 2)], [(4, 0), (2, 2)]][at]
            else:
                turn = [(at + 1, 0), (at - 1, 1), (at - 2, 2)]
            for p, n in turn:
                if (3 if n else 1) <= p < n_pieces or at < 4:
                    advance(p, n)

        pack_copy = remote(pack, pack_other, side_sem, (n_pieces,), side_peer)
        first_copy = remote(first_ref, first_other, side_sem, (n_pieces + 1,), side_peer)
        loads = [
            pltpu.make_async_copy(mel_ref.at[section], mel, load_sem.at[0]),
            pltpu.make_async_copy(positions_ref, place, load_sem.at[1]),
        ]

        def conv_copies(mine):
            return first_held.copies(mine, first_ref, first_other, conv_first, weight_sem.at[0]) + second_held.copies(
                mine, own[0], other[0], conv_second, weight_sem.at[1]
            )

        def weight_copy(mine):
            return pltpu.make_async_copy(own[1] if mine == 0 else other[1], weight, weight_sem.at[2])

        def keep(n):
            return pltpu.make_async_copy(held[n], results[n], out_sem.at[n])

        barrier = pltpu.get_barrier_semaphore()
        peers = [side_peer] + [peer(bit) for bit in (1, 2, 4)]
        for device in peers:
            pl.semaphore_signal(barrier, inc=1, device_id=device, device_id_type=pl.DeviceIdType.MESH)
        for copy in loads:
            copy.start()
        pack[0:3, :] = gain[...].astype(f32)
        pack[3:6, :] = shift[...].astype(f32)
        pack[6:12, :] = biases[...].astype(f32)
        for n in range(hidden // width):
            pack[12 + n : 13 + n, :] = up_bias[:, n * width : n * width + width].astype(f32)
        pack[16:17, 0:lanes] = first_bias[...].astype(f32)
        pack[16:17, lanes:width] = jnp.zeros((1, lanes), f32)
        pack[17:24, :] = jnp.zeros((7, width), f32)
        pl.semaphore_wait(barrier, len(peers))
        side_copy(0).start()
        first_copy.start()
        pack_copy.start()
        for p in range(1, flying):
            side_copy(p).start()

        turned[0:8, :] = jnp.zeros((8, 128), f32)
        turned[8 + mel_frames : 16 + mel_frames, :] = jnp.zeros((8, 128), f32)
        carry[...] = jnp.zeros(carry.shape, f32)
        clear_pads(conv_first, bands)
        for copy in loads:
            copy.wait()
        band_at = lax.broadcasted_iota(jnp.int32, (bands, block), 0)
        frame_at = lax.broadcasted_iota(jnp.int32, (bands, block), 1)
        time_from, band_from = times[section], bands_from[section]
        time_to, band_to = time_from + time_spans[section], band_from + band_spans[section]
        band_keep = jnp.logical_or(band_at < band_from, band_at >= band_to)
        for n in range(mel_frames // block):
            at = frame_at + n * block
            keep_here = jnp.logical_and(band_keep, jnp.logical_or(at < time_from, at >= time_to))
            values = jnp.where(keep_here, mel[:, n * block : n * block + block].astype(f32), 0.0)
            values = jnp.concatenate([values, jnp.zeros((128 - bands, block), f32)], axis=0)
            turned[8 + n * block : 8 + n * block + block, :] = values.T
        for n, start in enumerate((7, 8, 9, 10)):
            taps[:, n * 128 : n * 128 + 128] = turned[pl.ds(start, frames, stride=2), :].astype(low)
        keep(0).start()

        for n in range(len(hops)):
            advance(0, n)
        first_copy.wait_recv()
        pack_copy.wait_recv()
        for which in range(2):

            @pl.when(section == which)
            def _(which=which):
                for copy in conv_copies(which):
                    copy.start()

        first_section = section == 0
        a_small[...] = jnp.where(first_section, pack[...], pack_other[...])
        t_small[...] = jnp.where(first_section, pack_other[...], pack[...])
        for n in range(hidden // width):
            a_ups[:, n * width : n * width + width] = a_small[12 + n : 13 + n, :]
            t_ups[:, n * width : n * width + width] = t_small[12 + n : 13 + n, :]
        bias = jnp.concatenate([a_small[16:17, 0:lanes], t_small[16:17, 0:lanes]], axis=1)
        for copy in conv_copies(0):
            copy.wait()

        def stem_block(i):
            here = pl.ds(pl.multiple_of(i * block, block), block)
            value, slope = gelu_both(dot(taps[here, 0:384], conv_first[...]) + bias)
            even = value.astype(low)
            even_act[here] = even
            even_slope[here] = slope.astype(low)
            value, slope = gelu_both(dot(taps[here, 128:512], conv_first[...]) + bias)
            odd = value.astype(low)
            odd_act[here] = odd
            odd_slope[here] = slope.astype(low)
            prior = dot(odd, conv_second[0:width])
            at_row = lax.broadcasted_iota(jnp.int32, (block, width), 0)
            moved = jnp.where(at_row == 0, carry[0:1, :], pltpu.roll(prior, 1, 0))
            carry[0:1, :] = prior[block - 1 : block, :]
            pre = moved + dot(even, conv_second[width : 2 * width]) + dot(odd, conv_second[2 * width :]) + row(a_small, 10)
            value, slope = gelu_both(pre)
            slope_second[here] = slope.astype(low)
            encoded[here] = value + place[here].astype(f32)

        for i in range(blocks):
            stem_block(i)
            tick(i)
        for n in range(1, 7):
            keep(n).start()
        for which in range(2):

            @pl.when(section == which)
            def _(which=which):
                weight_copy(which).start()

        weight_copy(0).wait()

        def project_block(i):
            here = pl.ds(pl.multiple_of(i * block, block), block)
            normed, inverse = norm_rows(encoded[here])
            rounded = (normed * row(a_small, 0) + row(a_small, 3)).astype(low)
            norm[here] = rounded
            joint[here, 0:width] = (dot(rounded, weight[:, 0:width]) + row(a_small, 6)).astype(low) * 0.125
            joint[here, width : 2 * width] = dot(rounded, weight[:, width : 2 * width]).astype(low)
            joint[here, 2 * width :] = (dot(rounded, weight[:, 2 * width :]) + row(a_small, 7)).astype(low)

        for i in range(blocks):
            project_block(i)
        tick(blocks)
        keep(7).start()
        keep(8).start()

        def attention(pair):
            lane = lax.broadcasted_iota(jnp.int32, (1, 128), 1)

            def cols(start):
                return pl.ds(pl.multiple_of(start + pair * 128, 128), 128)

            key, value = joint[:, cols(width)], joint[:, cols(2 * width)]

            @pl.loop(0, blocks)
            def _(i):
                here = pl.ds(pl.multiple_of(i * block, block), block)
                query = joint[here, cols(0)]
                found, log = [], []
                for head in range(2):
                    scores = dot_t(jnp.where(lane // 64 == head, query, jnp.zeros_like(query)), key)
                    top = jnp.max(scores, axis=1, keepdims=True) * log2_e
                    exponent = jnp.exp2(scores * log2_e - top)
                    total = jnp.sum(exponent, axis=1, keepdims=True)
                    found.append(dot(exponent.astype(low), value) * (1.0 / total))
                    log.append(top + jnp.log2(total))
                mixed[here, cols(0)] = jnp.where(lane < 64, found[0], found[1]).astype(low)
                both = jnp.where(lane == 0, log[0], log[1])
                logs[pl.ds(pl.multiple_of(pair * 8, 8), 8), here] = both.T[0:8, :]

        done = blocks + 1
        for pair in range(HEADS // 2):
            attention(pair)
            tick(done)
            done += 1
        while done < n_pieces + len(hops) - 1:
            tick(done)
            done += 1
        keep(9).start()
        keep(10).start()
        for p in range(n_pieces):
            for hop in hops:
                for copy in hop(p):
                    copy.wait_send()
        first_copy.wait_send()
        pack_copy.wait_send()
        for n in range(len(held)):
            keep(n).wait()

    def sems(*shape):
        return pltpu.SemaphoreType.DMA(shape)

    shape = (frames, width)
    kept = [(shape, low), (shape, f32)] + [(shape, low)] * 6 + [((frames, 3 * width), low), (shape, low), ((4 * HEADS, frames), f32)]
    everywhere, on_chip = pl.BlockSpec(memory_space=pl.ANY), pl.BlockSpec(memory_space=pltpu.VMEM)
    return pl.pallas_call(
        kernel,
        name="begin",
        in_specs=[everywhere] * n_any + [pl.BlockSpec(memory_space=pltpu.SMEM)] * 4 + [on_chip] * 5,
        out_specs=[everywhere] * (1 + n_sent) + [on_chip] * 4 + [everywhere] * len(kept),
        out_shape=[jax.ShapeDtypeStruct(a.shape, a.dtype) for a in [first] + sent]
        + [jax.ShapeDtypeStruct(s, f32) for s in ((24, width), (24, width), (1, hidden), (1, hidden))]
        + [jax.ShapeDtypeStruct(s, d) for s, d in kept],
        scratch_shapes=[pltpu.VMEM(s, d) for s, d in kept]
        + [
            pltpu.VMEM((bands, mel_frames), low), pltpu.VMEM((mel_frames + 16, 128), f32), pltpu.VMEM(shape, low),
            pltpu.VMEM((384, width), low), pltpu.VMEM((3 * width, width), low), pltpu.VMEM((width, 3 * width), low),
            pltpu.VMEM((8, width), f32), pltpu.VMEM((24, width), f32), pltpu.VMEM((24, width), f32),
            sems(2), sems(3), sems(len(kept)), sems(2, n_pieces + 2), sems(2, n_pieces), sems(2, 2, n_pieces),
        ],
        compiler_params=pltpu.CompilerParams(collective_id=1, has_side_effects=True, vmem_limit_bytes=VMEM_BYTES),
        cost_estimate=pl.CostEstimate(flops=10**10, bytes_accessed=10**8, transcendentals=0),
    )(mel_input, positions, first, *sent, *spans, gain, shift, biases, up_bias, first_bias)


def factors_of(size):
    found, rest = [], size // 2
    while rest > 1:
        radix = 2 if rest in (2, 8) or rest % 4 else 4
        found.append(radix)
        rest //= radix
    return found


def finish_backward(audio, text, joint, logs, mixed_grad, grad, encoded, slopes, smalls, weight, second, first, acts, small, bands):
    width, tile_rows = 512, 512
    half = tile_rows // 2
    lanes = width // 2
    frames, text_rows = joint.shape[0], text[0][0].shape[0]
    tiles = len(audio)
    count = tiles + 2
    early = 11
    flying = 3
    rows = count * tile_rows
    block = 256
    blocks = frames // block
    replicas = lax.axis_size("dp")
    factors = factors_of(replicas)
    levels = len(factors)
    befores, sizes, scatters = [], [], []
    for radix in factors:
        before = sizes[-1] if sizes else half
        befores.append(before)
        scatters.append(before % (16 * radix) == 0)
        sizes.append(before // radix if scatters[-1] else before)

    arrays, places = [], {}

    def place(array):
        if id(array) not in places:
            places[id(array)] = len(arrays)
            arrays.append(array)
        return places[id(array)]

    def job(x, xc, y, yc):
        return (place(x), xc, y if isinstance(y, int) else (place(y),), yc)

    audio_jobs = [job(*one) for one in audio]
    text_jobs = [job(*one) for one in text]
    at_joint, at_logs, at_mixed, at_grad, at_encoded = [place(a) for a in (joint, logs, mixed_grad, grad, encoded)]
    at_slopes = [place(a) for a in slopes]
    odd_act, even_act, taps = acts
    at_odd, at_even, at_taps = place(odd_act), place(even_act), place(taps)
    at_weight = (place(weight.own), place(weight.other))
    at_second = (place(second.own), place(second.other))
    at_first = (place(first.own), place(first.other))
    n_any = len(arrays)

    def kernel(*refs):
        given = refs[:n_any]
        smalls, small = refs[n_any : n_any + 2]
        out_ref, keep_ref, got_ref = refs[n_any + 2 : n_any + 5]
        (
            tile, core_recv, side_send, side_recv, work, final, x_audio, y_audio, x_text, y_text,
            joint, logs, mixed_grad, query_grad, key_grad, value_grad, key_acc, value_acc, key_turned, sums,
            encoded_in, grad_in, slope_in, weight, second, first, second_low, next_low, even_low, odd_low, taps_grad,
            carry, conv_buf, small_buf, mel_buf, mel_send,
            in_sem, load_sem, weight_sem, block_sem, keep_sem, core_sem, side_sem, back_sem, out_sem, mel_sem,
        ) = refs[n_any + 5 : n_any + 51]
        recvs = refs[n_any + 51 : n_any + 51 + levels]
        rs_sems = refs[n_any + 51 + levels : n_any + 51 + 2 * levels]
        ag_sems = refs[n_any + 51 + 2 * levels :]
        own_grads = (query_grad, key_grad, value_grad)

        section, replica = lax.axis_index("section"), lax.axis_index("dp")
        core = replica % 2
        digits, strides, rest, stride = [], [], replica // 2, 2
        for radix in factors:
            digits.append(rest % radix)
            strides.append(stride)
            rest, stride = rest // radix, stride * radix
        core_peer = {"dp": replica + 1 - 2 * core}
        side_peer = {"section": 1 - section}

        def peer(level, distance):
            digit = (digits[level] + distance) % factors[level]
            return digit, {"dp": replica + (digit - digits[level]) * strides[level]}

        def remote(source, target, sems, at, device):
            return pltpu.make_async_remote_copy(
                src_ref=source, dst_ref=target, send_sem=sems.at[(0,) + at], recv_sem=sems.at[(1,) + at],
                device_id=device, device_id_type=pl.DeviceIdType.MESH,
            )

        def rows_at(start, size):
            return pl.ds(pl.multiple_of(start, 16), size)

        def offset(level):
            found = 0
            for n in range(level):
                if scatters[n]:
                    found = found + digits[n] * sizes[n]
            return found

        def core_copy(k):
            return remote(
                tile.at[k % 2, :, rows_at((1 - core) * half, half)], core_recv.at[k % 4], core_sem, (k,), core_peer
            )

        def side_copy(k):
            here = rows_at(k * half, half)
            return remote(side_send.at[here], side_recv.at[here], side_sem, (k,), side_peer)

        def scatter_copy(k, level, distance):
            digit, device = peer(level, distance)
            size = sizes[level]
            start = k * half + offset(level) + (digit * size if scatters[level] else 0)
            return remote(
                work.at[rows_at(start, size)], recvs[level].at[distance - 1, rows_at(k * size, size)],
                rs_sems[level], (distance - 1, k), device,
            )

        def gather_copy(k, level, distance):
            digit, device = peer(level, distance)
            here = final.at[rows_at(k * tile_rows + core * half + offset(level + 1), sizes[level])]
            return remote(here, here, ag_sems[level], (distance - 1, k), device)

        def back_copy(k):
            here = final.at[rows_at(k * tile_rows + core * half, half)]
            return remote(here, here, back_sem, (k,), core_peer)

        def store(k):
            here = rows_at(k * tile_rows, tile_rows)
            return pltpu.make_async_copy(final.at[here], out_ref.at[here], out_sem.at[k])

        def mel_copy():
            return remote(mel_send, got_ref, mel_sem, (), side_peer)

        def stage_core(k):
            core_copy(k).wait_recv()
            here, mine = rows_at(k * half, half), rows_at(core * half, half)
            slot, from_peer = k % 2, k % 4
            side_send[here] = (
                tile[slot, 1 - section, mine].astype(f32) + core_recv[from_peer, 1 - section].astype(f32)
            ).astype(low)

            @when(jnp.logical_or(k < flying, k == tiles))
            def _():
                side_copy(k).start()

            work[here] = (tile[slot, section, mine].astype(f32) + core_recv[from_peer, section].astype(f32)).astype(low)

        scatter_levels = [n for n in range(levels) if scatters[n]]

        def next_exchange(k, level):
            if level + 1 < levels:
                for distance in range(1, factors[level + 1]):
                    scatter_copy(k, level + 1, distance).start()
            elif scatter_levels:
                for distance in range(1, factors[scatter_levels[-1]]):
                    gather_copy(k, scatter_levels[-1], distance).start()
            else:
                back_copy(k).start()

        def put(k, level, total):
            if level + 1 < levels:
                work[rows_at(k * half + offset(level + 1), total.shape[0])] = total.astype(low)
            else:
                start = k * tile_rows + core * half + offset(level + 1)
                final[rows_at(start, total.shape[0])] = total.astype(low)
            next_exchange(k, level)

        def stage_side(k):
            side_copy(k).wait_recv()
            later = k + flying

            @when(jnp.logical_and(later < count, later != tiles))
            def _():
                side_copy(later).start()

            here = rows_at(k * half, half)
            put(k, -1, work[here].astype(f32) + side_recv[here].astype(f32))

        def stage_scatter(k, level):
            size = sizes[level]
            for distance in range(1, factors[level]):
                scatter_copy(k, level, distance).wait_recv()
            total = work[rows_at(k * half + offset(level + 1), size)].astype(f32)
            for distance in range(1, factors[level]):
                total += recvs[level][distance - 1, rows_at(k * size, size)].astype(f32)
            if not scatters[level]:
                for distance in range(1, factors[level]):
                    scatter_copy(k, level, distance).wait_send()
            put(k, level, total)

        def stage_gather(k, level):
            for distance in range(1, factors[level]):
                gather_copy(k, level, distance).wait_recv()
            if level != scatter_levels[0]:
                below = scatter_levels[scatter_levels.index(level) - 1]
                for distance in range(1, factors[below]):
                    gather_copy(k, below, distance).start()
            else:
                back_copy(k).start()

        def stage_back(k):
            back_copy(k).wait_recv()
            store(k).start()

        stages = [stage_side]
        stages += [functools.partial(stage_scatter, level=n) for n in range(levels)]
        stages += [functools.partial(stage_gather, level=n) for n in reversed(scatter_levels)]
        stages.append(stage_back)

        def tick(at):
            for n, stage in enumerate(stages):

                @pl.when(jnp.logical_and(at >= n, at < count + n))
                def _(n=n, stage=stage):
                    stage(at - n)

        def when(cond):
            return pl.when(cond)

        def fetch_copies(job, x_buf, y_buf, slot, sems):
            x, xc, y, yc = job
            x_from = given[x].at[:, xc * width : (xc + 1) * width]
            y_from = own_grads[y] if isinstance(y, int) else given[y[0]].at[:, yc * width : (yc + 1) * width]
            return (
                pltpu.make_async_copy(x_from, x_buf.at[slot], sems.at[0, slot]),
                pltpu.make_async_copy(y_from, y_buf.at[slot], sems.at[1, slot]),
            )

        def fetch(k, first_k, last_k):
            for n in range(first_k, last_k):

                @when(k == n)
                def _(n=n):
                    for copy in fetch_copies(audio_jobs[n], x_audio, y_audio, n % 2, in_sem.at[0]):
                        copy.start()
                    for copy in fetch_copies(text_jobs[n], x_text, y_text, n % 2, in_sem.at[1]):
                        copy.start()

        def fetch_wait(k):
            slot = k % 2
            for copy in fetch_copies(audio_jobs[0], x_audio, y_audio, slot, in_sem.at[0]):
                copy.wait()
            for copy in fetch_copies(text_jobs[0], x_text, y_text, slot, in_sem.at[1]):
                copy.wait()

        def tile_grads(k, last_k, first_k):
            slot = k % 2

            @when(k + 1 < last_k)
            def _():
                fetch(k + 1, first_k, last_k)

            fetch_wait(k)

            @when(k >= 2)
            def _():
                core_copy(k - 2).wait_send()

            tile[slot, 0] = dot_tt(x_audio[slot], y_audio[slot]).astype(low)
            tile[slot, 1] = dot_tt(x_text[slot], y_text[slot]).astype(low)
            core_copy(k).start()

            @when(k > first_k)
            def _():
                stage_core(k - 1)

        attn_loads = [
            pltpu.make_async_copy(given[at_joint], joint, load_sem.at[0]),
            pltpu.make_async_copy(given[at_logs], logs, load_sem.at[1]),
            pltpu.make_async_copy(given[at_mixed], mixed_grad, load_sem.at[2]),
        ]

        def attention(step):
            pair, part_at = step // blocks, step % blocks
            lane = lax.broadcasted_iota(jnp.int32, (1, 128), 1)
            sub = lax.broadcasted_iota(jnp.int32, (128, 1), 0)

            def cols(start):
                return pl.ds(pl.multiple_of(start + pair * 128, 128), 128)

            here = rows_at(part_at * block, block)

            @when(part_at == 0)
            def _():
                key_acc[...] = jnp.zeros(key_acc.shape, f32)
                value_acc[...] = jnp.zeros(value_acc.shape, f32)
                key_turned[...] = joint[:, cols(width)].astype(f32).T.astype(low)

            query, key, value = joint[here, cols(0)], joint[:, cols(width)], joint[:, cols(2 * width)]
            grad = mixed_grad[here, cols(0)]
            log = logs[pl.ds(pl.multiple_of(pair * 8, 8), 8), pl.ds(pl.multiple_of(part_at * block, block), block)]
            turned = key_turned[...]
            query_turned = jnp.zeros((128, block), f32)
            for head in range(2):
                part = jnp.where(lane // 64 == head, query, jnp.zeros_like(query))
                grad_part = jnp.where(lane // 64 == head, grad, jnp.zeros_like(grad))
                chance = jnp.exp2(dot_t(key, part) * log2_e - log[head : head + 1, :])
                product = chance * dot_t(value, grad_part)
                grad_scores = (product - chance * jnp.sum(product, axis=0, keepdims=True)).astype(low)
                value_acc[...] += dot(chance.astype(low), grad_part)
                key_acc[...] += dot(grad_scores, part)
                query_turned += dot(jnp.where(sub // 64 == head, turned, jnp.zeros_like(turned)), grad_scores)
            grad_query = query_turned.T * 0.125
            query_grad[here, cols(0)] = grad_query.astype(low)
            sums[0:1, cols(0)] += col_sum(grad_query)

            @when(part_at == blocks - 1)
            def _():
                key_grad[:, cols(0)] = key_acc[...].astype(low)
                value_grad[:, cols(0)] = value_acc[...].astype(low)
                sums[1:2, cols(0)] = col_sum(value_acc[...])

        def weight_copies(mine):
            found = [pltpu.make_async_copy(given[at_weight[0 if mine == 0 else 1]], weight, weight_sem.at[0])]
            for n, (split, at, held) in enumerate(((second_side, at_second, second), (first_side, at_first, first))):
                found += split.copies(mine, given[at[0]], given[at[1]], held, weight_sem.at[1 + n])
            return found

        def block_copies(i, slot):
            here = rows_at(i * block, block)
            found = [
                pltpu.make_async_copy(given[at_encoded].at[here], encoded_in.at[slot], block_sem.at[0, slot]),
                pltpu.make_async_copy(given[at_grad].at[here], grad_in.at[slot], block_sem.at[1, slot]),
            ]
            for n in range(3):
                found.append(
                    pltpu.make_async_copy(given[at_slopes[n]].at[here], slope_in.at[slot, n], block_sem.at[2 + n, slot])
                )
            return found

        def stem_block(step):
            i = blocks - 1 - step
            slot = step % 2

            @when(step + 1 < blocks)
            def _():
                for copy in block_copies(i - 1, 1 - slot):
                    copy.start()

            for copy in block_copies(i, slot):
                copy.wait()
            here = rows_at(i * block, block)
            back = (
                dot_t(query_grad[here], weight[:, :width])
                + dot_t(key_grad[here], weight[:, width : 2 * width])
                + dot_t(value_grad[here], weight[:, 2 * width :])
            )
            normed, inverse = norm_rows(encoded_in[slot])
            sums[2:3, :] += col_sum(back * normed)
            sums[3:4, :] += col_sum(back)
            total = grad_in[slot] + norm_back(back, row(smalls, 0), normed, inverse)
            total = total * slope_in[slot, 0].astype(f32)
            sums[4:5, :] += col_sum(total)
            rounded = total.astype(low)
            second_low[here] = rounded
            at_row = lax.broadcasted_iota(jnp.int32, (block, width), 0)
            wide = rounded.astype(f32)
            moved = jnp.where(at_row == block - 1, carry[0:1, :], pltpu.roll(wide, block - 1, 0))
            carry[0:1, :] = wide[0:1, :]
            moved = moved.astype(low)
            next_low[here] = moved
            grad_even = dot_t(rounded, second[width : 2 * width]) * slope_in[slot, 1].astype(f32)
            grad_odd = (dot_t(rounded, second[2 * width :]) + dot_t(moved, second[0:width])) * slope_in[slot, 2].astype(f32)
            sums[5:6, :] += col_sum(grad_even) + col_sum(grad_odd)
            grad_even = grad_even.astype(low)
            grad_odd = grad_odd.astype(low)
            even_low[here] = grad_even
            odd_low[here] = grad_odd
            taps_even = dot_t(grad_even, first[...])
            taps_odd = dot_t(grad_odd, first[...])
            taps_grad[here, 0:128] = taps_even[:, 0:128]
            taps_grad[here, 128:256] = taps_even[:, 128:256] + taps_odd[:, 0:128]
            taps_grad[here, 256:384] = taps_even[:, 256:384] + taps_odd[:, 128:256]
            taps_grad[here, 384:512] = taps_odd[:, 256:384]

        def mel_rows():
            at_row = lax.broadcasted_iota(jnp.int32, (frames, 128), 0)
            before = jnp.where(at_row == 0, 0.0, pltpu.roll(taps_grad[:, 384:512], 1, 0))
            mel_buf[:, 0:128] = taps_grad[:, 128:256] + before
            after = jnp.where(at_row == frames - 1, 0.0, pltpu.roll(taps_grad[:, 0:128], frames - 1, 0))
            mel_buf[:, 128:256] = taps_grad[:, 256:384] + after
            mel_send[...] = mel_buf[rows_at((1 - section) * (frames // 2), frames // 2)].astype(low)

        def keep_copy():
            return pltpu.make_async_copy(mel_buf.at[rows_at(section * (frames // 2), frames // 2)], keep_ref, keep_sem)

        conv_jobs = [(at_odd, next_low), (at_even, second_low), (at_odd, second_low)]

        def conv_copies(n, slot):
            x, y = conv_jobs[n]
            return (
                pltpu.make_async_copy(given[x], x_audio.at[slot], in_sem.at[0, 0, slot]),
                pltpu.make_async_copy(y, y_audio.at[slot], in_sem.at[0, 1, slot]),
            )

        def tap_copies():
            return [
                pltpu.make_async_copy(given[at_taps].at[:, n * 128 : n * 128 + 384], x_audio.at[n, :, 0:384], in_sem.at[0, 0, n])
                for n in range(2)
            ]

        barrier = pltpu.get_barrier_semaphore()
        peers = [core_peer, side_peer]
        peers += [peer(n, d)[1] for n in range(levels) for d in range(1, factors[n])]
        for device in peers:
            pl.semaphore_signal(barrier, inc=1, device_id=device, device_id_type=pl.DeviceIdType.MESH)

        fetch(0, 0, 1)
        for copy in attn_loads:
            copy.start()
        for which in range(2):

            @when(section == which)
            def _(which=which):
                for copy in weight_copies(which):
                    copy.start()

        for copy in block_copies(blocks - 1, 0):
            copy.start()
        sums[...] = jnp.zeros(sums.shape, f32)
        carry[...] = jnp.zeros(carry.shape, f32)
        pl.semaphore_wait(barrier, len(peers))

        @pl.loop(0, early)
        def _(k):
            tile_grads(k, early, 0)

        stage_core(early - 1)
        for copy in attn_loads:
            copy.wait()

        @pl.loop(0, 4 * blocks)
        def _(step):
            attention(step)

            @when(jnp.logical_or(step < 3, step % 3 == 1))
            def _():
                tick(jnp.where(step < 3, step, 3 + (step - 4) // 3))

        fetch(early, early, early + 1)

        @pl.loop(early, tiles)
        def _(k):
            tile_grads(k, tiles, early)
            tick(k - early + 7)

        stage_core(tiles - 1)
        for copy in weight_copies(0):
            copy.wait()
        clear_pads(first, bands)

        @pl.loop(0, blocks)
        def _(step):
            stem_block(step)

            @when(step % 2 == 1)
            def _():
                tick(10 + step // 2)

        for copy in conv_copies(0, 0):
            copy.start()

        @pl.loop(0, 3)
        def _(n):
            slot = n % 2
            for which in range(1, 3):

                @when(n + 1 == which)
                def _(which=which):
                    for copy in conv_copies(which, which % 2):
                        copy.start()

            for copy in conv_copies(0, slot):
                copy.wait()
            conv_buf[n] = dot_tt(x_audio[slot], y_audio[slot]).astype(low)

        for copy in tap_copies():
            copy.start()
        core_copy(tiles - 2).wait_send()
        slot = tiles % 2
        for s in range(2):
            cols = slice(s * lanes, s * lanes + lanes)
            tile[slot, s, :, 0:lanes] = conv_buf[0, :, cols]
            tile[slot, s, 0:half, lanes:width] = conv_buf[1, half:tile_rows, cols]
            tile[slot, s, half:tile_rows, lanes:width] = conv_buf[2, 0:half, cols]
        core_copy(tiles).start()
        for copy in tap_copies():
            copy.wait()
        first_grad = (
            dot_tt(x_audio[0, :, 0:384], even_low[...]) + dot_tt(x_audio[1, :, 0:384], odd_low[...])
        ).astype(low)
        stage_core(tiles)
        core_copy(tiles - 1).wait_send()
        slot = 1 - slot
        small_buf[...] = small[...]
        small_buf[0, 6:8, :] = sums[0:2, :]
        small_buf[0, 0:1, :] = sums[2:3, :]
        small_buf[0, 3:4, :] = sums[3:4, :]
        small_buf[0, 10:11, :] = sums[4:5, :]
        small_buf[0, 16:17, 0:lanes] = sums[5:6, 0:lanes]
        small_buf[1, 16:17, 0:lanes] = sums[5:6, lanes:width]
        for s in range(2):
            cols = slice(s * lanes, s * lanes + lanes)
            tile[slot, s, 0:half, 0:lanes] = conv_buf[1, 0:half, cols]
            tile[slot, s, 0:half, lanes:width] = conv_buf[2, half:tile_rows, cols]
            tile[slot, s, half : half + 192, 0:lanes] = first_grad[0:192, cols]
            tile[slot, s, half : half + 192, lanes:width] = first_grad[192:384, cols]
            tile[slot, s, half + 192 : half + 224, :] = small_buf[s].astype(low)
            tile[slot, s, half + 224 : tile_rows, :] = jnp.zeros((32, width), low)
        core_copy(tiles + 1).start()
        mel_rows()
        keep_copy().start()
        stage_core(tiles + 1)
        mel_copy().start()

        @pl.loop(12, count + len(stages) - 1)
        def _(at):
            tick(at)

        keep_copy().wait()
        mel_copy().wait()
        for k in (count - 2, count - 1):
            core_copy(k).wait_send()

        @pl.loop(0, count)
        def _(k):
            side_copy(k).wait_send()
            for level in range(levels):
                for distance in range(1, factors[level]):
                    if scatters[level]:
                        scatter_copy(k, level, distance).wait_send()
                        gather_copy(k, level, distance).wait_send()
            back_copy(k).wait_send()
            store(k).wait()

    second_side, first_side = second, first

    def sems(*shape):
        return pltpu.SemaphoreType.DMA(shape)

    def vmem(*shape, dtype=low):
        return pltpu.VMEM(shape, dtype)

    whole = (frames, width)
    return pl.pallas_call(
        kernel,
        name="finish_backward",
        in_specs=[pl.BlockSpec(memory_space=pl.ANY)] * n_any + [pl.BlockSpec(memory_space=pltpu.VMEM)] * 2,
        out_specs=[pl.BlockSpec(memory_space=pl.ANY)] * 3,
        out_shape=[
            jax.ShapeDtypeStruct((rows, width), low),
            jax.ShapeDtypeStruct((frames // 2, 256), f32),
            jax.ShapeDtypeStruct((frames // 2, 256), low),
        ],
        scratch_shapes=[
            vmem(2, 2, tile_rows, width), vmem(4, 2, half, width), vmem(count * half, width), vmem(count * half, width),
            vmem(count * half, width), vmem(rows, width),
            vmem(2, *whole), vmem(2, *whole), vmem(2, text_rows, width), vmem(2, text_rows, width),
            vmem(frames, 3 * width), vmem(32, frames, dtype=f32), vmem(*whole), vmem(*whole), vmem(*whole), vmem(*whole),
            vmem(frames, 128, dtype=f32), vmem(frames, 128, dtype=f32), vmem(128, frames), vmem(8, width, dtype=f32),
            vmem(2, block, width, dtype=f32), vmem(2, block, width, dtype=f32), vmem(2, 3, block, width),
            vmem(width, 3 * width), vmem(*second.shape), vmem(*first.shape),
            vmem(*whole), vmem(*whole), vmem(*whole), vmem(*whole), vmem(*whole, dtype=f32),
            vmem(8, width, dtype=f32), vmem(3, tile_rows, width), vmem(2, 32, width, dtype=f32),
            vmem(frames, 256, dtype=f32), vmem(frames // 2, 256),
            sems(2, 2, 2), sems(3), sems(3), sems(5, 2), pltpu.SemaphoreType.DMA, sems(2, count), sems(2, count), sems(2, count),
            sems(count), sems(2),
            *[vmem(r - 1, count * s, width) for r, s in zip(factors, sizes)],
            *[sems(2, r - 1, count) for r in factors],
            *[sems(2, r - 1, count) for r in factors],
        ],
        compiler_params=pltpu.CompilerParams(
            collective_id=0, has_side_effects=True, vmem_limit_bytes=63 << 20
        ),
        cost_estimate=pl.CostEstimate(flops=10**11, bytes_accessed=10**8, transcendentals=0),
    )(*arrays, smalls, small)


def shards(
    mel_input,
    time_start,
    time_width,
    freq_start,
    freq_width,
    text_len,
    text_embed,
    cotangent,
    positions,
    conv_first,
    conv_first_bias,
    conv_second,
    norm_gain,
    norm_shift,
    attn_in,
    attn_out,
    mlp_up,
    mlp_down,
    up_bias,
    small_bias,
    cross_first,
    cross_second,
):
    mine = lax.axis_index("section")
    is_first = mine == 0
    frames, width = positions.shape
    bands, mel_frames = mel_input.shape[1], mel_input.shape[2]
    text_rows = text_embed.shape[1]
    audio_block = 256
    text_block = 224
    swap_pairs = [(0, 1), (1, 0)]

    def own(array):
        return lax.dynamic_index_in_dim(array, mine, 0, keepdims=False)

    def partner(array):
        return lax.ppermute(array, "section", swap_pairs)

    first_own = conv_first.reshape(3 * bands, -1)
    second_own = conv_second.reshape(3 * width, -1)
    owns = [w[0] for w in (attn_in, attn_out, mlp_up, mlp_down, cross_first, cross_second)]
    (
        first_other, second_other, *others, a_small, t_small, a_ups, t_ups,
        taps, encoded, even_act, odd_act, even_slope, odd_slope, slope_second, a_norm, a_joint, a_mixed, a_logs,
    ) = begin(
        mel_input, (time_start, time_width, freq_start, freq_width), norm_gain[0], norm_shift[0], small_bias[0], up_bias,
        conv_first_bias[None], first_own, second_own, owns[0], owns[1:], positions,
    )
    a_in, a_out, a_up, a_down, a_cross_a, a_cross_b = [Side(0, o, p) for o, p in zip(owns, others)]
    t_in, t_out, t_up, t_down, t_cross_a, t_cross_b = [Side(1, o, p) for o, p in zip(owns, others)]
    first_all = Split(first_own, first_other, 3, 128)
    second_all = Split(second_own, second_other, 3, width)
    band_at = jnp.arange(bands, dtype=jnp.int32)

    a_middle, a_feed_norm, a_hidden, a_slope, a_ending, memory, memory_keys, memory_values = audio_feed(
        encoded, a_mixed, a_out, a_small, a_ups, a_up, a_down, a_cross_a, a_cross_b, audio_block
    )

    text_clip, cot_clip = own(text_embed), own(cotangent)
    t_norm, t_joint = project(text_clip, t_in, t_small, text_block)
    t_mixed, t_logs = attend(t_joint, t_joint, t_joint, (0, 4, 8), True, text_rows)
    t_middle, cross_low, cross_query = text_middle(text_clip, t_mixed, t_out, t_small, t_cross_a, text_block)
    c_mixed, c_logs = attend(cross_query, memory_keys, memory_values, (0, 0, 0), False, text_rows)
    (
        decoded_keep, decoded_send, t_feed_norm, t_hidden, t_pre, cot_low, after_grad, after_low, c_mixed_grad, feed_sums, feed_wide,
    ) = text_feed(
        own(text_len)[None], t_middle, c_mixed, cot_clip, t_cross_b, t_small, t_ups, t_up, t_down, text_block
    )
    query_grad, key_grad, value_grad, c_sums = attend_back(
        cross_query, memory_keys, memory_values, (0, 0, 0), c_logs, c_mixed_grad, False, True, text_rows
    )
    middle_grad, middle_low, t_mixed_grad, cross_sums = text_cross_back(
        query_grad, t_middle, after_grad, t_small, t_cross_a, t_out, text_block
    )
    tq_grad, tk_grad, tv_grad, t_sums = attend_back(
        t_joint, t_joint, t_joint, (0, 4, 8), t_logs, t_mixed_grad, True, False, text_rows
    )
    text_keep, text_send, text_sums = project_back(
        tq_grad, tk_grad, tv_grad, text_clip, middle_grad, t_small, t_in, text_block
    )

    decoded_got, text_got = partner(decoded_send), partner(text_send)
    end_low, a_pre, a_grad, a_grad_low, a_mixed_grad, a_feed_sums, a_feed_wide = audio_feed_back(
        key_grad, value_grad, a_ending, a_middle, a_slope, a_small, a_cross_a, a_cross_b, a_up, a_down, a_out, audio_block
    )
    half = width // 2

    blank = jnp.zeros((width,), f32)
    a_rows = [
        blank, a_feed_sums[3], a_feed_sums[0], blank, a_feed_sums[4], a_feed_sums[1],
        blank, blank, a_feed_sums[5], a_feed_sums[2], blank, c_sums[1],
    ]
    t_rows = [
        text_sums[0], cross_sums[0], feed_sums[0], text_sums[1], cross_sums[1], feed_sums[1],
        t_sums[0], t_sums[1], cross_sums[2], feed_sums[2], c_sums[0], feed_sums[3],
    ]
    a_rows += [a_feed_wide[0, n * width : n * width + width] for n in range(4)]
    t_rows += [feed_wide[0, n * width : n * width + width] for n in range(4)]
    small = jnp.stack([jnp.stack(rows + [blank, feed_sums[3]] + [blank] * 14) for rows in (a_rows, t_rows)])
    audio = [(a_feed_norm, 0, a_pre, n) for n in range(4)] + [(a_hidden, n, end_low, 0) for n in range(4)]
    audio += [(memory, 0, key_grad, 0), (memory, 0, value_grad, 0), (a_mixed, 0, a_grad_low, 0)]
    audio += [(a_norm, 0, n, 0) for n in range(3)]
    text = [(t_feed_norm, 0, t_pre, n) for n in range(4)] + [(t_hidden, n, cot_low, 0) for n in range(4)]
    text += [(cross_low, 0, query_grad, 0), (c_mixed, 0, after_low, 0), (t_mixed, 0, middle_low, 0)]
    text += [(t_norm, 0, part, 0) for part in (tq_grad, tk_grad, tv_grad)]
    small, decoded_got, text_got = lax.optimization_barrier((small, decoded_got, text_got))
    total, mel_keep, mel_got = finish_backward(
        audio, text, a_joint, a_logs, a_mixed_grad, a_grad, encoded, (slope_second, even_slope, odd_slope), a_small, a_in,
        second_all, first_all, (odd_act, even_act, taps), small, bands,
    )

    def lay(part):
        return part.reshape(frames // 2, 2, 128)[:, :, :bands].reshape(frames, bands).T.astype(f32)

    keep_lay, got_lay = lay(mel_keep), lay(mel_got)
    mel_out = jnp.where(is_first, jnp.stack([keep_lay, got_lay]), jnp.stack([got_lay, keep_lay]))
    half_at = mine * frames + jnp.arange(frames, dtype=jnp.int32)

    def outside(at, start, span):
        return jnp.logical_or(at[None] < start[:, None], at[None] >= (start + span)[:, None])

    keep = jnp.logical_and(
        outside(band_at, freq_start, freq_width)[:, :, None], outside(half_at, time_start, time_width)[:, None, :]
    )
    mel_out = jnp.where(keep, mel_out, 0.0)
    decoded, text_grad = finish([(decoded_keep, decoded_got), (text_keep, text_got)])
    joint, out, up, down, cross_a, cross_b, first, bias, second, gain, shift, wide, small, cross = unpack(total, bands)
    cross_bias = jnp.where(is_first, cross[0, :half], cross[0, half:])
    return (
        decoded, text_grad, mel_out, first, bias[0], second, gain, shift, joint, out, up, down, wide, small, cross_a, cross_b,
        cross_bias,
    )


def solution(mesh):
    return jax.shard_map(
        shards,
        mesh=mesh,
        in_specs=(
            P("dp", None, None),
            P("dp"),
            P("dp"),
            P("dp"),
            P("dp"),
            P("dp"),
            P("dp", None, None),
            P("dp", None, None),
            P(),
            P(None, None, "section"),
            P("section"),
            P(None, None, "section"),
            P("section", None, None),
            P("section", None, None),
            P("section", None, None),
            P("section", None, None),
            P("section", None, None),
            P("section", None, None),
            P("section", None),
            P("section", None, None),
            P("section", None, None),
            P("section", None, None),
        ),
        out_specs=(
            P("dp", None, "section"),
            P("dp", None, "section"),
            P("dp", None, "section"),
            P(None, None, "section"),
            P("section"),
            P(None, None, "section"),
            P("section", None, None),
            P("section", None, None),
            P("section", None, None),
            P("section", None, None),
            P("section", None, None),
            P("section", None, None),
            P("section", None),
            P("section", None, None),
            P("section", None, None),
            P("section", None, None),
            P("section"),
        ),
        check_vma=False,
    )
```

```python
import functools

import jax
import jax.numpy as jnp
from jax import lax
from jax.experimental import pallas as pl
from jax.experimental.pallas import tpu as pltpu
from jax.sharding import PartitionSpec as P

HEADS = 8
epsilon = 1e-05
root_half = 0.7071067811865476
gauss_norm = 0.3989422804014327
log2_e = 1.4426950408889634
VMEM_BYTES = 56 << 20

f32 = jnp.float32
low = jnp.bfloat16


def dot(left, right):
    return lax.dot_general(left, right, (((1,), (0,)), ((), ())), preferred_element_type=f32)


def dot_t(left, right):
    return lax.dot_general(left, right, (((1,), (1,)), ((), ())), preferred_element_type=f32)


def dot_tt(left, right):
    return lax.dot_general(left, right, (((0,), (0,)), ((), ())), preferred_element_type=f32)


def gelu_both(inputs):
    ratio = 1.0 / (1.0 + (0.3275911 * root_half) * jnp.abs(inputs))
    bell = jnp.exp2((-0.5 * log2_e) * inputs * inputs)
    tail = ratio * (
        0.127414796
        + ratio * (-0.142248368 + ratio * (0.7107068705 + ratio * (-0.7265760135 + ratio * 0.5307027145)))
    )
    tail = tail * bell
    below = jnp.where(inputs >= 0.0, 1.0 - tail, tail)
    return inputs * below, below + inputs * bell * gauss_norm


def norm_rows(inputs):
    centred = inputs - jnp.mean(inputs, axis=-1, keepdims=True)
    inverse = lax.rsqrt(jnp.mean(centred * centred, axis=-1, keepdims=True) + epsilon)
    return centred * inverse, inverse


def norm_back(grad, gain, normed, inverse):
    scaled = grad * gain
    return inverse * (
        scaled
        - jnp.mean(scaled, axis=-1, keepdims=True)
        - normed * jnp.mean(scaled * normed, axis=-1, keepdims=True)
    )


def col_sum(inputs):
    return jnp.sum(inputs, axis=0, keepdims=True)


class Side:
    def __init__(self, side, own, other):
        self.side, self.own, self.other, self.shape = side, own, other, own.shape

    def copies(self, mine, own, other, held, sem):
        return [pltpu.make_async_copy(own if mine == self.side else other, held, sem)]


class Split:
    def __init__(self, own, other, groups, apart):
        self.own, self.other, self.groups, self.apart = own, other, groups, apart
        self.shape = (groups * apart, 2 * own.shape[1])

    def copies(self, mine, own, other, held, sem):
        size, half = self.own.shape[0] // self.groups, self.own.shape[1]
        found = []
        for which, ref in ((mine, own), (1 - mine, other)):
            cols = slice(which * half, which * half + half)
            for n in range(self.groups):
                found.append(
                    pltpu.make_async_copy(
                        ref.at[n * size : n * size + size], held.at[n * self.apart : n * self.apart + size, cols], sem
                    )
                )
        return found


def call(body, name, steps, block, ins, outs, scratch=(), reverse=False, flops=0, grid=None):
    arrays, specs, kinds, weight_scratch = [], [], [], []
    at = (lambda i: steps - 1 - i) if reverse else (lambda i: i)
    for array, kind in ins:
        if kind in ("side", "split"):
            arrays += [array.own, array.other]
            specs += [pl.BlockSpec(memory_space=pl.ANY)] * 2
            weight_scratch.append(pltpu.VMEM(array.shape, array.own.dtype))
        elif kind == "rows":
            arrays.append(array)
            specs.append(pl.BlockSpec((block, array.shape[1]), lambda i: (at(i), 0)))
        elif kind == "clip":
            arrays.append(array)
            specs.append(pl.BlockSpec((None, block, array.shape[2]), lambda i: (lax.axis_index("section"), at(i), 0)))
        elif kind == "smem":
            arrays.append(array)
            specs.append(pl.BlockSpec(memory_space=pltpu.SMEM))
        else:
            arrays.append(array)
            specs.append(
                pl.BlockSpec(
                    array.shape,
                    lambda i, n=array.ndim: (0,) * n,
                    pipeline_mode=pl.Buffered(1),
                )
            )
        kinds.append((kind, array if kind in ("side", "split") else None))
    out_specs = [
        pl.BlockSpec((block, shape[1]), lambda i: (at(i), 0))
        if kind == "rows"
        else pl.BlockSpec(shape, lambda i, n=len(shape): (0,) * n)
        for shape, dtype, kind in outs
    ]
    n_in, n_out, n_weight = len(arrays), len(outs), len(weight_scratch)

    def kernel(*refs):
        in_refs, out_refs = refs[:n_in], refs[n_in : n_in + n_out]
        weights = refs[n_in + n_out : n_in + n_out + n_weight]
        extra = refs[n_in + n_out + n_weight :]
        given, r, w, loads = [], 0, 0, []
        for kind, array in kinds:
            if kind in ("side", "split"):
                loads.append((array, in_refs[r], in_refs[r + 1], weights[w]))
                given.append(weights[w])
                r, w = r + 2, w + 1
            else:
                given.append(in_refs[r])
                r += 1
        step = pl.program_id(0)
        if loads:
            sem = extra[-1]
            extra = extra[:-1]

            @pl.when(step == 0)
            def _():
                mine = lax.axis_index("section")
                for n, load in enumerate(loads):
                    for which in range(2):

                        @pl.when(mine == which)
                        def _(load=load, n=n, which=which):
                            array, own, other, held = load
                            for copy in array.copies(which, own, other, held, sem.at[n]):
                                copy.start()

                for n, (array, own, other, held) in enumerate(loads):
                    for copy in array.copies(0, own, other, held, sem.at[n]):
                        copy.wait()

        for ref, (shape, dtype, kind) in zip(out_refs, outs):
            if kind == "sums":

                @pl.when(step == 0)
                def _(ref=ref):
                    ref[...] = jnp.zeros(ref.shape, ref.dtype)

        body(step, given, out_refs, extra)

    scratch_shapes = weight_scratch + list(scratch)
    if weight_scratch:
        scratch_shapes.append(pltpu.SemaphoreType.DMA((n_weight,)))
    total = sum(a.size * a.dtype.itemsize for a in arrays) + sum(
        2 * s[0] * s[1] for s, d, k in outs
    )
    return pl.pallas_call(
        kernel,
        name=name,
        grid=(steps,),
        in_specs=specs,
        out_specs=out_specs,
        out_shape=[jax.ShapeDtypeStruct(shape, dtype) for shape, dtype, kind in outs],
        scratch_shapes=scratch_shapes,
        compiler_params=pltpu.CompilerParams(
            dimension_semantics=("arbitrary",), vmem_limit_bytes=VMEM_BYTES
        ),
        cost_estimate=pl.CostEstimate(flops=int(flops), bytes_accessed=int(total), transcendentals=0),
    )(*arrays)


def row(ref, n):
    return ref[n : n + 1, :].astype(f32)


def clear_pads(weight, bands):
    for n in range(3):
        weight[n * 128 + bands : n * 128 + 128, :] = jnp.zeros((128 - bands, weight.shape[1]), weight.dtype)


def write_halves(values, keep, send):
    half = values.shape[1] // 2
    mine = lax.axis_index("section")
    first, second = values[:, :half], values[:, half:]

    @pl.when(mine == 0)
    def _():
        keep[...] = first
        send[...] = second.astype(low)

    @pl.when(mine != 0)
    def _():
        keep[...] = second
        send[...] = first.astype(low)


def project(inputs, weight, smalls, block):
    rows, width = inputs.shape[1:]

    def body(step, given, outs, extra):
        inputs, weight, smalls = given
        low_out, joint_out = outs
        normed, inverse = norm_rows(inputs[...].astype(f32))
        rounded = (normed * row(smalls, 0) + row(smalls, 3)).astype(low)
        low_out[...] = rounded
        part = dot(rounded, weight[:, :width])
        joint_out[:, :width] = (part + row(smalls, 6)).astype(low) * 0.125
        joint_out[:, width : 2 * width] = dot(rounded, weight[:, width : 2 * width]).astype(low)
        part = dot(rounded, weight[:, 2 * width :])
        joint_out[:, 2 * width :] = (part + row(smalls, 7)).astype(low)

    return call(
        body, "project", rows // block, block,
        [(inputs, "clip"), (weight, "side"), (smalls, "full")],
        [((rows, width), low, "rows"), ((rows, 3 * width), low, "rows")],
        flops=6 * rows * width * width,
    )


def attend(queries, keys, values, cols, causal, block):
    rows, key_rows = queries.shape[0], keys.shape[0]
    pairs, steps = HEADS // 2, rows // block

    def kernel(query_ref, key_ref, value_ref, mixed_ref, log_ref):
        lane = lax.broadcasted_iota(jnp.int32, (1, 128), 1)
        query, key, value = query_ref[...], key_ref[...], value_ref[...]
        mixed, logs = [], []
        for head in range(2):
            part = jnp.where(lane // 64 == head, query, jnp.zeros_like(query))
            scores = dot_t(part, key)
            if causal:
                key_at = lax.broadcasted_iota(jnp.int32, scores.shape, 1)
                query_at = lax.broadcasted_iota(jnp.int32, scores.shape, 0) + pl.program_id(1) * block
                scores = jnp.where(key_at <= query_at, scores, -1e30)
            top = jnp.max(scores, axis=1, keepdims=True) * log2_e
            exponent = jnp.exp2(scores * log2_e - top)
            total = jnp.sum(exponent, axis=1, keepdims=True)
            mixed.append(dot(exponent.astype(low), value) * (1.0 / total))
            logs.append(top + jnp.log2(total))
        mixed_ref[...] = jnp.where(lane < 64, mixed[0], mixed[1]).astype(low)
        both = jnp.where(lane == 0, logs[0], logs[1])
        log_ref[...] = both.T[0:8, :]

    q_at, k_at, v_at = cols
    return pl.pallas_call(
        kernel,
        name="attend",
        grid=(pairs, steps),
        in_specs=[
            pl.BlockSpec((block, 128), lambda h, i: (i, q_at + h)),
            pl.BlockSpec((key_rows, 128), lambda h, i: (0, k_at + h)),
            pl.BlockSpec((key_rows, 128), lambda h, i: (0, v_at + h)),
        ],
        out_specs=[
            pl.BlockSpec((block, 128), lambda h, i: (i, h)),
            pl.BlockSpec((8, block), lambda h, i: (h, i)),
        ],
        out_shape=[
            jax.ShapeDtypeStruct((rows, 128 * pairs), low),
            jax.ShapeDtypeStruct((8 * pairs, rows), f32),
        ],
        compiler_params=pltpu.CompilerParams(
            dimension_semantics=("arbitrary", "arbitrary"), vmem_limit_bytes=VMEM_BYTES
        ),
        cost_estimate=pl.CostEstimate(
            flops=16 * rows * key_rows * 512, bytes_accessed=2 * 512 * (2 * rows + 2 * key_rows), transcendentals=0
        ),
    )(queries, keys, values)


def attend_back(queries, keys, values, cols, logs, grad, causal, round_sums, block):
    rows, key_rows = queries.shape[0], keys.shape[0]
    pairs, steps = HEADS // 2, rows // block

    def kernel(
        query_ref, key_ref, value_ref, log_ref, grad_ref,
        query_out, key_out, value_out, sum_out, key_acc, value_acc, key_turned,
    ):
        step = pl.program_id(1)
        lane = lax.broadcasted_iota(jnp.int32, (1, 128), 1)

        @pl.when(step == 0)
        def _():
            key_acc[...] = jnp.zeros(key_acc.shape, f32)
            value_acc[...] = jnp.zeros(value_acc.shape, f32)
            sum_out[...] = jnp.zeros(sum_out.shape, f32)
            key_turned[...] = key_ref[...].astype(f32).T.astype(low)

        query, key, value, grad = query_ref[...], key_ref[...], value_ref[...], grad_ref[...]
        turned = key_turned[...]
        sub = lax.broadcasted_iota(jnp.int32, (128, 1), 0)
        query_turned = jnp.zeros((128, block), f32)
        for head in range(2):
            part = jnp.where(lane // 64 == head, query, jnp.zeros_like(query))
            grad_part = jnp.where(lane // 64 == head, grad, jnp.zeros_like(grad))
            scores = dot_t(key, part)
            chance = jnp.exp2(scores * log2_e - log_ref[head : head + 1, :])
            if causal:
                key_at = lax.broadcasted_iota(jnp.int32, scores.shape, 0)
                query_at = lax.broadcasted_iota(jnp.int32, scores.shape, 1) + step * block
                chance = jnp.where(key_at <= query_at, chance, 0.0)
            grad_chance = dot_t(value, grad_part)
            product = chance * grad_chance
            grad_scores = (product - chance * jnp.sum(product, axis=0, keepdims=True)).astype(low)
            value_acc[...] += dot(chance.astype(low), grad_part)
            key_acc[...] += dot(grad_scores, part)
            query_turned += dot(jnp.where(sub // 64 == head, turned, jnp.zeros_like(turned)), grad_scores)
        grad_query = query_turned.T * 0.125
        query_out[...] = grad_query.astype(low)
        sum_out[0:1, :] += col_sum(grad_query)

        @pl.when(step == steps - 1)
        def _():
            key_out[...] = key_acc[...].astype(low)
            rounded = value_acc[...].astype(low)
            value_out[...] = rounded
            sum_out[1:2, :] = col_sum(rounded.astype(f32) if round_sums else value_acc[...])

    q_at, k_at, v_at = cols
    row_spec = pl.BlockSpec((block, 128), lambda h, i: (i, h))
    key_spec = pl.BlockSpec((key_rows, 128), lambda h, i: (0, h))
    return pl.pallas_call(
        kernel,
        name="attend_back",
        grid=(pairs, steps),
        in_specs=[
            pl.BlockSpec((block, 128), lambda h, i: (i, q_at + h)),
            pl.BlockSpec((key_rows, 128), lambda h, i: (0, k_at + h)),
            pl.BlockSpec((key_rows, 128), lambda h, i: (0, v_at + h)),
            pl.BlockSpec((8, block), lambda h, i: (h, i)),
            row_spec,
        ],
        out_specs=[row_spec, key_spec, key_spec, pl.BlockSpec((8, 128), lambda h, i: (0, h))],
        out_shape=[
            jax.ShapeDtypeStruct((rows, 128 * pairs), low),
            jax.ShapeDtypeStruct((key_rows, 128 * pairs), low),
            jax.ShapeDtypeStruct((key_rows, 128 * pairs), low),
            jax.ShapeDtypeStruct((8, 128 * pairs), f32),
        ],
        scratch_shapes=[
            pltpu.VMEM((key_rows, 128), f32),
            pltpu.VMEM((key_rows, 128), f32),
            pltpu.VMEM((128, key_rows), low),
        ],
        compiler_params=pltpu.CompilerParams(
            dimension_semantics=("arbitrary", "arbitrary"), vmem_limit_bytes=VMEM_BYTES
        ),
        cost_estimate=pl.CostEstimate(
            flops=40 * rows * key_rows * 512, bytes_accessed=2 * 512 * (4 * rows + 4 * key_rows), transcendentals=0
        ),
    )(queries, keys, values, logs, grad)


def audio_feed(inputs, mixed, weight_out, smalls, ups, weight_up, weight_down, cross_a, cross_b, block):
    rows, width = inputs.shape
    hidden = ups.shape[1]

    def body(step, given, outs, extra):
        inputs, mixed, weight_out, smalls, ups, weight_up, weight_down, cross_a, cross_b = given
        middle_out, norm_out, hidden_out, slope_out, ending_out, memory_out, key_out, value_out = outs
        middle = inputs[...] + dot(mixed[...], weight_out[...]) + row(smalls, 8)
        middle_out[...] = middle
        normed, inverse = norm_rows(middle)
        rounded = (normed * row(smalls, 1) + row(smalls, 4)).astype(low)
        norm_out[...] = rounded
        ending = middle + row(smalls, 9)
        for part in range(hidden // 512):
            cols = slice(part * 512, part * 512 + 512)
            pre = dot(rounded, weight_up[:, cols]) + ups[:, cols].astype(f32)
            value, slope = gelu_both(pre)
            act = value.astype(low)
            hidden_out[:, cols] = act
            slope_out[:, cols] = slope.astype(low)
            ending += dot(act, weight_down[cols, :])
        ending_out[...] = ending
        normed, inverse = norm_rows(ending)
        memory = (normed * row(smalls, 2) + row(smalls, 5)).astype(low)
        memory_out[...] = memory
        key_out[...] = dot(memory, cross_a[...]).astype(low)
        value_out[...] = (dot(memory, cross_b[...]) + row(smalls, 11)).astype(low)

    wide, shape = (rows, hidden), (rows, width)
    return call(
        body, "audio_feed", rows // block, block,
        [(inputs, "rows"), (mixed, "rows"), (weight_out, "side"), (smalls, "full"), (ups, "full"),
         (weight_up, "side"), (weight_down, "side"), (cross_a, "side"), (cross_b, "side")],
        [(shape, f32, "rows"), (shape, low, "rows"), (wide, low, "rows"), (wide, low, "rows"),
         (shape, f32, "rows"), (shape, low, "rows"), (shape, low, "rows"), (shape, low, "rows")],
        flops=2 * rows * width * (3 * width + 2 * hidden),
    )


def text_middle(inputs, mixed, weight_out, smalls, cross_a, block):
    rows, width = mixed.shape

    def body(step, given, outs, extra):
        inputs, mixed, weight_out, smalls, cross_a = given
        middle_out, low_out, query_out = outs
        middle = inputs[...].astype(f32) + dot(mixed[...], weight_out[...]) + row(smalls, 8)
        middle_out[...] = middle
        normed, inverse = norm_rows(middle)
        rounded = (normed * row(smalls, 1) + row(smalls, 4)).astype(low)
        low_out[...] = rounded
        query_out[...] = (dot(rounded, cross_a[...]) + row(smalls, 10)).astype(low) * 0.125

    shape = (rows, width)
    return call(
        body, "text_middle", rows // block, block,
        [(inputs, "clip"), (mixed, "rows"), (weight_out, "side"), (smalls, "full"), (cross_a, "side")],
        [(shape, f32, "rows"), (shape, low, "rows"), (shape, low, "rows")],
        flops=4 * rows * width * width,
    )


def text_feed(length, middle, mixed, cotangent, cross_b, smalls, ups, weight_up, weight_down, block):
    rows, width = middle.shape
    hidden = ups.shape[1]

    def body(step, given, outs, extra):
        length, middle, mixed, cotangent, cross_b, smalls, ups, weight_up, weight_down = given
        decoded_keep, decoded_send, norm_out, hidden_out, pre_out, cot_out, grad_out, grad_low, mixed_out, sums, wide_sums = outs
        after = middle[...] + dot(mixed[...], cross_b[...]) + row(smalls, 11)
        normed, inverse = norm_rows(after)
        rounded = (normed * row(smalls, 2) + row(smalls, 5)).astype(low)
        norm_out[...] = rounded
        at_row = lax.broadcasted_iota(jnp.int32, (block, 1), 0) + step * block
        valid = at_row < length[lax.axis_index("section")]
        grad = jnp.where(valid, cotangent[...].astype(f32), 0.0)
        cot = grad.astype(low)
        cot_out[...] = cot
        ending = after + row(smalls, 9)
        back = jnp.zeros((block, width), f32)
        for part in range(hidden // 512):
            cols = slice(part * 512, part * 512 + 512)
            pre = dot(rounded, weight_up[:, cols]) + ups[:, cols].astype(f32)
            value, slope = gelu_both(pre)
            act = value.astype(low)
            hidden_out[:, cols] = act
            ending += dot(act, weight_down[cols, :])
            grad_pre = dot_t(cot, weight_down[cols, :]) * slope
            wide_sums[0:1, cols] += col_sum(grad_pre)
            pre_low = grad_pre.astype(low)
            pre_out[:, cols] = pre_low
            back += dot_t(pre_low, weight_up[:, cols])
        write_halves(jnp.where(valid, ending, 0.0), decoded_keep, decoded_send)
        sums[0:1, :] += col_sum(back * normed)
        sums[1:2, :] += col_sum(back)
        sums[2:3, :] += col_sum(grad)
        grad = grad + norm_back(back, row(smalls, 2), normed, inverse)
        sums[3:4, :] += col_sum(grad)
        grad_out[...] = grad
        rounded = grad.astype(low)
        grad_low[...] = rounded
        mixed_out[...] = dot_t(rounded, cross_b[...]).astype(low)

    wide, shape = (rows, hidden), (rows, width)
    return call(
        body, "text_feed", rows // block, block,
        [(length, "smem"), (middle, "rows"), (mixed, "rows"), (cotangent, "clip"), (cross_b, "side"),
         (smalls, "full"), (ups, "full"), (weight_up, "side"), (weight_down, "side")],
        [((rows, width // 2), f32, "rows"), ((rows, width // 2), low, "rows"), (shape, low, "rows"), (wide, low, "rows"),
         (wide, low, "rows"), (shape, low, "rows"), (shape, f32, "rows"), (shape, low, "rows"), (shape, low, "rows"),
         ((8, width), f32, "sums"), ((8, hidden), f32, "sums")],
        flops=2 * rows * width * (2 * width + 4 * hidden),
    )


def text_cross_back(query_grad, middle, grad, smalls, cross_a, weight_out, block):
    rows, width = middle.shape

    def body(step, given, outs, extra):
        query_grad, middle, grad, smalls, cross_a, weight_out = given
        grad_out, low_out, mixed_out, sums = outs
        back = dot_t(query_grad[...], cross_a[...])
        normed, inverse = norm_rows(middle[...])
        sums[0:1, :] += col_sum(back * normed)
        sums[1:2, :] += col_sum(back)
        total = grad[...] + norm_back(back, row(smalls, 1), normed, inverse)
        sums[2:3, :] += col_sum(total)
        grad_out[...] = total
        rounded = total.astype(low)
        low_out[...] = rounded
        mixed_out[...] = dot_t(rounded, weight_out[...]).astype(low)

    shape = (rows, width)
    return call(
        body, "text_cross_back", rows // block, block,
        [(query_grad, "rows"), (middle, "rows"), (grad, "rows"), (smalls, "full"), (cross_a, "side"), (weight_out, "side")],
        [(shape, f32, "rows"), (shape, low, "rows"), (shape, low, "rows"), ((8, width), f32, "sums")],
        flops=4 * rows * width * width,
    )


def project_back(query_grad, key_grad, value_grad, inputs, grad, smalls, weight, block):
    rows, width = grad.shape

    def body(step, given, outs, extra):
        query_grad, key_grad, value_grad, inputs, grad, smalls, weight = given
        grad_keep, grad_send, sums = outs
        back = (
            dot_t(query_grad[...], weight[:, :width])
            + dot_t(key_grad[...], weight[:, width : 2 * width])
            + dot_t(value_grad[...], weight[:, 2 * width :])
        )
        normed, inverse = norm_rows(inputs[...].astype(f32))
        sums[0:1, :] += col_sum(back * normed)
        sums[1:2, :] += col_sum(back)
        write_halves(grad[...] + norm_back(back, row(smalls, 0), normed, inverse), grad_keep, grad_send)

    return call(
        body, "project_back", rows // block, block,
        [(query_grad, "rows"), (key_grad, "rows"), (value_grad, "rows"), (inputs, "clip"), (grad, "rows"),
         (smalls, "full"), (weight, "side")],
        [((rows, width // 2), f32, "rows"), ((rows, width // 2), low, "rows"), ((8, width), f32, "sums")],
        flops=6 * rows * width * width,
    )


def audio_feed_back(key_grad, value_grad, ending, middle, slope, smalls, cross_a, cross_b, weight_up, weight_down, weight_out, block):
    rows, width = ending.shape
    hidden = slope.shape[1]

    def body(step, given, outs, extra):
        key_grad, value_grad, ending, middle, slope, smalls, cross_a, cross_b, weight_up, weight_down, weight_out = given
        end_low, pre_out, grad_out, grad_low, mixed_out, sums, wide_sums = outs
        back = dot_t(key_grad[...], cross_a[...]) + dot_t(value_grad[...], cross_b[...])
        normed, inverse = norm_rows(ending[...])
        sums[0:1, :] += col_sum(back * normed)
        sums[1:2, :] += col_sum(back)
        grad = norm_back(back, row(smalls, 2), normed, inverse)
        sums[2:3, :] += col_sum(grad)
        rounded = grad.astype(low)
        end_low[...] = rounded
        back = jnp.zeros((block, width), f32)
        for part in range(hidden // 512):
            cols = slice(part * 512, part * 512 + 512)
            grad_pre = dot_t(rounded, weight_down[cols, :]) * slope[:, cols].astype(f32)
            wide_sums[0:1, cols] += col_sum(grad_pre)
            pre_low = grad_pre.astype(low)
            pre_out[:, cols] = pre_low
            back += dot_t(pre_low, weight_up[:, cols])
        normed, inverse = norm_rows(middle[...])
        sums[3:4, :] += col_sum(back * normed)
        sums[4:5, :] += col_sum(back)
        grad = grad + norm_back(back, row(smalls, 1), normed, inverse)
        sums[5:6, :] += col_sum(grad)
        grad_out[...] = grad
        rounded = grad.astype(low)
        grad_low[...] = rounded
        mixed_out[...] = dot_t(rounded, weight_out[...]).astype(low)

    wide, shape = (rows, hidden), (rows, width)
    return call(
        body, "audio_feed_back", rows // block, block,
        [(key_grad, "rows"), (value_grad, "rows"), (ending, "rows"), (middle, "rows"), (slope, "rows"), (smalls, "full"),
         (cross_a, "side"), (cross_b, "side"), (weight_up, "side"), (weight_down, "side"), (weight_out, "side")],
        [(shape, low, "rows"), (wide, low, "rows"), (shape, f32, "rows"), (shape, low, "rows"), (shape, low, "rows"),
         ((8, width), f32, "sums"), ((8, hidden), f32, "sums")],
        flops=2 * rows * width * (3 * width + 2 * hidden),
    )


def unpack(total, bands):
    width, half = total.shape[1], total.shape[1] // 2
    tiles = 14

    def kernel(total, joint, out, up, down, cross_a, cross_b, first, bias, second, gain, shift, wide, small, cross, held, found, in_sem, out_sem):
        def load(n):
            here = pl.ds(pl.multiple_of(n * width, width), width)
            return pltpu.make_async_copy(total.at[here], held.at[n], in_sem.at[n])

        def target(n):
            cols = lambda k: slice(k * width, k * width + width)
            if n < 4:
                return up.at[0, :, cols(n)]
            if n < 8:
                return down.at[0, cols(n - 4)]
            if n < 11:
                return (cross_a, cross_b, out)[n - 8].at[0]
            return joint.at[0, :, cols(n - 11)]

        def store(n):
            return pltpu.make_async_copy(found.at[n], target(n), out_sem.at[n])

        @pl.loop(0, tiles + 2)
        def _(n):
            load(n).start()

        @pl.loop(0, tiles)
        def _(n):
            load(n).wait()
            found[n] = held[n].astype(f32)
            for k in range(tiles):

                @pl.when(n == k)
                def _(k=k):
                    store(k).start()

        load(tiles).wait()
        load(tiles + 1).wait()
        tile = held.at[tiles]
        second[0] = tile[:, 0:half].astype(f32)
        second[1, half:width] = tile[0:half, half:width].astype(f32)
        second[2, 0:half] = tile[half:width, half:width].astype(f32)
        tile = held.at[tiles + 1]
        second[1, 0:half] = tile[0:half, 0:half].astype(f32)
        second[2, half:width] = tile[0:half, half:width].astype(f32)
        first[0] = tile[half : half + bands, 0:half].astype(f32)
        first[1, 0:64] = tile[half + 128 : half + 192, 0:half].astype(f32)
        first[1, 64:bands] = tile[half : half + bands - 64, half:width].astype(f32)
        first[2] = tile[half + 64 : half + 64 + bands, half:width].astype(f32)
        rows = tile[half + 192 : half + 224, :].astype(f32)
        gain[0] = rows[0:3]
        shift[0] = rows[3:6]
        small[0] = rows[6:12]
        for n in range(4):
            wide[:, n * width : (n + 1) * width] = rows[12 + n : 13 + n]
        bias[...] = rows[16:17, 0:half]
        mine = lax.axis_index("section")
        cross[...] = jnp.where(mine == 0, rows[17:18, 0:half], rows[17:18, half:width])
        for n in range(tiles):
            store(n).wait()

    shapes = [
        (1, width, 3 * width), (1, width, width), (1, width, 4 * width), (1, 4 * width, width), (1, width, width), (1, width, width),
        (3, bands, half), (1, half), (3, width, half), (1, 3, width), (1, 3, width), (1, 4 * width), (1, 6, width), (1, half),
    ]
    return pl.pallas_call(
        kernel,
        name="unpack",
        in_specs=[pl.BlockSpec(memory_space=pl.ANY)],
        out_specs=[pl.BlockSpec(memory_space=pl.ANY)] * 6 + [pl.BlockSpec(memory_space=pltpu.VMEM)] * 8,
        out_shape=[jax.ShapeDtypeStruct(shape, f32) for shape in shapes],
        scratch_shapes=[
            pltpu.VMEM((tiles + 2, width, width), low), pltpu.VMEM((tiles, width, width), f32),
            pltpu.SemaphoreType.DMA((tiles + 2,)), pltpu.SemaphoreType.DMA((tiles,)),
        ],
        compiler_params=pltpu.CompilerParams(vmem_limit_bytes=VMEM_BYTES),
        cost_estimate=pl.CostEstimate(flops=0, bytes_accessed=6 * total.size, transcendentals=0),
    )(total)


def finish(parts, mel_keep, mel_got, spans, bands):
    count = len(parts)
    pair_rows = mel_keep.shape[0]
    frames = 2 * pair_rows

    def kernel(*refs):
        pairs, (keep_ref, got_ref), marks = refs[: 2 * count], refs[2 * count : 2 * count + 2], refs[2 * count + 2 : 2 * count + 6]
        outs, mel_out, laid = refs[2 * count + 6 : 3 * count + 6], refs[3 * count + 6], refs[3 * count + 7]
        mine = lax.axis_index("section")
        for n, out in enumerate(outs):
            out[mine] = pairs[2 * n][...]
            out[1 - mine] = pairs[2 * n + 1][...].astype(f32)
        band_at = lax.broadcasted_iota(jnp.int32, (bands, frames), 0)
        frame_at = lax.broadcasted_iota(jnp.int32, (bands, frames), 1) + mine * frames
        for clip, ref in ((mine, keep_ref), (1 - mine, got_ref)):
            for n in range(2):
                laid[pl.ds(n, pair_rows, stride=2), :] = ref[:, n * 128 : n * 128 + 128].astype(f32)
            start, span, band, width = (mark[clip] for mark in marks)
            keep = jnp.logical_and(
                jnp.logical_or(band_at < band, band_at >= band + width),
                jnp.logical_or(frame_at < start, frame_at >= start + span),
            )
            mel_out[clip] = jnp.where(keep, laid[...].T[0:bands, :], 0.0)

    flat = [array for pair in parts for array in pair]
    return pl.pallas_call(
        kernel,
        name="finish",
        in_specs=[pl.BlockSpec(memory_space=pltpu.VMEM)] * (2 * count + 2) + [pl.BlockSpec(memory_space=pltpu.SMEM)] * 4,
        out_shape=[jax.ShapeDtypeStruct((2,) + keep.shape, f32) for keep, got in parts]
        + [jax.ShapeDtypeStruct((2, bands, frames), f32)],
        scratch_shapes=[pltpu.VMEM((frames, 128), f32)],
        compiler_params=pltpu.CompilerParams(vmem_limit_bytes=VMEM_BYTES),
        cost_estimate=pl.CostEstimate(flops=0, bytes_accessed=sum(8 * a.size for a in flat), transcendentals=0),
    )(*flat, mel_keep, mel_got, *spans)


def begin(mel_input, spans, gain, shift, biases, up_bias, first_bias, first, second, joint_weight, weights, positions):
    frames, width = positions.shape
    bands, mel_frames = mel_input.shape[1:]
    lanes = width // 2
    hidden = up_bias.shape[1]
    block = 256
    blocks = frames // block
    sent = [second, joint_weight] + weights
    n_sent = len(sent)
    pieces = []
    for n, array in enumerate(sent):
        cuts = 2 if array.size >= 700000 else 1
        size = array.shape[0] // cuts
        pieces += [(n, c * size, size) for c in range(cuts)]
    n_pieces = len(pieces)
    flying = 2
    first_held = Split(first, first, 3, 128)
    second_held = Split(second, second, 3, width)
    n_any = n_sent + 3

    def kernel(*refs):
        mel_ref, positions_ref, first_ref = refs[:3]
        own = refs[3:n_any]
        times, time_spans, bands_from, band_spans = refs[n_any : n_any + 4]
        gain, shift, biases, up_bias, first_bias = refs[n_any + 4 : n_any + 9]
        outs = refs[n_any + 9 :]
        first_other = outs[0]
        other = outs[1 : 1 + n_sent]
        a_small, t_small, a_ups, t_ups = outs[1 + n_sent : 5 + n_sent]
        results = outs[5 + n_sent : 16 + n_sent]
        (
            taps, encoded, even_act, odd_act, even_slope, odd_slope, slope_second, norm, joint, mixed, logs,
            mel, turned, place, conv_first, conv_second, weight, carry, pack, pack_other,
            load_sem, weight_sem, out_sem, side_sem, near_sem, core_sem,
        ) = outs[16 + n_sent :]
        held = (taps, encoded, even_act, odd_act, even_slope, odd_slope, slope_second, norm, joint, mixed, logs)

        section, replica = lax.axis_index("section"), lax.axis_index("dp")
        side_peer = {"section": 1 - section}

        def flipped(value, bit):
            return value + bit - 2 * bit * ((value // bit) % 2)

        def peer(bit):
            return {"dp": flipped(replica, bit)}

        def remote(source, target, sems, at, device):
            return pltpu.make_async_remote_copy(
                src_ref=source, dst_ref=target, send_sem=sems.at[(0,) + at], recv_sem=sems.at[(1,) + at],
                device_id=device, device_id_type=pl.DeviceIdType.MESH,
            )

        def part(p, q):
            n, start, size = pieces[p]
            return pl.ds(pl.multiple_of(start + q * (size // 4), 16), size // 4)

        def near(p):
            bit = 4 if p % 2 else 2
            quarter = replica % 2 + 2 * ((replica // bit) % 2)
            return bit, (quarter, flipped(quarter, 2))

        def side_copy(p):
            n = pieces[p][0]
            here = part(p, near(p)[1][0])
            return remote(own[n].at[here], other[n].at[here], side_sem, (p,), side_peer)

        def pass_on(p, q, sems, at, bit):
            here = other[pieces[p][0]].at[part(p, q)]
            return remote(here, here, sems, at, peer(bit))

        def near_copies(p):
            bit, quarters = near(p)
            return [pass_on(p, quarters[0], near_sem, (p,), bit)]

        def core_copies(p):
            return [pass_on(p, q, core_sem, (b, p), 1) for b, q in enumerate(near(p)[1])]

        hops = (lambda p: [side_copy(p)], near_copies, core_copies)

        def advance(p, n):
            for copy in hops[n](p):
                copy.wait_recv()
            if n == 0 and p + flying < n_pieces:
                side_copy(p + flying).start()
            if n + 1 < len(hops):
                for copy in hops[n + 1](p):
                    copy.start()

        def tick(at):
            if at < 4:
                turn = [[(1, 0)], [(2, 0), (1, 1)], [(3, 0), (2, 1), (1, 2)], [(4, 0), (2, 2)]][at]
            else:
                turn = [(at + 1, 0), (at - 1, 1), (at - 2, 2)]
            for p, n in turn:
                if (3 if n else 1) <= p < n_pieces or at < 4:
                    advance(p, n)

        pack_copy = remote(pack, pack_other, side_sem, (n_pieces,), side_peer)
        first_copy = remote(first_ref, first_other, side_sem, (n_pieces + 1,), side_peer)
        loads = [
            pltpu.make_async_copy(mel_ref.at[section], mel, load_sem.at[0]),
            pltpu.make_async_copy(positions_ref, place, load_sem.at[1]),
        ]

        def conv_copies(mine):
            return first_held.copies(mine, first_ref, first_other, conv_first, weight_sem.at[0]) + second_held.copies(
                mine, own[0], other[0], conv_second, weight_sem.at[1]
            )

        def weight_copy(mine):
            return pltpu.make_async_copy(own[1] if mine == 0 else other[1], weight, weight_sem.at[2])

        def keep(n):
            return pltpu.make_async_copy(held[n], results[n], out_sem.at[n])

        barrier = pltpu.get_barrier_semaphore()
        peers = [side_peer] + [peer(bit) for bit in (1, 2, 4)]
        for device in peers:
            pl.semaphore_signal(barrier, inc=1, device_id=device, device_id_type=pl.DeviceIdType.MESH)
        for copy in loads:
            copy.start()
        pack[0:3, :] = gain[...].astype(f32)
        pack[3:6, :] = shift[...].astype(f32)
        pack[6:12, :] = biases[...].astype(f32)
        for n in range(hidden // width):
            pack[12 + n : 13 + n, :] = up_bias[:, n * width : n * width + width].astype(f32)
        pack[16:17, 0:lanes] = first_bias[...].astype(f32)
        pack[16:17, lanes:width] = jnp.zeros((1, lanes), f32)
        pack[17:24, :] = jnp.zeros((7, width), f32)
        pl.semaphore_wait(barrier, len(peers))
        side_copy(0).start()
        first_copy.start()
        pack_copy.start()
        for p in range(1, flying):
            side_copy(p).start()

        turned[0:8, :] = jnp.zeros((8, 128), f32)
        turned[8 + mel_frames : 16 + mel_frames, :] = jnp.zeros((8, 128), f32)
        carry[...] = jnp.zeros(carry.shape, f32)
        clear_pads(conv_first, bands)
        for copy in loads:
            copy.wait()
        band_at = lax.broadcasted_iota(jnp.int32, (bands, block), 0)
        frame_at = lax.broadcasted_iota(jnp.int32, (bands, block), 1)
        time_from, band_from = times[section], bands_from[section]
        time_to, band_to = time_from + time_spans[section], band_from + band_spans[section]
        band_keep = jnp.logical_or(band_at < band_from, band_at >= band_to)
        for n in range(mel_frames // block):
            at = frame_at + n * block
            keep_here = jnp.logical_and(band_keep, jnp.logical_or(at < time_from, at >= time_to))
            values = jnp.where(keep_here, mel[:, n * block : n * block + block].astype(f32), 0.0)
            values = jnp.concatenate([values, jnp.zeros((128 - bands, block), f32)], axis=0)
            turned[8 + n * block : 8 + n * block + block, :] = values.T
        for n, start in enumerate((7, 8, 9, 10)):
            taps[:, n * 128 : n * 128 + 128] = turned[pl.ds(start, frames, stride=2), :].astype(low)
        keep(0).start()

        for n in range(len(hops)):
            advance(0, n)
        first_copy.wait_recv()
        pack_copy.wait_recv()
        for which in range(2):

            @pl.when(section == which)
            def _(which=which):
                for copy in conv_copies(which):
                    copy.start()

        first_section = section == 0
        a_small[...] = jnp.where(first_section, pack[...], pack_other[...])
        t_small[...] = jnp.where(first_section, pack_other[...], pack[...])
        for n in range(hidden // width):
            a_ups[:, n * width : n * width + width] = a_small[12 + n : 13 + n, :]
            t_ups[:, n * width : n * width + width] = t_small[12 + n : 13 + n, :]
        bias = jnp.concatenate([a_small[16:17, 0:lanes], t_small[16:17, 0:lanes]], axis=1)
        for copy in conv_copies(0):
            copy.wait()

        def stem_block(i):
            here = pl.ds(pl.multiple_of(i * block, block), block)
            value, slope = gelu_both(dot(taps[here, 0:384], conv_first[...]) + bias)
            even = value.astype(low)
            even_act[here] = even
            even_slope[here] = slope.astype(low)
            value, slope = gelu_both(dot(taps[here, 128:512], conv_first[...]) + bias)
            odd = value.astype(low)
            odd_act[here] = odd
            odd_slope[here] = slope.astype(low)
            prior = dot(odd, conv_second[0:width])
            at_row = lax.broadcasted_iota(jnp.int32, (block, width), 0)
            moved = jnp.where(at_row == 0, carry[0:1, :], pltpu.roll(prior, 1, 0))
            carry[0:1, :] = prior[block - 1 : block, :]
            pre = moved + dot(even, conv_second[width : 2 * width]) + dot(odd, conv_second[2 * width :]) + row(a_small, 10)
            value, slope = gelu_both(pre)
            slope_second[here] = slope.astype(low)
            encoded[here] = value + place[here].astype(f32)

        for i in range(blocks):
            stem_block(i)
            tick(i)
        for n in range(1, 7):
            keep(n).start()
        for which in range(2):

            @pl.when(section == which)
            def _(which=which):
                weight_copy(which).start()

        weight_copy(0).wait()

        def project_block(i):
            here = pl.ds(pl.multiple_of(i * block, block), block)
            normed, inverse = norm_rows(encoded[here])
            rounded = (normed * row(a_small, 0) + row(a_small, 3)).astype(low)
            norm[here] = rounded
            joint[here, 0:width] = (dot(rounded, weight[:, 0:width]) + row(a_small, 6)).astype(low) * 0.125
            joint[here, width : 2 * width] = dot(rounded, weight[:, width : 2 * width]).astype(low)
            joint[here, 2 * width :] = (dot(rounded, weight[:, 2 * width :]) + row(a_small, 7)).astype(low)

        for i in range(blocks):
            project_block(i)
        tick(blocks)
        keep(7).start()
        keep(8).start()

        def attention(pair):
            lane = lax.broadcasted_iota(jnp.int32, (1, 128), 1)

            def cols(start):
                return pl.ds(pl.multiple_of(start + pair * 128, 128), 128)

            key, value = joint[:, cols(width)], joint[:, cols(2 * width)]

            @pl.loop(0, blocks)
            def _(i):
                here = pl.ds(pl.multiple_of(i * block, block), block)
                query = joint[here, cols(0)]
                found, log = [], []
                for head in range(2):
                    scores = dot_t(jnp.where(lane // 64 == head, query, jnp.zeros_like(query)), key)
                    top = jnp.max(scores, axis=1, keepdims=True) * log2_e
                    exponent = jnp.exp2(scores * log2_e - top)
                    total = jnp.sum(exponent, axis=1, keepdims=True)
                    found.append(dot(exponent.astype(low), value) * (1.0 / total))
                    log.append(top + jnp.log2(total))
                mixed[here, cols(0)] = jnp.where(lane < 64, found[0], found[1]).astype(low)
                both = jnp.where(lane == 0, log[0], log[1])
                logs[pl.ds(pl.multiple_of(pair * 8, 8), 8), here] = both.T[0:8, :]

        done = blocks + 1
        for pair in range(HEADS // 2):
            attention(pair)
            tick(done)
            done += 1
        while done < n_pieces + len(hops) - 1:
            tick(done)
            done += 1
        keep(9).start()
        keep(10).start()
        for p in range(n_pieces):
            for hop in hops:
                for copy in hop(p):
                    copy.wait_send()
        first_copy.wait_send()
        pack_copy.wait_send()
        for n in range(len(held)):
            keep(n).wait()

    def sems(*shape):
        return pltpu.SemaphoreType.DMA(shape)

    shape = (frames, width)
    kept = [(shape, low), (shape, f32)] + [(shape, low)] * 6 + [((frames, 3 * width), low), (shape, low), ((4 * HEADS, frames), f32)]
    everywhere, on_chip = pl.BlockSpec(memory_space=pl.ANY), pl.BlockSpec(memory_space=pltpu.VMEM)
    return pl.pallas_call(
        kernel,
        name="begin",
        in_specs=[everywhere] * n_any + [pl.BlockSpec(memory_space=pltpu.SMEM)] * 4 + [on_chip] * 5,
        out_specs=[everywhere] * (1 + n_sent) + [on_chip] * 4 + [everywhere] * len(kept),
        out_shape=[jax.ShapeDtypeStruct(a.shape, a.dtype) for a in [first] + sent]
        + [jax.ShapeDtypeStruct(s, f32) for s in ((24, width), (24, width), (1, hidden), (1, hidden))]
        + [jax.ShapeDtypeStruct(s, d) for s, d in kept],
        scratch_shapes=[pltpu.VMEM(s, d) for s, d in kept]
        + [
            pltpu.VMEM((bands, mel_frames), low), pltpu.VMEM((mel_frames + 16, 128), f32), pltpu.VMEM(shape, low),
            pltpu.VMEM((384, width), low), pltpu.VMEM((3 * width, width), low), pltpu.VMEM((width, 3 * width), low),
            pltpu.VMEM((8, width), f32), pltpu.VMEM((24, width), f32), pltpu.VMEM((24, width), f32),
            sems(2), sems(3), sems(len(kept)), sems(2, n_pieces + 2), sems(2, n_pieces), sems(2, 2, n_pieces),
        ],
        compiler_params=pltpu.CompilerParams(collective_id=1, has_side_effects=True, vmem_limit_bytes=VMEM_BYTES),
        cost_estimate=pl.CostEstimate(flops=10**10, bytes_accessed=10**8, transcendentals=0),
    )(mel_input, positions, first, *sent, *spans, gain, shift, biases, up_bias, first_bias)


def factors_of(size):
    found, rest = [], size // 2
    while rest > 1:
        radix = 2 if rest in (2, 8) or rest % 4 else 4
        found.append(radix)
        rest //= radix
    return found


def finish_backward(audio, text, joint, logs, mixed_grad, grad, encoded, slopes, smalls, weight, second, first, acts, audio_sums, text_sums, bands):
    width, tile_rows = 512, 512
    half = tile_rows // 2
    lanes = width // 2
    frames, text_rows = joint.shape[0], text[0][0].shape[0]
    tiles = len(audio)
    count = tiles + 2
    early = 11
    flying = 3
    rows = count * tile_rows
    block = 256
    blocks = frames // block
    replicas = lax.axis_size("dp")
    factors = factors_of(replicas)
    levels = len(factors)
    befores, sizes, scatters = [], [], []
    for radix in factors:
        before = sizes[-1] if sizes else half
        befores.append(before)
        scatters.append(before % (16 * radix) == 0)
        sizes.append(before // radix if scatters[-1] else before)

    arrays, places = [], {}

    def place(array):
        if id(array) not in places:
            places[id(array)] = len(arrays)
            arrays.append(array)
        return places[id(array)]

    def job(x, xc, y, yc):
        return (place(x), xc, y if isinstance(y, int) else (place(y),), yc)

    audio_jobs = [job(*one) for one in audio]
    text_jobs = [job(*one) for one in text]
    at_joint, at_logs, at_mixed, at_grad, at_encoded = [place(a) for a in (joint, logs, mixed_grad, grad, encoded)]
    at_slopes = [place(a) for a in slopes]
    odd_act, even_act, taps = acts
    at_odd, at_even, at_taps = place(odd_act), place(even_act), place(taps)
    at_weight = (place(weight.own), place(weight.other))
    at_second = (place(second.own), place(second.other))
    at_first = (place(first.own), place(first.other))
    n_any = len(arrays)
    n_chip = 1 + len(audio_sums) + len(text_sums)

    def kernel(*refs):
        given = refs[:n_any]
        smalls, *known = refs[n_any : n_any + n_chip]
        audio_sums, text_sums = known[:2], known[2:]
        out_ref, keep_ref, got_ref = refs[n_any + n_chip : n_any + n_chip + 3]
        refs = refs[n_any + n_chip + 3 :]
        (
            tile, core_recv, side_send, side_recv, work, final, x_audio, y_audio, x_text, y_text,
            joint, logs, mixed_grad, query_grad, key_grad, value_grad, key_acc, value_acc, key_turned, sums,
            encoded_in, grad_in, slope_in, weight, second, first, second_low, next_low, even_low, odd_low, taps_grad,
            carry, conv_buf, small_buf, mel_buf, mel_send,
            in_sem, load_sem, weight_sem, block_sem, keep_sem, core_sem, side_sem, back_sem, out_sem, mel_sem,
        ) = refs[:46]
        recvs = refs[46 : 46 + levels]
        rs_sems = refs[46 + levels : 46 + 2 * levels]
        ag_sems = refs[46 + 2 * levels :]
        own_grads = (query_grad, key_grad, value_grad)

        section, replica = lax.axis_index("section"), lax.axis_index("dp")
        core = replica % 2
        digits, strides, rest, stride = [], [], replica // 2, 2
        for radix in factors:
            digits.append(rest % radix)
            strides.append(stride)
            rest, stride = rest // radix, stride * radix
        core_peer = {"dp": replica + 1 - 2 * core}
        side_peer = {"section": 1 - section}

        def peer(level, distance):
            digit = (digits[level] + distance) % factors[level]
            return digit, {"dp": replica + (digit - digits[level]) * strides[level]}

        def remote(source, target, sems, at, device):
            return pltpu.make_async_remote_copy(
                src_ref=source, dst_ref=target, send_sem=sems.at[(0,) + at], recv_sem=sems.at[(1,) + at],
                device_id=device, device_id_type=pl.DeviceIdType.MESH,
            )

        def rows_at(start, size):
            return pl.ds(pl.multiple_of(start, 16), size)

        def offset(level):
            found = 0
            for n in range(level):
                if scatters[n]:
                    found = found + digits[n] * sizes[n]
            return found

        def core_copy(k):
            return remote(
                tile.at[k % 2, :, rows_at((1 - core) * half, half)], core_recv.at[k % 4], core_sem, (k,), core_peer
            )

        def side_copy(k):
            here = rows_at(k * half, half)
            return remote(side_send.at[here], side_recv.at[here], side_sem, (k,), side_peer)

        def scatter_copy(k, level, distance):
            digit, device = peer(level, distance)
            size = sizes[level]
            start = k * half + offset(level) + (digit * size if scatters[level] else 0)
            return remote(
                work.at[rows_at(start, size)], recvs[level].at[distance - 1, rows_at(k * size, size)],
                rs_sems[level], (distance - 1, k), device,
            )

        def gather_copy(k, level, distance):
            digit, device = peer(level, distance)
            here = final.at[rows_at(k * tile_rows + core * half + offset(level + 1), sizes[level])]
            return remote(here, here, ag_sems[level], (distance - 1, k), device)

        def back_copy(k):
            here = final.at[rows_at(k * tile_rows + core * half, half)]
            return remote(here, here, back_sem, (k,), core_peer)

        def store(k):
            here = rows_at(k * tile_rows, tile_rows)
            return pltpu.make_async_copy(final.at[here], out_ref.at[here], out_sem.at[k])

        def mel_copy():
            return remote(mel_send, got_ref, mel_sem, (), side_peer)

        def stage_core(k):
            core_copy(k).wait_recv()
            here, mine = rows_at(k * half, half), rows_at(core * half, half)
            slot, from_peer = k % 2, k % 4
            side_send[here] = (
                tile[slot, 1 - section, mine].astype(f32) + core_recv[from_peer, 1 - section].astype(f32)
            ).astype(low)

            @when(jnp.logical_or(k < flying, k == tiles))
            def _():
                side_copy(k).start()

            work[here] = (tile[slot, section, mine].astype(f32) + core_recv[from_peer, section].astype(f32)).astype(low)

        scatter_levels = [n for n in range(levels) if scatters[n]]

        def next_exchange(k, level):
            if level + 1 < levels:
                for distance in range(1, factors[level + 1]):
                    scatter_copy(k, level + 1, distance).start()
            elif scatter_levels:
                for distance in range(1, factors[scatter_levels[-1]]):
                    gather_copy(k, scatter_levels[-1], distance).start()
            else:
                back_copy(k).start()

        def put(k, level, total):
            if level + 1 < levels:
                work[rows_at(k * half + offset(level + 1), total.shape[0])] = total.astype(low)
            else:
                start = k * tile_rows + core * half + offset(level + 1)
                final[rows_at(start, total.shape[0])] = total.astype(low)
            next_exchange(k, level)

        def stage_side(k):
            side_copy(k).wait_recv()
            later = k + flying

            @when(jnp.logical_and(later < count, later != tiles))
            def _():
                side_copy(later).start()

            here = rows_at(k * half, half)
            put(k, -1, work[here].astype(f32) + side_recv[here].astype(f32))

        def stage_scatter(k, level):
            size = sizes[level]
            for distance in range(1, factors[level]):
                scatter_copy(k, level, distance).wait_recv()
            total = work[rows_at(k * half + offset(level + 1), size)].astype(f32)
            for distance in range(1, factors[level]):
                total += recvs[level][distance - 1, rows_at(k * size, size)].astype(f32)
            if not scatters[level]:
                for distance in range(1, factors[level]):
                    scatter_copy(k, level, distance).wait_send()
            put(k, level, total)

        def stage_gather(k, level):
            for distance in range(1, factors[level]):
                gather_copy(k, level, distance).wait_recv()
            if level != scatter_levels[0]:
                below = scatter_levels[scatter_levels.index(level) - 1]
                for distance in range(1, factors[below]):
                    gather_copy(k, below, distance).start()
            else:
                back_copy(k).start()

        def stage_back(k):
            back_copy(k).wait_recv()
            store(k).start()

        stages = [stage_side]
        stages += [functools.partial(stage_scatter, level=n) for n in range(levels)]
        stages += [functools.partial(stage_gather, level=n) for n in reversed(scatter_levels)]
        stages.append(stage_back)

        def tick(at):
            for n, stage in enumerate(stages):

                @pl.when(jnp.logical_and(at >= n, at < count + n))
                def _(n=n, stage=stage):
                    stage(at - n)

        def when(cond):
            return pl.when(cond)

        def fetch_copies(job, x_buf, y_buf, slot, sems):
            x, xc, y, yc = job
            x_from = given[x].at[:, xc * width : (xc + 1) * width]
            y_from = own_grads[y] if isinstance(y, int) else given[y[0]].at[:, yc * width : (yc + 1) * width]
            return (
                pltpu.make_async_copy(x_from, x_buf.at[slot], sems.at[0, slot]),
                pltpu.make_async_copy(y_from, y_buf.at[slot], sems.at[1, slot]),
            )

        def fetch(k, first_k, last_k):
            for n in range(first_k, last_k):

                @when(k == n)
                def _(n=n):
                    for copy in fetch_copies(audio_jobs[n], x_audio, y_audio, n % 2, in_sem.at[0]):
                        copy.start()
                    for copy in fetch_copies(text_jobs[n], x_text, y_text, n % 2, in_sem.at[1]):
                        copy.start()

        def fetch_wait(k):
            slot = k % 2
            for copy in fetch_copies(audio_jobs[0], x_audio, y_audio, slot, in_sem.at[0]):
                copy.wait()
            for copy in fetch_copies(text_jobs[0], x_text, y_text, slot, in_sem.at[1]):
                copy.wait()

        def tile_grads(k, last_k, first_k):
            slot = k % 2

            @when(k + 1 < last_k)
            def _():
                fetch(k + 1, first_k, last_k)

            fetch_wait(k)

            @when(k >= 2)
            def _():
                core_copy(k - 2).wait_send()

            tile[slot, 0] = dot_tt(x_audio[slot], y_audio[slot]).astype(low)
            tile[slot, 1] = dot_tt(x_text[slot], y_text[slot]).astype(low)
            core_copy(k).start()

            @when(k > first_k)
            def _():
                stage_core(k - 1)

        attn_loads = [
            pltpu.make_async_copy(given[at_joint], joint, load_sem.at[0]),
            pltpu.make_async_copy(given[at_logs], logs, load_sem.at[1]),
            pltpu.make_async_copy(given[at_mixed], mixed_grad, load_sem.at[2]),
        ]

        def attention(step):
            pair, part_at = step // blocks, step % blocks
            lane = lax.broadcasted_iota(jnp.int32, (1, 128), 1)
            sub = lax.broadcasted_iota(jnp.int32, (128, 1), 0)

            def cols(start):
                return pl.ds(pl.multiple_of(start + pair * 128, 128), 128)

            here = rows_at(part_at * block, block)

            @when(part_at == 0)
            def _():
                key_acc[...] = jnp.zeros(key_acc.shape, f32)
                value_acc[...] = jnp.zeros(value_acc.shape, f32)
                key_turned[...] = joint[:, cols(width)].astype(f32).T.astype(low)

            query, key, value = joint[here, cols(0)], joint[:, cols(width)], joint[:, cols(2 * width)]
            grad = mixed_grad[here, cols(0)]
            log = logs[pl.ds(pl.multiple_of(pair * 8, 8), 8), pl.ds(pl.multiple_of(part_at * block, block), block)]
            turned = key_turned[...]
            query_turned = jnp.zeros((128, block), f32)
            for head in range(2):
                part = jnp.where(lane // 64 == head, query, jnp.zeros_like(query))
                grad_part = jnp.where(lane // 64 == head, grad, jnp.zeros_like(grad))
                chance = jnp.exp2(dot_t(key, part) * log2_e - log[head : head + 1, :])
                product = chance * dot_t(value, grad_part)
                grad_scores = (product - chance * jnp.sum(product, axis=0, keepdims=True)).astype(low)
                value_acc[...] += dot(chance.astype(low), grad_part)
                key_acc[...] += dot(grad_scores, part)
                query_turned += dot(jnp.where(sub // 64 == head, turned, jnp.zeros_like(turned)), grad_scores)
            grad_query = query_turned.T * 0.125
            query_grad[here, cols(0)] = grad_query.astype(low)
            sums[0:1, cols(0)] += col_sum(grad_query)

            @when(part_at == blocks - 1)
            def _():
                key_grad[:, cols(0)] = key_acc[...].astype(low)
                value_grad[:, cols(0)] = value_acc[...].astype(low)
                sums[1:2, cols(0)] = col_sum(value_acc[...])

        def weight_copies(mine):
            found = [pltpu.make_async_copy(given[at_weight[0 if mine == 0 else 1]], weight, weight_sem.at[0])]
            for n, (split, at, held) in enumerate(((second_side, at_second, second), (first_side, at_first, first))):
                found += split.copies(mine, given[at[0]], given[at[1]], held, weight_sem.at[1 + n])
            return found

        def block_copies(i, slot):
            here = rows_at(i * block, block)
            found = [
                pltpu.make_async_copy(given[at_encoded].at[here], encoded_in.at[slot], block_sem.at[0, slot]),
                pltpu.make_async_copy(given[at_grad].at[here], grad_in.at[slot], block_sem.at[1, slot]),
            ]
            for n in range(3):
                found.append(
                    pltpu.make_async_copy(given[at_slopes[n]].at[here], slope_in.at[slot, n], block_sem.at[2 + n, slot])
                )
            return found

        def stem_block(step):
            i = blocks - 1 - step
            slot = step % 2

            @when(step + 1 < blocks)
            def _():
                for copy in block_copies(i - 1, 1 - slot):
                    copy.start()

            for copy in block_copies(i, slot):
                copy.wait()
            here = rows_at(i * block, block)
            back = (
                dot_t(query_grad[here], weight[:, :width])
                + dot_t(key_grad[here], weight[:, width : 2 * width])
                + dot_t(value_grad[here], weight[:, 2 * width :])
            )
            normed, inverse = norm_rows(encoded_in[slot])
            sums[2:3, :] += col_sum(back * normed)
            sums[3:4, :] += col_sum(back)
            total = grad_in[slot] + norm_back(back, row(smalls, 0), normed, inverse)
            total = total * slope_in[slot, 0].astype(f32)
            sums[4:5, :] += col_sum(total)
            rounded = total.astype(low)
            second_low[here] = rounded
            at_row = lax.broadcasted_iota(jnp.int32, (block, width), 0)
            wide = rounded.astype(f32)
            moved = jnp.where(at_row == block - 1, carry[0:1, :], pltpu.roll(wide, block - 1, 0))
            carry[0:1, :] = wide[0:1, :]
            moved = moved.astype(low)
            next_low[here] = moved
            grad_even = dot_t(rounded, second[width : 2 * width]) * slope_in[slot, 1].astype(f32)
            grad_odd = (dot_t(rounded, second[2 * width :]) + dot_t(moved, second[0:width])) * slope_in[slot, 2].astype(f32)
            sums[5:6, :] += col_sum(grad_even) + col_sum(grad_odd)
            grad_even = grad_even.astype(low)
            grad_odd = grad_odd.astype(low)
            even_low[here] = grad_even
            odd_low[here] = grad_odd
            taps_even = dot_t(grad_even, first[...])
            taps_odd = dot_t(grad_odd, first[...])
            taps_grad[here, 0:128] = taps_even[:, 0:128]
            taps_grad[here, 128:256] = taps_even[:, 128:256] + taps_odd[:, 0:128]
            taps_grad[here, 256:384] = taps_even[:, 256:384] + taps_odd[:, 128:256]
            taps_grad[here, 384:512] = taps_odd[:, 256:384]

        def mel_rows():
            at_row = lax.broadcasted_iota(jnp.int32, (frames, 128), 0)
            before = jnp.where(at_row == 0, 0.0, pltpu.roll(taps_grad[:, 384:512], 1, 0))
            mel_buf[:, 0:128] = taps_grad[:, 128:256] + before
            after = jnp.where(at_row == frames - 1, 0.0, pltpu.roll(taps_grad[:, 0:128], frames - 1, 0))
            mel_buf[:, 128:256] = taps_grad[:, 256:384] + after
            mel_send[...] = mel_buf[rows_at((1 - section) * (frames // 2), frames // 2)].astype(low)

        def keep_copy():
            return pltpu.make_async_copy(mel_buf.at[rows_at(section * (frames // 2), frames // 2)], keep_ref, keep_sem)

        conv_jobs = [(at_odd, next_low), (at_even, second_low), (at_odd, second_low)]

        def conv_copies(n, slot):
            x, y = conv_jobs[n]
            return (
                pltpu.make_async_copy(given[x], x_audio.at[slot], in_sem.at[0, 0, slot]),
                pltpu.make_async_copy(y, y_audio.at[slot], in_sem.at[0, 1, slot]),
            )

        def tap_copies():
            return [
                pltpu.make_async_copy(given[at_taps].at[:, n * 128 : n * 128 + 384], x_audio.at[n, :, 0:384], in_sem.at[0, 0, n])
                for n in range(2)
            ]

        barrier = pltpu.get_barrier_semaphore()
        peers = [core_peer, side_peer]
        peers += [peer(n, d)[1] for n in range(levels) for d in range(1, factors[n])]
        for device in peers:
            pl.semaphore_signal(barrier, inc=1, device_id=device, device_id_type=pl.DeviceIdType.MESH)

        fetch(0, 0, 1)
        for copy in attn_loads:
            copy.start()
        for which in range(2):

            @when(section == which)
            def _(which=which):
                for copy in weight_copies(which):
                    copy.start()

        for copy in block_copies(blocks - 1, 0):
            copy.start()
        sums[...] = jnp.zeros(sums.shape, f32)
        carry[...] = jnp.zeros(carry.shape, f32)
        pl.semaphore_wait(barrier, len(peers))

        @pl.loop(0, early)
        def _(k):
            tile_grads(k, early, 0)

        stage_core(early - 1)
        for copy in attn_loads:
            copy.wait()

        @pl.loop(0, 4 * blocks)
        def _(step):
            attention(step)

            @when(jnp.logical_or(step < 3, step % 3 == 1))
            def _():
                tick(jnp.where(step < 3, step, 3 + (step - 4) // 3))

        fetch(early, early, early + 1)

        @pl.loop(early, tiles)
        def _(k):
            tile_grads(k, tiles, early)
            tick(k - early + 7)

        stage_core(tiles - 1)
        for copy in weight_copies(0):
            copy.wait()
        clear_pads(first, bands)

        @pl.loop(0, blocks)
        def _(step):
            stem_block(step)

            @when(step % 2 == 1)
            def _():
                tick(10 + step // 2)

        for copy in conv_copies(0, 0):
            copy.start()

        @pl.loop(0, 3)
        def _(n):
            slot = n % 2
            for which in range(1, 3):

                @when(n + 1 == which)
                def _(which=which):
                    for copy in conv_copies(which, which % 2):
                        copy.start()

            for copy in conv_copies(0, slot):
                copy.wait()
            conv_buf[n] = dot_tt(x_audio[slot], y_audio[slot]).astype(low)

        for copy in tap_copies():
            copy.start()
        core_copy(tiles - 2).wait_send()
        slot = tiles % 2
        for s in range(2):
            cols = slice(s * lanes, s * lanes + lanes)
            tile[slot, s, :, 0:lanes] = conv_buf[0, :, cols]
            tile[slot, s, 0:half, lanes:width] = conv_buf[1, half:tile_rows, cols]
            tile[slot, s, half:tile_rows, lanes:width] = conv_buf[2, 0:half, cols]
        core_copy(tiles).start()
        for copy in tap_copies():
            copy.wait()
        first_grad = (
            dot_tt(x_audio[0, :, 0:384], even_low[...]) + dot_tt(x_audio[1, :, 0:384], odd_low[...])
        ).astype(low)
        stage_core(tiles)
        core_copy(tiles - 1).wait_send()
        slot = 1 - slot
        feed, wide_feed = audio_sums
        text_feed_sums, text_wide, text_cross, cross_sums, text_attn, text_first = text_sums
        small_buf[...] = jnp.zeros(small_buf.shape, f32)
        text_rows_from = (
            (text_first, 0), (text_cross, 0), (text_feed_sums, 0), (text_first, 1), (text_cross, 1), (text_feed_sums, 1),
            (text_attn, 0), (text_attn, 1), (text_cross, 2), (text_feed_sums, 2), (cross_sums, 0), (text_feed_sums, 3),
        )
        for at, (ref, n) in enumerate(text_rows_from):
            small_buf[1, at : at + 1, :] = ref[n : n + 1, :]
        for at, ref, n in (
            (1, feed, 3), (2, feed, 0), (4, feed, 4), (5, feed, 1), (8, feed, 5), (9, feed, 2), (11, cross_sums, 1),
        ):
            small_buf[0, at : at + 1, :] = ref[n : n + 1, :]
        for n in range(4):
            cols = slice(n * width, n * width + width)
            small_buf[0, 12 + n : 13 + n, :] = wide_feed[0:1, cols]
            small_buf[1, 12 + n : 13 + n, :] = text_wide[0:1, cols]
        for s in range(2):
            small_buf[s, 17:18, :] = text_feed_sums[3:4, :]
        small_buf[0, 6:8, :] = sums[0:2, :]
        small_buf[0, 0:1, :] = sums[2:3, :]
        small_buf[0, 3:4, :] = sums[3:4, :]
        small_buf[0, 10:11, :] = sums[4:5, :]
        small_buf[0, 16:17, 0:lanes] = sums[5:6, 0:lanes]
        small_buf[1, 16:17, 0:lanes] = sums[5:6, lanes:width]
        for s in range(2):
            cols = slice(s * lanes, s * lanes + lanes)
            tile[slot, s, 0:half, 0:lanes] = conv_buf[1, 0:half, cols]
            tile[slot, s, 0:half, lanes:width] = conv_buf[2, half:tile_rows, cols]
            tile[slot, s, half : half + 192, 0:lanes] = first_grad[0:192, cols]
            tile[slot, s, half : half + 192, lanes:width] = first_grad[192:384, cols]
            tile[slot, s, half + 192 : half + 224, :] = small_buf[s].astype(low)
            tile[slot, s, half + 224 : tile_rows, :] = jnp.zeros((32, width), low)
        core_copy(tiles + 1).start()
        mel_rows()
        keep_copy().start()
        stage_core(tiles + 1)
        mel_copy().start()

        @pl.loop(12, count + len(stages) - 1)
        def _(at):
            tick(at)

        keep_copy().wait()
        mel_copy().wait()
        for k in (count - 2, count - 1):
            core_copy(k).wait_send()

        @pl.loop(0, count)
        def _(k):
            side_copy(k).wait_send()
            for level in range(levels):
                for distance in range(1, factors[level]):
                    if scatters[level]:
                        scatter_copy(k, level, distance).wait_send()
                        gather_copy(k, level, distance).wait_send()
            back_copy(k).wait_send()
            store(k).wait()

    second_side, first_side = second, first

    def sems(*shape):
        return pltpu.SemaphoreType.DMA(shape)

    def vmem(*shape, dtype=low):
        return pltpu.VMEM(shape, dtype)

    whole = (frames, width)
    return pl.pallas_call(
        kernel,
        name="finish_backward",
        in_specs=[pl.BlockSpec(memory_space=pl.ANY)] * n_any + [pl.BlockSpec(memory_space=pltpu.VMEM)] * n_chip,
        out_specs=[pl.BlockSpec(memory_space=pl.ANY)] * 3,
        out_shape=[
            jax.ShapeDtypeStruct((rows, width), low),
            jax.ShapeDtypeStruct((frames // 2, 256), f32),
            jax.ShapeDtypeStruct((frames // 2, 256), low),
        ],
        scratch_shapes=[
            vmem(2, 2, tile_rows, width), vmem(4, 2, half, width), vmem(count * half, width), vmem(count * half, width),
            vmem(count * half, width), vmem(rows, width),
            vmem(2, *whole), vmem(2, *whole), vmem(2, text_rows, width), vmem(2, text_rows, width),
            vmem(frames, 3 * width), vmem(32, frames, dtype=f32), vmem(*whole), vmem(*whole), vmem(*whole), vmem(*whole),
            vmem(frames, 128, dtype=f32), vmem(frames, 128, dtype=f32), vmem(128, frames), vmem(8, width, dtype=f32),
            vmem(2, block, width, dtype=f32), vmem(2, block, width, dtype=f32), vmem(2, 3, block, width),
            vmem(width, 3 * width), vmem(*second.shape), vmem(*first.shape),
            vmem(*whole), vmem(*whole), vmem(*whole), vmem(*whole), vmem(*whole, dtype=f32),
            vmem(8, width, dtype=f32), vmem(3, tile_rows, width), vmem(2, 32, width, dtype=f32),
            vmem(frames, 256, dtype=f32), vmem(frames // 2, 256),
            sems(2, 2, 2), sems(3), sems(3), sems(5, 2), pltpu.SemaphoreType.DMA, sems(2, count), sems(2, count), sems(2, count),
            sems(count), sems(2),
            *[vmem(r - 1, count * s, width) for r, s in zip(factors, sizes)],
            *[sems(2, r - 1, count) for r in factors],
            *[sems(2, r - 1, count) for r in factors],
        ],
        compiler_params=pltpu.CompilerParams(
            collective_id=0, has_side_effects=True, vmem_limit_bytes=63 << 20
        ),
        cost_estimate=pl.CostEstimate(flops=10**11, bytes_accessed=10**8, transcendentals=0),
    )(*arrays, smalls, *audio_sums, *text_sums)


def shards(
    mel_input,
    time_start,
    time_width,
    freq_start,
    freq_width,
    text_len,
    text_embed,
    cotangent,
    positions,
    conv_first,
    conv_first_bias,
    conv_second,
    norm_gain,
    norm_shift,
    attn_in,
    attn_out,
    mlp_up,
    mlp_down,
    up_bias,
    small_bias,
    cross_first,
    cross_second,
):
    frames, width = positions.shape
    bands, mel_frames = mel_input.shape[1], mel_input.shape[2]
    text_rows = text_embed.shape[1]
    audio_block = frames // 2
    text_block = text_rows
    swap_pairs = [(0, 1), (1, 0)]

    def partner(array):
        return lax.ppermute(array, "section", swap_pairs)

    first_own = conv_first.reshape(3 * bands, -1)
    second_own = conv_second.reshape(3 * width, -1)
    owns = [w[0] for w in (attn_in, attn_out, mlp_up, mlp_down, cross_first, cross_second)]
    (
        first_other, second_other, *others, a_small, t_small, a_ups, t_ups,
        taps, encoded, even_act, odd_act, even_slope, odd_slope, slope_second, a_norm, a_joint, a_mixed, a_logs,
    ) = begin(
        mel_input, (time_start, time_width, freq_start, freq_width), norm_gain[0], norm_shift[0], small_bias[0], up_bias,
        conv_first_bias[None], first_own, second_own, owns[0], owns[1:], positions,
    )
    a_in, a_out, a_up, a_down, a_cross_a, a_cross_b = [Side(0, o, p) for o, p in zip(owns, others)]
    t_in, t_out, t_up, t_down, t_cross_a, t_cross_b = [Side(1, o, p) for o, p in zip(owns, others)]
    first_all = Split(first_own, first_other, 3, 128)
    second_all = Split(second_own, second_other, 3, width)

    a_middle, a_feed_norm, a_hidden, a_slope, a_ending, memory, memory_keys, memory_values = audio_feed(
        encoded, a_mixed, a_out, a_small, a_ups, a_up, a_down, a_cross_a, a_cross_b, audio_block
    )

    t_norm, t_joint = project(text_embed, t_in, t_small, text_block)
    t_mixed, t_logs = attend(t_joint, t_joint, t_joint, (0, 4, 8), True, text_rows)
    t_middle, cross_low, cross_query = text_middle(text_embed, t_mixed, t_out, t_small, t_cross_a, text_block)
    c_mixed, c_logs = attend(cross_query, memory_keys, memory_values, (0, 0, 0), False, text_rows)
    (
        decoded_keep, decoded_send, t_feed_norm, t_hidden, t_pre, cot_low, after_grad, after_low, c_mixed_grad, feed_sums, feed_wide,
    ) = text_feed(
        text_len, t_middle, c_mixed, cotangent, t_cross_b, t_small, t_ups, t_up, t_down, text_block
    )
    query_grad, key_grad, value_grad, c_sums = attend_back(
        cross_query, memory_keys, memory_values, (0, 0, 0), c_logs, c_mixed_grad, False, True, text_rows
    )
    middle_grad, middle_low, t_mixed_grad, cross_sums = text_cross_back(
        query_grad, t_middle, after_grad, t_small, t_cross_a, t_out, text_block
    )
    tq_grad, tk_grad, tv_grad, t_sums = attend_back(
        t_joint, t_joint, t_joint, (0, 4, 8), t_logs, t_mixed_grad, True, False, text_rows
    )
    text_keep, text_send, text_sums = project_back(
        tq_grad, tk_grad, tv_grad, text_embed, middle_grad, t_small, t_in, text_block
    )

    decoded_got, text_got = partner(decoded_send), partner(text_send)
    end_low, a_pre, a_grad, a_grad_low, a_mixed_grad, a_feed_sums, a_feed_wide = audio_feed_back(
        key_grad, value_grad, a_ending, a_middle, a_slope, a_small, a_cross_a, a_cross_b, a_up, a_down, a_out, audio_block
    )

    audio = [(a_feed_norm, 0, a_pre, n) for n in range(4)] + [(a_hidden, n, end_low, 0) for n in range(4)]
    audio += [(memory, 0, key_grad, 0), (memory, 0, value_grad, 0), (a_mixed, 0, a_grad_low, 0)]
    audio += [(a_norm, 0, n, 0) for n in range(3)]
    text = [(t_feed_norm, 0, t_pre, n) for n in range(4)] + [(t_hidden, n, cot_low, 0) for n in range(4)]
    text += [(cross_low, 0, query_grad, 0), (c_mixed, 0, after_low, 0), (t_mixed, 0, middle_low, 0)]
    text += [(t_norm, 0, part, 0) for part in (tq_grad, tk_grad, tv_grad)]
    a_feed_sums, decoded_got, text_got = lax.optimization_barrier((a_feed_sums, decoded_got, text_got))
    total, mel_keep, mel_got = finish_backward(
        audio, text, a_joint, a_logs, a_mixed_grad, a_grad, encoded, (slope_second, even_slope, odd_slope), a_small, a_in,
        second_all, first_all, (odd_act, even_act, taps), (a_feed_sums, a_feed_wide),
        (feed_sums, feed_wide, cross_sums, c_sums, t_sums, text_sums), bands,
    )

    decoded, text_grad, mel_out = finish(
        [(decoded_keep, decoded_got), (text_keep, text_got)], mel_keep, mel_got,
        (time_start, time_width, freq_start, freq_width), bands,
    )
    joint, out, up, down, cross_a, cross_b, first, bias, second, gain, shift, wide, small, cross = unpack(total, bands)
    return (
        decoded, text_grad, mel_out, first, bias[0], second, gain, shift, joint, out, up, down, wide, small, cross_a, cross_b,
        cross[0],
    )


def solution(mesh):
    return jax.shard_map(
        shards,
        mesh=mesh,
        in_specs=(
            P("dp", None, None),
            P("dp"),
            P("dp"),
            P("dp"),
            P("dp"),
            P("dp"),
            P("dp", None, None),
            P("dp", None, None),
            P(),
            P(None, None, "section"),
            P("section"),
            P(None, None, "section"),
            P("section", None, None),
            P("section", None, None),
            P("section", None, None),
            P("section", None, None),
            P("section", None, None),
            P("section", None, None),
            P("section", None),
            P("section", None, None),
            P("section", None, None),
            P("section", None, None),
        ),
        out_specs=(
            P("dp", None, "section"),
            P("dp", None, "section"),
            P("dp", None, "section"),
            P(None, None, "section"),
            P("section"),
            P(None, None, "section"),
            P("section", None, None),
            P("section", None, None),
            P("section", None, None),
            P("section", None, None),
            P("section", None, None),
            P("section", None, None),
            P("section", None),
            P("section", None, None),
            P("section", None, None),
            P("section", None, None),
            P("section"),
        ),
        check_vma=False,
    )
```

```python
import functools

import jax
import jax.numpy as jnp
from jax import lax
from jax.experimental import pallas as pl
from jax.experimental.pallas import tpu as pltpu
from jax.sharding import PartitionSpec as P

HEADS = 8
epsilon = 1e-05
root_half = 0.7071067811865476
gauss_norm = 0.3989422804014327
log2_e = 1.4426950408889634
VMEM_BYTES = 56 << 20

f32 = jnp.float32
low = jnp.bfloat16


def dot(left, right):
    return lax.dot_general(left, right, (((1,), (0,)), ((), ())), preferred_element_type=f32)


def dot_t(left, right):
    return lax.dot_general(left, right, (((1,), (1,)), ((), ())), preferred_element_type=f32)


def dot_tt(left, right):
    return lax.dot_general(left, right, (((0,), (0,)), ((), ())), preferred_element_type=f32)


def gelu_both(inputs):
    ratio = 1.0 / (1.0 + (0.3275911 * root_half) * jnp.abs(inputs))
    bell = jnp.exp2((-0.5 * log2_e) * inputs * inputs)
    tail = ratio * (
        0.127414796
        + ratio * (-0.142248368 + ratio * (0.7107068705 + ratio * (-0.7265760135 + ratio * 0.5307027145)))
    )
    tail = tail * bell
    below = jnp.where(inputs >= 0.0, 1.0 - tail, tail)
    return inputs * below, below + inputs * bell * gauss_norm


def norm_rows(inputs):
    centred = inputs - jnp.mean(inputs, axis=-1, keepdims=True)
    inverse = lax.rsqrt(jnp.mean(centred * centred, axis=-1, keepdims=True) + epsilon)
    return centred * inverse, inverse


def norm_back(grad, gain, normed, inverse):
    scaled = grad * gain
    return inverse * (
        scaled
        - jnp.mean(scaled, axis=-1, keepdims=True)
        - normed * jnp.mean(scaled * normed, axis=-1, keepdims=True)
    )


def col_sum(inputs):
    return jnp.sum(inputs, axis=0, keepdims=True)


class Side:
    def __init__(self, side, own, other):
        self.side, self.own, self.other, self.shape = side, own, other, own.shape

    def copies(self, mine, own, other, held, sem):
        return [pltpu.make_async_copy(own if mine == self.side else other, held, sem)]


class Split:
    def __init__(self, own, other, groups, apart):
        self.own, self.other, self.groups, self.apart = own, other, groups, apart
        self.shape = (groups * apart, 2 * own.shape[1])

    def copies(self, mine, own, other, held, sem, parts=(0, 1)):
        size, half = self.own.shape[0] // self.groups, self.own.shape[1]
        found = []
        for which, ref in [((mine, own), (1 - mine, other))[n] for n in parts]:
            cols = slice(which * half, which * half + half)
            for n in range(self.groups):
                found.append(
                    pltpu.make_async_copy(
                        ref.at[n * size : n * size + size], held.at[n * self.apart : n * self.apart + size, cols], sem
                    )
                )
        return found


def call(body, name, steps, block, ins, outs, scratch=(), reverse=False, flops=0, grid=None):
    arrays, specs, kinds, weight_scratch = [], [], [], []
    at = (lambda i: steps - 1 - i) if reverse else (lambda i: i)
    for array, kind in ins:
        if kind in ("side", "split"):
            arrays += [array.own, array.other]
            specs += [pl.BlockSpec(memory_space=pl.ANY)] * 2
            weight_scratch.append(pltpu.VMEM(array.shape, array.own.dtype))
        elif kind == "rows":
            arrays.append(array)
            specs.append(pl.BlockSpec((block, array.shape[1]), lambda i: (at(i), 0)))
        elif kind == "clip":
            arrays.append(array)
            specs.append(pl.BlockSpec((None, block, array.shape[2]), lambda i: (lax.axis_index("section"), at(i), 0)))
        elif kind == "smem":
            arrays.append(array)
            specs.append(pl.BlockSpec(memory_space=pltpu.SMEM))
        else:
            arrays.append(array)
            specs.append(
                pl.BlockSpec(
                    array.shape,
                    lambda i, n=array.ndim: (0,) * n,
                    pipeline_mode=pl.Buffered(1),
                )
            )
        kinds.append((kind, array if kind in ("side", "split") else None))
    out_specs = [
        pl.BlockSpec((block, shape[1]), lambda i: (at(i), 0))
        if kind == "rows"
        else pl.BlockSpec(shape, lambda i, n=len(shape): (0,) * n)
        for shape, dtype, kind in outs
    ]
    n_in, n_out, n_weight = len(arrays), len(outs), len(weight_scratch)

    def kernel(*refs):
        in_refs, out_refs = refs[:n_in], refs[n_in : n_in + n_out]
        weights = refs[n_in + n_out : n_in + n_out + n_weight]
        extra = refs[n_in + n_out + n_weight :]
        given, r, w, loads = [], 0, 0, []
        for kind, array in kinds:
            if kind in ("side", "split"):
                loads.append((array, in_refs[r], in_refs[r + 1], weights[w]))
                given.append(weights[w])
                r, w = r + 2, w + 1
            else:
                given.append(in_refs[r])
                r += 1
        step = pl.program_id(0)
        if loads:
            sem = extra[-1]
            extra = extra[:-1]

            @pl.when(step == 0)
            def _():
                mine = lax.axis_index("section")
                for n, load in enumerate(loads):
                    for which in range(2):

                        @pl.when(mine == which)
                        def _(load=load, n=n, which=which):
                            array, own, other, held = load
                            for copy in array.copies(which, own, other, held, sem.at[n]):
                                copy.start()

                for n, (array, own, other, held) in enumerate(loads):
                    for copy in array.copies(0, own, other, held, sem.at[n]):
                        copy.wait()

        for ref, (shape, dtype, kind) in zip(out_refs, outs):
            if kind == "sums":

                @pl.when(step == 0)
                def _(ref=ref):
                    ref[...] = jnp.zeros(ref.shape, ref.dtype)

        body(step, given, out_refs, extra)

    scratch_shapes = weight_scratch + list(scratch)
    if weight_scratch:
        scratch_shapes.append(pltpu.SemaphoreType.DMA((n_weight,)))
    total = sum(a.size * a.dtype.itemsize for a in arrays) + sum(
        2 * s[0] * s[1] for s, d, k in outs
    )
    return pl.pallas_call(
        kernel,
        name=name,
        grid=(steps,),
        in_specs=specs,
        out_specs=out_specs,
        out_shape=[jax.ShapeDtypeStruct(shape, dtype) for shape, dtype, kind in outs],
        scratch_shapes=scratch_shapes,
        compiler_params=pltpu.CompilerParams(
            dimension_semantics=("arbitrary",), vmem_limit_bytes=VMEM_BYTES
        ),
        cost_estimate=pl.CostEstimate(flops=int(flops), bytes_accessed=int(total), transcendentals=0),
    )(*arrays)


def row(ref, n):
    return ref[n : n + 1, :].astype(f32)


def clear_pads(weight, bands):
    for n in range(3):
        weight[n * 128 + bands : n * 128 + 128, :] = jnp.zeros((128 - bands, weight.shape[1]), weight.dtype)


def write_halves(values, keep, send):
    half = values.shape[1] // 2
    mine = lax.axis_index("section")
    first, second = values[:, :half], values[:, half:]

    @pl.when(mine == 0)
    def _():
        keep[...] = first
        send[...] = second.astype(low)

    @pl.when(mine != 0)
    def _():
        keep[...] = second
        send[...] = first.astype(low)


def pair_cols(start, pair):
    return pl.ds(pl.multiple_of(start + pair * 128, 128), 128)


def seen(shape, key_axis):
    return lax.broadcasted_iota(jnp.int32, shape, key_axis) <= lax.broadcasted_iota(jnp.int32, shape, 1 - key_axis)


def attend_pair(query, key, value, causal):
    lane = lax.broadcasted_iota(jnp.int32, (1, 128), 1)
    mixed, logs = [], []
    for head in range(2):
        scores = dot_t(jnp.where(lane // 64 == head, query, jnp.zeros_like(query)), key)
        if causal:
            scores = jnp.where(seen(scores.shape, 1), scores, -1e30)
        top = jnp.max(scores, axis=1, keepdims=True) * log2_e
        exponent = jnp.exp2(scores * log2_e - top)
        total = jnp.sum(exponent, axis=1, keepdims=True)
        mixed.append(dot(exponent.astype(low), value) * (1.0 / total))
        logs.append(top + jnp.log2(total))
    both = jnp.where(lane == 0, logs[0], logs[1])
    return jnp.where(lane < 64, mixed[0], mixed[1]).astype(low), both.T[0:8, :]


def attend_pair_back(query, key, value, logs, grad, causal):
    lane = lax.broadcasted_iota(jnp.int32, (1, 128), 1)
    sub = lax.broadcasted_iota(jnp.int32, (128, 1), 0)
    turned = key.astype(f32).T.astype(low)
    found = []
    for head in range(2):
        part = jnp.where(lane // 64 == head, query, jnp.zeros_like(query))
        grad_part = jnp.where(lane // 64 == head, grad, jnp.zeros_like(grad))
        chance = jnp.exp2(dot_t(key, part) * log2_e - logs[head : head + 1, :])
        if causal:
            chance = jnp.where(seen(chance.shape, 0), chance, 0.0)
        product = chance * dot_t(value, grad_part)
        grad_scores = (product - chance * jnp.sum(product, axis=0, keepdims=True)).astype(low)
        found.append(
            (
                dot(jnp.where(sub // 64 == head, turned, jnp.zeros_like(turned)), grad_scores),
                dot(grad_scores, part),
                dot(chance.astype(low), grad_part),
            )
        )
    turned, key_grad, value_grad = (one + two for one, two in zip(*found))
    return turned.T * 0.125, key_grad, value_grad


def audio_feed(inputs, mixed, weight_out, smalls, ups, weight_up, weight_down, cross_a, cross_b, block):
    rows, width = inputs.shape
    hidden = ups.shape[1]

    def body(step, given, outs, extra):
        inputs, mixed, weight_out, smalls, ups, weight_up, weight_down, cross_a, cross_b = given
        middle_out, norm_out, hidden_out, slope_out, ending_out, memory_out, key_out, value_out = outs
        middle = inputs[...] + dot(mixed[...], weight_out[...]) + row(smalls, 8)
        middle_out[...] = middle
        normed, inverse = norm_rows(middle)
        rounded = (normed * row(smalls, 1) + row(smalls, 4)).astype(low)
        norm_out[...] = rounded
        ending = middle + row(smalls, 9)
        for part in range(hidden // 512):
            cols = slice(part * 512, part * 512 + 512)
            pre = dot(rounded, weight_up[:, cols]) + ups[:, cols].astype(f32)
            value, slope = gelu_both(pre)
            act = value.astype(low)
            hidden_out[:, cols] = act
            slope_out[:, cols] = slope.astype(low)
            ending += dot(act, weight_down[cols, :])
        ending_out[...] = ending
        normed, inverse = norm_rows(ending)
        memory = (normed * row(smalls, 2) + row(smalls, 5)).astype(low)
        memory_out[...] = memory
        key_out[...] = dot(memory, cross_a[...]).astype(low)
        value_out[...] = (dot(memory, cross_b[...]) + row(smalls, 11)).astype(low)

    wide, shape = (rows, hidden), (rows, width)
    return call(
        body, "audio_feed", rows // block, block,
        [(inputs, "rows"), (mixed, "rows"), (weight_out, "side"), (smalls, "full"), (ups, "full"),
         (weight_up, "side"), (weight_down, "side"), (cross_a, "side"), (cross_b, "side")],
        [(shape, f32, "rows"), (shape, low, "rows"), (wide, low, "rows"), (wide, low, "rows"),
         (shape, f32, "rows"), (shape, low, "rows"), (shape, low, "rows"), (shape, low, "rows")],
        flops=2 * rows * width * (3 * width + 2 * hidden),
    )


def text_start(inputs, weight, weight_out, smalls, cross_a):
    rows, width = inputs.shape[1:]

    def body(step, given, outs, extra):
        inputs, weight, weight_out, smalls, cross_a = given
        norm_out, joint, mixed, logs, middle_out, low_out, query_out = outs
        normed, inverse = norm_rows(inputs[...].astype(f32))
        rounded = (normed * row(smalls, 0) + row(smalls, 3)).astype(low)
        norm_out[...] = rounded
        joint[:, :width] = (dot(rounded, weight[:, :width]) + row(smalls, 6)).astype(low) * 0.125
        joint[:, width : 2 * width] = dot(rounded, weight[:, width : 2 * width]).astype(low)
        joint[:, 2 * width :] = (dot(rounded, weight[:, 2 * width :]) + row(smalls, 7)).astype(low)

        @pl.loop(0, HEADS // 2)
        def _(pair):
            cols = pair_cols(0, pair)
            mixed[:, cols], logs[pl.ds(pl.multiple_of(pair * 8, 8), 8), :] = attend_pair(
                joint[:, cols], joint[:, pair_cols(width, pair)], joint[:, pair_cols(2 * width, pair)], True
            )

        middle = inputs[...].astype(f32) + dot(mixed[...], weight_out[...]) + row(smalls, 8)
        middle_out[...] = middle
        normed, inverse = norm_rows(middle)
        rounded = (normed * row(smalls, 1) + row(smalls, 4)).astype(low)
        low_out[...] = rounded
        query_out[...] = (dot(rounded, cross_a[...]) + row(smalls, 10)).astype(low) * 0.125

    shape = (rows, width)
    return call(
        body, "text_start", 1, rows,
        [(inputs, "clip"), (weight, "side"), (weight_out, "side"), (smalls, "full"), (cross_a, "side")],
        [(shape, low, "rows"), ((rows, 3 * width), low, "rows"), (shape, low, "rows"), ((4 * HEADS, rows), f32, "whole"),
         (shape, f32, "rows"), (shape, low, "rows"), (shape, low, "rows")],
        flops=10 * rows * width * width,
    )


def text_cross(length, queries, keys, values, middle, cotangent, cross_b, smalls, ups, weight_up, weight_down):
    rows, width = middle.shape
    hidden = ups.shape[1]
    block, key_rows = rows, keys.shape[0]

    def body(step, given, outs, extra):
        length, queries, keys, values, middle, cotangent, cross_b, smalls, ups, weight_up, weight_down = given
        decoded_keep, decoded_send, norm_out, hidden_out, pre_out, cot_out, grad_out, grad_low, mixed, query_out, key_out, value_out, sums, wide_sums, cross_sums = outs
        logs, mixed_grad = extra

        @pl.loop(0, HEADS // 2)
        def _(pair):
            cols = pair_cols(0, pair)
            mixed[:, cols], logs[pl.ds(pl.multiple_of(pair * 8, 8), 8), :] = attend_pair(
                queries[:, cols], keys[:, cols], values[:, cols], False
            )

        after = middle[...] + dot(mixed[...], cross_b[...]) + row(smalls, 11)
        normed, inverse = norm_rows(after)
        rounded = (normed * row(smalls, 2) + row(smalls, 5)).astype(low)
        norm_out[...] = rounded
        at_row = lax.broadcasted_iota(jnp.int32, (block, 1), 0) + step * block
        valid = at_row < length[lax.axis_index("section")]
        grad = jnp.where(valid, cotangent[...].astype(f32), 0.0)
        cot = grad.astype(low)
        cot_out[...] = cot
        ending = after + row(smalls, 9)
        back = jnp.zeros((block, width), f32)
        for part in range(hidden // 512):
            cols = slice(part * 512, part * 512 + 512)
            pre = dot(rounded, weight_up[:, cols]) + ups[:, cols].astype(f32)
            value, slope = gelu_both(pre)
            act = value.astype(low)
            hidden_out[:, cols] = act
            ending += dot(act, weight_down[cols, :])
            grad_pre = dot_t(cot, weight_down[cols, :]) * slope
            wide_sums[0:1, cols] += col_sum(grad_pre)
            pre_low = grad_pre.astype(low)
            pre_out[:, cols] = pre_low
            back += dot_t(pre_low, weight_up[:, cols])
        write_halves(jnp.where(valid, ending, 0.0), decoded_keep, decoded_send)
        sums[0:1, :] += col_sum(back * normed)
        sums[1:2, :] += col_sum(back)
        sums[2:3, :] += col_sum(grad)
        grad = grad + norm_back(back, row(smalls, 2), normed, inverse)
        sums[3:4, :] += col_sum(grad)
        grad_out[...] = grad
        rounded = grad.astype(low)
        grad_low[...] = rounded
        mixed_grad[...] = dot_t(rounded, cross_b[...]).astype(low)

        @pl.loop(0, HEADS // 2)
        def _(pair):
            cols = pair_cols(0, pair)
            query_grad, key_grad, value_grad = attend_pair_back(
                queries[:, cols], keys[:, cols], values[:, cols], logs[pl.ds(pl.multiple_of(pair * 8, 8), 8), :],
                mixed_grad[:, cols], False,
            )
            query_out[:, cols] = query_grad.astype(low)
            key_out[:, cols] = key_grad.astype(low)
            value_grad = value_grad.astype(low)
            value_out[:, cols] = value_grad
            cross_sums[0:1, cols] = col_sum(query_grad)
            cross_sums[1:2, cols] = col_sum(value_grad.astype(f32))

    wide, shape = (rows, hidden), (rows, width)
    return call(
        body, "text_cross", 1, rows,
        [(length, "smem"), (queries, "rows"), (keys, "full"), (values, "full"), (middle, "rows"), (cotangent, "clip"), (cross_b, "side"),
         (smalls, "full"), (ups, "full"), (weight_up, "side"), (weight_down, "side")],
        [((rows, width // 2), f32, "rows"), ((rows, width // 2), low, "rows"), (shape, low, "rows"), (wide, low, "rows"),
         (wide, low, "rows"), (shape, low, "rows"), (shape, f32, "rows"), (shape, low, "rows"), (shape, low, "rows"), (shape, low, "rows"),
         ((key_rows, width), low, "whole"), ((key_rows, width), low, "whole"),
         ((8, width), f32, "sums"), ((8, hidden), f32, "sums"), ((8, width), f32, "sums")],
        scratch=[pltpu.VMEM((4 * HEADS, rows), f32), pltpu.VMEM(shape, low)],
        flops=2 * rows * width * (2 * width + 4 * hidden),
    )


def text_back(query_grad, middle, grad, joint, logs, inputs, smalls, cross_a, weight_out, weight):
    rows, width = middle.shape

    def body(step, given, outs, extra):
        query_grad, middle, grad, joint, logs, inputs, smalls, cross_a, weight_out, weight = given
        keep, send, low_out, query_out, key_out, value_out, cross_sums, attn_sums, first_sums = outs
        total, mixed_grad = extra
        back = dot_t(query_grad[...], cross_a[...])
        normed, inverse = norm_rows(middle[...])
        cross_sums[0:1, :] = col_sum(back * normed)
        cross_sums[1:2, :] = col_sum(back)
        total[...] = grad[...] + norm_back(back, row(smalls, 1), normed, inverse)
        cross_sums[2:3, :] = col_sum(total[...])
        rounded = total[...].astype(low)
        low_out[...] = rounded
        mixed_grad[...] = dot_t(rounded, weight_out[...]).astype(low)

        @pl.loop(0, HEADS // 2)
        def _(pair):
            cols = pair_cols(0, pair)
            query, key, value = attend_pair_back(
                joint[:, cols], joint[:, pair_cols(width, pair)], joint[:, pair_cols(2 * width, pair)],
                logs[pl.ds(pl.multiple_of(pair * 8, 8), 8), :], mixed_grad[:, cols], True,
            )
            query_out[:, cols] = query.astype(low)
            key_out[:, cols] = key.astype(low)
            value_out[:, cols] = value.astype(low)
            attn_sums[0:1, cols] = col_sum(query)
            attn_sums[1:2, cols] = col_sum(value)

        back = (
            dot_t(query_out[...], weight[:, :width])
            + dot_t(key_out[...], weight[:, width : 2 * width])
            + dot_t(value_out[...], weight[:, 2 * width :])
        )
        normed, inverse = norm_rows(inputs[...].astype(f32))
        first_sums[0:1, :] = col_sum(back * normed)
        first_sums[1:2, :] = col_sum(back)
        write_halves(total[...] + norm_back(back, row(smalls, 0), normed, inverse), keep, send)

    shape = (rows, width)
    return call(
        body, "text_back", 1, rows,
        [(query_grad, "rows"), (middle, "rows"), (grad, "rows"), (joint, "rows"), (logs, "full"), (inputs, "clip"),
         (smalls, "full"), (cross_a, "side"), (weight_out, "side"), (weight, "side")],
        [((rows, width // 2), f32, "rows"), ((rows, width // 2), low, "rows")] + [(shape, low, "rows")] * 4
        + [((8, width), f32, "sums")] * 3,
        scratch=[pltpu.VMEM(shape, f32), pltpu.VMEM(shape, low)],
        flops=14 * rows * width * width,
    )


def audio_feed_back(key_grad, value_grad, ending, middle, slope, smalls, cross_a, cross_b, weight_up, weight_down, weight_out, block):
    rows, width = ending.shape
    hidden = slope.shape[1]

    def body(step, given, outs, extra):
        key_grad, value_grad, ending, middle, slope, smalls, cross_a, cross_b, weight_up, weight_down, weight_out = given
        end_low, pre_out, grad_out, grad_low, mixed_out, sums, wide_sums = outs
        back = dot_t(key_grad[...], cross_a[...]) + dot_t(value_grad[...], cross_b[...])
        normed, inverse = norm_rows(ending[...])
        sums[0:1, :] += col_sum(back * normed)
        sums[1:2, :] += col_sum(back)
        grad = norm_back(back, row(smalls, 2), normed, inverse)
        sums[2:3, :] += col_sum(grad)
        rounded = grad.astype(low)
        end_low[...] = rounded
        back = jnp.zeros((block, width), f32)
        for part in range(hidden // 512):
            cols = slice(part * 512, part * 512 + 512)
            grad_pre = dot_t(rounded, weight_down[cols, :]) * slope[:, cols].astype(f32)
            wide_sums[0:1, cols] += col_sum(grad_pre)
            pre_low = grad_pre.astype(low)
            pre_out[:, cols] = pre_low
            back += dot_t(pre_low, weight_up[:, cols])
        normed, inverse = norm_rows(middle[...])
        sums[3:4, :] += col_sum(back * normed)
        sums[4:5, :] += col_sum(back)
        grad = grad + norm_back(back, row(smalls, 1), normed, inverse)
        sums[5:6, :] += col_sum(grad)
        grad_out[...] = grad
        rounded = grad.astype(low)
        grad_low[...] = rounded
        mixed_out[...] = dot_t(rounded, weight_out[...]).astype(low)

    wide, shape = (rows, hidden), (rows, width)
    return call(
        body, "audio_feed_back", rows // block, block,
        [(key_grad, "rows"), (value_grad, "rows"), (ending, "rows"), (middle, "rows"), (slope, "rows"), (smalls, "full"),
         (cross_a, "side"), (cross_b, "side"), (weight_up, "side"), (weight_down, "side"), (weight_out, "side")],
        [(shape, low, "rows"), (wide, low, "rows"), (shape, f32, "rows"), (shape, low, "rows"), (shape, low, "rows"),
         ((8, width), f32, "sums"), ((8, hidden), f32, "sums")],
        flops=2 * rows * width * (3 * width + 2 * hidden),
    )


def unpack(total, bands):
    width, half = total.shape[1], total.shape[1] // 2
    tiles = 14

    def kernel(total, joint, out, up, down, cross_a, cross_b, first, bias, second, gain, shift, wide, small, cross, held, found, in_sem, out_sem):
        def load(n):
            here = pl.ds(pl.multiple_of(n * width, width), width)
            return pltpu.make_async_copy(total.at[here], held.at[n], in_sem.at[n])

        def target(n):
            cols = lambda k: slice(k * width, k * width + width)
            if n < 4:
                return up.at[0, :, cols(n)]
            if n < 8:
                return down.at[0, cols(n - 4)]
            if n < 11:
                return (cross_a, cross_b, out)[n - 8].at[0]
            return joint.at[0, :, cols(n - 11)]

        def store(n):
            return pltpu.make_async_copy(found.at[n], target(n), out_sem.at[n])

        @pl.loop(0, tiles + 2)
        def _(n):
            load(n).start()

        @pl.loop(0, tiles)
        def _(n):
            load(n).wait()
            found[n] = held[n].astype(f32)
            for k in range(tiles):

                @pl.when(n == k)
                def _(k=k):
                    store(k).start()

        load(tiles).wait()
        load(tiles + 1).wait()
        tile = held.at[tiles]
        second[0] = tile[:, 0:half].astype(f32)
        second[1, half:width] = tile[0:half, half:width].astype(f32)
        second[2, 0:half] = tile[half:width, half:width].astype(f32)
        tile = held.at[tiles + 1]
        second[1, 0:half] = tile[0:half, 0:half].astype(f32)
        second[2, half:width] = tile[0:half, half:width].astype(f32)
        first[0] = tile[half : half + bands, 0:half].astype(f32)
        first[1, 0:64] = tile[half + 128 : half + 192, 0:half].astype(f32)
        first[1, 64:bands] = tile[half : half + bands - 64, half:width].astype(f32)
        first[2] = tile[half + 64 : half + 64 + bands, half:width].astype(f32)
        rows = tile[half + 192 : half + 224, :].astype(f32)
        gain[0] = rows[0:3]
        shift[0] = rows[3:6]
        small[0] = rows[6:12]
        for n in range(4):
            wide[:, n * width : (n + 1) * width] = rows[12 + n : 13 + n]
        bias[...] = rows[16:17, 0:half]
        mine = lax.axis_index("section")
        cross[...] = jnp.where(mine == 0, rows[17:18, 0:half], rows[17:18, half:width])
        for n in range(tiles):
            store(n).wait()

    shapes = [
        (1, width, 3 * width), (1, width, width), (1, width, 4 * width), (1, 4 * width, width), (1, width, width), (1, width, width),
        (3, bands, half), (1, half), (3, width, half), (1, 3, width), (1, 3, width), (1, 4 * width), (1, 6, width), (1, half),
    ]
    return pl.pallas_call(
        kernel,
        name="unpack",
        in_specs=[pl.BlockSpec(memory_space=pl.ANY)],
        out_specs=[pl.BlockSpec(memory_space=pl.ANY)] * 6 + [pl.BlockSpec(memory_space=pltpu.VMEM)] * 8,
        out_shape=[jax.ShapeDtypeStruct(shape, f32) for shape in shapes],
        scratch_shapes=[
            pltpu.VMEM((tiles + 2, width, width), low), pltpu.VMEM((tiles, width, width), f32),
            pltpu.SemaphoreType.DMA((tiles + 2,)), pltpu.SemaphoreType.DMA((tiles,)),
        ],
        compiler_params=pltpu.CompilerParams(vmem_limit_bytes=VMEM_BYTES),
        cost_estimate=pl.CostEstimate(flops=0, bytes_accessed=6 * total.size, transcendentals=0),
    )(total)


def finish(parts, mel_keep, mel_got, spans, bands):
    count = len(parts)
    pair_rows = mel_keep.shape[0]
    frames = 2 * pair_rows

    def kernel(*refs):
        pairs, (keep_ref, got_ref), marks = refs[: 2 * count], refs[2 * count : 2 * count + 2], refs[2 * count + 2 : 2 * count + 6]
        outs, mel_out, laid = refs[2 * count + 6 : 3 * count + 6], refs[3 * count + 6], refs[3 * count + 7]
        mine = lax.axis_index("section")
        for n, out in enumerate(outs):
            out[mine] = pairs[2 * n][...]
            out[1 - mine] = pairs[2 * n + 1][...].astype(f32)
        band_at = lax.broadcasted_iota(jnp.int32, (bands, frames), 0)
        frame_at = lax.broadcasted_iota(jnp.int32, (bands, frames), 1) + mine * frames
        for clip, ref in ((mine, keep_ref), (1 - mine, got_ref)):
            for n in range(2):
                laid[pl.ds(n, pair_rows, stride=2), :] = ref[:, n * 128 : n * 128 + 128].astype(f32)
            start, span, band, width = (mark[clip] for mark in marks)
            keep = jnp.logical_and(
                jnp.logical_or(band_at < band, band_at >= band + width),
                jnp.logical_or(frame_at < start, frame_at >= start + span),
            )
            mel_out[clip] = jnp.where(keep, laid[...].T[0:bands, :], 0.0)

    flat = [array for pair in parts for array in pair]
    return pl.pallas_call(
        kernel,
        name="finish",
        in_specs=[pl.BlockSpec(memory_space=pltpu.VMEM)] * (2 * count + 2) + [pl.BlockSpec(memory_space=pltpu.SMEM)] * 4,
        out_shape=[jax.ShapeDtypeStruct((2,) + keep.shape, f32) for keep, got in parts]
        + [jax.ShapeDtypeStruct((2, bands, frames), f32)],
        scratch_shapes=[pltpu.VMEM((frames, 128), f32)],
        compiler_params=pltpu.CompilerParams(vmem_limit_bytes=VMEM_BYTES),
        cost_estimate=pl.CostEstimate(flops=0, bytes_accessed=sum(8 * a.size for a in flat), transcendentals=0),
    )(*flat, mel_keep, mel_got, *spans)


def begin(mel_input, spans, gain, shift, biases, up_bias, first_bias, first, second, joint_weight, weights, positions):
    frames, width = positions.shape
    bands, mel_frames = mel_input.shape[1:]
    lanes = width // 2
    hidden = up_bias.shape[1]
    block = 256
    blocks = frames // block
    sent = [second, joint_weight] + weights
    n_sent = len(sent)
    pieces = []
    for n, array in enumerate(sent):
        cuts = 2 if array.size >= 700000 else 1
        size = array.shape[0] // cuts
        pieces += [(n, c * size, size) for c in range(cuts)]
    n_pieces = len(pieces)
    flying = 2
    first_held = Split(first, first, 3, 128)
    second_held = Split(second, second, 3, width)
    n_any = n_sent + 3

    def kernel(*refs):
        mel_ref, positions_ref, first_ref = refs[:3]
        own = refs[3:n_any]
        times, time_spans, bands_from, band_spans = refs[n_any : n_any + 4]
        gain, shift, biases, up_bias, first_bias = refs[n_any + 4 : n_any + 9]
        outs = refs[n_any + 9 :]
        first_other = outs[0]
        other = outs[1 : 1 + n_sent]
        a_small, t_small, a_ups, t_ups = outs[1 + n_sent : 5 + n_sent]
        results = outs[5 + n_sent : 16 + n_sent]
        (
            taps, encoded, even_act, odd_act, even_slope, odd_slope, slope_second, norm, joint, mixed, logs,
            mel, turned, place, conv_first, conv_second, weight, carry, pack, pack_other,
            load_sem, weight_sem, out_sem, side_sem, near_sem, core_sem,
        ) = outs[16 + n_sent :]
        held = (taps, encoded, even_act, odd_act, even_slope, odd_slope, slope_second, norm, joint, mixed, logs)

        section, replica = lax.axis_index("section"), lax.axis_index("dp")
        side_peer = {"section": 1 - section}

        def flipped(value, bit):
            return value + bit - 2 * bit * ((value // bit) % 2)

        def peer(bit):
            return {"dp": flipped(replica, bit)}

        def remote(source, target, sems, at, device):
            return pltpu.make_async_remote_copy(
                src_ref=source, dst_ref=target, send_sem=sems.at[(0,) + at], recv_sem=sems.at[(1,) + at],
                device_id=device, device_id_type=pl.DeviceIdType.MESH,
            )

        def part(p, q):
            n, start, size = pieces[p]
            return pl.ds(pl.multiple_of(start + q * (size // 4), 16), size // 4)

        def near(p):
            bit = 4 if p % 2 else 2
            quarter = replica % 2 + 2 * ((replica // bit) % 2)
            return bit, (quarter, flipped(quarter, 2))

        def side_copy(p):
            n = pieces[p][0]
            here = part(p, near(p)[1][0])
            return remote(own[n].at[here], other[n].at[here], side_sem, (p,), side_peer)

        def pass_on(p, q, sems, at, bit):
            here = other[pieces[p][0]].at[part(p, q)]
            return remote(here, here, sems, at, peer(bit))

        def near_copies(p):
            bit, quarters = near(p)
            return [pass_on(p, quarters[0], near_sem, (p,), bit)]

        def core_copies(p):
            return [pass_on(p, q, core_sem, (b, p), 1) for b, q in enumerate(near(p)[1])]

        hops = (lambda p: [side_copy(p)], near_copies, core_copies)

        def advance(p, n):
            for copy in hops[n](p):
                copy.wait_recv()
            if n == 0 and p + flying < n_pieces:
                side_copy(p + flying).start()
            if n + 1 < len(hops):
                for copy in hops[n + 1](p):
                    copy.start()

        def tick(at):
            if at < 4:
                turn = [[(1, 0)], [(2, 0), (1, 1)], [(3, 0), (2, 1), (1, 2)], [(4, 0), (2, 2)]][at]
            else:
                turn = [(at + 1, 0), (at - 1, 1), (at - 2, 2)]
            for p, n in turn:
                if (3 if n else 1) <= p < n_pieces or at < 4:
                    advance(p, n)

        pack_copy = remote(pack, pack_other, side_sem, (n_pieces,), side_peer)
        first_copy = remote(first_ref, first_other, side_sem, (n_pieces + 1,), side_peer)
        loads = [
            pltpu.make_async_copy(mel_ref.at[section], mel, load_sem.at[0]),
            pltpu.make_async_copy(positions_ref, place, load_sem.at[1]),
        ]

        def conv_copies(mine):
            return first_held.copies(mine, first_ref, first_other, conv_first, weight_sem.at[0]) + second_held.copies(
                mine, own[0], other[0], conv_second, weight_sem.at[1]
            )

        def weight_copy(mine):
            return pltpu.make_async_copy(own[1] if mine == 0 else other[1], weight, weight_sem.at[2])

        def keep(n):
            return pltpu.make_async_copy(held[n], results[n], out_sem.at[n])

        barrier = pltpu.get_barrier_semaphore()
        peers = [side_peer] + [peer(bit) for bit in (1, 2, 4)]
        for device in peers:
            pl.semaphore_signal(barrier, inc=1, device_id=device, device_id_type=pl.DeviceIdType.MESH)
        for copy in loads:
            copy.start()
        pack[0:3, :] = gain[...].astype(f32)
        pack[3:6, :] = shift[...].astype(f32)
        pack[6:12, :] = biases[...].astype(f32)
        for n in range(hidden // width):
            pack[12 + n : 13 + n, :] = up_bias[:, n * width : n * width + width].astype(f32)
        pack[16:17, 0:lanes] = first_bias[...].astype(f32)
        pack[16:17, lanes:width] = jnp.zeros((1, lanes), f32)
        pack[17:24, :] = jnp.zeros((7, width), f32)
        pl.semaphore_wait(barrier, len(peers))
        side_copy(0).start()
        first_copy.start()
        pack_copy.start()
        for p in range(1, flying):
            side_copy(p).start()

        turned[0:8, :] = jnp.zeros((8, 128), f32)
        turned[8 + mel_frames : 16 + mel_frames, :] = jnp.zeros((8, 128), f32)
        carry[...] = jnp.zeros(carry.shape, f32)
        clear_pads(conv_first, bands)
        for copy in loads:
            copy.wait()
        band_at = lax.broadcasted_iota(jnp.int32, (bands, block), 0)
        frame_at = lax.broadcasted_iota(jnp.int32, (bands, block), 1)
        time_from, band_from = times[section], bands_from[section]
        time_to, band_to = time_from + time_spans[section], band_from + band_spans[section]
        band_keep = jnp.logical_or(band_at < band_from, band_at >= band_to)
        for n in range(mel_frames // block):
            at = frame_at + n * block
            keep_here = jnp.logical_and(band_keep, jnp.logical_or(at < time_from, at >= time_to))
            values = jnp.where(keep_here, mel[:, n * block : n * block + block].astype(f32), 0.0)
            values = jnp.concatenate([values, jnp.zeros((128 - bands, block), f32)], axis=0)
            turned[8 + n * block : 8 + n * block + block, :] = values.T
        for n, start in enumerate((7, 8, 9, 10)):
            taps[:, n * 128 : n * 128 + 128] = turned[pl.ds(start, frames, stride=2), :].astype(low)
        keep(0).start()

        for n in range(len(hops)):
            advance(0, n)
        first_copy.wait_recv()
        pack_copy.wait_recv()
        for which in range(2):

            @pl.when(section == which)
            def _(which=which):
                for copy in conv_copies(which):
                    copy.start()

        first_section = section == 0
        a_small[...] = jnp.where(first_section, pack[...], pack_other[...])
        t_small[...] = jnp.where(first_section, pack_other[...], pack[...])
        for n in range(hidden // width):
            a_ups[:, n * width : n * width + width] = a_small[12 + n : 13 + n, :]
            t_ups[:, n * width : n * width + width] = t_small[12 + n : 13 + n, :]
        bias = jnp.concatenate([a_small[16:17, 0:lanes], t_small[16:17, 0:lanes]], axis=1)
        for copy in conv_copies(0):
            copy.wait()

        def stem_block(i):
            here = pl.ds(pl.multiple_of(i * block, block), block)
            value, slope = gelu_both(dot(taps[here, 0:384], conv_first[...]) + bias)
            even = value.astype(low)
            even_act[here] = even
            even_slope[here] = slope.astype(low)
            value, slope = gelu_both(dot(taps[here, 128:512], conv_first[...]) + bias)
            odd = value.astype(low)
            odd_act[here] = odd
            odd_slope[here] = slope.astype(low)
            prior = dot(odd, conv_second[0:width])
            at_row = lax.broadcasted_iota(jnp.int32, (block, width), 0)
            moved = jnp.where(at_row == 0, carry[0:1, :], pltpu.roll(prior, 1, 0))
            carry[0:1, :] = prior[block - 1 : block, :]
            pre = moved + dot(even, conv_second[width : 2 * width]) + dot(odd, conv_second[2 * width :]) + row(a_small, 10)
            value, slope = gelu_both(pre)
            slope_second[here] = slope.astype(low)
            encoded[here] = value + place[here].astype(f32)

        for i in range(blocks):
            stem_block(i)
            tick(i)
        for n in range(1, 7):
            keep(n).start()
        for which in range(2):

            @pl.when(section == which)
            def _(which=which):
                weight_copy(which).start()

        weight_copy(0).wait()

        def project_block(i):
            here = pl.ds(pl.multiple_of(i * block, block), block)
            normed, inverse = norm_rows(encoded[here])
            rounded = (normed * row(a_small, 0) + row(a_small, 3)).astype(low)
            norm[here] = rounded
            joint[here, 0:width] = (dot(rounded, weight[:, 0:width]) + row(a_small, 6)).astype(low) * 0.125
            joint[here, width : 2 * width] = dot(rounded, weight[:, width : 2 * width]).astype(low)
            joint[here, 2 * width :] = (dot(rounded, weight[:, 2 * width :]) + row(a_small, 7)).astype(low)

        for i in range(blocks):
            project_block(i)
        tick(blocks)
        keep(7).start()
        keep(8).start()

        def attention(pair):
            lane = lax.broadcasted_iota(jnp.int32, (1, 128), 1)

            def cols(start):
                return pl.ds(pl.multiple_of(start + pair * 128, 128), 128)

            key, value = joint[:, cols(width)], joint[:, cols(2 * width)]

            @pl.loop(0, blocks)
            def _(i):
                here = pl.ds(pl.multiple_of(i * block, block), block)
                query = joint[here, cols(0)]
                found, log = [], []
                for head in range(2):
                    scores = dot_t(jnp.where(lane // 64 == head, query, jnp.zeros_like(query)), key)
                    top = jnp.max(scores, axis=1, keepdims=True) * log2_e
                    exponent = jnp.exp2(scores * log2_e - top)
                    total = jnp.sum(exponent, axis=1, keepdims=True)
                    found.append(dot(exponent.astype(low), value) * (1.0 / total))
                    log.append(top + jnp.log2(total))
                mixed[here, cols(0)] = jnp.where(lane < 64, found[0], found[1]).astype(low)
                both = jnp.where(lane == 0, log[0], log[1])
                logs[pl.ds(pl.multiple_of(pair * 8, 8), 8), here] = both.T[0:8, :]

        done = blocks + 1
        for pair in range(HEADS // 2):
            attention(pair)
            tick(done)
            done += 1
        while done < n_pieces + len(hops) - 1:
            tick(done)
            done += 1
        keep(9).start()
        keep(10).start()
        for p in range(n_pieces):
            for hop in hops:
                for copy in hop(p):
                    copy.wait_send()
        first_copy.wait_send()
        pack_copy.wait_send()
        for n in range(len(held)):
            keep(n).wait()

    def sems(*shape):
        return pltpu.SemaphoreType.DMA(shape)

    shape = (frames, width)
    kept = [(shape, low), (shape, f32)] + [(shape, low)] * 6 + [((frames, 3 * width), low), (shape, low), ((4 * HEADS, frames), f32)]
    everywhere, on_chip = pl.BlockSpec(memory_space=pl.ANY), pl.BlockSpec(memory_space=pltpu.VMEM)
    return pl.pallas_call(
        kernel,
        name="begin",
        in_specs=[everywhere] * n_any + [pl.BlockSpec(memory_space=pltpu.SMEM)] * 4 + [on_chip] * 5,
        out_specs=[everywhere] * (1 + n_sent) + [on_chip] * 4 + [everywhere] * len(kept),
        out_shape=[jax.ShapeDtypeStruct(a.shape, a.dtype) for a in [first] + sent]
        + [jax.ShapeDtypeStruct(s, f32) for s in ((24, width), (24, width), (1, hidden), (1, hidden))]
        + [jax.ShapeDtypeStruct(s, d) for s, d in kept],
        scratch_shapes=[pltpu.VMEM(s, d) for s, d in kept]
        + [
            pltpu.VMEM((bands, mel_frames), low), pltpu.VMEM((mel_frames + 16, 128), f32), pltpu.VMEM(shape, low),
            pltpu.VMEM((384, width), low), pltpu.VMEM((3 * width, width), low), pltpu.VMEM((width, 3 * width), low),
            pltpu.VMEM((8, width), f32), pltpu.VMEM((24, width), f32), pltpu.VMEM((24, width), f32),
            sems(2), sems(3), sems(len(kept)), sems(2, n_pieces + 2), sems(2, n_pieces), sems(2, 2, n_pieces),
        ],
        compiler_params=pltpu.CompilerParams(collective_id=1, has_side_effects=True, vmem_limit_bytes=VMEM_BYTES),
        cost_estimate=pl.CostEstimate(flops=10**10, bytes_accessed=10**8, transcendentals=0),
    )(mel_input, positions, first, *sent, *spans, gain, shift, biases, up_bias, first_bias)


def factors_of(size):
    found, rest = [], size // 2
    while rest > 1:
        radix = 2 if size <= 16 or rest % 4 else 4
        found.append(radix)
        rest //= radix
    return found


def finish_backward(audio, text, joint, logs, mixed_grad, grad, encoded, slopes, smalls, weight, second, first, acts, audio_sums, text_sums, bands):
    width, tile_rows = 512, 512
    half = tile_rows // 2
    lanes = width // 2
    frames, text_rows = joint.shape[0], text[0][0].shape[0]
    tiles = len(audio)
    count = tiles + 2
    early = 11
    flying = 3
    lag = 1
    rows = count * tile_rows
    block = 256
    blocks = frames // block
    replicas = lax.axis_size("dp")
    factors = factors_of(replicas)
    levels = len(factors)
    befores, sizes, scatters = [], [], []
    for radix in factors:
        before = sizes[-1] if sizes else half
        befores.append(before)
        scatters.append(before % (16 * radix) == 0)
        sizes.append(before // radix if scatters[-1] else before)

    arrays, places = [], {}

    def place(array):
        if id(array) not in places:
            places[id(array)] = len(arrays)
            arrays.append(array)
        return places[id(array)]

    def job(x, xc, y, yc):
        return (place(x), xc, y if isinstance(y, int) else (place(y),), yc)

    audio_jobs = [job(*one) for one in audio]
    text_jobs = [job(*one) for one in text]
    at_joint, at_logs, at_mixed, at_grad, at_encoded = [place(a) for a in (joint, logs, mixed_grad, grad, encoded)]
    at_slopes = [place(a) for a in slopes]
    odd_act, even_act, taps = acts
    at_odd, at_even, at_taps = place(odd_act), place(even_act), place(taps)
    at_weight = (place(weight.own), place(weight.other))
    at_second = (place(second.own), place(second.other))
    at_first = (place(first.own), place(first.other))
    n_any = len(arrays)
    n_chip = 1 + len(audio_sums) + len(text_sums)

    def kernel(*refs):
        given = refs[:n_any]
        smalls, *known = refs[n_any : n_any + n_chip]
        audio_sums, text_sums = known[:2], known[2:]
        out_ref, keep_ref, got_ref = refs[n_any + n_chip : n_any + n_chip + 3]
        refs = refs[n_any + n_chip + 3 :]
        (
            tile, core_recv, side_send, side_recv, work, final, x_audio, y_audio, x_text, y_text,
            joint, logs, mixed_grad, query_grad, key_grad, value_grad, key_acc, value_acc, key_turned, sums,
            encoded_in, grad_in, slope_in, weight, second, first, second_low, next_low, even_low, odd_low, taps_grad,
            carry, small_buf, mel_buf, mel_send,
            in_sem, load_sem, weight_sem, block_sem, keep_sem, core_sem, side_sem, back_sem, out_sem, mel_sem, sent_sem,
        ) = refs[:46]
        recvs = refs[46 : 46 + levels]
        rs_sems = refs[46 + levels : 46 + 2 * levels]
        ag_sems = refs[46 + 2 * levels :]
        own_grads = (query_grad, key_grad, value_grad)

        section, replica = lax.axis_index("section"), lax.axis_index("dp")
        core = replica % 2
        digits, strides, rest, stride = [], [], replica // 2, 2
        for radix in factors:
            digits.append(rest % radix)
            strides.append(stride)
            rest, stride = rest // radix, stride * radix
        core_peer = {"dp": replica + 1 - 2 * core}
        side_peer = {"section": 1 - section}

        def peer(level, distance):
            digit = (digits[level] + distance) % factors[level]
            return digit, {"dp": replica + (digit - digits[level]) * strides[level]}

        def remote(source, target, sent, sems, k, device):
            return pltpu.make_async_remote_copy(
                src_ref=source, dst_ref=target, send_sem=sent, recv_sem=sems.at[k],
                device_id=device, device_id_type=pl.DeviceIdType.MESH,
            )

        def rows_at(start, size):
            return pl.ds(pl.multiple_of(start, 16), size)

        def offset(level):
            found = 0
            for n in range(level):
                if scatters[n]:
                    found = found + digits[n] * sizes[n]
            return found

        def core_copy(k):
            return remote(
                tile.at[k % 2, :, rows_at((1 - core) * half, half)], core_recv.at[k % 4], core_sem.at[1, k], core_sem.at[0], k, core_peer
            )

        def side_copy(k):
            here = rows_at(k * half, half)
            return remote(side_send.at[here], side_recv.at[here], sent_sem.at[0], side_sem, k, side_peer)

        def scatter_copy(k, level, distance):
            digit, device = peer(level, distance)
            size = sizes[level]
            start = k * half + offset(level) + (digit * size if scatters[level] else 0)
            return remote(
                work.at[rows_at(start, size)], recvs[level].at[distance - 1, rows_at(k * size, size)],
                sent_sem.at[2 + 2 * level], rs_sems[level], k, device,
            )

        def scatter_wait(k, level):
            here = recvs[level].at[:, rows_at(k * sizes[level], sizes[level])]
            remote(here, here, sent_sem.at[0], rs_sems[level], k, side_peer).wait_recv()

        def gather_copy(k, level, distance):
            digit, device = peer(level, distance)
            here = final.at[rows_at(k * tile_rows + core * half + offset(level + 1), sizes[level])]
            return remote(here, here, sent_sem.at[3 + 2 * level], ag_sems[level], k, device)

        def gather_wait(k, level):
            here = recvs[level].at[:, rows_at(k * sizes[level], sizes[level])]
            remote(here, here, sent_sem.at[0], ag_sems[level], k, side_peer).wait_recv()

        def scatter_sent(level, start, size):
            here = recvs[level].at[:, rows_at(start, size)]
            remote(here, here, sent_sem.at[2 + 2 * level], rs_sems[level], 0, side_peer).wait_send()

        def all_sent():
            remote(side_send, side_recv, sent_sem.at[0], side_sem, 0, side_peer).wait_send()
            remote(side_send, side_recv, sent_sem.at[1], back_sem, 0, core_peer).wait_send()
            for level in range(levels):
                if scatters[level]:
                    scatter_sent(level, 0, count * sizes[level])
                    here = recvs[level]
                    remote(here, here, sent_sem.at[3 + 2 * level], ag_sems[level], 0, side_peer).wait_send()
            pltpu.make_async_copy(final, out_ref, out_sem).wait()

        def back_copy(k):
            here = final.at[rows_at(k * tile_rows + core * half, half)]
            return remote(here, here, sent_sem.at[1], back_sem, k, core_peer)

        def store(k):
            here = rows_at(k * tile_rows, tile_rows)
            return pltpu.make_async_copy(final.at[here], out_ref.at[here], out_sem)

        def mel_copy():
            return remote(mel_send, got_ref, mel_sem.at[1], mel_sem, 0, side_peer)

        def stage_core(k):
            core_copy(k).wait_recv()
            here, mine = rows_at(k * half, half), rows_at(core * half, half)
            slot, from_peer = k % 2, k % 4
            side_send[here] = tile[slot, 1 - section, mine] + core_recv[from_peer, 1 - section]

            @when(jnp.logical_or(k < flying, k == tiles))
            def _():
                side_copy(k).start()

            work[here] = tile[slot, section, mine] + core_recv[from_peer, section]

        scatter_levels = [n for n in range(levels) if scatters[n]]

        def next_exchange(k, level):
            if level + 1 < levels:
                for distance in range(1, factors[level + 1]):
                    scatter_copy(k, level + 1, distance).start()
            elif scatter_levels:
                for distance in range(1, factors[scatter_levels[-1]]):
                    gather_copy(k, scatter_levels[-1], distance).start()
            else:
                back_copy(k).start()

        def put(k, level, total):
            if level + 1 < levels:
                work[rows_at(k * half + offset(level + 1), total.shape[0])] = total.astype(low)
            else:
                start = k * tile_rows + core * half + offset(level + 1)
                final[rows_at(start, total.shape[0])] = total.astype(low)
            next_exchange(k, level)

        def stage_side(k):
            side_copy(k).wait_recv()
            later = k + flying

            @when(jnp.logical_and(later < count, later != tiles))
            def _():
                side_copy(later).start()

            here = rows_at(k * half, half)
            put(k, -1, work[here] + side_recv[here])

        def stage_scatter(k, level):
            size = sizes[level]
            scatter_wait(k, level)
            kind = f32 if factors[level] > 2 else low
            total = work[rows_at(k * half + offset(level + 1), size)].astype(kind)
            for distance in range(1, factors[level]):
                total += recvs[level][distance - 1, rows_at(k * size, size)].astype(kind)
            if not scatters[level]:
                scatter_sent(level, k * sizes[level], sizes[level])
            put(k, level, total)

        def stage_gather(k, level):
            gather_wait(k, level)
            if level != scatter_levels[0]:
                below = scatter_levels[scatter_levels.index(level) - 1]
                for distance in range(1, factors[below]):
                    gather_copy(k, below, distance).start()
            else:
                back_copy(k).start()

        def stage_back(k):
            back_copy(k).wait_recv()
            store(k).start()

        stages = [stage_side]
        stages += [functools.partial(stage_scatter, level=n) for n in range(levels)]
        stages += [functools.partial(stage_gather, level=n) for n in reversed(scatter_levels)]
        stages.append(stage_back)

        def tick(at):
            for n, stage in enumerate(stages):

                @pl.when(jnp.logical_and(at >= lag * n, at < count + lag * n))
                def _(n=n, stage=stage):
                    stage(at - lag * n)

        def when(cond):
            return pl.when(cond)

        def fetch_copies(job, x_buf, y_buf, slot, sems):
            x, xc, y, yc = job
            x_from = given[x].at[:, xc * width : (xc + 1) * width]
            y_from = own_grads[y] if isinstance(y, int) else given[y[0]].at[:, yc * width : (yc + 1) * width]
            return (
                pltpu.make_async_copy(x_from, x_buf.at[slot], sems.at[0, slot]),
                pltpu.make_async_copy(y_from, y_buf.at[slot], sems.at[1, slot]),
            )

        def fetch(k, first_k, last_k):
            for n in range(first_k, last_k):

                @when(k == n)
                def _(n=n):
                    for copy in fetch_copies(audio_jobs[n], x_audio, y_audio, n % 2, in_sem.at[0]):
                        copy.start()
                    for copy in fetch_copies(text_jobs[n], x_text, y_text, n % 2, in_sem.at[1]):
                        copy.start()

        def fetch_wait(k):
            slot = k % 2
            for copy in fetch_copies(audio_jobs[0], x_audio, y_audio, slot, in_sem.at[0]):
                copy.wait()
            for copy in fetch_copies(text_jobs[0], x_text, y_text, slot, in_sem.at[1]):
                copy.wait()

        def tile_grads(k, last_k, first_k):
            slot = k % 2

            @when(k + 1 < last_k)
            def _():
                fetch(k + 1, first_k, last_k)

            fetch_wait(k)

            @when(k >= 2)
            def _():
                core_copy(k - 2).wait_send()

            tile[slot, 0] = dot_tt(x_audio[slot], y_audio[slot]).astype(low)
            tile[slot, 1] = dot_tt(x_text[slot], y_text[slot]).astype(low)
            core_copy(k).start()

            @when(k > first_k)
            def _():
                stage_core(k - 1)

        attn_loads = [
            pltpu.make_async_copy(given[at_joint], joint, load_sem.at[0]),
            pltpu.make_async_copy(given[at_logs], logs, load_sem.at[1]),
            pltpu.make_async_copy(given[at_mixed], mixed_grad, load_sem.at[2]),
        ]

        def attention(step):
            pair, part_at = step // blocks, step % blocks
            lane = lax.broadcasted_iota(jnp.int32, (1, 128), 1)
            sub = lax.broadcasted_iota(jnp.int32, (128, 1), 0)

            def cols(start):
                return pl.ds(pl.multiple_of(start + pair * 128, 128), 128)

            here = rows_at(part_at * block, block)

            @when(part_at == 0)
            def _():
                key_acc[...] = jnp.zeros(key_acc.shape, f32)
                value_acc[...] = jnp.zeros(value_acc.shape, f32)
                key_turned[...] = joint[:, cols(width)].astype(f32).T.astype(low)

            query, key, value = joint[here, cols(0)], joint[:, cols(width)], joint[:, cols(2 * width)]
            grad = mixed_grad[here, cols(0)]
            log = logs[pl.ds(pl.multiple_of(pair * 8, 8), 8), pl.ds(pl.multiple_of(part_at * block, block), block)]
            turned = key_turned[...]
            found = []
            for head in range(2):
                part = jnp.where(lane // 64 == head, query, jnp.zeros_like(query))
                grad_part = jnp.where(lane // 64 == head, grad, jnp.zeros_like(grad))
                chance = jnp.exp2(dot_t(key, part) * log2_e - log[head : head + 1, :])
                product = chance * dot_t(value, grad_part)
                grad_scores = (product - chance * jnp.sum(product, axis=0, keepdims=True)).astype(low)
                found.append(
                    (
                        dot(chance.astype(low), grad_part),
                        dot(grad_scores, part),
                        dot(jnp.where(sub // 64 == head, turned, jnp.zeros_like(turned)), grad_scores),
                    )
                )
            value_acc[...] += found[0][0] + found[1][0]
            key_acc[...] += found[0][1] + found[1][1]
            query_turned = found[0][2] + found[1][2]
            grad_query = query_turned.T * 0.125
            query_grad[here, cols(0)] = grad_query.astype(low)
            sums[0:1, cols(0)] += col_sum(grad_query)

            @when(part_at == blocks - 1)
            def _():
                key_grad[:, cols(0)] = key_acc[...].astype(low)
                value_grad[:, cols(0)] = value_acc[...].astype(low)
                sums[1:2, cols(0)] = col_sum(value_acc[...])

        def weight_copies(mine):
            found = [pltpu.make_async_copy(given[at_weight[0 if mine == 0 else 1]], weight, weight_sem.at[0])]
            for n, (split, at, held) in enumerate(((second_side, at_second, second), (first_side, at_first, first))):
                found += split.copies(mine, given[at[0]], given[at[1]], held, weight_sem.at[1 + n])
            return found

        def block_copies(i, slot):
            here = rows_at(i * block, block)
            found = [
                pltpu.make_async_copy(given[at_encoded].at[here], encoded_in.at[slot], block_sem.at[0, slot]),
                pltpu.make_async_copy(given[at_grad].at[here], grad_in.at[slot], block_sem.at[1, slot]),
            ]
            for n in range(3):
                found.append(
                    pltpu.make_async_copy(given[at_slopes[n]].at[here], slope_in.at[slot, n], block_sem.at[2 + n, slot])
                )
            return found

        def stem_block(step):
            i = blocks - 1 - step
            slot = step % 2

            @when(step + 1 < blocks)
            def _():
                for copy in block_copies(i - 1, 1 - slot):
                    copy.start()

            for copy in block_copies(i, slot):
                copy.wait()
            here = rows_at(i * block, block)
            back = (
                dot_t(query_grad[here], weight[:, :width])
                + dot_t(key_grad[here], weight[:, width : 2 * width])
                + dot_t(value_grad[here], weight[:, 2 * width :])
            )
            normed, inverse = norm_rows(encoded_in[slot])
            sums[2:3, :] += col_sum(back * normed)
            sums[3:4, :] += col_sum(back)
            total = grad_in[slot] + norm_back(back, row(smalls, 0), normed, inverse)
            total = total * slope_in[slot, 0].astype(f32)
            sums[4:5, :] += col_sum(total)
            rounded = total.astype(low)
            second_low[here] = rounded
            at_row = lax.broadcasted_iota(jnp.int32, (block, width), 0)
            wide = rounded.astype(f32)
            moved = jnp.where(at_row == block - 1, carry[0:1, :], pltpu.roll(wide, block - 1, 0))
            carry[0:1, :] = wide[0:1, :]
            moved = moved.astype(low)
            next_low[here] = moved
            grad_even = dot_t(rounded, second[width : 2 * width]) * slope_in[slot, 1].astype(f32)
            grad_odd = (dot_t(rounded, second[2 * width :]) + dot_t(moved, second[0:width])) * slope_in[slot, 2].astype(f32)
            sums[5:6, :] += col_sum(grad_even) + col_sum(grad_odd)
            grad_even = grad_even.astype(low)
            grad_odd = grad_odd.astype(low)
            even_low[here] = grad_even
            odd_low[here] = grad_odd
            taps_even = dot_t(grad_even, first[...])
            taps_odd = dot_t(grad_odd, first[...])
            taps_grad[here, 0:128] = taps_even[:, 0:128]
            taps_grad[here, 128:256] = taps_even[:, 128:256] + taps_odd[:, 0:128]
            taps_grad[here, 256:384] = taps_even[:, 256:384] + taps_odd[:, 128:256]
            taps_grad[here, 384:512] = taps_odd[:, 256:384]

        def mel_rows():
            at_row = lax.broadcasted_iota(jnp.int32, (frames, 128), 0)
            before = jnp.where(at_row == 0, 0.0, pltpu.roll(taps_grad[:, 384:512], 1, 0))
            mel_buf[:, 0:128] = taps_grad[:, 128:256] + before
            after = jnp.where(at_row == frames - 1, 0.0, pltpu.roll(taps_grad[:, 0:128], frames - 1, 0))
            mel_buf[:, 128:256] = taps_grad[:, 256:384] + after
            mel_send[...] = mel_buf[rows_at((1 - section) * (frames // 2), frames // 2)].astype(low)

        def keep_copy():
            return pltpu.make_async_copy(mel_buf.at[rows_at(section * (frames // 2), frames // 2)], keep_ref, keep_sem)

        conv_jobs = [(at_odd, next_low), (at_even, second_low), (at_odd, second_low)]

        def conv_copies(n, slot):
            x, y = conv_jobs[n]
            return (
                pltpu.make_async_copy(given[x], x_audio.at[slot], in_sem.at[0, 0, slot]),
                pltpu.make_async_copy(y, y_audio.at[slot], in_sem.at[0, 1, slot]),
            )

        def tap_copies():
            return [
                pltpu.make_async_copy(given[at_taps].at[:, n * 128 : n * 128 + 384], x_audio.at[n, :, 0:384], in_sem.at[0, 0, n])
                for n in range(2)
            ]

        barrier = pltpu.get_barrier_semaphore()
        peers = [core_peer, side_peer]
        peers += [peer(n, d)[1] for n in range(levels) for d in range(1, factors[n])]
        for device in peers:
            pl.semaphore_signal(barrier, inc=1, device_id=device, device_id_type=pl.DeviceIdType.MESH)

        fetch(0, 0, 1)
        for copy in attn_loads:
            copy.start()
        for which in range(2):

            @when(section == which)
            def _(which=which):
                for copy in weight_copies(which):
                    copy.start()

        for copy in block_copies(blocks - 1, 0):
            copy.start()
        sums[...] = jnp.zeros(sums.shape, f32)
        carry[...] = jnp.zeros(carry.shape, f32)
        pl.semaphore_wait(barrier, len(peers))

        @pl.loop(0, early)
        def _(k):
            tile_grads(k, early, 0)

        stage_core(early - 1)
        for copy in attn_loads:
            copy.wait()

        @pl.loop(0, 4 * blocks)
        def _(step):
            attention(step)

            @when(jnp.logical_or(step < 3, step % 3 == 1))
            def _():
                tick(jnp.where(step < 3, step, 3 + (step - 4) // 3))

        fetch(early, early, early + 1)

        @pl.loop(early, tiles)
        def _(k):
            tile_grads(k, tiles, early)
            tick(k - early + 7)

        stage_core(tiles - 1)
        for copy in weight_copies(0):
            copy.wait()
        clear_pads(first, bands)

        @pl.loop(0, blocks)
        def _(step):
            stem_block(step)

            @when(step % 2 == 1)
            def _():
                tick(10 + step // 2)

        for copy in conv_copies(0, 0):
            copy.start()

        @pl.loop(0, 3)
        def _(n):
            slot = n % 2
            for which in range(1, 3):

                @when(n + 1 == which)
                def _(which=which):
                    for copy in conv_copies(which, which % 2):
                        copy.start()

            for copy in conv_copies(0, slot):
                copy.wait()
            joint[0:tile_rows, pl.ds(pl.multiple_of(n * width, width), width)] = dot_tt(x_audio[slot], y_audio[slot]).astype(low)

        for copy in tap_copies():
            copy.start()
        core_copy(tiles - 2).wait_send()
        slot = tiles % 2

        def conv_part(tap, start, s):
            cols = slice(tap * width + s * lanes, tap * width + s * lanes + lanes)
            return joint[start : start + half, cols]

        for s in range(2):
            tile[slot, s, 0:half, 0:lanes] = conv_part(0, 0, s)
            tile[slot, s, half:tile_rows, 0:lanes] = conv_part(0, half, s)
            tile[slot, s, 0:half, lanes:width] = conv_part(1, half, s)
            tile[slot, s, half:tile_rows, lanes:width] = conv_part(2, 0, s)
        core_copy(tiles).start()
        for copy in tap_copies():
            copy.wait()
        first_grad = (
            dot_tt(x_audio[0, :, 0:384], even_low[...]) + dot_tt(x_audio[1, :, 0:384], odd_low[...])
        ).astype(low)
        stage_core(tiles)
        core_copy(tiles - 1).wait_send()
        slot = 1 - slot
        feed, wide_feed = audio_sums
        text_feed_sums, text_wide, text_cross, cross_sums, text_attn, text_first = text_sums
        small_buf[...] = jnp.zeros(small_buf.shape, f32)
        text_rows_from = (
            (text_first, 0), (text_cross, 0), (text_feed_sums, 0), (text_first, 1), (text_cross, 1), (text_feed_sums, 1),
            (text_attn, 0), (text_attn, 1), (text_cross, 2), (text_feed_sums, 2), (cross_sums, 0), (text_feed_sums, 3),
        )
        for at, (ref, n) in enumerate(text_rows_from):
            small_buf[1, at : at + 1, :] = ref[n : n + 1, :]
        for at, ref, n in (
            (1, feed, 3), (2, feed, 0), (4, feed, 4), (5, feed, 1), (8, feed, 5), (9, feed, 2), (11, cross_sums, 1),
        ):
            small_buf[0, at : at + 1, :] = ref[n : n + 1, :]
        for n in range(4):
            cols = slice(n * width, n * width + width)
            small_buf[0, 12 + n : 13 + n, :] = wide_feed[0:1, cols]
            small_buf[1, 12 + n : 13 + n, :] = text_wide[0:1, cols]
        for s in range(2):
            small_buf[s, 17:18, :] = text_feed_sums[3:4, :]
        small_buf[0, 6:8, :] = sums[0:2, :]
        small_buf[0, 0:1, :] = sums[2:3, :]
        small_buf[0, 3:4, :] = sums[3:4, :]
        small_buf[0, 10:11, :] = sums[4:5, :]
        small_buf[0, 16:17, 0:lanes] = sums[5:6, 0:lanes]
        small_buf[1, 16:17, 0:lanes] = sums[5:6, lanes:width]
        for s in range(2):
            cols = slice(s * lanes, s * lanes + lanes)
            tile[slot, s, 0:half, 0:lanes] = conv_part(1, 0, s)
            tile[slot, s, 0:half, lanes:width] = conv_part(2, half, s)
            tile[slot, s, half : half + 192, 0:lanes] = first_grad[0:192, cols]
            tile[slot, s, half : half + 192, lanes:width] = first_grad[192:384, cols]
            tile[slot, s, half + 192 : half + 224, :] = small_buf[s].astype(low)
            tile[slot, s, half + 224 : tile_rows, :] = jnp.zeros((32, width), low)
        core_copy(tiles + 1).start()
        mel_rows()
        keep_copy().start()
        stage_core(tiles + 1)
        mel_copy().start()

        @pl.loop(12, count + lag * (len(stages) - 1))
        def _(at):
            tick(at)

        keep_copy().wait()
        mel_copy().wait()
        for k in (count - 2, count - 1):
            core_copy(k).wait_send()

        all_sent()

    second_side, first_side = second, first

    def sems(*shape):
        return pltpu.SemaphoreType.DMA(shape)

    def vmem(*shape, dtype=low):
        return pltpu.VMEM(shape, dtype)

    whole = (frames, width)
    return pl.pallas_call(
        kernel,
        name="finish_backward",
        in_specs=[pl.BlockSpec(memory_space=pl.ANY)] * n_any + [pl.BlockSpec(memory_space=pltpu.VMEM)] * n_chip,
        out_specs=[pl.BlockSpec(memory_space=pl.ANY)] * 3,
        out_shape=[
            jax.ShapeDtypeStruct((rows, width), low),
            jax.ShapeDtypeStruct((frames // 2, 256), f32),
            jax.ShapeDtypeStruct((frames // 2, 256), low),
        ],
        scratch_shapes=[
            vmem(2, 2, tile_rows, width), vmem(4, 2, half, width), vmem(count * half, width), vmem(count * half, width),
            vmem(count * half, width), vmem(rows, width),
            vmem(2, *whole), vmem(2, *whole), vmem(2, text_rows, width), vmem(2, text_rows, width),
            vmem(frames, 3 * width), vmem(32, frames, dtype=f32), vmem(*whole), vmem(*whole), vmem(*whole), vmem(*whole),
            vmem(frames, 128, dtype=f32), vmem(frames, 128, dtype=f32), vmem(128, frames), vmem(8, width, dtype=f32),
            vmem(2, block, width, dtype=f32), vmem(2, block, width, dtype=f32), vmem(2, 3, block, width),
            vmem(width, 3 * width), vmem(*second.shape), vmem(*first.shape),
            vmem(*whole), vmem(*whole), vmem(*whole), vmem(*whole), vmem(*whole, dtype=f32),
            vmem(8, width, dtype=f32), vmem(2, 32, width, dtype=f32),
            vmem(frames, 256, dtype=f32), vmem(frames // 2, 256),
            sems(2, 2, 2), sems(3), sems(3), sems(5, 2), pltpu.SemaphoreType.DMA, sems(2, count), sems(count), sems(count),
            pltpu.SemaphoreType.DMA, sems(2), sems(2 + 2 * levels),
            *[vmem(r - 1, count * s, width) for r, s in zip(factors, sizes)],
            *[sems(count) for r in factors],
            *[sems(count) for r in factors],
        ],
        compiler_params=pltpu.CompilerParams(
            collective_id=0, has_side_effects=True, vmem_limit_bytes=63 << 20
        ),
        cost_estimate=pl.CostEstimate(flops=10**11, bytes_accessed=10**8, transcendentals=0),
    )(*arrays, smalls, *audio_sums, *text_sums)


def shards(
    mel_input,
    time_start,
    time_width,
    freq_start,
    freq_width,
    text_len,
    text_embed,
    cotangent,
    positions,
    conv_first,
    conv_first_bias,
    conv_second,
    norm_gain,
    norm_shift,
    attn_in,
    attn_out,
    mlp_up,
    mlp_down,
    up_bias,
    small_bias,
    cross_first,
    cross_second,
):
    frames, width = positions.shape
    bands, mel_frames = mel_input.shape[1], mel_input.shape[2]
    audio_block = frames // 2
    swap_pairs = [(0, 1), (1, 0)]

    def partner(array):
        return lax.ppermute(array, "section", swap_pairs)

    first_own = conv_first.reshape(3 * bands, -1)
    second_own = conv_second.reshape(3 * width, -1)
    owns = [w[0] for w in (attn_in, attn_out, mlp_up, mlp_down, cross_first, cross_second)]
    (
        first_other, second_other, *others, a_small, t_small, a_ups, t_ups,
        taps, encoded, even_act, odd_act, even_slope, odd_slope, slope_second, a_norm, a_joint, a_mixed, a_logs,
    ) = begin(
        mel_input, (time_start, time_width, freq_start, freq_width), norm_gain[0], norm_shift[0], small_bias[0], up_bias,
        conv_first_bias[None], first_own, second_own, owns[0], owns[1:], positions,
    )
    a_in, a_out, a_up, a_down, a_cross_a, a_cross_b = [Side(0, o, p) for o, p in zip(owns, others)]
    t_in, t_out, t_up, t_down, t_cross_a, t_cross_b = [Side(1, o, p) for o, p in zip(owns, others)]
    first_all = Split(first_own, first_other, 3, 128)
    second_all = Split(second_own, second_other, 3, width)

    a_middle, a_feed_norm, a_hidden, a_slope, a_ending, memory, memory_keys, memory_values = audio_feed(
        encoded, a_mixed, a_out, a_small, a_ups, a_up, a_down, a_cross_a, a_cross_b, audio_block
    )

    t_norm, t_joint, t_mixed, t_logs, t_middle, cross_low, cross_query = text_start(
        text_embed, t_in, t_out, t_small, t_cross_a
    )
    (
        decoded_keep, decoded_send, t_feed_norm, t_hidden, t_pre, cot_low, after_grad, after_low, c_mixed,
        query_grad, key_grad, value_grad, feed_sums, feed_wide, c_sums,
    ) = text_cross(
        text_len, cross_query, memory_keys, memory_values, t_middle, cotangent, t_cross_b, t_small, t_ups, t_up, t_down
    )
    text_keep, text_send, middle_low, tq_grad, tk_grad, tv_grad, cross_sums, t_sums, text_sums = text_back(
        query_grad, t_middle, after_grad, t_joint, t_logs, text_embed, t_small, t_cross_a, t_out, t_in
    )
    decoded_got, text_got = partner(decoded_send), partner(text_send)
    end_low, a_pre, a_grad, a_grad_low, a_mixed_grad, a_feed_sums, a_feed_wide = audio_feed_back(
        key_grad, value_grad, a_ending, a_middle, a_slope, a_small, a_cross_a, a_cross_b, a_up, a_down, a_out, audio_block
    )

    audio = [(a_feed_norm, 0, a_pre, n) for n in range(4)] + [(a_hidden, n, end_low, 0) for n in range(4)]
    audio += [(memory, 0, key_grad, 0), (memory, 0, value_grad, 0), (a_mixed, 0, a_grad_low, 0)]
    audio += [(a_norm, 0, n, 0) for n in range(3)]
    text = [(t_feed_norm, 0, t_pre, n) for n in range(4)] + [(t_hidden, n, cot_low, 0) for n in range(4)]
    text += [(cross_low, 0, query_grad, 0), (c_mixed, 0, after_low, 0), (t_mixed, 0, middle_low, 0)]
    text += [(t_norm, 0, part, 0) for part in (tq_grad, tk_grad, tv_grad)]
    a_feed_sums, decoded_got, text_got = lax.optimization_barrier((a_feed_sums, decoded_got, text_got))
    total, mel_keep, mel_got = finish_backward(
        audio, text, a_joint, a_logs, a_mixed_grad, a_grad, encoded, (slope_second, even_slope, odd_slope), a_small, a_in,
        second_all, first_all, (odd_act, even_act, taps), (a_feed_sums, a_feed_wide),
        (feed_sums, feed_wide, cross_sums, c_sums, t_sums, text_sums), bands,
    )

    decoded, text_grad, mel_out = finish(
        [(decoded_keep, decoded_got), (text_keep, text_got)], mel_keep, mel_got,
        (time_start, time_width, freq_start, freq_width), bands,
    )
    joint, out, up, down, cross_a, cross_b, first, bias, second, gain, shift, wide, small, cross = unpack(total, bands)
    return (
        decoded, text_grad, mel_out, first, bias[0], second, gain, shift, joint, out, up, down, wide, small, cross_a, cross_b,
        cross[0],
    )


def solution(mesh):
    return jax.shard_map(
        shards,
        mesh=mesh,
        in_specs=(
            P("dp", None, None),
            P("dp"),
            P("dp"),
            P("dp"),
            P("dp"),
            P("dp"),
            P("dp", None, None),
            P("dp", None, None),
            P(),
            P(None, None, "section"),
            P("section"),
            P(None, None, "section"),
            P("section", None, None),
            P("section", None, None),
            P("section", None, None),
            P("section", None, None),
            P("section", None, None),
            P("section", None, None),
            P("section", None),
            P("section", None, None),
            P("section", None, None),
            P("section", None, None),
        ),
        out_specs=(
            P("dp", None, "section"),
            P("dp", None, "section"),
            P("dp", None, "section"),
            P(None, None, "section"),
            P("section"),
            P(None, None, "section"),
            P("section", None, None),
            P("section", None, None),
            P("section", None, None),
            P("section", None, None),
            P("section", None, None),
            P("section", None, None),
            P("section", None),
            P("section", None, None),
            P("section", None, None),
            P("section", None, None),
            P("section"),
        ),
        check_vma=False,
    )
```

```python
import functools

import jax
import jax.numpy as jnp
from jax import lax
from jax.experimental import pallas as pl
from jax.experimental.pallas import tpu as pltpu
from jax.sharding import PartitionSpec as P

HEADS = 8
epsilon = 1e-05
root_half = 0.7071067811865476
gauss_norm = 0.3989422804014327
log2_e = 1.4426950408889634
VMEM_BYTES = 56 << 20

f32 = jnp.float32
low = jnp.bfloat16


def dot(left, right):
    return lax.dot_general(left, right, (((1,), (0,)), ((), ())), preferred_element_type=f32)


def dot_t(left, right):
    return lax.dot_general(left, right, (((1,), (1,)), ((), ())), preferred_element_type=f32)


def dot_tt(left, right):
    return lax.dot_general(left, right, (((0,), (0,)), ((), ())), preferred_element_type=f32)


def gelu_both(inputs):
    ratio = 1.0 / (1.0 + (0.3275911 * root_half) * jnp.abs(inputs))
    bell = jnp.exp2((-0.5 * log2_e) * inputs * inputs)
    tail = ratio * (
        0.127414796
        + ratio * (-0.142248368 + ratio * (0.7107068705 + ratio * (-0.7265760135 + ratio * 0.5307027145)))
    )
    tail = tail * bell
    below = jnp.where(inputs >= 0.0, 1.0 - tail, tail)
    return inputs * below, below + inputs * bell * gauss_norm


def norm_rows(inputs):
    centred = inputs - jnp.mean(inputs, axis=-1, keepdims=True)
    inverse = lax.rsqrt(jnp.mean(centred * centred, axis=-1, keepdims=True) + epsilon)
    return centred * inverse, inverse


def norm_back(grad, gain, normed, inverse):
    scaled = grad * gain
    return inverse * (
        scaled
        - jnp.mean(scaled, axis=-1, keepdims=True)
        - normed * jnp.mean(scaled * normed, axis=-1, keepdims=True)
    )


def col_sum(inputs):
    return jnp.sum(inputs, axis=0, keepdims=True)


class Side:
    def __init__(self, side, own, other):
        self.side, self.own, self.other, self.shape = side, own, other, own.shape

    def copies(self, mine, own, other, held, sem):
        return [pltpu.make_async_copy(own if mine == self.side else other, held, sem)]


class Split:
    def __init__(self, own, other, groups, apart):
        self.own, self.other, self.groups, self.apart = own, other, groups, apart
        self.shape = (groups * apart, 2 * own.shape[1])

    def copies(self, mine, own, other, held, sem, parts=(0, 1)):
        size, half = self.own.shape[0] // self.groups, self.own.shape[1]
        found = []
        for which, ref in [((mine, own), (1 - mine, other))[n] for n in parts]:
            cols = slice(which * half, which * half + half)
            for n in range(self.groups):
                found.append(
                    pltpu.make_async_copy(
                        ref.at[n * size : n * size + size], held.at[n * self.apart : n * self.apart + size, cols], sem
                    )
                )
        return found


def call(body, name, steps, block, ins, outs, scratch=(), reverse=False, flops=0, grid=None):
    arrays, specs, kinds, weight_scratch = [], [], [], []
    at = (lambda i: steps - 1 - i) if reverse else (lambda i: i)
    for array, kind in ins:
        if kind in ("side", "split"):
            arrays += [array.own, array.other]
            specs += [pl.BlockSpec(memory_space=pl.ANY)] * 2
            weight_scratch.append(pltpu.VMEM(array.shape, array.own.dtype))
        elif kind == "rows":
            arrays.append(array)
            specs.append(pl.BlockSpec((block, array.shape[1]), lambda i: (at(i), 0)))
        elif kind == "clip":
            arrays.append(array)
            specs.append(pl.BlockSpec((None, block, array.shape[2]), lambda i: (lax.axis_index("section"), at(i), 0)))
        elif kind == "smem":
            arrays.append(array)
            specs.append(pl.BlockSpec(memory_space=pltpu.SMEM))
        else:
            arrays.append(array)
            specs.append(
                pl.BlockSpec(
                    array.shape,
                    lambda i, n=array.ndim: (0,) * n,
                    pipeline_mode=pl.Buffered(1),
                )
            )
        kinds.append((kind, array if kind in ("side", "split") else None))
    out_specs = [
        pl.BlockSpec((block, shape[1]), lambda i: (at(i), 0))
        if kind == "rows"
        else pl.BlockSpec(shape, lambda i, n=len(shape): (0,) * n)
        for shape, dtype, kind in outs
    ]
    n_in, n_out, n_weight = len(arrays), len(outs), len(weight_scratch)

    def kernel(*refs):
        in_refs, out_refs = refs[:n_in], refs[n_in : n_in + n_out]
        weights = refs[n_in + n_out : n_in + n_out + n_weight]
        extra = refs[n_in + n_out + n_weight :]
        given, r, w, loads = [], 0, 0, []
        for kind, array in kinds:
            if kind in ("side", "split"):
                loads.append((array, in_refs[r], in_refs[r + 1], weights[w]))
                given.append(weights[w])
                r, w = r + 2, w + 1
            else:
                given.append(in_refs[r])
                r += 1
        step = pl.program_id(0)
        if loads:
            sem = extra[-1]
            extra = extra[:-1]

            @pl.when(step == 0)
            def _():
                mine = lax.axis_index("section")
                for n, load in enumerate(loads):
                    for which in range(2):

                        @pl.when(mine == which)
                        def _(load=load, n=n, which=which):
                            array, own, other, held = load
                            for copy in array.copies(which, own, other, held, sem.at[n]):
                                copy.start()

                for n, (array, own, other, held) in enumerate(loads):
                    for copy in array.copies(0, own, other, held, sem.at[n]):
                        copy.wait()

        for ref, (shape, dtype, kind) in zip(out_refs, outs):
            if kind == "sums":

                @pl.when(step == 0)
                def _(ref=ref):
                    ref[...] = jnp.zeros(ref.shape, ref.dtype)

        body(step, given, out_refs, extra)

    scratch_shapes = weight_scratch + list(scratch)
    if weight_scratch:
        scratch_shapes.append(pltpu.SemaphoreType.DMA((n_weight,)))
    total = sum(a.size * a.dtype.itemsize for a in arrays) + sum(
        2 * s[0] * s[1] for s, d, k in outs
    )
    return pl.pallas_call(
        kernel,
        name=name,
        grid=(steps,),
        in_specs=specs,
        out_specs=out_specs,
        out_shape=[jax.ShapeDtypeStruct(shape, dtype) for shape, dtype, kind in outs],
        scratch_shapes=scratch_shapes,
        compiler_params=pltpu.CompilerParams(
            dimension_semantics=("arbitrary",), vmem_limit_bytes=VMEM_BYTES
        ),
        cost_estimate=pl.CostEstimate(flops=int(flops), bytes_accessed=int(total), transcendentals=0),
    )(*arrays)


def row(ref, n):
    return ref[n : n + 1, :].astype(f32)


def clear_pads(weight, bands):
    for n in range(3):
        weight[n * 128 + bands : n * 128 + 128, :] = jnp.zeros((128 - bands, weight.shape[1]), weight.dtype)


def write_halves(values, keep, send):
    half = values.shape[1] // 2
    mine = lax.axis_index("section")
    first, second = values[:, :half], values[:, half:]

    @pl.when(mine == 0)
    def _():
        keep[...] = first
        send[...] = second.astype(low)

    @pl.when(mine != 0)
    def _():
        keep[...] = second
        send[...] = first.astype(low)


def pair_cols(start, pair):
    return pl.ds(pl.multiple_of(start + pair * 128, 128), 128)


def seen(shape, key_axis):
    return lax.broadcasted_iota(jnp.int32, shape, key_axis) <= lax.broadcasted_iota(jnp.int32, shape, 1 - key_axis)


def attend_pair(query, key, value, causal):
    lane = lax.broadcasted_iota(jnp.int32, (1, 128), 1)
    mixed, logs = [], []
    for head in range(2):
        scores = dot_t(jnp.where(lane // 64 == head, query, jnp.zeros_like(query)), key)
        if causal:
            scores = jnp.where(seen(scores.shape, 1), scores, -1e30)
        top = jnp.max(scores, axis=1, keepdims=True) * log2_e
        exponent = jnp.exp2(scores * log2_e - top)
        total = jnp.sum(exponent, axis=1, keepdims=True)
        mixed.append(dot(exponent.astype(low), value) * (1.0 / total))
        logs.append(top + jnp.log2(total))
    both = jnp.where(lane == 0, logs[0], logs[1])
    return jnp.where(lane < 64, mixed[0], mixed[1]).astype(low), both.T[0:8, :]


def attend_pair_back(query, key, value, logs, grad, causal):
    lane = lax.broadcasted_iota(jnp.int32, (1, 128), 1)
    sub = lax.broadcasted_iota(jnp.int32, (128, 1), 0)
    turned = key.astype(f32).T.astype(low)
    found = []
    for head in range(2):
        part = jnp.where(lane // 64 == head, query, jnp.zeros_like(query))
        grad_part = jnp.where(lane // 64 == head, grad, jnp.zeros_like(grad))
        chance = jnp.exp2(dot_t(key, part) * log2_e - logs[head : head + 1, :])
        if causal:
            chance = jnp.where(seen(chance.shape, 0), chance, 0.0)
        product = chance * dot_t(value, grad_part)
        grad_scores = (product - chance * jnp.sum(product, axis=0, keepdims=True)).astype(low)
        found.append(
            (
                dot(jnp.where(sub // 64 == head, turned, jnp.zeros_like(turned)), grad_scores),
                dot(grad_scores, part),
                dot(chance.astype(low), grad_part),
            )
        )
    turned, key_grad, value_grad = (one + two for one, two in zip(*found))
    return turned.T * 0.125, key_grad, value_grad


def audio_feed(inputs, mixed, weight_out, smalls, ups, weight_up, weight_down, cross_a, cross_b, block):
    rows, width = inputs.shape
    hidden = ups.shape[1]

    def body(step, given, outs, extra):
        inputs, mixed, weight_out, smalls, ups, weight_up, weight_down, cross_a, cross_b = given
        middle_out, norm_out, hidden_out, slope_out, ending_out, memory_out, key_out, value_out = outs
        middle = inputs[...] + dot(mixed[...], weight_out[...]) + row(smalls, 8)
        middle_out[...] = middle
        normed, inverse = norm_rows(middle)
        rounded = (normed * row(smalls, 1) + row(smalls, 4)).astype(low)
        norm_out[...] = rounded
        ending = middle + row(smalls, 9)
        for part in range(hidden // 512):
            cols = slice(part * 512, part * 512 + 512)
            pre = dot(rounded, weight_up[:, cols]) + ups[:, cols].astype(f32)
            value, slope = gelu_both(pre)
            act = value.astype(low)
            hidden_out[:, cols] = act
            slope_out[:, cols] = slope.astype(low)
            ending += dot(act, weight_down[cols, :])
        ending_out[...] = ending
        normed, inverse = norm_rows(ending)
        memory = (normed * row(smalls, 2) + row(smalls, 5)).astype(low)
        memory_out[...] = memory
        key_out[...] = dot(memory, cross_a[...]).astype(low)
        value_out[...] = (dot(memory, cross_b[...]) + row(smalls, 11)).astype(low)

    wide, shape = (rows, hidden), (rows, width)
    return call(
        body, "audio_feed", rows // block, block,
        [(inputs, "rows"), (mixed, "rows"), (weight_out, "side"), (smalls, "full"), (ups, "full"),
         (weight_up, "side"), (weight_down, "side"), (cross_a, "side"), (cross_b, "side")],
        [(shape, f32, "rows"), (shape, low, "rows"), (wide, low, "rows"), (wide, low, "rows"),
         (shape, f32, "rows"), (shape, low, "rows"), (shape, low, "rows"), (shape, low, "rows")],
        flops=2 * rows * width * (3 * width + 2 * hidden),
    )


def text_start(inputs, weight, weight_out, smalls, cross_a):
    rows, width = inputs.shape[1:]

    def body(step, given, outs, extra):
        inputs, weight, weight_out, smalls, cross_a = given
        norm_out, joint, mixed, logs, middle_out, low_out, query_out = outs
        normed, inverse = norm_rows(inputs[...].astype(f32))
        rounded = (normed * row(smalls, 0) + row(smalls, 3)).astype(low)
        norm_out[...] = rounded
        joint[:, :width] = (dot(rounded, weight[:, :width]) + row(smalls, 6)).astype(low) * 0.125
        joint[:, width : 2 * width] = dot(rounded, weight[:, width : 2 * width]).astype(low)
        joint[:, 2 * width :] = (dot(rounded, weight[:, 2 * width :]) + row(smalls, 7)).astype(low)

        @pl.loop(0, HEADS // 2)
        def _(pair):
            cols = pair_cols(0, pair)
            mixed[:, cols], logs[pl.ds(pl.multiple_of(pair * 8, 8), 8), :] = attend_pair(
                joint[:, cols], joint[:, pair_cols(width, pair)], joint[:, pair_cols(2 * width, pair)], True
            )

        middle = inputs[...].astype(f32) + dot(mixed[...], weight_out[...]) + row(smalls, 8)
        middle_out[...] = middle
        normed, inverse = norm_rows(middle)
        rounded = (normed * row(smalls, 1) + row(smalls, 4)).astype(low)
        low_out[...] = rounded
        query_out[...] = (dot(rounded, cross_a[...]) + row(smalls, 10)).astype(low) * 0.125

    shape = (rows, width)
    return call(
        body, "text_start", 1, rows,
        [(inputs, "clip"), (weight, "side"), (weight_out, "side"), (smalls, "full"), (cross_a, "side")],
        [(shape, low, "rows"), ((rows, 3 * width), low, "rows"), (shape, low, "rows"), ((4 * HEADS, rows), f32, "whole"),
         (shape, f32, "rows"), (shape, low, "rows"), (shape, low, "rows")],
        flops=10 * rows * width * width,
    )


def text_cross(length, queries, keys, values, middle, cotangent, cross_b, smalls, ups, weight_up, weight_down):
    rows, width = middle.shape
    hidden = ups.shape[1]
    block, key_rows = rows, keys.shape[0]

    def body(step, given, outs, extra):
        length, queries, keys, values, middle, cotangent, cross_b, smalls, ups, weight_up, weight_down = given
        decoded_keep, decoded_send, norm_out, hidden_out, pre_out, cot_out, grad_out, grad_low, mixed, query_out, key_out, value_out, sums, wide_sums, cross_sums = outs
        logs, mixed_grad = extra

        @pl.loop(0, HEADS // 2)
        def _(pair):
            cols = pair_cols(0, pair)
            mixed[:, cols], logs[pl.ds(pl.multiple_of(pair * 8, 8), 8), :] = attend_pair(
                queries[:, cols], keys[:, cols], values[:, cols], False
            )

        after = middle[...] + dot(mixed[...], cross_b[...]) + row(smalls, 11)
        normed, inverse = norm_rows(after)
        rounded = (normed * row(smalls, 2) + row(smalls, 5)).astype(low)
        norm_out[...] = rounded
        at_row = lax.broadcasted_iota(jnp.int32, (block, 1), 0) + step * block
        valid = at_row < length[lax.axis_index("section")]
        grad = jnp.where(valid, cotangent[...].astype(f32), 0.0)
        cot = grad.astype(low)
        cot_out[...] = cot
        ending = after + row(smalls, 9)
        back = jnp.zeros((block, width), f32)
        for part in range(hidden // 512):
            cols = slice(part * 512, part * 512 + 512)
            pre = dot(rounded, weight_up[:, cols]) + ups[:, cols].astype(f32)
            value, slope = gelu_both(pre)
            act = value.astype(low)
            hidden_out[:, cols] = act
            ending += dot(act, weight_down[cols, :])
            grad_pre = dot_t(cot, weight_down[cols, :]) * slope
            wide_sums[0:1, cols] += col_sum(grad_pre)
            pre_low = grad_pre.astype(low)
            pre_out[:, cols] = pre_low
            back += dot_t(pre_low, weight_up[:, cols])
        write_halves(jnp.where(valid, ending, 0.0), decoded_keep, decoded_send)
        sums[0:1, :] += col_sum(back * normed)
        sums[1:2, :] += col_sum(back)
        sums[2:3, :] += col_sum(grad)
        grad = grad + norm_back(back, row(smalls, 2), normed, inverse)
        sums[3:4, :] += col_sum(grad)
        grad_out[...] = grad
        rounded = grad.astype(low)
        grad_low[...] = rounded
        mixed_grad[...] = dot_t(rounded, cross_b[...]).astype(low)

        @pl.loop(0, HEADS // 2)
        def _(pair):
            cols = pair_cols(0, pair)
            query_grad, key_grad, value_grad = attend_pair_back(
                queries[:, cols], keys[:, cols], values[:, cols], logs[pl.ds(pl.multiple_of(pair * 8, 8), 8), :],
                mixed_grad[:, cols], False,
            )
            query_out[:, cols] = query_grad.astype(low)
            key_out[:, cols] = key_grad.astype(low)
            value_grad = value_grad.astype(low)
            value_out[:, cols] = value_grad
            cross_sums[0:1, cols] = col_sum(query_grad)
            cross_sums[1:2, cols] = col_sum(value_grad.astype(f32))

    wide, shape = (rows, hidden), (rows, width)
    return call(
        body, "text_cross", 1, rows,
        [(length, "smem"), (queries, "rows"), (keys, "full"), (values, "full"), (middle, "rows"), (cotangent, "clip"), (cross_b, "side"),
         (smalls, "full"), (ups, "full"), (weight_up, "side"), (weight_down, "side")],
        [((rows, width // 2), f32, "rows"), ((rows, width // 2), low, "rows"), (shape, low, "rows"), (wide, low, "rows"),
         (wide, low, "rows"), (shape, low, "rows"), (shape, f32, "rows"), (shape, low, "rows"), (shape, low, "rows"), (shape, low, "rows"),
         ((key_rows, width), low, "whole"), ((key_rows, width), low, "whole"),
         ((8, width), f32, "sums"), ((8, hidden), f32, "sums"), ((8, width), f32, "sums")],
        scratch=[pltpu.VMEM((4 * HEADS, rows), f32), pltpu.VMEM(shape, low)],
        flops=2 * rows * width * (2 * width + 4 * hidden),
    )


def text_back(query_grad, middle, grad, joint, logs, inputs, smalls, cross_a, weight_out, weight):
    rows, width = middle.shape

    def body(step, given, outs, extra):
        query_grad, middle, grad, joint, logs, inputs, smalls, cross_a, weight_out, weight = given
        keep, send, low_out, query_out, key_out, value_out, cross_sums, attn_sums, first_sums = outs
        total, mixed_grad = extra
        back = dot_t(query_grad[...], cross_a[...])
        normed, inverse = norm_rows(middle[...])
        cross_sums[0:1, :] = col_sum(back * normed)
        cross_sums[1:2, :] = col_sum(back)
        total[...] = grad[...] + norm_back(back, row(smalls, 1), normed, inverse)
        cross_sums[2:3, :] = col_sum(total[...])
        rounded = total[...].astype(low)
        low_out[...] = rounded
        mixed_grad[...] = dot_t(rounded, weight_out[...]).astype(low)

        @pl.loop(0, HEADS // 2)
        def _(pair):
            cols = pair_cols(0, pair)
            query, key, value = attend_pair_back(
                joint[:, cols], joint[:, pair_cols(width, pair)], joint[:, pair_cols(2 * width, pair)],
                logs[pl.ds(pl.multiple_of(pair * 8, 8), 8), :], mixed_grad[:, cols], True,
            )
            query_out[:, cols] = query.astype(low)
            key_out[:, cols] = key.astype(low)
            value_out[:, cols] = value.astype(low)
            attn_sums[0:1, cols] = col_sum(query)
            attn_sums[1:2, cols] = col_sum(value)

        back = (
            dot_t(query_out[...], weight[:, :width])
            + dot_t(key_out[...], weight[:, width : 2 * width])
            + dot_t(value_out[...], weight[:, 2 * width :])
        )
        normed, inverse = norm_rows(inputs[...].astype(f32))
        first_sums[0:1, :] = col_sum(back * normed)
        first_sums[1:2, :] = col_sum(back)
        write_halves(total[...] + norm_back(back, row(smalls, 0), normed, inverse), keep, send)

    shape = (rows, width)
    return call(
        body, "text_back", 1, rows,
        [(query_grad, "rows"), (middle, "rows"), (grad, "rows"), (joint, "rows"), (logs, "full"), (inputs, "clip"),
         (smalls, "full"), (cross_a, "side"), (weight_out, "side"), (weight, "side")],
        [((rows, width // 2), f32, "rows"), ((rows, width // 2), low, "rows")] + [(shape, low, "rows")] * 4
        + [((8, width), f32, "sums")] * 3,
        scratch=[pltpu.VMEM(shape, f32), pltpu.VMEM(shape, low)],
        flops=14 * rows * width * width,
    )


def audio_feed_back(key_grad, value_grad, ending, middle, slope, smalls, cross_a, cross_b, weight_up, weight_down, weight_out, block):
    rows, width = ending.shape
    hidden = slope.shape[1]

    def body(step, given, outs, extra):
        key_grad, value_grad, ending, middle, slope, smalls, cross_a, cross_b, weight_up, weight_down, weight_out = given
        end_low, pre_out, grad_out, grad_low, mixed_out, sums, wide_sums = outs
        back = dot_t(key_grad[...], cross_a[...]) + dot_t(value_grad[...], cross_b[...])
        normed, inverse = norm_rows(ending[...])
        sums[0:1, :] += col_sum(back * normed)
        sums[1:2, :] += col_sum(back)
        grad = norm_back(back, row(smalls, 2), normed, inverse)
        sums[2:3, :] += col_sum(grad)
        rounded = grad.astype(low)
        end_low[...] = rounded
        back = jnp.zeros((block, width), f32)
        for part in range(hidden // 512):
            cols = slice(part * 512, part * 512 + 512)
            grad_pre = dot_t(rounded, weight_down[cols, :]) * slope[:, cols].astype(f32)
            wide_sums[0:1, cols] += col_sum(grad_pre)
            pre_low = grad_pre.astype(low)
            pre_out[:, cols] = pre_low
            back += dot_t(pre_low, weight_up[:, cols])
        normed, inverse = norm_rows(middle[...])
        sums[3:4, :] += col_sum(back * normed)
        sums[4:5, :] += col_sum(back)
        grad = grad + norm_back(back, row(smalls, 1), normed, inverse)
        sums[5:6, :] += col_sum(grad)
        grad_out[...] = grad
        rounded = grad.astype(low)
        grad_low[...] = rounded
        mixed_out[...] = dot_t(rounded, weight_out[...]).astype(low)

    wide, shape = (rows, hidden), (rows, width)
    return call(
        body, "audio_feed_back", rows // block, block,
        [(key_grad, "rows"), (value_grad, "rows"), (ending, "rows"), (middle, "rows"), (slope, "rows"), (smalls, "full"),
         (cross_a, "side"), (cross_b, "side"), (weight_up, "side"), (weight_down, "side"), (weight_out, "side")],
        [(shape, low, "rows"), (wide, low, "rows"), (shape, f32, "rows"), (shape, low, "rows"), (shape, low, "rows"),
         ((8, width), f32, "sums"), ((8, hidden), f32, "sums")],
        flops=2 * rows * width * (3 * width + 2 * hidden),
    )


def unpack(total, bands):
    width, half = total.shape[1], total.shape[1] // 2
    tiles = 14

    def kernel(total, joint, out, up, down, cross_a, cross_b, first, bias, second, gain, shift, wide, small, cross, held, found, in_sem, out_sem):
        def load(n):
            here = pl.ds(pl.multiple_of(n * width, width), width)
            return pltpu.make_async_copy(total.at[here], held.at[n], in_sem.at[n])

        def target(n):
            cols = lambda k: slice(k * width, k * width + width)
            if n < 4:
                return up.at[0, :, cols(n)]
            if n < 8:
                return down.at[0, cols(n - 4)]
            if n < 11:
                return (cross_a, cross_b, out)[n - 8].at[0]
            return joint.at[0, :, cols(n - 11)]

        def store(n):
            return pltpu.make_async_copy(found.at[n], target(n), out_sem.at[n])

        @pl.loop(0, tiles + 2)
        def _(n):
            load(n).start()

        @pl.loop(0, tiles)
        def _(n):
            load(n).wait()
            found[n] = held[n].astype(f32)
            for k in range(tiles):

                @pl.when(n == k)
                def _(k=k):
                    store(k).start()

        load(tiles).wait()
        load(tiles + 1).wait()
        tile = held.at[tiles]
        second[0] = tile[:, 0:half].astype(f32)
        second[1, half:width] = tile[0:half, half:width].astype(f32)
        second[2, 0:half] = tile[half:width, half:width].astype(f32)
        tile = held.at[tiles + 1]
        second[1, 0:half] = tile[0:half, 0:half].astype(f32)
        second[2, half:width] = tile[0:half, half:width].astype(f32)
        first[0] = tile[half : half + bands, 0:half].astype(f32)
        first[1, 0:64] = tile[half + 128 : half + 192, 0:half].astype(f32)
        first[1, 64:bands] = tile[half : half + bands - 64, half:width].astype(f32)
        first[2] = tile[half + 64 : half + 64 + bands, half:width].astype(f32)
        rows = tile[half + 192 : half + 224, :].astype(f32)
        gain[0] = rows[0:3]
        shift[0] = rows[3:6]
        small[0] = rows[6:12]
        for n in range(4):
            wide[:, n * width : (n + 1) * width] = rows[12 + n : 13 + n]
        bias[...] = rows[16:17, 0:half]
        mine = lax.axis_index("section")
        cross[...] = jnp.where(mine == 0, rows[17:18, 0:half], rows[17:18, half:width])
        for n in range(tiles):
            store(n).wait()

    shapes = [
        (1, width, 3 * width), (1, width, width), (1, width, 4 * width), (1, 4 * width, width), (1, width, width), (1, width, width),
        (3, bands, half), (1, half), (3, width, half), (1, 3, width), (1, 3, width), (1, 4 * width), (1, 6, width), (1, half),
    ]
    return pl.pallas_call(
        kernel,
        name="unpack",
        in_specs=[pl.BlockSpec(memory_space=pl.ANY)],
        out_specs=[pl.BlockSpec(memory_space=pl.ANY)] * 6 + [pl.BlockSpec(memory_space=pltpu.VMEM)] * 8,
        out_shape=[jax.ShapeDtypeStruct(shape, f32) for shape in shapes],
        scratch_shapes=[
            pltpu.VMEM((tiles + 2, width, width), low), pltpu.VMEM((tiles, width, width), f32),
            pltpu.SemaphoreType.DMA((tiles + 2,)), pltpu.SemaphoreType.DMA((tiles,)),
        ],
        compiler_params=pltpu.CompilerParams(vmem_limit_bytes=VMEM_BYTES),
        cost_estimate=pl.CostEstimate(flops=0, bytes_accessed=6 * total.size, transcendentals=0),
    )(total)


def finish(parts, mel_keep, mel_got, spans, bands):
    count = len(parts)
    pair_rows = mel_keep.shape[0]
    frames = 2 * pair_rows

    def kernel(*refs):
        pairs, (keep_ref, got_ref), marks = refs[: 2 * count], refs[2 * count : 2 * count + 2], refs[2 * count + 2 : 2 * count + 6]
        outs, mel_out, laid = refs[2 * count + 6 : 3 * count + 6], refs[3 * count + 6], refs[3 * count + 7]
        mine = lax.axis_index("section")
        for n, out in enumerate(outs):
            out[mine] = pairs[2 * n][...]
            out[1 - mine] = pairs[2 * n + 1][...].astype(f32)
        band_at = lax.broadcasted_iota(jnp.int32, (bands, frames), 0)
        frame_at = lax.broadcasted_iota(jnp.int32, (bands, frames), 1) + mine * frames
        for clip, ref in ((mine, keep_ref), (1 - mine, got_ref)):
            for n in range(2):
                laid[pl.ds(n, pair_rows, stride=2), :] = ref[:, n * 128 : n * 128 + 128].astype(f32)
            start, span, band, width = (mark[clip] for mark in marks)
            keep = jnp.logical_and(
                jnp.logical_or(band_at < band, band_at >= band + width),
                jnp.logical_or(frame_at < start, frame_at >= start + span),
            )
            mel_out[clip] = jnp.where(keep, laid[...].T[0:bands, :], 0.0)

    def full(shape):
        return pl.BlockSpec(shape, lambda i, n=len(shape): (0,) * n)

    flat = [array for pair in parts for array in pair]
    shapes = [(2,) + keep.shape for keep, got in parts] + [(2, bands, frames)]
    return pl.pallas_call(
        kernel,
        name="finish",
        grid=(1,),
        in_specs=[full(array.shape) for array in flat + [mel_keep, mel_got]] + [pl.BlockSpec(memory_space=pltpu.SMEM)] * 4,
        out_specs=[full(shape) for shape in shapes],
        out_shape=[jax.ShapeDtypeStruct(shape, f32) for shape in shapes],
        scratch_shapes=[pltpu.VMEM((frames, 128), f32)],
        compiler_params=pltpu.CompilerParams(vmem_limit_bytes=VMEM_BYTES),
        cost_estimate=pl.CostEstimate(flops=0, bytes_accessed=sum(8 * a.size for a in flat), transcendentals=0),
    )(*flat, mel_keep, mel_got, *spans)


def begin(mel_input, spans, gain, shift, biases, up_bias, first_bias, first, second, joint_weight, weights, positions):
    frames, width = positions.shape
    bands, mel_frames = mel_input.shape[1:]
    lanes = width // 2
    hidden = up_bias.shape[1]
    block = 256
    blocks = frames // block
    sent = [second, joint_weight] + weights
    n_sent = len(sent)
    pieces = []
    for n, array in enumerate(sent):
        cuts = 2 if array.size >= 700000 else 1
        size = array.shape[0] // cuts
        pieces += [(n, c * size, size) for c in range(cuts)]
    n_pieces = len(pieces)
    flying = 2
    first_held = Split(first, first, 3, 128)
    second_held = Split(second, second, 3, width)
    n_any = n_sent + 3

    def kernel(*refs):
        mel_ref, positions_ref, first_ref = refs[:3]
        own = refs[3:n_any]
        times, time_spans, bands_from, band_spans = refs[n_any : n_any + 4]
        gain, shift, biases, up_bias, first_bias = refs[n_any + 4 : n_any + 9]
        outs = refs[n_any + 9 :]
        first_other = outs[0]
        other = outs[1 : 1 + n_sent]
        a_small, t_small, a_ups, t_ups = outs[1 + n_sent : 5 + n_sent]
        results = outs[5 + n_sent : 16 + n_sent]
        (
            taps, encoded, even_act, odd_act, even_slope, odd_slope, slope_second, norm, joint, mixed, logs,
            mel, turned, place, conv_first, conv_second, weight, carry, pack, pack_other,
            load_sem, weight_sem, out_sem, side_sem, near_sem, core_sem, sent_sem,
        ) = outs[16 + n_sent :]
        held = (taps, encoded, even_act, odd_act, even_slope, odd_slope, slope_second, norm, joint, mixed, logs)

        section, replica = lax.axis_index("section"), lax.axis_index("dp")
        side_peer = {"section": 1 - section}

        def flipped(value, bit):
            return value + bit - 2 * bit * ((value // bit) % 2)

        def peer(bit):
            return {"dp": flipped(replica, bit)}

        def remote(source, target, sent, sems, at, device):
            return pltpu.make_async_remote_copy(
                src_ref=source, dst_ref=target, send_sem=sent_sem.at[sent], recv_sem=sems.at[at],
                device_id=device, device_id_type=pl.DeviceIdType.MESH,
            )

        def part(p, q):
            n, start, size = pieces[p]
            return pl.ds(pl.multiple_of(start + q * (size // 4), 16), size // 4)

        def near(p):
            bit = 4 if p % 2 else 2
            quarter = replica % 2 + 2 * ((replica // bit) % 2)
            return bit, (quarter, flipped(quarter, 2))

        def side_copy(p):
            n = pieces[p][0]
            here = part(p, near(p)[1][0])
            return remote(own[n].at[here], other[n].at[here], n, side_sem, (p,), side_peer)

        def pass_on(p, q, sems, at, bit):
            n = pieces[p][0]
            here = other[n].at[part(p, q)]
            return remote(here, here, n, sems, at, peer(bit))

        def near_copies(p):
            bit, quarters = near(p)
            return [pass_on(p, quarters[0], near_sem, (p,), bit)]

        def core_copies(p):
            return [pass_on(p, q, core_sem, (b, p), 1) for b, q in enumerate(near(p)[1])]

        hops = (lambda p: [side_copy(p)], near_copies, core_copies)

        def advance(p, n):
            for copy in hops[n](p):
                copy.wait_recv()
            if n == 0 and p + flying < n_pieces:
                side_copy(p + flying).start()
            if n + 1 < len(hops):
                for copy in hops[n + 1](p):
                    copy.start()

        def tick(at):
            if at < 4:
                turn = [[(1, 0)], [(2, 0), (1, 1)], [(3, 0), (2, 1), (1, 2)], [(4, 0), (2, 2)]][at]
            else:
                turn = [(at + 1, 0), (at - 1, 1), (at - 2, 2)]
            for p, n in turn:
                if (3 if n else 1) <= p < n_pieces or at < 4:
                    advance(p, n)

        pack_copy = remote(pack, pack_other, n_sent, side_sem, (n_pieces,), side_peer)
        first_copy = remote(first_ref, first_other, n_sent + 1, side_sem, (n_pieces + 1,), side_peer)
        loads = [
            pltpu.make_async_copy(mel_ref.at[section], mel, load_sem.at[0]),
            pltpu.make_async_copy(positions_ref, place, load_sem.at[1]),
        ]

        def conv_copies(mine):
            return first_held.copies(mine, first_ref, first_other, conv_first, weight_sem.at[0]) + second_held.copies(
                mine, own[0], other[0], conv_second, weight_sem.at[1]
            )

        def weight_copy(mine):
            return pltpu.make_async_copy(own[1] if mine == 0 else other[1], weight, weight_sem.at[2])

        def keep(n):
            return pltpu.make_async_copy(held[n], results[n], out_sem.at[n])

        barrier = pltpu.get_barrier_semaphore()
        peers = [side_peer] + [peer(bit) for bit in (1, 2, 4)]
        for device in peers:
            pl.semaphore_signal(barrier, inc=1, device_id=device, device_id_type=pl.DeviceIdType.MESH)
        for copy in loads:
            copy.start()
        pack[0:3, :] = gain[...].astype(f32)
        pack[3:6, :] = shift[...].astype(f32)
        pack[6:12, :] = biases[...].astype(f32)
        for n in range(hidden // width):
            pack[12 + n : 13 + n, :] = up_bias[:, n * width : n * width + width].astype(f32)
        pack[16:17, 0:lanes] = first_bias[...].astype(f32).reshape(1, lanes)
        pack[16:17, lanes:width] = jnp.zeros((1, lanes), f32)
        pack[17:24, :] = jnp.zeros((7, width), f32)
        pl.semaphore_wait(barrier, len(peers))
        side_copy(0).start()
        first_copy.start()
        pack_copy.start()
        for p in range(1, flying):
            side_copy(p).start()

        turned[0:8, :] = jnp.zeros((8, 128), f32)
        turned[8 + mel_frames : 16 + mel_frames, :] = jnp.zeros((8, 128), f32)
        carry[...] = jnp.zeros(carry.shape, f32)
        clear_pads(conv_first, bands)
        for copy in loads:
            copy.wait()
        band_at = lax.broadcasted_iota(jnp.int32, (bands, block), 0)
        frame_at = lax.broadcasted_iota(jnp.int32, (bands, block), 1)
        time_from, band_from = times[section], bands_from[section]
        time_to, band_to = time_from + time_spans[section], band_from + band_spans[section]
        band_keep = jnp.logical_or(band_at < band_from, band_at >= band_to)
        for n in range(mel_frames // block):
            at = frame_at + n * block
            keep_here = jnp.logical_and(band_keep, jnp.logical_or(at < time_from, at >= time_to))
            values = jnp.where(keep_here, mel[:, n * block : n * block + block].astype(f32), 0.0)
            values = jnp.concatenate([values, jnp.zeros((128 - bands, block), f32)], axis=0)
            turned[8 + n * block : 8 + n * block + block, :] = values.T
        for n, start in enumerate((7, 8, 9, 10)):
            taps[:, n * 128 : n * 128 + 128] = turned[pl.ds(start, frames, stride=2), :].astype(low)
        keep(0).start()

        for n in range(len(hops)):
            advance(0, n)
        first_copy.wait_recv()
        pack_copy.wait_recv()
        for which in range(2):

            @pl.when(section == which)
            def _(which=which):
                for copy in conv_copies(which):
                    copy.start()

        first_section = section == 0
        a_small[...] = jnp.where(first_section, pack[...], pack_other[...])
        t_small[...] = jnp.where(first_section, pack_other[...], pack[...])
        for n in range(hidden // width):
            a_ups[:, n * width : n * width + width] = a_small[12 + n : 13 + n, :]
            t_ups[:, n * width : n * width + width] = t_small[12 + n : 13 + n, :]
        bias = jnp.concatenate([a_small[16:17, 0:lanes], t_small[16:17, 0:lanes]], axis=1)
        for copy in conv_copies(0):
            copy.wait()

        def stem_block(i):
            here = pl.ds(pl.multiple_of(i * block, block), block)
            value, slope = gelu_both(dot(taps[here, 0:384], conv_first[...]) + bias)
            even = value.astype(low)
            even_act[here] = even
            even_slope[here] = slope.astype(low)
            value, slope = gelu_both(dot(taps[here, 128:512], conv_first[...]) + bias)
            odd = value.astype(low)
            odd_act[here] = odd
            odd_slope[here] = slope.astype(low)
            prior = dot(odd, conv_second[0:width])
            at_row = lax.broadcasted_iota(jnp.int32, (block, width), 0)
            moved = jnp.where(at_row == 0, carry[0:1, :], pltpu.roll(prior, 1, 0))
            carry[0:1, :] = prior[block - 1 : block, :]
            pre = moved + dot(even, conv_second[width : 2 * width]) + dot(odd, conv_second[2 * width :]) + row(a_small, 10)
            value, slope = gelu_both(pre)
            slope_second[here] = slope.astype(low)
            encoded[here] = value + place[here].astype(f32)

        for i in range(blocks):
            stem_block(i)
            tick(i)
        for n in range(1, 7):
            keep(n).start()
        for which in range(2):

            @pl.when(section == which)
            def _(which=which):
                weight_copy(which).start()

        weight_copy(0).wait()

        def project_block(i):
            here = pl.ds(pl.multiple_of(i * block, block), block)
            normed, inverse = norm_rows(encoded[here])
            rounded = (normed * row(a_small, 0) + row(a_small, 3)).astype(low)
            norm[here] = rounded
            joint[here, 0:width] = (dot(rounded, weight[:, 0:width]) + row(a_small, 6)).astype(low) * 0.125
            joint[here, width : 2 * width] = dot(rounded, weight[:, width : 2 * width]).astype(low)
            joint[here, 2 * width :] = (dot(rounded, weight[:, 2 * width :]) + row(a_small, 7)).astype(low)

        for i in range(blocks):
            project_block(i)
        tick(blocks)
        keep(7).start()
        keep(8).start()

        def attention(pair):
            lane = lax.broadcasted_iota(jnp.int32, (1, 128), 1)

            def cols(start):
                return pl.ds(pl.multiple_of(start + pair * 128, 128), 128)

            key, value = joint[:, cols(width)], joint[:, cols(2 * width)]

            @pl.loop(0, blocks)
            def _(i):
                here = pl.ds(pl.multiple_of(i * block, block), block)
                query = joint[here, cols(0)]
                found, log = [], []
                for head in range(2):
                    scores = dot_t(jnp.where(lane // 64 == head, query, jnp.zeros_like(query)), key)
                    top = jnp.max(scores, axis=1, keepdims=True) * log2_e
                    exponent = jnp.exp2(scores * log2_e - top)
                    total = jnp.sum(exponent, axis=1, keepdims=True)
                    found.append(dot(exponent.astype(low), value) * (1.0 / total))
                    log.append(top + jnp.log2(total))
                mixed[here, cols(0)] = jnp.where(lane < 64, found[0], found[1]).astype(low)
                both = jnp.where(lane == 0, log[0], log[1])
                logs[pl.ds(pl.multiple_of(pair * 8, 8), 8), here] = both.T[0:8, :]

        done = blocks + 1
        for pair in range(HEADS // 2):
            attention(pair)
            tick(done)
            done += 1
        while done < n_pieces + len(hops) - 1:
            tick(done)
            done += 1
        keep(9).start()
        keep(10).start()
        for n in range(n_sent):
            remote(own[n], other[n], n, side_sem, (0,), side_peer).wait_send()
        first_copy.wait_send()
        pack_copy.wait_send()
        for n in range(len(held)):
            keep(n).wait()

    def sems(*shape):
        return pltpu.SemaphoreType.DMA(shape)

    shape = (frames, width)
    kept = [(shape, low), (shape, f32)] + [(shape, low)] * 6 + [((frames, 3 * width), low), (shape, low), ((4 * HEADS, frames), f32)]
    everywhere, on_chip = pl.BlockSpec(memory_space=pl.ANY), pl.BlockSpec(memory_space=pltpu.VMEM)
    return pl.pallas_call(
        kernel,
        name="begin",
        in_specs=[everywhere] * n_any + [pl.BlockSpec(memory_space=pltpu.SMEM)] * 4 + [on_chip] * 5,
        out_specs=[everywhere] * (1 + n_sent) + [on_chip] * 4 + [everywhere] * len(kept),
        out_shape=[jax.ShapeDtypeStruct(a.shape, a.dtype) for a in [first] + sent]
        + [jax.ShapeDtypeStruct(s, f32) for s in ((24, width), (24, width), (1, hidden), (1, hidden))]
        + [jax.ShapeDtypeStruct(s, d) for s, d in kept],
        scratch_shapes=[pltpu.VMEM(s, d) for s, d in kept]
        + [
            pltpu.VMEM((bands, mel_frames), low), pltpu.VMEM((mel_frames + 16, 128), f32), pltpu.VMEM(shape, low),
            pltpu.VMEM((384, width), low), pltpu.VMEM((3 * width, width), low), pltpu.VMEM((width, 3 * width), low),
            pltpu.VMEM((8, width), f32), pltpu.VMEM((24, width), f32), pltpu.VMEM((24, width), f32),
            sems(2), sems(3), sems(len(kept)), sems(n_pieces + 2), sems(n_pieces), sems(2, n_pieces),
            sems(n_sent + 2),
        ],
        compiler_params=pltpu.CompilerParams(collective_id=1, has_side_effects=True, vmem_limit_bytes=VMEM_BYTES),
        cost_estimate=pl.CostEstimate(flops=10**10, bytes_accessed=10**8, transcendentals=0),
    )(mel_input, positions, first, *sent, *spans, gain, shift, biases, up_bias, first_bias)


def factors_of(size):
    found, rest = [], size // 2
    while rest > 1:
        radix = 2 if size <= 16 or rest % 4 else 4
        found.append(radix)
        rest //= radix
    return found


def finish_backward(audio, text, joint, logs, mixed_grad, grad, encoded, slopes, smalls, weight, second, first, acts, audio_sums, text_sums, bands):
    width, tile_rows = 512, 512
    half = tile_rows // 2
    lanes = width // 2
    frames, text_rows = joint.shape[0], text[0][0].shape[0]
    tiles = len(audio)
    count = tiles + 2
    early = 11
    flying = 3
    lag = 1
    rows = count * tile_rows
    block = 256
    blocks = frames // block
    replicas = lax.axis_size("dp")
    factors = factors_of(replicas)
    levels = len(factors)
    befores, sizes, scatters = [], [], []
    for radix in factors:
        before = sizes[-1] if sizes else half
        befores.append(before)
        scatters.append(before % (16 * radix) == 0)
        sizes.append(before // radix if scatters[-1] else before)

    arrays, places = [], {}

    def place(array):
        if id(array) not in places:
            places[id(array)] = len(arrays)
            arrays.append(array)
        return places[id(array)]

    def job(x, xc, y, yc):
        return (place(x), xc, y if isinstance(y, int) else (place(y),), yc)

    audio_jobs = [job(*one) for one in audio]
    text_jobs = [job(*one) for one in text]
    at_joint, at_logs, at_mixed, at_grad, at_encoded = [place(a) for a in (joint, logs, mixed_grad, grad, encoded)]
    at_slopes = [place(a) for a in slopes]
    odd_act, even_act, taps = acts
    at_odd, at_even, at_taps = place(odd_act), place(even_act), place(taps)
    at_weight = (place(weight.own), place(weight.other))
    at_second = (place(second.own), place(second.other))
    at_first = (place(first.own), place(first.other))
    n_any = len(arrays)
    n_chip = 1 + len(audio_sums) + len(text_sums)

    def kernel(*refs):
        given = refs[:n_any]
        smalls, *known = refs[n_any : n_any + n_chip]
        audio_sums, text_sums = known[:2], known[2:]
        out_ref, keep_ref, got_ref = refs[n_any + n_chip : n_any + n_chip + 3]
        refs = refs[n_any + n_chip + 3 :]
        (
            tile, core_recv, side_send, side_recv, work, final, x_audio, y_audio, x_text, y_text,
            joint, logs, mixed_grad, query_grad, key_grad, value_grad, key_acc, value_acc, key_turned, sums,
            encoded_in, grad_in, slope_in, weight, second, first, second_low, next_low, even_low, odd_low, taps_grad,
            carry, small_buf, mel_buf, mel_send,
            in_sem, load_sem, weight_sem, block_sem, keep_sem, core_sem, side_sem, back_sem, out_sem, mel_sem, sent_sem,
        ) = refs[:46]
        recvs = refs[46 : 46 + levels]
        rs_sems = refs[46 + levels : 46 + 2 * levels]
        ag_sems = refs[46 + 2 * levels :]
        own_grads = (query_grad, key_grad, value_grad)

        section, replica = lax.axis_index("section"), lax.axis_index("dp")
        core = replica % 2
        digits, strides, rest, stride = [], [], replica // 2, 2
        for radix in factors:
            digits.append(rest % radix)
            strides.append(stride)
            rest, stride = rest // radix, stride * radix
        core_peer = {"dp": replica + 1 - 2 * core}
        side_peer = {"section": 1 - section}

        def peer(level, distance):
            digit = (digits[level] + distance) % factors[level]
            return digit, {"dp": replica + (digit - digits[level]) * strides[level]}

        def remote(source, target, sent, sems, k, device):
            return pltpu.make_async_remote_copy(
                src_ref=source, dst_ref=target, send_sem=sent, recv_sem=sems.at[k],
                device_id=device, device_id_type=pl.DeviceIdType.MESH,
            )

        def rows_at(start, size):
            return pl.ds(pl.multiple_of(start, 16), size)

        def offset(level):
            found = 0
            for n in range(level):
                if scatters[n]:
                    found = found + digits[n] * sizes[n]
            return found

        def core_copy(k):
            return remote(
                tile.at[k % 2, :, rows_at((1 - core) * half, half)], core_recv.at[k % 4], core_sem.at[1, k], core_sem.at[0], k, core_peer
            )

        def side_copy(k):
            here = rows_at(k * half, half)
            return remote(side_send.at[here], side_recv.at[here], sent_sem.at[0], side_sem, k, side_peer)

        def scatter_copy(k, level, distance):
            digit, device = peer(level, distance)
            size = sizes[level]
            start = k * half + offset(level) + (digit * size if scatters[level] else 0)
            return remote(
                work.at[rows_at(start, size)], recvs[level].at[distance - 1, rows_at(k * size, size)],
                sent_sem.at[2 + 2 * level], rs_sems[level], k, device,
            )

        def scatter_wait(k, level):
            here = recvs[level].at[:, rows_at(k * sizes[level], sizes[level])]
            remote(here, here, sent_sem.at[0], rs_sems[level], k, side_peer).wait_recv()

        def gather_copy(k, level, distance):
            digit, device = peer(level, distance)
            here = final.at[rows_at(k * tile_rows + core * half + offset(level + 1), sizes[level])]
            return remote(here, here, sent_sem.at[3 + 2 * level], ag_sems[level], k, device)

        def gather_wait(k, level):
            here = recvs[level].at[:, rows_at(k * sizes[level], sizes[level])]
            remote(here, here, sent_sem.at[0], ag_sems[level], k, side_peer).wait_recv()

        def scatter_sent(level, start, size):
            here = recvs[level].at[:, rows_at(start, size)]
            remote(here, here, sent_sem.at[2 + 2 * level], rs_sems[level], 0, side_peer).wait_send()

        def all_sent():
            remote(side_send, side_recv, sent_sem.at[0], side_sem, 0, side_peer).wait_send()
            remote(side_send, side_recv, sent_sem.at[1], back_sem, 0, core_peer).wait_send()
            for level in range(levels):
                if scatters[level]:
                    scatter_sent(level, 0, count * sizes[level])
                    here = recvs[level]
                    remote(here, here, sent_sem.at[3 + 2 * level], ag_sems[level], 0, side_peer).wait_send()
            pltpu.make_async_copy(final, out_ref, out_sem).wait()

        def back_copy(k):
            here = final.at[rows_at(k * tile_rows + core * half, half)]
            return remote(here, here, sent_sem.at[1], back_sem, k, core_peer)

        def store(k):
            here = rows_at(k * tile_rows, tile_rows)
            return pltpu.make_async_copy(final.at[here], out_ref.at[here], out_sem)

        def mel_copy():
            return remote(mel_send, got_ref, mel_sem.at[1], mel_sem, 0, side_peer)

        def stage_core(k):
            core_copy(k).wait_recv()
            here, mine = rows_at(k * half, half), rows_at(core * half, half)
            slot, from_peer = k % 2, k % 4
            side_send[here] = tile[slot, 1 - section, mine] + core_recv[from_peer, 1 - section]

            @when(jnp.logical_or(k < flying, k == tiles))
            def _():
                side_copy(k).start()

            work[here] = tile[slot, section, mine] + core_recv[from_peer, section]

        scatter_levels = [n for n in range(levels) if scatters[n]]

        def next_exchange(k, level):
            if level + 1 < levels:
                for distance in range(1, factors[level + 1]):
                    scatter_copy(k, level + 1, distance).start()
            elif scatter_levels:
                for distance in range(1, factors[scatter_levels[-1]]):
                    gather_copy(k, scatter_levels[-1], distance).start()
            else:
                back_copy(k).start()

        def put(k, level, total):
            if level + 1 < levels:
                work[rows_at(k * half + offset(level + 1), total.shape[0])] = total.astype(low)
            else:
                start = k * tile_rows + core * half + offset(level + 1)
                final[rows_at(start, total.shape[0])] = total.astype(low)
            next_exchange(k, level)

        def stage_side(k):
            side_copy(k).wait_recv()
            later = k + flying

            @when(jnp.logical_and(later < count, later != tiles))
            def _():
                side_copy(later).start()

            here = rows_at(k * half, half)
            put(k, -1, work[here] + side_recv[here])

        def stage_scatter(k, level):
            size = sizes[level]
            scatter_wait(k, level)
            kind = f32 if factors[level] > 2 else low
            total = work[rows_at(k * half + offset(level + 1), size)].astype(kind)
            for distance in range(1, factors[level]):
                total += recvs[level][distance - 1, rows_at(k * size, size)].astype(kind)
            if not scatters[level]:
                scatter_sent(level, k * sizes[level], sizes[level])
            put(k, level, total)

        def stage_gather(k, level):
            gather_wait(k, level)
            if level != scatter_levels[0]:
                below = scatter_levels[scatter_levels.index(level) - 1]
                for distance in range(1, factors[below]):
                    gather_copy(k, below, distance).start()
            else:
                back_copy(k).start()

        def stage_back(k):
            back_copy(k).wait_recv()
            store(k).start()

        stages = [stage_side]
        stages += [functools.partial(stage_scatter, level=n) for n in range(levels)]
        stages += [functools.partial(stage_gather, level=n) for n in reversed(scatter_levels)]
        stages.append(stage_back)

        def tick(at):
            for n, stage in enumerate(stages):

                @pl.when(jnp.logical_and(at >= lag * n, at < count + lag * n))
                def _(n=n, stage=stage):
                    stage(at - lag * n)

        def when(cond):
            return pl.when(cond)

        def fetch_copies(job, x_buf, y_buf, slot, sems):
            x, xc, y, yc = job
            x_from = given[x].at[:, xc * width : (xc + 1) * width]
            y_from = own_grads[y] if isinstance(y, int) else given[y[0]].at[:, yc * width : (yc + 1) * width]
            return (
                pltpu.make_async_copy(x_from, x_buf.at[slot], sems.at[0, slot]),
                pltpu.make_async_copy(y_from, y_buf.at[slot], sems.at[1, slot]),
            )

        def fetch(k, first_k, last_k):
            for n in range(first_k, last_k):

                @when(k == n)
                def _(n=n):
                    for copy in fetch_copies(audio_jobs[n], x_audio, y_audio, n % 2, in_sem.at[0]):
                        copy.start()
                    for copy in fetch_copies(text_jobs[n], x_text, y_text, n % 2, in_sem.at[1]):
                        copy.start()

        def fetch_wait(k):
            slot = k % 2
            for copy in fetch_copies(audio_jobs[0], x_audio, y_audio, slot, in_sem.at[0]):
                copy.wait()
            for copy in fetch_copies(text_jobs[0], x_text, y_text, slot, in_sem.at[1]):
                copy.wait()

        def tile_grads(k, last_k, first_k):
            slot = k % 2

            @when(k + 1 < last_k)
            def _():
                fetch(k + 1, first_k, last_k)

            fetch_wait(k)

            @when(k >= 2)
            def _():
                core_copy(k - 2).wait_send()

            tile[slot, 0] = dot_tt(x_audio[slot], y_audio[slot]).astype(low)
            tile[slot, 1] = dot_tt(x_text[slot], y_text[slot]).astype(low)
            core_copy(k).start()

            @when(k > first_k)
            def _():
                stage_core(k - 1)

        attn_loads = [
            pltpu.make_async_copy(given[at_joint], joint, load_sem.at[0]),
            pltpu.make_async_copy(given[at_logs], logs, load_sem.at[1]),
            pltpu.make_async_copy(given[at_mixed], mixed_grad, load_sem.at[2]),
        ]

        def attention(step):
            pair, part_at = step // blocks, step % blocks
            lane = lax.broadcasted_iota(jnp.int32, (1, 128), 1)
            sub = lax.broadcasted_iota(jnp.int32, (128, 1), 0)

            def cols(start):
                return pl.ds(pl.multiple_of(start + pair * 128, 128), 128)

            here = rows_at(part_at * block, block)

            @when(part_at == 0)
            def _():
                key_acc[...] = jnp.zeros(key_acc.shape, f32)
                value_acc[...] = jnp.zeros(value_acc.shape, f32)
                key_turned[...] = joint[:, cols(width)].astype(f32).T.astype(low)

            query, key, value = joint[here, cols(0)], joint[:, cols(width)], joint[:, cols(2 * width)]
            grad = mixed_grad[here, cols(0)]
            log = logs[pl.ds(pl.multiple_of(pair * 8, 8), 8), pl.ds(pl.multiple_of(part_at * block, block), block)]
            turned = key_turned[...]
            found = []
            for head in range(2):
                part = jnp.where(lane // 64 == head, query, jnp.zeros_like(query))
                grad_part = jnp.where(lane // 64 == head, grad, jnp.zeros_like(grad))
                chance = jnp.exp2(dot_t(key, part) * log2_e - log[head : head + 1, :])
                product = chance * dot_t(value, grad_part)
                grad_scores = (product - chance * jnp.sum(product, axis=0, keepdims=True)).astype(low)
                found.append(
                    (
                        dot(chance.astype(low), grad_part),
                        dot(grad_scores, part),
                        dot(jnp.where(sub // 64 == head, turned, jnp.zeros_like(turned)), grad_scores),
                    )
                )
            value_acc[...] += found[0][0] + found[1][0]
            key_acc[...] += found[0][1] + found[1][1]
            query_turned = found[0][2] + found[1][2]
            grad_query = query_turned.T * 0.125
            query_grad[here, cols(0)] = grad_query.astype(low)
            sums[0:1, cols(0)] += col_sum(grad_query)

            @when(part_at == blocks - 1)
            def _():
                key_grad[:, cols(0)] = key_acc[...].astype(low)
                value_grad[:, cols(0)] = value_acc[...].astype(low)
                sums[1:2, cols(0)] = col_sum(value_acc[...])

        def weight_copies(mine):
            found = [pltpu.make_async_copy(given[at_weight[0 if mine == 0 else 1]], weight, weight_sem.at[0])]
            for n, (split, at, held) in enumerate(((second_side, at_second, second), (first_side, at_first, first))):
                found += split.copies(mine, given[at[0]], given[at[1]], held, weight_sem.at[1 + n])
            return found

        def block_copies(i, slot):
            here = rows_at(i * block, block)
            found = [
                pltpu.make_async_copy(given[at_encoded].at[here], encoded_in.at[slot], block_sem.at[0, slot]),
                pltpu.make_async_copy(given[at_grad].at[here], grad_in.at[slot], block_sem.at[1, slot]),
            ]
            for n in range(3):
                found.append(
                    pltpu.make_async_copy(given[at_slopes[n]].at[here], slope_in.at[slot, n], block_sem.at[2 + n, slot])
                )
            return found

        def stem_block(step):
            i = blocks - 1 - step
            slot = step % 2

            @when(step + 1 < blocks)
            def _():
                for copy in block_copies(i - 1, 1 - slot):
                    copy.start()

            for copy in block_copies(i, slot):
                copy.wait()
            here = rows_at(i * block, block)
            back = (
                dot_t(query_grad[here], weight[:, :width])
                + dot_t(key_grad[here], weight[:, width : 2 * width])
                + dot_t(value_grad[here], weight[:, 2 * width :])
            )
            normed, inverse = norm_rows(encoded_in[slot])
            sums[2:3, :] += col_sum(back * normed)
            sums[3:4, :] += col_sum(back)
            total = grad_in[slot] + norm_back(back, row(smalls, 0), normed, inverse)
            total = total * slope_in[slot, 0].astype(f32)
            sums[4:5, :] += col_sum(total)
            rounded = total.astype(low)
            second_low[here] = rounded
            at_row = lax.broadcasted_iota(jnp.int32, (block, width), 0)
            wide = rounded.astype(f32)
            moved = jnp.where(at_row == block - 1, carry[0:1, :], pltpu.roll(wide, block - 1, 0))
            carry[0:1, :] = wide[0:1, :]
            moved = moved.astype(low)
            next_low[here] = moved
            grad_even = dot_t(rounded, second[width : 2 * width]) * slope_in[slot, 1].astype(f32)
            grad_odd = (dot_t(rounded, second[2 * width :]) + dot_t(moved, second[0:width])) * slope_in[slot, 2].astype(f32)
            sums[5:6, :] += col_sum(grad_even) + col_sum(grad_odd)
            grad_even = grad_even.astype(low)
            grad_odd = grad_odd.astype(low)
            even_low[here] = grad_even
            odd_low[here] = grad_odd
            taps_even = dot_t(grad_even, first[...])
            taps_odd = dot_t(grad_odd, first[...])
            taps_grad[here, 0:128] = taps_even[:, 0:128]
            taps_grad[here, 128:256] = taps_even[:, 128:256] + taps_odd[:, 0:128]
            taps_grad[here, 256:384] = taps_even[:, 256:384] + taps_odd[:, 128:256]
            taps_grad[here, 384:512] = taps_odd[:, 256:384]

        def mel_rows():
            at_row = lax.broadcasted_iota(jnp.int32, (frames, 128), 0)
            before = jnp.where(at_row == 0, 0.0, pltpu.roll(taps_grad[:, 384:512], 1, 0))
            mel_buf[:, 0:128] = taps_grad[:, 128:256] + before
            after = jnp.where(at_row == frames - 1, 0.0, pltpu.roll(taps_grad[:, 0:128], frames - 1, 0))
            mel_buf[:, 128:256] = taps_grad[:, 256:384] + after
            mel_send[...] = mel_buf[rows_at((1 - section) * (frames // 2), frames // 2)].astype(low)

        def keep_copy():
            return pltpu.make_async_copy(mel_buf.at[rows_at(section * (frames // 2), frames // 2)], keep_ref, keep_sem)

        conv_jobs = [(at_odd, next_low), (at_even, second_low), (at_odd, second_low)]

        def conv_copies(n, slot):
            x, y = conv_jobs[n]
            return (
                pltpu.make_async_copy(given[x], x_audio.at[slot], in_sem.at[0, 0, slot]),
                pltpu.make_async_copy(y, y_audio.at[slot], in_sem.at[0, 1, slot]),
            )

        def tap_copies():
            return [
                pltpu.make_async_copy(given[at_taps].at[:, n * 128 : n * 128 + 384], x_audio.at[n, :, 0:384], in_sem.at[0, 0, n])
                for n in range(2)
            ]

        barrier = pltpu.get_barrier_semaphore()
        peers = [core_peer, side_peer]
        peers += [peer(n, d)[1] for n in range(levels) for d in range(1, factors[n])]
        for device in peers:
            pl.semaphore_signal(barrier, inc=1, device_id=device, device_id_type=pl.DeviceIdType.MESH)

        fetch(0, 0, 1)
        for copy in attn_loads:
            copy.start()
        for which in range(2):

            @when(section == which)
            def _(which=which):
                for copy in weight_copies(which):
                    copy.start()

        for copy in block_copies(blocks - 1, 0):
            copy.start()
        sums[...] = jnp.zeros(sums.shape, f32)
        carry[...] = jnp.zeros(carry.shape, f32)
        pl.semaphore_wait(barrier, len(peers))

        @pl.loop(0, early)
        def _(k):
            tile_grads(k, early, 0)

        stage_core(early - 1)
        for copy in attn_loads:
            copy.wait()

        @pl.loop(0, 4 * blocks)
        def _(step):
            attention(step)

            @when(jnp.logical_or(step < 3, step % 3 == 1))
            def _():
                tick(jnp.where(step < 3, step, 3 + (step - 4) // 3))

        fetch(early, early, early + 1)

        @pl.loop(early, tiles)
        def _(k):
            tile_grads(k, tiles, early)
            tick(k - early + 7)

        stage_core(tiles - 1)
        for copy in weight_copies(0):
            copy.wait()
        clear_pads(first, bands)

        @pl.loop(0, blocks)
        def _(step):
            stem_block(step)

            @when(step % 2 == 1)
            def _():
                tick(10 + step // 2)

        for copy in conv_copies(0, 0):
            copy.start()

        @pl.loop(0, 3)
        def _(n):
            slot = n % 2
            for which in range(1, 3):

                @when(n + 1 == which)
                def _(which=which):
                    for copy in conv_copies(which, which % 2):
                        copy.start()

            for copy in conv_copies(0, slot):
                copy.wait()
            joint[0:tile_rows, pl.ds(pl.multiple_of(n * width, width), width)] = dot_tt(x_audio[slot], y_audio[slot]).astype(low)

        for copy in tap_copies():
            copy.start()
        core_copy(tiles - 2).wait_send()
        slot = tiles % 2

        def conv_part(tap, start, s):
            cols = slice(tap * width + s * lanes, tap * width + s * lanes + lanes)
            return joint[start : start + half, cols]

        for s in range(2):
            tile[slot, s, 0:half, 0:lanes] = conv_part(0, 0, s)
            tile[slot, s, half:tile_rows, 0:lanes] = conv_part(0, half, s)
            tile[slot, s, 0:half, lanes:width] = conv_part(1, half, s)
            tile[slot, s, half:tile_rows, lanes:width] = conv_part(2, 0, s)
        core_copy(tiles).start()
        for copy in tap_copies():
            copy.wait()
        first_grad = (
            dot_tt(x_audio[0, :, 0:384], even_low[...]) + dot_tt(x_audio[1, :, 0:384], odd_low[...])
        ).astype(low)
        stage_core(tiles)
        core_copy(tiles - 1).wait_send()
        slot = 1 - slot
        feed, wide_feed = audio_sums
        text_feed_sums, text_wide, text_cross, cross_sums, text_attn, text_first = text_sums
        small_buf[...] = jnp.zeros(small_buf.shape, f32)
        text_rows_from = (
            (text_first, 0), (text_cross, 0), (text_feed_sums, 0), (text_first, 1), (text_cross, 1), (text_feed_sums, 1),
            (text_attn, 0), (text_attn, 1), (text_cross, 2), (text_feed_sums, 2), (cross_sums, 0), (text_feed_sums, 3),
        )
        for at, (ref, n) in enumerate(text_rows_from):
            small_buf[1, at : at + 1, :] = ref[n : n + 1, :]
        for at, ref, n in (
            (1, feed, 3), (2, feed, 0), (4, feed, 4), (5, feed, 1), (8, feed, 5), (9, feed, 2), (11, cross_sums, 1),
        ):
            small_buf[0, at : at + 1, :] = ref[n : n + 1, :]
        for n in range(4):
            cols = slice(n * width, n * width + width)
            small_buf[0, 12 + n : 13 + n, :] = wide_feed[0:1, cols]
            small_buf[1, 12 + n : 13 + n, :] = text_wide[0:1, cols]
        for s in range(2):
            small_buf[s, 17:18, :] = text_feed_sums[3:4, :]
        small_buf[0, 6:8, :] = sums[0:2, :]
        small_buf[0, 0:1, :] = sums[2:3, :]
        small_buf[0, 3:4, :] = sums[3:4, :]
        small_buf[0, 10:11, :] = sums[4:5, :]
        small_buf[0, 16:17, 0:lanes] = sums[5:6, 0:lanes]
        small_buf[1, 16:17, 0:lanes] = sums[5:6, lanes:width]
        for s in range(2):
            cols = slice(s * lanes, s * lanes + lanes)
            tile[slot, s, 0:half, 0:lanes] = conv_part(1, 0, s)
            tile[slot, s, 0:half, lanes:width] = conv_part(2, half, s)
            tile[slot, s, half : half + 192, 0:lanes] = first_grad[0:192, cols]
            tile[slot, s, half : half + 192, lanes:width] = first_grad[192:384, cols]
            tile[slot, s, half + 192 : half + 224, :] = small_buf[s].astype(low)
            tile[slot, s, half + 224 : tile_rows, :] = jnp.zeros((32, width), low)
        core_copy(tiles + 1).start()
        mel_rows()
        keep_copy().start()
        stage_core(tiles + 1)
        mel_copy().start()

        @pl.loop(12, count + lag * (len(stages) - 1))
        def _(at):
            tick(at)

        keep_copy().wait()
        mel_copy().wait()
        for k in (count - 2, count - 1):
            core_copy(k).wait_send()

        all_sent()

    second_side, first_side = second, first

    def sems(*shape):
        return pltpu.SemaphoreType.DMA(shape)

    def vmem(*shape, dtype=low):
        return pltpu.VMEM(shape, dtype)

    whole = (frames, width)
    return pl.pallas_call(
        kernel,
        name="finish_backward",
        in_specs=[pl.BlockSpec(memory_space=pl.ANY)] * n_any + [pl.BlockSpec(memory_space=pltpu.VMEM)] * n_chip,
        out_specs=[pl.BlockSpec(memory_space=pl.ANY)] * 3,
        out_shape=[
            jax.ShapeDtypeStruct((rows, width), low),
            jax.ShapeDtypeStruct((frames // 2, 256), f32),
            jax.ShapeDtypeStruct((frames // 2, 256), low),
        ],
        scratch_shapes=[
            vmem(2, 2, tile_rows, width), vmem(4, 2, half, width), vmem(count * half, width), vmem(count * half, width),
            vmem(count * half, width), vmem(rows, width),
            vmem(2, *whole), vmem(2, *whole), vmem(2, text_rows, width), vmem(2, text_rows, width),
            vmem(frames, 3 * width), vmem(32, frames, dtype=f32), vmem(*whole), vmem(*whole), vmem(*whole), vmem(*whole),
            vmem(frames, 128, dtype=f32), vmem(frames, 128, dtype=f32), vmem(128, frames), vmem(8, width, dtype=f32),
            vmem(2, block, width, dtype=f32), vmem(2, block, width, dtype=f32), vmem(2, 3, block, width),
            vmem(width, 3 * width), vmem(*second.shape), vmem(*first.shape),
            vmem(*whole), vmem(*whole), vmem(*whole), vmem(*whole), vmem(*whole, dtype=f32),
            vmem(8, width, dtype=f32), vmem(2, 32, width, dtype=f32),
            vmem(frames, 256, dtype=f32), vmem(frames // 2, 256),
            sems(2, 2, 2), sems(3), sems(3), sems(5, 2), pltpu.SemaphoreType.DMA, sems(2, count), sems(count), sems(count),
            pltpu.SemaphoreType.DMA, sems(2), sems(2 + 2 * levels),
            *[vmem(r - 1, count * s, width) for r, s in zip(factors, sizes)],
            *[sems(count) for r in factors],
            *[sems(count) for r in factors],
        ],
        compiler_params=pltpu.CompilerParams(
            collective_id=0, has_side_effects=True, vmem_limit_bytes=63 << 20
        ),
        cost_estimate=pl.CostEstimate(flops=10**11, bytes_accessed=10**8, transcendentals=0),
    )(*arrays, smalls, *audio_sums, *text_sums)


def shards(
    mel_input,
    time_start,
    time_width,
    freq_start,
    freq_width,
    text_len,
    text_embed,
    cotangent,
    positions,
    conv_first,
    conv_first_bias,
    conv_second,
    norm_gain,
    norm_shift,
    attn_in,
    attn_out,
    mlp_up,
    mlp_down,
    up_bias,
    small_bias,
    cross_first,
    cross_second,
):
    frames, width = positions.shape
    bands, mel_frames = mel_input.shape[1], mel_input.shape[2]
    audio_block = frames // 2
    swap_pairs = [(0, 1), (1, 0)]

    def partner(array):
        return lax.ppermute(array, "section", swap_pairs)

    first_own = conv_first.reshape(3 * bands, -1)
    second_own = conv_second.reshape(3 * width, -1)
    owns = [w[0] for w in (attn_in, attn_out, mlp_up, mlp_down, cross_first, cross_second)]
    (
        first_other, second_other, *others, a_small, t_small, a_ups, t_ups,
        taps, encoded, even_act, odd_act, even_slope, odd_slope, slope_second, a_norm, a_joint, a_mixed, a_logs,
    ) = begin(
        mel_input, (time_start, time_width, freq_start, freq_width), norm_gain[0], norm_shift[0], small_bias[0], up_bias,
        conv_first_bias, first_own, second_own, owns[0], owns[1:], positions,
    )
    a_in, a_out, a_up, a_down, a_cross_a, a_cross_b = [Side(0, o, p) for o, p in zip(owns, others)]
    t_in, t_out, t_up, t_down, t_cross_a, t_cross_b = [Side(1, o, p) for o, p in zip(owns, others)]
    first_all = Split(first_own, first_other, 3, 128)
    second_all = Split(second_own, second_other, 3, width)

    a_middle, a_feed_norm, a_hidden, a_slope, a_ending, memory, memory_keys, memory_values = audio_feed(
        encoded, a_mixed, a_out, a_small, a_ups, a_up, a_down, a_cross_a, a_cross_b, audio_block
    )

    t_norm, t_joint, t_mixed, t_logs, t_middle, cross_low, cross_query = text_start(
        text_embed, t_in, t_out, t_small, t_cross_a
    )
    (
        decoded_keep, decoded_send, t_feed_norm, t_hidden, t_pre, cot_low, after_grad, after_low, c_mixed,
        query_grad, key_grad, value_grad, feed_sums, feed_wide, c_sums,
    ) = text_cross(
        text_len, cross_query, memory_keys, memory_values, t_middle, cotangent, t_cross_b, t_small, t_ups, t_up, t_down
    )
    text_keep, text_send, middle_low, tq_grad, tk_grad, tv_grad, cross_sums, t_sums, text_sums = text_back(
        query_grad, t_middle, after_grad, t_joint, t_logs, text_embed, t_small, t_cross_a, t_out, t_in
    )
    decoded_got, text_got = partner(decoded_send), partner(text_send)
    end_low, a_pre, a_grad, a_grad_low, a_mixed_grad, a_feed_sums, a_feed_wide = audio_feed_back(
        key_grad, value_grad, a_ending, a_middle, a_slope, a_small, a_cross_a, a_cross_b, a_up, a_down, a_out, audio_block
    )

    audio = [(a_feed_norm, 0, a_pre, n) for n in range(4)] + [(a_hidden, n, end_low, 0) for n in range(4)]
    audio += [(memory, 0, key_grad, 0), (memory, 0, value_grad, 0), (a_mixed, 0, a_grad_low, 0)]
    audio += [(a_norm, 0, n, 0) for n in range(3)]
    text = [(t_feed_norm, 0, t_pre, n) for n in range(4)] + [(t_hidden, n, cot_low, 0) for n in range(4)]
    text += [(cross_low, 0, query_grad, 0), (c_mixed, 0, after_low, 0), (t_mixed, 0, middle_low, 0)]
    text += [(t_norm, 0, part, 0) for part in (tq_grad, tk_grad, tv_grad)]
    a_feed_sums, decoded_got, text_got = lax.optimization_barrier((a_feed_sums, decoded_got, text_got))
    total, mel_keep, mel_got = finish_backward(
        audio, text, a_joint, a_logs, a_mixed_grad, a_grad, encoded, (slope_second, even_slope, odd_slope), a_small, a_in,
        second_all, first_all, (odd_act, even_act, taps), (a_feed_sums, a_feed_wide),
        (feed_sums, feed_wide, cross_sums, c_sums, t_sums, text_sums), bands,
    )

    decoded, text_grad, mel_out = finish(
        [(decoded_keep, decoded_got), (text_keep, text_got)], mel_keep, mel_got,
        (time_start, time_width, freq_start, freq_width), bands,
    )
    joint, out, up, down, cross_a, cross_b, first, bias, second, gain, shift, wide, small, cross = unpack(total, bands)
    return (
        decoded, text_grad, mel_out, first, bias[0], second, gain, shift, joint, out, up, down, wide, small, cross_a, cross_b,
        cross[0],
    )


def solution(mesh):
    return jax.shard_map(
        shards,
        mesh=mesh,
        in_specs=(
            P("dp", None, None),
            P("dp"),
            P("dp"),
            P("dp"),
            P("dp"),
            P("dp"),
            P("dp", None, None),
            P("dp", None, None),
            P(),
            P(None, None, "section"),
            P("section"),
            P(None, None, "section"),
            P("section", None, None),
            P("section", None, None),
            P("section", None, None),
            P("section", None, None),
            P("section", None, None),
            P("section", None, None),
            P("section", None),
            P("section", None, None),
            P("section", None, None),
            P("section", None, None),
        ),
        out_specs=(
            P("dp", None, "section"),
            P("dp", None, "section"),
            P("dp", None, "section"),
            P(None, None, "section"),
            P("section"),
            P(None, None, "section"),
            P("section", None, None),
            P("section", None, None),
            P("section", None, None),
            P("section", None, None),
            P("section", None, None),
            P("section", None, None),
            P("section", None),
            P("section", None, None),
            P("section", None, None),
            P("section", None, None),
            P("section"),
        ),
        check_vma=False,
    )
```

```python
import functools

import jax
import jax.numpy as jnp
from jax import lax
from jax.experimental import pallas as pl
from jax.experimental.pallas import tpu as pltpu
from jax.sharding import PartitionSpec as P

HEADS = 8
epsilon = 1e-05
root_half = 0.7071067811865476
gauss_norm = 0.3989422804014327
log2_e = 1.4426950408889634
VMEM_BYTES = 56 << 20

f32 = jnp.float32
low = jnp.bfloat16


def dot(left, right):
    return lax.dot_general(left, right, (((1,), (0,)), ((), ())), preferred_element_type=f32)


def dot_t(left, right):
    return lax.dot_general(left, right, (((1,), (1,)), ((), ())), preferred_element_type=f32)


def dot_tt(left, right):
    return lax.dot_general(left, right, (((0,), (0,)), ((), ())), preferred_element_type=f32)


def gelu_both(inputs):
    ratio = 1.0 / (1.0 + (0.3275911 * root_half) * jnp.abs(inputs))
    bell = jnp.exp2((-0.5 * log2_e) * inputs * inputs)
    tail = ratio * (
        0.127414796
        + ratio * (-0.142248368 + ratio * (0.7107068705 + ratio * (-0.7265760135 + ratio * 0.5307027145)))
    )
    tail = tail * bell
    below = jnp.where(inputs >= 0.0, 1.0 - tail, tail)
    return inputs * below, below + inputs * bell * gauss_norm


def norm_rows(inputs):
    centred = inputs - jnp.mean(inputs, axis=-1, keepdims=True)
    inverse = lax.rsqrt(jnp.mean(centred * centred, axis=-1, keepdims=True) + epsilon)
    return centred * inverse, inverse


def norm_back(grad, gain, normed, inverse):
    scaled = grad * gain
    return inverse * (
        scaled
        - jnp.mean(scaled, axis=-1, keepdims=True)
        - normed * jnp.mean(scaled * normed, axis=-1, keepdims=True)
    )


def col_sum(inputs):
    return jnp.sum(inputs, axis=0, keepdims=True)


class Side:
    def __init__(self, side, own, other):
        self.side, self.own, self.other, self.shape = side, own, other, own.shape

    def copies(self, mine, own, other, held, sem):
        return [pltpu.make_async_copy(own if mine == self.side else other, held, sem)]


class Split:
    def __init__(self, own, other, groups, apart):
        self.own, self.other, self.groups, self.apart = own, other, groups, apart
        self.shape = (groups * apart, 2 * own.shape[1])

    def copies(self, mine, own, other, held, sem, parts=(0, 1)):
        size, half = self.own.shape[0] // self.groups, self.own.shape[1]
        found = []
        for which, ref in [((mine, own), (1 - mine, other))[n] for n in parts]:
            cols = slice(which * half, which * half + half)
            for n in range(self.groups):
                found.append(
                    pltpu.make_async_copy(
                        ref.at[n * size : n * size + size], held.at[n * self.apart : n * self.apart + size, cols], sem
                    )
                )
        return found


def call(body, name, steps, block, ins, outs, scratch=(), reverse=False, flops=0, grid=None):
    arrays, specs, kinds, weight_scratch = [], [], [], []
    at = (lambda i: steps - 1 - i) if reverse else (lambda i: i)
    for array, kind in ins:
        if kind in ("side", "split"):
            arrays += [array.own, array.other]
            specs += [pl.BlockSpec(memory_space=pl.ANY)] * 2
            weight_scratch.append(pltpu.VMEM(array.shape, array.own.dtype))
        elif kind == "rows":
            arrays.append(array)
            specs.append(pl.BlockSpec((block, array.shape[1]), lambda i: (at(i), 0)))
        elif kind == "clip":
            arrays.append(array)
            specs.append(pl.BlockSpec((None, block, array.shape[2]), lambda i: (lax.axis_index("section"), at(i), 0)))
        elif kind == "smem":
            arrays.append(array)
            specs.append(pl.BlockSpec(memory_space=pltpu.SMEM))
        else:
            arrays.append(array)
            specs.append(
                pl.BlockSpec(
                    array.shape,
                    lambda i, n=array.ndim: (0,) * n,
                    pipeline_mode=pl.Buffered(1),
                )
            )
        kinds.append((kind, array if kind in ("side", "split") else None))
    out_specs = [
        pl.BlockSpec((block, shape[1]), lambda i: (at(i), 0))
        if kind == "rows"
        else pl.BlockSpec(shape, lambda i, n=len(shape): (0,) * n)
        for shape, dtype, kind in outs
    ]
    n_in, n_out, n_weight = len(arrays), len(outs), len(weight_scratch)

    def kernel(*refs):
        in_refs, out_refs = refs[:n_in], refs[n_in : n_in + n_out]
        weights = refs[n_in + n_out : n_in + n_out + n_weight]
        extra = refs[n_in + n_out + n_weight :]
        given, r, w, loads = [], 0, 0, []
        for kind, array in kinds:
            if kind in ("side", "split"):
                loads.append((array, in_refs[r], in_refs[r + 1], weights[w]))
                given.append(weights[w])
                r, w = r + 2, w + 1
            else:
                given.append(in_refs[r])
                r += 1
        step = pl.program_id(0)
        if loads:
            sem = extra[-1]
            extra = extra[:-1]

            @pl.when(step == 0)
            def _():
                mine = lax.axis_index("section")
                for n, load in enumerate(loads):
                    for which in range(2):

                        @pl.when(mine == which)
                        def _(load=load, n=n, which=which):
                            array, own, other, held = load
                            for copy in array.copies(which, own, other, held, sem.at[n]):
                                copy.start()

                for n, (array, own, other, held) in enumerate(loads):
                    for copy in array.copies(0, own, other, held, sem.at[n]):
                        copy.wait()

        for ref, (shape, dtype, kind) in zip(out_refs, outs):
            if kind == "sums":

                @pl.when(step == 0)
                def _(ref=ref):
                    ref[...] = jnp.zeros(ref.shape, ref.dtype)

        body(step, given, out_refs, extra)

    scratch_shapes = weight_scratch + list(scratch)
    if weight_scratch:
        scratch_shapes.append(pltpu.SemaphoreType.DMA((n_weight,)))
    total = sum(a.size * a.dtype.itemsize for a in arrays) + sum(
        2 * s[0] * s[1] for s, d, k in outs
    )
    return pl.pallas_call(
        kernel,
        name=name,
        grid=(steps,),
        in_specs=specs,
        out_specs=out_specs,
        out_shape=[jax.ShapeDtypeStruct(shape, dtype) for shape, dtype, kind in outs],
        scratch_shapes=scratch_shapes,
        compiler_params=pltpu.CompilerParams(
            dimension_semantics=("arbitrary",), vmem_limit_bytes=VMEM_BYTES
        ),
        cost_estimate=pl.CostEstimate(flops=int(flops), bytes_accessed=int(total), transcendentals=0),
    )(*arrays)


def row(ref, n):
    return ref[n : n + 1, :].astype(f32)


def clear_pads(weight, bands):
    for n in range(3):
        weight[n * 128 + bands : n * 128 + 128, :] = jnp.zeros((128 - bands, weight.shape[1]), weight.dtype)


def write_halves(values, keep, send):
    half = values.shape[1] // 2
    mine = lax.axis_index("section")
    first, second = values[:, :half], values[:, half:]

    @pl.when(mine == 0)
    def _():
        keep[...] = first
        send[...] = second.astype(low)

    @pl.when(mine != 0)
    def _():
        keep[...] = second
        send[...] = first.astype(low)


def pair_cols(start, pair):
    return pl.ds(pl.multiple_of(start + pair * 128, 128), 128)


def seen(shape, key_axis):
    return lax.broadcasted_iota(jnp.int32, shape, key_axis) <= lax.broadcasted_iota(jnp.int32, shape, 1 - key_axis)


def attend_pair(query, key, value, causal):
    lane = lax.broadcasted_iota(jnp.int32, (1, 128), 1)
    mixed, logs = [], []
    for head in range(2):
        scores = dot_t(jnp.where(lane // 64 == head, query, jnp.zeros_like(query)), key)
        if causal:
            scores = jnp.where(seen(scores.shape, 1), scores, -1e30)
        top = jnp.max(scores, axis=1, keepdims=True) * log2_e
        exponent = jnp.exp2(scores * log2_e - top)
        total = jnp.sum(exponent, axis=1, keepdims=True)
        mixed.append(dot(exponent.astype(low), value) * (1.0 / total))
        logs.append(top + jnp.log2(total))
    both = jnp.where(lane == 0, logs[0], logs[1])
    return jnp.where(lane < 64, mixed[0], mixed[1]).astype(low), both.T[0:8, :]


def attend_pair_back(query, key, value, logs, grad, causal):
    lane = lax.broadcasted_iota(jnp.int32, (1, 128), 1)
    sub = lax.broadcasted_iota(jnp.int32, (128, 1), 0)
    turned = key.astype(f32).T.astype(low)
    found = []
    for head in range(2):
        part = jnp.where(lane // 64 == head, query, jnp.zeros_like(query))
        grad_part = jnp.where(lane // 64 == head, grad, jnp.zeros_like(grad))
        chance = jnp.exp2(dot_t(key, part) * log2_e - logs[head : head + 1, :])
        if causal:
            chance = jnp.where(seen(chance.shape, 0), chance, 0.0)
        product = chance * dot_t(value, grad_part)
        grad_scores = (product - chance * jnp.sum(product, axis=0, keepdims=True)).astype(low)
        found.append(
            (
                dot(jnp.where(sub // 64 == head, turned, jnp.zeros_like(turned)), grad_scores),
                dot(grad_scores, part),
                dot(chance.astype(low), grad_part),
            )
        )
    turned, key_grad, value_grad = (one + two for one, two in zip(*found))
    return turned.T * 0.125, key_grad, value_grad


def audio_feed(inputs, mixed, weight_out, smalls, ups, weight_up, weight_down, cross_a, cross_b, block):
    rows, width = inputs.shape
    hidden = ups.shape[1]

    def body(step, given, outs, extra):
        inputs, mixed, weight_out, smalls, ups, weight_up, weight_down, cross_a, cross_b = given
        middle_out, norm_out, hidden_out, slope_out, ending_out, memory_out, key_out, value_out = outs
        middle = inputs[...] + dot(mixed[...], weight_out[...]) + row(smalls, 8)
        middle_out[...] = middle
        normed, inverse = norm_rows(middle)
        rounded = (normed * row(smalls, 1) + row(smalls, 4)).astype(low)
        norm_out[...] = rounded
        ending = middle + row(smalls, 9)
        for part in range(hidden // 512):
            cols = slice(part * 512, part * 512 + 512)
            pre = dot(rounded, weight_up[:, cols]) + ups[:, cols].astype(f32)
            value, slope = gelu_both(pre)
            act = value.astype(low)
            hidden_out[:, cols] = act
            slope_out[:, cols] = slope.astype(low)
            ending += dot(act, weight_down[cols, :])
        ending_out[...] = ending
        normed, inverse = norm_rows(ending)
        memory = (normed * row(smalls, 2) + row(smalls, 5)).astype(low)
        memory_out[...] = memory
        key_out[...] = dot(memory, cross_a[...]).astype(low)
        value_out[...] = (dot(memory, cross_b[...]) + row(smalls, 11)).astype(low)

    wide, shape = (rows, hidden), (rows, width)
    return call(
        body, "audio_feed", rows // block, block,
        [(inputs, "rows"), (mixed, "rows"), (weight_out, "side"), (smalls, "full"), (ups, "full"),
         (weight_up, "side"), (weight_down, "side"), (cross_a, "side"), (cross_b, "side")],
        [(shape, f32, "rows"), (shape, low, "rows"), (wide, low, "rows"), (wide, low, "rows"),
         (shape, f32, "rows"), (shape, low, "rows"), (shape, low, "rows"), (shape, low, "rows")],
        flops=2 * rows * width * (3 * width + 2 * hidden),
    )


def text_start(inputs, weight, weight_out, smalls, cross_a):
    rows, width = inputs.shape[1:]

    def body(step, given, outs, extra):
        inputs, weight, weight_out, smalls, cross_a = given
        norm_out, joint, mixed, logs, middle_out, low_out, query_out = outs
        normed, inverse = norm_rows(inputs[...].astype(f32))
        rounded = (normed * row(smalls, 0) + row(smalls, 3)).astype(low)
        norm_out[...] = rounded
        joint[:, :width] = (dot(rounded, weight[:, :width]) + row(smalls, 6)).astype(low) * 0.125
        joint[:, width : 2 * width] = dot(rounded, weight[:, width : 2 * width]).astype(low)
        joint[:, 2 * width :] = (dot(rounded, weight[:, 2 * width :]) + row(smalls, 7)).astype(low)

        @pl.loop(0, HEADS // 2)
        def _(pair):
            cols = pair_cols(0, pair)
            mixed[:, cols], logs[pl.ds(pl.multiple_of(pair * 8, 8), 8), :] = attend_pair(
                joint[:, cols], joint[:, pair_cols(width, pair)], joint[:, pair_cols(2 * width, pair)], True
            )

        middle = inputs[...].astype(f32) + dot(mixed[...], weight_out[...]) + row(smalls, 8)
        middle_out[...] = middle
        normed, inverse = norm_rows(middle)
        rounded = (normed * row(smalls, 1) + row(smalls, 4)).astype(low)
        low_out[...] = rounded
        query_out[...] = (dot(rounded, cross_a[...]) + row(smalls, 10)).astype(low) * 0.125

    shape = (rows, width)
    return call(
        body, "text_start", 1, rows,
        [(inputs, "clip"), (weight, "side"), (weight_out, "side"), (smalls, "full"), (cross_a, "side")],
        [(shape, low, "rows"), ((rows, 3 * width), low, "rows"), (shape, low, "rows"), ((4 * HEADS, rows), f32, "whole"),
         (shape, f32, "rows"), (shape, low, "rows"), (shape, low, "rows")],
        flops=10 * rows * width * width,
    )


def text_cross(length, queries, keys, values, middle, cotangent, cross_b, smalls, ups, weight_up, weight_down):
    rows, width = middle.shape
    hidden = ups.shape[1]
    block, key_rows = rows, keys.shape[0]

    def body(step, given, outs, extra):
        length, queries, keys, values, middle, cotangent, cross_b, smalls, ups, weight_up, weight_down = given
        decoded_keep, decoded_send, norm_out, hidden_out, pre_out, cot_out, grad_out, grad_low, mixed, query_out, key_out, value_out, sums, wide_sums, cross_sums = outs
        logs, mixed_grad = extra

        @pl.loop(0, HEADS // 2)
        def _(pair):
            cols = pair_cols(0, pair)
            mixed[:, cols], logs[pl.ds(pl.multiple_of(pair * 8, 8), 8), :] = attend_pair(
                queries[:, cols], keys[:, cols], values[:, cols], False
            )

        after = middle[...] + dot(mixed[...], cross_b[...]) + row(smalls, 11)
        normed, inverse = norm_rows(after)
        rounded = (normed * row(smalls, 2) + row(smalls, 5)).astype(low)
        norm_out[...] = rounded
        at_row = lax.broadcasted_iota(jnp.int32, (block, 1), 0) + step * block
        valid = at_row < length[lax.axis_index("section")]
        grad = jnp.where(valid, cotangent[...].astype(f32), 0.0)
        cot = grad.astype(low)
        cot_out[...] = cot
        ending = after + row(smalls, 9)
        back = jnp.zeros((block, width), f32)
        for part in range(hidden // 512):
            cols = slice(part * 512, part * 512 + 512)
            pre = dot(rounded, weight_up[:, cols]) + ups[:, cols].astype(f32)
            value, slope = gelu_both(pre)
            act = value.astype(low)
            hidden_out[:, cols] = act
            ending += dot(act, weight_down[cols, :])
            grad_pre = dot_t(cot, weight_down[cols, :]) * slope
            wide_sums[0:1, cols] += col_sum(grad_pre)
            pre_low = grad_pre.astype(low)
            pre_out[:, cols] = pre_low
            back += dot_t(pre_low, weight_up[:, cols])
        write_halves(jnp.where(valid, ending, 0.0), decoded_keep, decoded_send)
        sums[0:1, :] += col_sum(back * normed)
        sums[1:2, :] += col_sum(back)
        sums[2:3, :] += col_sum(grad)
        grad = grad + norm_back(back, row(smalls, 2), normed, inverse)
        sums[3:4, :] += col_sum(grad)
        grad_out[...] = grad
        rounded = grad.astype(low)
        grad_low[...] = rounded
        mixed_grad[...] = dot_t(rounded, cross_b[...]).astype(low)

        @pl.loop(0, HEADS // 2)
        def _(pair):
            cols = pair_cols(0, pair)
            query_grad, key_grad, value_grad = attend_pair_back(
                queries[:, cols], keys[:, cols], values[:, cols], logs[pl.ds(pl.multiple_of(pair * 8, 8), 8), :],
                mixed_grad[:, cols], False,
            )
            query_out[:, cols] = query_grad.astype(low)
            key_out[:, cols] = key_grad.astype(low)
            value_grad = value_grad.astype(low)
            value_out[:, cols] = value_grad
            cross_sums[0:1, cols] = col_sum(query_grad)
            cross_sums[1:2, cols] = col_sum(value_grad.astype(f32))

    wide, shape = (rows, hidden), (rows, width)
    return call(
        body, "text_cross", 1, rows,
        [(length, "smem"), (queries, "rows"), (keys, "full"), (values, "full"), (middle, "rows"), (cotangent, "clip"), (cross_b, "side"),
         (smalls, "full"), (ups, "full"), (weight_up, "side"), (weight_down, "side")],
        [((rows, width // 2), f32, "rows"), ((rows, width // 2), low, "rows"), (shape, low, "rows"), (wide, low, "rows"),
         (wide, low, "rows"), (shape, low, "rows"), (shape, f32, "rows"), (shape, low, "rows"), (shape, low, "rows"), (shape, low, "rows"),
         ((key_rows, width), low, "whole"), ((key_rows, width), low, "whole"),
         ((8, width), f32, "sums"), ((8, hidden), f32, "sums"), ((8, width), f32, "sums")],
        scratch=[pltpu.VMEM((4 * HEADS, rows), f32), pltpu.VMEM(shape, low)],
        flops=2 * rows * width * (2 * width + 4 * hidden),
    )


def text_back(query_grad, middle, grad, joint, logs, inputs, smalls, cross_a, weight_out, weight):
    rows, width = middle.shape

    def body(step, given, outs, extra):
        query_grad, middle, grad, joint, logs, inputs, smalls, cross_a, weight_out, weight = given
        keep, send, low_out, query_out, key_out, value_out, cross_sums, attn_sums, first_sums = outs
        total, mixed_grad = extra
        back = dot_t(query_grad[...], cross_a[...])
        normed, inverse = norm_rows(middle[...])
        cross_sums[0:1, :] = col_sum(back * normed)
        cross_sums[1:2, :] = col_sum(back)
        total[...] = grad[...] + norm_back(back, row(smalls, 1), normed, inverse)
        cross_sums[2:3, :] = col_sum(total[...])
        rounded = total[...].astype(low)
        low_out[...] = rounded
        mixed_grad[...] = dot_t(rounded, weight_out[...]).astype(low)

        @pl.loop(0, HEADS // 2)
        def _(pair):
            cols = pair_cols(0, pair)
            query, key, value = attend_pair_back(
                joint[:, cols], joint[:, pair_cols(width, pair)], joint[:, pair_cols(2 * width, pair)],
                logs[pl.ds(pl.multiple_of(pair * 8, 8), 8), :], mixed_grad[:, cols], True,
            )
            query_out[:, cols] = query.astype(low)
            key_out[:, cols] = key.astype(low)
            value_out[:, cols] = value.astype(low)
            attn_sums[0:1, cols] = col_sum(query)
            attn_sums[1:2, cols] = col_sum(value)

        back = (
            dot_t(query_out[...], weight[:, :width])
            + dot_t(key_out[...], weight[:, width : 2 * width])
            + dot_t(value_out[...], weight[:, 2 * width :])
        )
        normed, inverse = norm_rows(inputs[...].astype(f32))
        first_sums[0:1, :] = col_sum(back * normed)
        first_sums[1:2, :] = col_sum(back)
        write_halves(total[...] + norm_back(back, row(smalls, 0), normed, inverse), keep, send)

    shape = (rows, width)
    return call(
        body, "text_back", 1, rows,
        [(query_grad, "rows"), (middle, "rows"), (grad, "rows"), (joint, "rows"), (logs, "full"), (inputs, "clip"),
         (smalls, "full"), (cross_a, "side"), (weight_out, "side"), (weight, "side")],
        [((rows, width // 2), f32, "rows"), ((rows, width // 2), low, "rows")] + [(shape, low, "rows")] * 4
        + [((8, width), f32, "sums")] * 3,
        scratch=[pltpu.VMEM(shape, f32), pltpu.VMEM(shape, low)],
        flops=14 * rows * width * width,
    )


def audio_feed_back(key_grad, value_grad, ending, middle, slope, smalls, cross_a, cross_b, weight_up, weight_down, weight_out, block):
    rows, width = ending.shape
    hidden = slope.shape[1]

    def body(step, given, outs, extra):
        key_grad, value_grad, ending, middle, slope, smalls, cross_a, cross_b, weight_up, weight_down, weight_out = given
        end_low, pre_out, grad_out, grad_low, mixed_out, sums, wide_sums = outs
        back = dot_t(key_grad[...], cross_a[...]) + dot_t(value_grad[...], cross_b[...])
        normed, inverse = norm_rows(ending[...])
        sums[0:1, :] += col_sum(back * normed)
        sums[1:2, :] += col_sum(back)
        grad = norm_back(back, row(smalls, 2), normed, inverse)
        sums[2:3, :] += col_sum(grad)
        rounded = grad.astype(low)
        end_low[...] = rounded
        back = jnp.zeros((block, width), f32)
        for part in range(hidden // 512):
            cols = slice(part * 512, part * 512 + 512)
            grad_pre = dot_t(rounded, weight_down[cols, :]) * slope[:, cols].astype(f32)
            wide_sums[0:1, cols] += col_sum(grad_pre)
            pre_low = grad_pre.astype(low)
            pre_out[:, cols] = pre_low
            back += dot_t(pre_low, weight_up[:, cols])
        normed, inverse = norm_rows(middle[...])
        sums[3:4, :] += col_sum(back * normed)
        sums[4:5, :] += col_sum(back)
        grad = grad + norm_back(back, row(smalls, 1), normed, inverse)
        sums[5:6, :] += col_sum(grad)
        grad_out[...] = grad
        rounded = grad.astype(low)
        grad_low[...] = rounded
        mixed_out[...] = dot_t(rounded, weight_out[...]).astype(low)

    wide, shape = (rows, hidden), (rows, width)
    return call(
        body, "audio_feed_back", rows // block, block,
        [(key_grad, "rows"), (value_grad, "rows"), (ending, "rows"), (middle, "rows"), (slope, "rows"), (smalls, "full"),
         (cross_a, "side"), (cross_b, "side"), (weight_up, "side"), (weight_down, "side"), (weight_out, "side")],
        [(shape, low, "rows"), (wide, low, "rows"), (shape, f32, "rows"), (shape, low, "rows"), (shape, low, "rows"),
         ((8, width), f32, "sums"), ((8, hidden), f32, "sums")],
        flops=2 * rows * width * (3 * width + 2 * hidden),
    )


def unpack(total, bands):
    width, half = total.shape[1], total.shape[1] // 2
    tiles = 14

    def kernel(total, joint, out, up, down, cross_a, cross_b, first, bias, second, gain, shift, wide, small, cross, held, found, in_sem, out_sem):
        def load(n):
            here = pl.ds(pl.multiple_of(n * width, width), width)
            return pltpu.make_async_copy(total.at[here], held.at[n], in_sem.at[n])

        def target(n):
            cols = lambda k: slice(k * width, k * width + width)
            if n < 4:
                return up.at[0, :, cols(n)]
            if n < 8:
                return down.at[0, cols(n - 4)]
            if n < 11:
                return (cross_a, cross_b, out)[n - 8].at[0]
            return joint.at[0, :, cols(n - 11)]

        def store(n):
            return pltpu.make_async_copy(found.at[n], target(n), out_sem.at[n])

        @pl.loop(0, tiles + 2)
        def _(n):
            load(n).start()

        @pl.loop(0, tiles)
        def _(n):
            load(n).wait()
            found[n] = held[n].astype(f32)
            for k in range(tiles):

                @pl.when(n == k)
                def _(k=k):
                    store(k).start()

        load(tiles).wait()
        load(tiles + 1).wait()
        tile = held.at[tiles]
        second[0] = tile[:, 0:half].astype(f32)
        second[1, half:width] = tile[0:half, half:width].astype(f32)
        second[2, 0:half] = tile[half:width, half:width].astype(f32)
        tile = held.at[tiles + 1]
        second[1, 0:half] = tile[0:half, 0:half].astype(f32)
        second[2, half:width] = tile[0:half, half:width].astype(f32)
        first[0] = tile[half : half + bands, 0:half].astype(f32)
        first[1, 0:64] = tile[half + 128 : half + 192, 0:half].astype(f32)
        first[1, 64:bands] = tile[half : half + bands - 64, half:width].astype(f32)
        first[2] = tile[half + 64 : half + 64 + bands, half:width].astype(f32)
        rows = tile[half + 192 : half + 224, :].astype(f32)
        for n in range(3):
            gain[n] = rows[n : n + 1]
            shift[n] = rows[3 + n : 4 + n]
        for n in range(6):
            small[n] = rows[6 + n : 7 + n]
        for n in range(4):
            wide[:, n * width : (n + 1) * width] = rows[12 + n : 13 + n]
        bias[...] = rows[16:17, 0:half]
        mine = lax.axis_index("section")
        cross[...] = jnp.where(mine == 0, rows[17:18, 0:half], rows[17:18, half:width])
        for n in range(tiles):
            store(n).wait()

    shapes = [
        (1, width, 3 * width), (1, width, width), (1, width, 4 * width), (1, 4 * width, width), (1, width, width), (1, width, width),
        (3, bands, half), (1, half), (3, width, half), (3, 1, width), (3, 1, width), (1, 4 * width), (6, 1, width), (1, half),
    ]
    return pl.pallas_call(
        kernel,
        name="unpack",
        in_specs=[pl.BlockSpec(memory_space=pl.ANY)],
        out_specs=[pl.BlockSpec(memory_space=pl.ANY)] * 6 + [pl.BlockSpec(memory_space=pltpu.VMEM)] * 8,
        out_shape=[jax.ShapeDtypeStruct(shape, f32) for shape in shapes],
        scratch_shapes=[
            pltpu.VMEM((tiles + 2, width, width), low), pltpu.VMEM((tiles, width, width), f32),
            pltpu.SemaphoreType.DMA((tiles + 2,)), pltpu.SemaphoreType.DMA((tiles,)),
        ],
        compiler_params=pltpu.CompilerParams(vmem_limit_bytes=VMEM_BYTES),
        cost_estimate=pl.CostEstimate(flops=0, bytes_accessed=6 * total.size, transcendentals=0),
    )(total)


def finish(parts, mel_keep, mel_got, spans, bands):
    count = len(parts)
    pair_rows = mel_keep.shape[0]
    frames = 2 * pair_rows

    def kernel(*refs):
        pairs, (keep_ref, got_ref), marks = refs[: 2 * count], refs[2 * count : 2 * count + 2], refs[2 * count + 2 : 2 * count + 6]
        outs, mel_out, laid = refs[2 * count + 6 : 3 * count + 6], refs[3 * count + 6], refs[3 * count + 7]
        mine = lax.axis_index("section")
        for n, out in enumerate(outs):
            out[mine] = pairs[2 * n][...]
            out[1 - mine] = pairs[2 * n + 1][...].astype(f32)
        band_at = lax.broadcasted_iota(jnp.int32, (bands, frames), 0)
        frame_at = lax.broadcasted_iota(jnp.int32, (bands, frames), 1) + mine * frames
        for clip, ref in ((mine, keep_ref), (1 - mine, got_ref)):
            for n in range(2):
                laid[pl.ds(n, pair_rows, stride=2), :] = ref[:, n * 128 : n * 128 + 128].astype(f32)
            start, span, band, width = (mark[clip] for mark in marks)
            keep = jnp.logical_and(
                jnp.logical_or(band_at < band, band_at >= band + width),
                jnp.logical_or(frame_at < start, frame_at >= start + span),
            )
            mel_out[clip] = jnp.where(keep, laid[...].T[0:bands, :], 0.0)

    def full(shape):
        return pl.BlockSpec(shape, lambda i, n=len(shape): (0,) * n)

    flat = [array for pair in parts for array in pair]
    shapes = [(2,) + keep.shape for keep, got in parts] + [(2, bands, frames)]
    return pl.pallas_call(
        kernel,
        name="finish",
        grid=(1,),
        in_specs=[full(array.shape) for array in flat + [mel_keep, mel_got]] + [pl.BlockSpec(memory_space=pltpu.SMEM)] * 4,
        out_specs=[full(shape) for shape in shapes],
        out_shape=[jax.ShapeDtypeStruct(shape, f32) for shape in shapes],
        scratch_shapes=[pltpu.VMEM((frames, 128), f32)],
        compiler_params=pltpu.CompilerParams(vmem_limit_bytes=VMEM_BYTES),
        cost_estimate=pl.CostEstimate(flops=0, bytes_accessed=sum(8 * a.size for a in flat), transcendentals=0),
    )(*flat, mel_keep, mel_got, *spans)


def begin(mel_input, spans, gain, shift, biases, up_bias, first_bias, first, second, joint_weight, weights, positions):
    frames, width = positions.shape
    bands, mel_frames = mel_input.shape[1:]
    lanes = width // 2
    hidden = up_bias.shape[1]
    block = 256
    blocks = frames // block
    sent = [second, joint_weight] + weights
    n_sent = len(sent)
    pieces = []
    for n, array in enumerate(sent):
        cuts = 2 if array.size >= 700000 else 1
        size = array.shape[0] // cuts
        pieces += [(n, c * size, size) for c in range(cuts)]
    n_pieces = len(pieces)
    flying = 2
    first_held = Split(first, first, 3, 128)
    second_held = Split(second, second, 3, width)
    n_any = n_sent + 3

    def kernel(*refs):
        mel_ref, positions_ref, first_ref = refs[:3]
        own = refs[3:n_any]
        times, time_spans, bands_from, band_spans = refs[n_any : n_any + 4]
        gain, shift, biases, up_bias, first_bias = refs[n_any + 4 : n_any + 9]
        outs = refs[n_any + 9 :]
        first_other = outs[0]
        other = outs[1 : 1 + n_sent]
        a_small, t_small, a_ups, t_ups = outs[1 + n_sent : 5 + n_sent]
        results = outs[5 + n_sent : 16 + n_sent]
        (
            taps, encoded, even_act, odd_act, even_slope, odd_slope, slope_second, norm, joint, mixed, logs,
            mel, turned, place, conv_first, conv_second, weight, carry, pack, pack_other,
            load_sem, weight_sem, out_sem, side_sem, near_sem, core_sem, sent_sem,
        ) = outs[16 + n_sent :]
        held = (taps, encoded, even_act, odd_act, even_slope, odd_slope, slope_second, norm, joint, mixed, logs)

        section, replica = lax.axis_index("section"), lax.axis_index("dp")
        side_peer = {"section": 1 - section}

        def flipped(value, bit):
            return value + bit - 2 * bit * ((value // bit) % 2)

        def peer(bit):
            return {"dp": flipped(replica, bit)}

        def remote(source, target, sent, sems, at, device):
            return pltpu.make_async_remote_copy(
                src_ref=source, dst_ref=target, send_sem=sent_sem.at[sent], recv_sem=sems.at[at],
                device_id=device, device_id_type=pl.DeviceIdType.MESH,
            )

        def part(p, q):
            n, start, size = pieces[p]
            return pl.ds(pl.multiple_of(start + q * (size // 4), 16), size // 4)

        def near(p):
            bit = 4 if p % 2 else 2
            quarter = replica % 2 + 2 * ((replica // bit) % 2)
            return bit, (quarter, flipped(quarter, 2))

        def side_copy(p):
            n = pieces[p][0]
            here = part(p, near(p)[1][0])
            return remote(own[n].at[here], other[n].at[here], n, side_sem, (p,), side_peer)

        def pass_on(p, q, sems, at, bit):
            n = pieces[p][0]
            here = other[n].at[part(p, q)]
            return remote(here, here, n, sems, at, peer(bit))

        def near_copies(p):
            bit, quarters = near(p)
            return [pass_on(p, quarters[0], near_sem, (p,), bit)]

        def core_copies(p):
            return [pass_on(p, q, core_sem, (b, p), 1) for b, q in enumerate(near(p)[1])]

        hops = (lambda p: [side_copy(p)], near_copies, core_copies)

        def advance(p, n):
            for copy in hops[n](p):
                copy.wait_recv()
            if n == 0 and p + flying < n_pieces:
                side_copy(p + flying).start()
            if n + 1 < len(hops):
                for copy in hops[n + 1](p):
                    copy.start()

        def tick(at):
            if at < 4:
                turn = [[(1, 0)], [(2, 0), (1, 1)], [(3, 0), (2, 1), (1, 2)], [(4, 0), (2, 2)]][at]
            else:
                turn = [(at + 1, 0), (at - 1, 1), (at - 2, 2)]
            for p, n in turn:
                if (3 if n else 1) <= p < n_pieces or at < 4:
                    advance(p, n)

        pack_copy = remote(pack, pack_other, n_sent, side_sem, (n_pieces,), side_peer)
        first_copy = remote(first_ref, first_other, n_sent + 1, side_sem, (n_pieces + 1,), side_peer)
        loads = [
            pltpu.make_async_copy(mel_ref.at[section], mel, load_sem.at[0]),
            pltpu.make_async_copy(positions_ref, place, load_sem.at[1]),
        ]

        def conv_copies(mine):
            return first_held.copies(mine, first_ref, first_other, conv_first, weight_sem.at[0]) + second_held.copies(
                mine, own[0], other[0], conv_second, weight_sem.at[1]
            )

        def weight_copy(mine):
            return pltpu.make_async_copy(own[1] if mine == 0 else other[1], weight, weight_sem.at[2])

        def keep(n):
            return pltpu.make_async_copy(held[n], results[n], out_sem.at[n])

        barrier = pltpu.get_barrier_semaphore()
        peers = [side_peer] + [peer(bit) for bit in (1, 2, 4)]
        for device in peers:
            pl.semaphore_signal(barrier, inc=1, device_id=device, device_id_type=pl.DeviceIdType.MESH)
        for copy in loads:
            copy.start()
        pack[0:3, :] = gain[...].astype(f32)
        pack[3:6, :] = shift[...].astype(f32)
        pack[6:12, :] = biases[...].astype(f32)
        for n in range(hidden // width):
            pack[12 + n : 13 + n, :] = up_bias[:, n * width : n * width + width].astype(f32)
        pack[16:17, 0:lanes] = first_bias[...].astype(f32).reshape(1, lanes)
        pack[16:17, lanes:width] = jnp.zeros((1, lanes), f32)
        pack[17:24, :] = jnp.zeros((7, width), f32)
        pl.semaphore_wait(barrier, len(peers))
        side_copy(0).start()
        first_copy.start()
        pack_copy.start()
        for p in range(1, flying):
            side_copy(p).start()

        turned[0:8, :] = jnp.zeros((8, 128), f32)
        turned[8 + mel_frames : 16 + mel_frames, :] = jnp.zeros((8, 128), f32)
        carry[...] = jnp.zeros(carry.shape, f32)
        clear_pads(conv_first, bands)
        for copy in loads:
            copy.wait()
        band_at = lax.broadcasted_iota(jnp.int32, (bands, block), 0)
        frame_at = lax.broadcasted_iota(jnp.int32, (bands, block), 1)
        time_from, band_from = times[section], bands_from[section]
        time_to, band_to = time_from + time_spans[section], band_from + band_spans[section]
        band_keep = jnp.logical_or(band_at < band_from, band_at >= band_to)
        for n in range(mel_frames // block):
            at = frame_at + n * block
            keep_here = jnp.logical_and(band_keep, jnp.logical_or(at < time_from, at >= time_to))
            values = jnp.where(keep_here, mel[:, n * block : n * block + block].astype(f32), 0.0)
            values = jnp.concatenate([values, jnp.zeros((128 - bands, block), f32)], axis=0)
            turned[8 + n * block : 8 + n * block + block, :] = values.T
        for n, start in enumerate((7, 8, 9, 10)):
            taps[:, n * 128 : n * 128 + 128] = turned[pl.ds(start, frames, stride=2), :].astype(low)
        keep(0).start()

        for n in range(len(hops)):
            advance(0, n)
        first_copy.wait_recv()
        pack_copy.wait_recv()
        for which in range(2):

            @pl.when(section == which)
            def _(which=which):
                for copy in conv_copies(which):
                    copy.start()

        first_section = section == 0
        a_small[...] = jnp.where(first_section, pack[...], pack_other[...])
        t_small[...] = jnp.where(first_section, pack_other[...], pack[...])
        for n in range(hidden // width):
            a_ups[:, n * width : n * width + width] = a_small[12 + n : 13 + n, :]
            t_ups[:, n * width : n * width + width] = t_small[12 + n : 13 + n, :]
        bias = jnp.concatenate([a_small[16:17, 0:lanes], t_small[16:17, 0:lanes]], axis=1)
        for copy in conv_copies(0):
            copy.wait()

        def stem_block(i):
            here = pl.ds(pl.multiple_of(i * block, block), block)
            value, slope = gelu_both(dot(taps[here, 0:384], conv_first[...]) + bias)
            even = value.astype(low)
            even_act[here] = even
            even_slope[here] = slope.astype(low)
            value, slope = gelu_both(dot(taps[here, 128:512], conv_first[...]) + bias)
            odd = value.astype(low)
            odd_act[here] = odd
            odd_slope[here] = slope.astype(low)
            prior = dot(odd, conv_second[0:width])
            at_row = lax.broadcasted_iota(jnp.int32, (block, width), 0)
            moved = jnp.where(at_row == 0, carry[0:1, :], pltpu.roll(prior, 1, 0))
            carry[0:1, :] = prior[block - 1 : block, :]
            pre = moved + dot(even, conv_second[width : 2 * width]) + dot(odd, conv_second[2 * width :]) + row(a_small, 10)
            value, slope = gelu_both(pre)
            slope_second[here] = slope.astype(low)
            encoded[here] = value + place[here].astype(f32)

        for i in range(blocks):
            stem_block(i)
            tick(i)
        for n in range(1, 7):
            keep(n).start()
        for which in range(2):

            @pl.when(section == which)
            def _(which=which):
                weight_copy(which).start()

        weight_copy(0).wait()

        def project_block(i):
            here = pl.ds(pl.multiple_of(i * block, block), block)
            normed, inverse = norm_rows(encoded[here])
            rounded = (normed * row(a_small, 0) + row(a_small, 3)).astype(low)
            norm[here] = rounded
            joint[here, 0:width] = (dot(rounded, weight[:, 0:width]) + row(a_small, 6)).astype(low) * 0.125
            joint[here, width : 2 * width] = dot(rounded, weight[:, width : 2 * width]).astype(low)
            joint[here, 2 * width :] = (dot(rounded, weight[:, 2 * width :]) + row(a_small, 7)).astype(low)

        for i in range(blocks):
            project_block(i)
        tick(blocks)
        keep(7).start()
        keep(8).start()

        def attention(pair):
            lane = lax.broadcasted_iota(jnp.int32, (1, 128), 1)

            def cols(start):
                return pl.ds(pl.multiple_of(start + pair * 128, 128), 128)

            key, value = joint[:, cols(width)], joint[:, cols(2 * width)]

            @pl.loop(0, blocks)
            def _(i):
                here = pl.ds(pl.multiple_of(i * block, block), block)
                query = joint[here, cols(0)]
                found, log = [], []
                for head in range(2):
                    scores = dot_t(jnp.where(lane // 64 == head, query, jnp.zeros_like(query)), key)
                    top = jnp.max(scores, axis=1, keepdims=True) * log2_e
                    exponent = jnp.exp2(scores * log2_e - top)
                    total = jnp.sum(exponent, axis=1, keepdims=True)
                    found.append(dot(exponent.astype(low), value) * (1.0 / total))
                    log.append(top + jnp.log2(total))
                mixed[here, cols(0)] = jnp.where(lane < 64, found[0], found[1]).astype(low)
                both = jnp.where(lane == 0, log[0], log[1])
                logs[pl.ds(pl.multiple_of(pair * 8, 8), 8), here] = both.T[0:8, :]

        done = blocks + 1
        for pair in range(HEADS // 2):
            attention(pair)
            tick(done)
            done += 1
        while done < n_pieces + len(hops) - 1:
            tick(done)
            done += 1
        keep(9).start()
        keep(10).start()
        for n in range(n_sent):
            remote(own[n], other[n], n, side_sem, (0,), side_peer).wait_send()
        first_copy.wait_send()
        pack_copy.wait_send()
        for n in range(len(held)):
            keep(n).wait()

    def sems(*shape):
        return pltpu.SemaphoreType.DMA(shape)

    shape = (frames, width)
    kept = [(shape, low), (shape, f32)] + [(shape, low)] * 6 + [((frames, 3 * width), low), (shape, low), ((4 * HEADS, frames), f32)]
    everywhere, on_chip = pl.BlockSpec(memory_space=pl.ANY), pl.BlockSpec(memory_space=pltpu.VMEM)
    return pl.pallas_call(
        kernel,
        name="begin",
        in_specs=[everywhere] * n_any + [pl.BlockSpec(memory_space=pltpu.SMEM)] * 4 + [on_chip] * 5,
        out_specs=[everywhere] * (1 + n_sent) + [on_chip] * 4 + [everywhere] * len(kept),
        out_shape=[jax.ShapeDtypeStruct(a.shape, a.dtype) for a in [first] + sent]
        + [jax.ShapeDtypeStruct(s, f32) for s in ((24, width), (24, width), (1, hidden), (1, hidden))]
        + [jax.ShapeDtypeStruct(s, d) for s, d in kept],
        scratch_shapes=[pltpu.VMEM(s, d) for s, d in kept]
        + [
            pltpu.VMEM((bands, mel_frames), low), pltpu.VMEM((mel_frames + 16, 128), f32), pltpu.VMEM(shape, low),
            pltpu.VMEM((384, width), low), pltpu.VMEM((3 * width, width), low), pltpu.VMEM((width, 3 * width), low),
            pltpu.VMEM((8, width), f32), pltpu.VMEM((24, width), f32), pltpu.VMEM((24, width), f32),
            sems(2), sems(3), sems(len(kept)), sems(n_pieces + 2), sems(n_pieces), sems(2, n_pieces),
            sems(n_sent + 2),
        ],
        compiler_params=pltpu.CompilerParams(collective_id=1, has_side_effects=True, vmem_limit_bytes=VMEM_BYTES),
        cost_estimate=pl.CostEstimate(flops=10**10, bytes_accessed=10**8, transcendentals=0),
    )(mel_input, positions, first, *sent, *spans, gain, shift, biases, up_bias, first_bias)


def factors_of(size):
    found, rest = [], size // 2
    while rest > 1:
        radix = 2 if size <= 16 or rest % 4 else 4
        found.append(radix)
        rest //= radix
    return found


def finish_backward(audio, text, joint, logs, mixed_grad, grad, encoded, slopes, smalls, weight, second, first, acts, audio_sums, text_sums, bands):
    width, tile_rows = 512, 512
    half = tile_rows // 2
    lanes = width // 2
    frames, text_rows = joint.shape[0], text[0][0].shape[0]
    tiles = len(audio)
    count = tiles + 2
    early = 11
    flying = 3
    lag = 1
    rows = count * tile_rows
    block = 256
    blocks = frames // block
    replicas = lax.axis_size("dp")
    factors = factors_of(replicas)
    levels = len(factors)
    befores, sizes, scatters = [], [], []
    for radix in factors:
        before = sizes[-1] if sizes else half
        befores.append(before)
        scatters.append(before % (16 * radix) == 0)
        sizes.append(before // radix if scatters[-1] else before)

    arrays, places = [], {}

    def place(array):
        if id(array) not in places:
            places[id(array)] = len(arrays)
            arrays.append(array)
        return places[id(array)]

    def job(x, xc, y, yc):
        return (place(x), xc, y if isinstance(y, int) else (place(y),), yc)

    audio_jobs = [job(*one) for one in audio]
    text_jobs = [job(*one) for one in text]
    at_joint, at_logs, at_mixed, at_grad, at_encoded = [place(a) for a in (joint, logs, mixed_grad, grad, encoded)]
    at_slopes = [place(a) for a in slopes]
    odd_act, even_act, taps = acts
    at_odd, at_even, at_taps = place(odd_act), place(even_act), place(taps)
    at_weight = (place(weight.own), place(weight.other))
    at_second = (place(second.own), place(second.other))
    at_first = (place(first.own), place(first.other))
    n_any = len(arrays)
    n_chip = 1 + len(audio_sums) + len(text_sums)

    def kernel(*refs):
        given = refs[:n_any]
        smalls, *known = refs[n_any : n_any + n_chip]
        audio_sums, text_sums = known[:2], known[2:]
        out_ref, keep_ref, got_ref = refs[n_any + n_chip : n_any + n_chip + 3]
        refs = refs[n_any + n_chip + 3 :]
        (
            tile, core_recv, side_send, side_recv, work, final, x_audio, y_audio, x_text, y_text,
            joint, logs, mixed_grad, query_grad, key_grad, value_grad, key_acc, value_acc, key_turned, sums,
            encoded_in, grad_in, slope_in, weight, second, first, second_low, next_low, even_low, odd_low, taps_grad,
            carry, small_buf, mel_buf, mel_send,
            in_sem, load_sem, weight_sem, block_sem, keep_sem, core_sem, side_sem, back_sem, out_sem, mel_sem, sent_sem,
        ) = refs[:46]
        recvs = refs[46 : 46 + levels]
        rs_sems = refs[46 + levels : 46 + 2 * levels]
        ag_sems = refs[46 + 2 * levels :]
        own_grads = (query_grad, key_grad, value_grad)

        section, replica = lax.axis_index("section"), lax.axis_index("dp")
        core = replica % 2
        digits, strides, rest, stride = [], [], replica // 2, 2
        for radix in factors:
            digits.append(rest % radix)
            strides.append(stride)
            rest, stride = rest // radix, stride * radix
        core_peer = {"dp": replica + 1 - 2 * core}
        side_peer = {"section": 1 - section}

        def peer(level, distance):
            digit = (digits[level] + distance) % factors[level]
            return digit, {"dp": replica + (digit - digits[level]) * strides[level]}

        def remote(source, target, sent, sems, k, device):
            return pltpu.make_async_remote_copy(
                src_ref=source, dst_ref=target, send_sem=sent, recv_sem=sems.at[k],
                device_id=device, device_id_type=pl.DeviceIdType.MESH,
            )

        def rows_at(start, size):
            return pl.ds(pl.multiple_of(start, 16), size)

        def offset(level):
            found = 0
            for n in range(level):
                if scatters[n]:
                    found = found + digits[n] * sizes[n]
            return found

        def core_copy(k):
            return remote(
                tile.at[k % 2, :, rows_at((1 - core) * half, half)], core_recv.at[k % 4], core_sem.at[1, k], core_sem.at[0], k, core_peer
            )

        def side_copy(k):
            here = rows_at(k * half, half)
            return remote(side_send.at[here], side_recv.at[here], sent_sem.at[0], side_sem, k, side_peer)

        def scatter_copy(k, level, distance):
            digit, device = peer(level, distance)
            size = sizes[level]
            start = k * half + offset(level) + (digit * size if scatters[level] else 0)
            return remote(
                work.at[rows_at(start, size)], recvs[level].at[distance - 1, rows_at(k * size, size)],
                sent_sem.at[2 + 2 * level], rs_sems[level], k, device,
            )

        def scatter_wait(k, level):
            here = recvs[level].at[:, rows_at(k * sizes[level], sizes[level])]
            remote(here, here, sent_sem.at[0], rs_sems[level], k, side_peer).wait_recv()

        def gather_copy(k, level, distance):
            digit, device = peer(level, distance)
            here = final.at[rows_at(k * tile_rows + core * half + offset(level + 1), sizes[level])]
            return remote(here, here, sent_sem.at[3 + 2 * level], ag_sems[level], k, device)

        def gather_wait(k, level):
            here = recvs[level].at[:, rows_at(k * sizes[level], sizes[level])]
            remote(here, here, sent_sem.at[0], ag_sems[level], k, side_peer).wait_recv()

        def scatter_sent(level, start, size):
            here = recvs[level].at[:, rows_at(start, size)]
            remote(here, here, sent_sem.at[2 + 2 * level], rs_sems[level], 0, side_peer).wait_send()

        def all_sent():
            remote(side_send, side_recv, sent_sem.at[0], side_sem, 0, side_peer).wait_send()
            remote(side_send, side_recv, sent_sem.at[1], back_sem, 0, core_peer).wait_send()
            for level in range(levels):
                if scatters[level]:
                    scatter_sent(level, 0, count * sizes[level])
                    here = recvs[level]
                    remote(here, here, sent_sem.at[3 + 2 * level], ag_sems[level], 0, side_peer).wait_send()
            pltpu.make_async_copy(final, out_ref, out_sem).wait()

        def back_copy(k):
            here = final.at[rows_at(k * tile_rows + core * half, half)]
            return remote(here, here, sent_sem.at[1], back_sem, k, core_peer)

        def store(k):
            here = rows_at(k * tile_rows, tile_rows)
            return pltpu.make_async_copy(final.at[here], out_ref.at[here], out_sem)

        def mel_copy():
            return remote(mel_send, got_ref, mel_sem.at[1], mel_sem, 0, side_peer)

        def stage_core(k):
            core_copy(k).wait_recv()
            here, mine = rows_at(k * half, half), rows_at(core * half, half)
            slot, from_peer = k % 2, k % 4
            side_send[here] = tile[slot, 1 - section, mine] + core_recv[from_peer, 1 - section]

            @when(jnp.logical_or(k < flying, k == tiles))
            def _():
                side_copy(k).start()

            work[here] = tile[slot, section, mine] + core_recv[from_peer, section]

        scatter_levels = [n for n in range(levels) if scatters[n]]

        def next_exchange(k, level):
            if level + 1 < levels:
                for distance in range(1, factors[level + 1]):
                    scatter_copy(k, level + 1, distance).start()
            elif scatter_levels:
                for distance in range(1, factors[scatter_levels[-1]]):
                    gather_copy(k, scatter_levels[-1], distance).start()
            else:
                back_copy(k).start()

        def put(k, level, total):
            if level + 1 < levels:
                work[rows_at(k * half + offset(level + 1), total.shape[0])] = total.astype(low)
            else:
                start = k * tile_rows + core * half + offset(level + 1)
                final[rows_at(start, total.shape[0])] = total.astype(low)
            next_exchange(k, level)

        def stage_side(k):
            side_copy(k).wait_recv()
            later = k + flying

            @when(jnp.logical_and(later < count, later != tiles))
            def _():
                side_copy(later).start()

            here = rows_at(k * half, half)
            put(k, -1, work[here] + side_recv[here])

        def stage_scatter(k, level):
            size = sizes[level]
            scatter_wait(k, level)
            kind = f32 if factors[level] > 2 else low
            total = work[rows_at(k * half + offset(level + 1), size)].astype(kind)
            for distance in range(1, factors[level]):
                total += recvs[level][distance - 1, rows_at(k * size, size)].astype(kind)
            if not scatters[level]:
                scatter_sent(level, k * sizes[level], sizes[level])
            put(k, level, total)

        def stage_gather(k, level):
            gather_wait(k, level)
            if level != scatter_levels[0]:
                below = scatter_levels[scatter_levels.index(level) - 1]
                for distance in range(1, factors[below]):
                    gather_copy(k, below, distance).start()
            else:
                back_copy(k).start()

        def stage_back(k):
            back_copy(k).wait_recv()
            store(k).start()

        stages = [stage_side]
        stages += [functools.partial(stage_scatter, level=n) for n in range(levels)]
        stages += [functools.partial(stage_gather, level=n) for n in reversed(scatter_levels)]
        stages.append(stage_back)

        def tick(at):
            for n, stage in enumerate(stages):

                @pl.when(jnp.logical_and(at >= lag * n, at < count + lag * n))
                def _(n=n, stage=stage):
                    stage(at - lag * n)

        def when(cond):
            return pl.when(cond)

        def fetch_copies(job, x_buf, y_buf, slot, sems):
            x, xc, y, yc = job
            x_from = given[x].at[:, xc * width : (xc + 1) * width]
            y_from = own_grads[y] if isinstance(y, int) else given[y[0]].at[:, yc * width : (yc + 1) * width]
            return (
                pltpu.make_async_copy(x_from, x_buf.at[slot], sems.at[0, slot]),
                pltpu.make_async_copy(y_from, y_buf.at[slot], sems.at[1, slot]),
            )

        def fetch(k, first_k, last_k):
            for n in range(first_k, last_k):

                @when(k == n)
                def _(n=n):
                    for copy in fetch_copies(audio_jobs[n], x_audio, y_audio, n % 2, in_sem.at[0]):
                        copy.start()
                    for copy in fetch_copies(text_jobs[n], x_text, y_text, n % 2, in_sem.at[1]):
                        copy.start()

        def fetch_wait(k):
            slot = k % 2
            for copy in fetch_copies(audio_jobs[0], x_audio, y_audio, slot, in_sem.at[0]):
                copy.wait()
            for copy in fetch_copies(text_jobs[0], x_text, y_text, slot, in_sem.at[1]):
                copy.wait()

        def tile_grads(k, last_k, first_k):
            slot = k % 2

            @when(k + 1 < last_k)
            def _():
                fetch(k + 1, first_k, last_k)

            fetch_wait(k)

            @when(k >= 2)
            def _():
                core_copy(k - 2).wait_send()

            tile[slot, 0] = dot_tt(x_audio[slot], y_audio[slot]).astype(low)
            tile[slot, 1] = dot_tt(x_text[slot], y_text[slot]).astype(low)
            core_copy(k).start()

            @when(k > first_k)
            def _():
                stage_core(k - 1)

        attn_loads = [
            pltpu.make_async_copy(given[at_joint], joint, load_sem.at[0]),
            pltpu.make_async_copy(given[at_logs], logs, load_sem.at[1]),
            pltpu.make_async_copy(given[at_mixed], mixed_grad, load_sem.at[2]),
        ]

        def attention(step):
            pair, part_at = step // blocks, step % blocks
            lane = lax.broadcasted_iota(jnp.int32, (1, 128), 1)
            sub = lax.broadcasted_iota(jnp.int32, (128, 1), 0)

            def cols(start):
                return pl.ds(pl.multiple_of(start + pair * 128, 128), 128)

            here = rows_at(part_at * block, block)

            @when(part_at == 0)
            def _():
                key_acc[...] = jnp.zeros(key_acc.shape, f32)
                value_acc[...] = jnp.zeros(value_acc.shape, f32)
                key_turned[...] = joint[:, cols(width)].astype(f32).T.astype(low)

            query, key, value = joint[here, cols(0)], joint[:, cols(width)], joint[:, cols(2 * width)]
            grad = mixed_grad[here, cols(0)]
            log = logs[pl.ds(pl.multiple_of(pair * 8, 8), 8), pl.ds(pl.multiple_of(part_at * block, block), block)]
            turned = key_turned[...]
            found = []
            for head in range(2):
                part = jnp.where(lane // 64 == head, query, jnp.zeros_like(query))
                grad_part = jnp.where(lane // 64 == head, grad, jnp.zeros_like(grad))
                chance = jnp.exp2(dot_t(key, part) * log2_e - log[head : head + 1, :])
                product = chance * dot_t(value, grad_part)
                grad_scores = (product - chance * jnp.sum(product, axis=0, keepdims=True)).astype(low)
                found.append(
                    (
                        dot(chance.astype(low), grad_part),
                        dot(grad_scores, part),
                        dot(jnp.where(sub // 64 == head, turned, jnp.zeros_like(turned)), grad_scores),
                    )
                )
            value_acc[...] += found[0][0] + found[1][0]
            key_acc[...] += found[0][1] + found[1][1]
            query_turned = found[0][2] + found[1][2]
            grad_query = query_turned.T * 0.125
            query_grad[here, cols(0)] = grad_query.astype(low)
            sums[0:1, cols(0)] += col_sum(grad_query)

            @when(part_at == blocks - 1)
            def _():
                key_grad[:, cols(0)] = key_acc[...].astype(low)
                value_grad[:, cols(0)] = value_acc[...].astype(low)
                sums[1:2, cols(0)] = col_sum(value_acc[...])

        def weight_copies(mine):
            found = [pltpu.make_async_copy(given[at_weight[0 if mine == 0 else 1]], weight, weight_sem.at[0])]
            for n, (split, at, held) in enumerate(((second_side, at_second, second), (first_side, at_first, first))):
                found += split.copies(mine, given[at[0]], given[at[1]], held, weight_sem.at[1 + n])
            return found

        def block_copies(i, slot):
            here = rows_at(i * block, block)
            found = [
                pltpu.make_async_copy(given[at_encoded].at[here], encoded_in.at[slot], block_sem.at[0, slot]),
                pltpu.make_async_copy(given[at_grad].at[here], grad_in.at[slot], block_sem.at[1, slot]),
            ]
            for n in range(3):
                found.append(
                    pltpu.make_async_copy(given[at_slopes[n]].at[here], slope_in.at[slot, n], block_sem.at[2 + n, slot])
                )
            return found

        def stem_block(step):
            i = blocks - 1 - step
            slot = step % 2

            @when(step + 1 < blocks)
            def _():
                for copy in block_copies(i - 1, 1 - slot):
                    copy.start()

            for copy in block_copies(i, slot):
                copy.wait()
            here = rows_at(i * block, block)
            back = (
                dot_t(query_grad[here], weight[:, :width])
                + dot_t(key_grad[here], weight[:, width : 2 * width])
                + dot_t(value_grad[here], weight[:, 2 * width :])
            )
            normed, inverse = norm_rows(encoded_in[slot])
            sums[2:3, :] += col_sum(back * normed)
            sums[3:4, :] += col_sum(back)
            total = grad_in[slot] + norm_back(back, row(smalls, 0), normed, inverse)
            total = total * slope_in[slot, 0].astype(f32)
            sums[4:5, :] += col_sum(total)
            rounded = total.astype(low)
            second_low[here] = rounded
            at_row = lax.broadcasted_iota(jnp.int32, (block, width), 0)
            wide = rounded.astype(f32)
            moved = jnp.where(at_row == block - 1, carry[0:1, :], pltpu.roll(wide, block - 1, 0))
            carry[0:1, :] = wide[0:1, :]
            moved = moved.astype(low)
            next_low[here] = moved
            grad_even = dot_t(rounded, second[width : 2 * width]) * slope_in[slot, 1].astype(f32)
            grad_odd = (dot_t(rounded, second[2 * width :]) + dot_t(moved, second[0:width])) * slope_in[slot, 2].astype(f32)
            sums[5:6, :] += col_sum(grad_even) + col_sum(grad_odd)
            grad_even = grad_even.astype(low)
            grad_odd = grad_odd.astype(low)
            even_low[here] = grad_even
            odd_low[here] = grad_odd
            taps_even = dot_t(grad_even, first[...])
            taps_odd = dot_t(grad_odd, first[...])
            taps_grad[here, 0:128] = taps_even[:, 0:128]
            taps_grad[here, 128:256] = taps_even[:, 128:256] + taps_odd[:, 0:128]
            taps_grad[here, 256:384] = taps_even[:, 256:384] + taps_odd[:, 128:256]
            taps_grad[here, 384:512] = taps_odd[:, 256:384]

        def mel_rows():
            at_row = lax.broadcasted_iota(jnp.int32, (frames, 128), 0)
            before = jnp.where(at_row == 0, 0.0, pltpu.roll(taps_grad[:, 384:512], 1, 0))
            mel_buf[:, 0:128] = taps_grad[:, 128:256] + before
            after = jnp.where(at_row == frames - 1, 0.0, pltpu.roll(taps_grad[:, 0:128], frames - 1, 0))
            mel_buf[:, 128:256] = taps_grad[:, 256:384] + after
            mel_send[...] = mel_buf[rows_at((1 - section) * (frames // 2), frames // 2)].astype(low)

        def keep_copy():
            return pltpu.make_async_copy(mel_buf.at[rows_at(section * (frames // 2), frames // 2)], keep_ref, keep_sem)

        conv_jobs = [(at_odd, next_low), (at_even, second_low), (at_odd, second_low)]

        def conv_copies(n, slot):
            x, y = conv_jobs[n]
            return (
                pltpu.make_async_copy(given[x], x_audio.at[slot], in_sem.at[0, 0, slot]),
                pltpu.make_async_copy(y, y_audio.at[slot], in_sem.at[0, 1, slot]),
            )

        def tap_copies():
            return [
                pltpu.make_async_copy(given[at_taps].at[:, n * 128 : n * 128 + 384], x_audio.at[n, :, 0:384], in_sem.at[0, 0, n])
                for n in range(2)
            ]

        barrier = pltpu.get_barrier_semaphore()
        peers = [core_peer, side_peer]
        peers += [peer(n, d)[1] for n in range(levels) for d in range(1, factors[n])]
        for device in peers:
            pl.semaphore_signal(barrier, inc=1, device_id=device, device_id_type=pl.DeviceIdType.MESH)

        fetch(0, 0, 1)
        for copy in attn_loads:
            copy.start()
        for which in range(2):

            @when(section == which)
            def _(which=which):
                for copy in weight_copies(which):
                    copy.start()

        for copy in block_copies(blocks - 1, 0):
            copy.start()
        sums[...] = jnp.zeros(sums.shape, f32)
        carry[...] = jnp.zeros(carry.shape, f32)
        pl.semaphore_wait(barrier, len(peers))

        @pl.loop(0, early)
        def _(k):
            tile_grads(k, early, 0)

        stage_core(early - 1)
        for copy in attn_loads:
            copy.wait()

        @pl.loop(0, 4 * blocks)
        def _(step):
            attention(step)

            @when(jnp.logical_or(step < 3, step % 3 == 1))
            def _():
                tick(jnp.where(step < 3, step, 3 + (step - 4) // 3))

        fetch(early, early, early + 1)

        @pl.loop(early, tiles)
        def _(k):
            tile_grads(k, tiles, early)
            tick(k - early + 7)

        stage_core(tiles - 1)
        for copy in weight_copies(0):
            copy.wait()
        clear_pads(first, bands)

        @pl.loop(0, blocks)
        def _(step):
            stem_block(step)

            @when(step % 2 == 1)
            def _():
                tick(10 + step // 2)

        for copy in conv_copies(0, 0):
            copy.start()

        @pl.loop(0, 3)
        def _(n):
            slot = n % 2
            for which in range(1, 3):

                @when(n + 1 == which)
                def _(which=which):
                    for copy in conv_copies(which, which % 2):
                        copy.start()

            for copy in conv_copies(0, slot):
                copy.wait()
            joint[0:tile_rows, pl.ds(pl.multiple_of(n * width, width), width)] = dot_tt(x_audio[slot], y_audio[slot]).astype(low)

        for copy in tap_copies():
            copy.start()
        core_copy(tiles - 2).wait_send()
        slot = tiles % 2

        def conv_part(tap, start, s):
            cols = slice(tap * width + s * lanes, tap * width + s * lanes + lanes)
            return joint[start : start + half, cols]

        for s in range(2):
            tile[slot, s, 0:half, 0:lanes] = conv_part(0, 0, s)
            tile[slot, s, half:tile_rows, 0:lanes] = conv_part(0, half, s)
            tile[slot, s, 0:half, lanes:width] = conv_part(1, half, s)
            tile[slot, s, half:tile_rows, lanes:width] = conv_part(2, 0, s)
        core_copy(tiles).start()
        for copy in tap_copies():
            copy.wait()
        first_grad = (
            dot_tt(x_audio[0, :, 0:384], even_low[...]) + dot_tt(x_audio[1, :, 0:384], odd_low[...])
        ).astype(low)
        stage_core(tiles)
        core_copy(tiles - 1).wait_send()
        slot = 1 - slot
        feed, wide_feed = audio_sums
        text_feed_sums, text_wide, text_cross, cross_sums, text_attn, text_first = text_sums
        small_buf[...] = jnp.zeros(small_buf.shape, f32)
        text_rows_from = (
            (text_first, 0), (text_cross, 0), (text_feed_sums, 0), (text_first, 1), (text_cross, 1), (text_feed_sums, 1),
            (text_attn, 0), (text_attn, 1), (text_cross, 2), (text_feed_sums, 2), (cross_sums, 0), (text_feed_sums, 3),
        )
        for at, (ref, n) in enumerate(text_rows_from):
            small_buf[1, at : at + 1, :] = ref[n : n + 1, :]
        for at, ref, n in (
            (1, feed, 3), (2, feed, 0), (4, feed, 4), (5, feed, 1), (8, feed, 5), (9, feed, 2), (11, cross_sums, 1),
        ):
            small_buf[0, at : at + 1, :] = ref[n : n + 1, :]
        for n in range(4):
            cols = slice(n * width, n * width + width)
            small_buf[0, 12 + n : 13 + n, :] = wide_feed[0:1, cols]
            small_buf[1, 12 + n : 13 + n, :] = text_wide[0:1, cols]
        for s in range(2):
            small_buf[s, 17:18, :] = text_feed_sums[3:4, :]
        small_buf[0, 6:8, :] = sums[0:2, :]
        small_buf[0, 0:1, :] = sums[2:3, :]
        small_buf[0, 3:4, :] = sums[3:4, :]
        small_buf[0, 10:11, :] = sums[4:5, :]
        small_buf[0, 16:17, 0:lanes] = sums[5:6, 0:lanes]
        small_buf[1, 16:17, 0:lanes] = sums[5:6, lanes:width]
        for s in range(2):
            cols = slice(s * lanes, s * lanes + lanes)
            tile[slot, s, 0:half, 0:lanes] = conv_part(1, 0, s)
            tile[slot, s, 0:half, lanes:width] = conv_part(2, half, s)
            tile[slot, s, half : half + 192, 0:lanes] = first_grad[0:192, cols]
            tile[slot, s, half : half + 192, lanes:width] = first_grad[192:384, cols]
            tile[slot, s, half + 192 : half + 224, :] = small_buf[s].astype(low)
            tile[slot, s, half + 224 : tile_rows, :] = jnp.zeros((32, width), low)
        core_copy(tiles + 1).start()
        mel_rows()
        keep_copy().start()
        stage_core(tiles + 1)
        mel_copy().start()

        @pl.loop(12, count + lag * (len(stages) - 1))
        def _(at):
            tick(at)

        keep_copy().wait()
        mel_copy().wait()
        for k in (count - 2, count - 1):
            core_copy(k).wait_send()

        all_sent()

    second_side, first_side = second, first

    def sems(*shape):
        return pltpu.SemaphoreType.DMA(shape)

    def vmem(*shape, dtype=low):
        return pltpu.VMEM(shape, dtype)

    whole = (frames, width)
    return pl.pallas_call(
        kernel,
        name="finish_backward",
        in_specs=[pl.BlockSpec(memory_space=pl.ANY)] * n_any + [pl.BlockSpec(memory_space=pltpu.VMEM)] * n_chip,
        out_specs=[pl.BlockSpec(memory_space=pl.ANY)] * 3,
        out_shape=[
            jax.ShapeDtypeStruct((rows, width), low),
            jax.ShapeDtypeStruct((frames // 2, 256), f32),
            jax.ShapeDtypeStruct((frames // 2, 256), low),
        ],
        scratch_shapes=[
            vmem(2, 2, tile_rows, width), vmem(4, 2, half, width), vmem(count * half, width), vmem(count * half, width),
            vmem(count * half, width), vmem(rows, width),
            vmem(2, *whole), vmem(2, *whole), vmem(2, text_rows, width), vmem(2, text_rows, width),
            vmem(frames, 3 * width), vmem(32, frames, dtype=f32), vmem(*whole), vmem(*whole), vmem(*whole), vmem(*whole),
            vmem(frames, 128, dtype=f32), vmem(frames, 128, dtype=f32), vmem(128, frames), vmem(8, width, dtype=f32),
            vmem(2, block, width, dtype=f32), vmem(2, block, width, dtype=f32), vmem(2, 3, block, width),
            vmem(width, 3 * width), vmem(*second.shape), vmem(*first.shape),
            vmem(*whole), vmem(*whole), vmem(*whole), vmem(*whole), vmem(*whole, dtype=f32),
            vmem(8, width, dtype=f32), vmem(2, 32, width, dtype=f32),
            vmem(frames, 256, dtype=f32), vmem(frames // 2, 256),
            sems(2, 2, 2), sems(3), sems(3), sems(5, 2), pltpu.SemaphoreType.DMA, sems(2, count), sems(count), sems(count),
            pltpu.SemaphoreType.DMA, sems(2), sems(2 + 2 * levels),
            *[vmem(r - 1, count * s, width) for r, s in zip(factors, sizes)],
            *[sems(count) for r in factors],
            *[sems(count) for r in factors],
        ],
        compiler_params=pltpu.CompilerParams(
            collective_id=0, has_side_effects=True, vmem_limit_bytes=63 << 20
        ),
        cost_estimate=pl.CostEstimate(flops=10**11, bytes_accessed=10**8, transcendentals=0),
    )(*arrays, smalls, *audio_sums, *text_sums)


def shards(
    mel_input,
    time_start,
    time_width,
    freq_start,
    freq_width,
    text_len,
    text_embed,
    cotangent,
    positions,
    conv_first,
    conv_first_bias,
    conv_second,
    norm_gain,
    norm_shift,
    attn_in,
    attn_out,
    mlp_up,
    mlp_down,
    up_bias,
    small_bias,
    cross_first,
    cross_second,
):
    frames, width = positions.shape
    bands, mel_frames = mel_input.shape[1], mel_input.shape[2]
    audio_block = frames // 2
    swap_pairs = [(0, 1), (1, 0)]

    def partner(array):
        return lax.ppermute(array, "section", swap_pairs)

    first_own = conv_first.reshape(3 * bands, -1)
    second_own = conv_second.reshape(3 * width, -1)
    owns = [w[0] for w in (attn_in, attn_out, mlp_up, mlp_down, cross_first, cross_second)]
    (
        first_other, second_other, *others, a_small, t_small, a_ups, t_ups,
        taps, encoded, even_act, odd_act, even_slope, odd_slope, slope_second, a_norm, a_joint, a_mixed, a_logs,
    ) = begin(
        mel_input, (time_start, time_width, freq_start, freq_width), norm_gain[0], norm_shift[0], small_bias[0], up_bias,
        conv_first_bias, first_own, second_own, owns[0], owns[1:], positions,
    )
    a_in, a_out, a_up, a_down, a_cross_a, a_cross_b = [Side(0, o, p) for o, p in zip(owns, others)]
    t_in, t_out, t_up, t_down, t_cross_a, t_cross_b = [Side(1, o, p) for o, p in zip(owns, others)]
    first_all = Split(first_own, first_other, 3, 128)
    second_all = Split(second_own, second_other, 3, width)

    a_middle, a_feed_norm, a_hidden, a_slope, a_ending, memory, memory_keys, memory_values = audio_feed(
        encoded, a_mixed, a_out, a_small, a_ups, a_up, a_down, a_cross_a, a_cross_b, audio_block
    )

    t_norm, t_joint, t_mixed, t_logs, t_middle, cross_low, cross_query = text_start(
        text_embed, t_in, t_out, t_small, t_cross_a
    )
    (
        decoded_keep, decoded_send, t_feed_norm, t_hidden, t_pre, cot_low, after_grad, after_low, c_mixed,
        query_grad, key_grad, value_grad, feed_sums, feed_wide, c_sums,
    ) = text_cross(
        text_len, cross_query, memory_keys, memory_values, t_middle, cotangent, t_cross_b, t_small, t_ups, t_up, t_down
    )
    text_keep, text_send, middle_low, tq_grad, tk_grad, tv_grad, cross_sums, t_sums, text_sums = text_back(
        query_grad, t_middle, after_grad, t_joint, t_logs, text_embed, t_small, t_cross_a, t_out, t_in
    )
    decoded_got, text_got = partner(decoded_send), partner(text_send)
    end_low, a_pre, a_grad, a_grad_low, a_mixed_grad, a_feed_sums, a_feed_wide = audio_feed_back(
        key_grad, value_grad, a_ending, a_middle, a_slope, a_small, a_cross_a, a_cross_b, a_up, a_down, a_out, audio_block
    )

    audio = [(a_feed_norm, 0, a_pre, n) for n in range(4)] + [(a_hidden, n, end_low, 0) for n in range(4)]
    audio += [(memory, 0, key_grad, 0), (memory, 0, value_grad, 0), (a_mixed, 0, a_grad_low, 0)]
    audio += [(a_norm, 0, n, 0) for n in range(3)]
    text = [(t_feed_norm, 0, t_pre, n) for n in range(4)] + [(t_hidden, n, cot_low, 0) for n in range(4)]
    text += [(cross_low, 0, query_grad, 0), (c_mixed, 0, after_low, 0), (t_mixed, 0, middle_low, 0)]
    text += [(t_norm, 0, part, 0) for part in (tq_grad, tk_grad, tv_grad)]
    a_feed_sums, decoded_got, text_got = lax.optimization_barrier((a_feed_sums, decoded_got, text_got))
    total, mel_keep, mel_got = finish_backward(
        audio, text, a_joint, a_logs, a_mixed_grad, a_grad, encoded, (slope_second, even_slope, odd_slope), a_small, a_in,
        second_all, first_all, (odd_act, even_act, taps), (a_feed_sums, a_feed_wide),
        (feed_sums, feed_wide, cross_sums, c_sums, t_sums, text_sums), bands,
    )

    decoded, text_grad, mel_out = finish(
        [(decoded_keep, decoded_got), (text_keep, text_got)], mel_keep, mel_got,
        (time_start, time_width, freq_start, freq_width), bands,
    )
    joint, out, up, down, cross_a, cross_b, first, bias, second, gain, shift, wide, small, cross = unpack(total, bands)
    gain, shift, small = (jnp.transpose(rows, (1, 0, 2)) for rows in (gain, shift, small))
    return (
        decoded, text_grad, mel_out, first, bias[0], second, gain, shift, joint, out, up, down, wide, small, cross_a, cross_b,
        cross[0],
    )


def solution(mesh):
    return jax.shard_map(
        shards,
        mesh=mesh,
        in_specs=(
            P("dp", None, None),
            P("dp"),
            P("dp"),
            P("dp"),
            P("dp"),
            P("dp"),
            P("dp", None, None),
            P("dp", None, None),
            P(),
            P(None, None, "section"),
            P("section"),
            P(None, None, "section"),
            P("section", None, None),
            P("section", None, None),
            P("section", None, None),
            P("section", None, None),
            P("section", None, None),
            P("section", None, None),
            P("section", None),
            P("section", None, None),
            P("section", None, None),
            P("section", None, None),
        ),
        out_specs=(
            P("dp", None, "section"),
            P("dp", None, "section"),
            P("dp", None, "section"),
            P(None, None, "section"),
            P("section"),
            P(None, None, "section"),
            P("section", None, None),
            P("section", None, None),
            P("section", None, None),
            P("section", None, None),
            P("section", None, None),
            P("section", None, None),
            P("section", None),
            P("section", None, None),
            P("section", None, None),
            P("section", None, None),
            P("section"),
        ),
        check_vma=False,
    )
```

```python
import functools

import jax
import jax.numpy as jnp
from jax import lax
from jax.experimental import pallas as pl
from jax.experimental.pallas import tpu as pltpu
from jax.sharding import PartitionSpec as P

HEADS = 8
epsilon = 1e-05
root_half = 0.7071067811865476
gauss_norm = 0.3989422804014327
log2_e = 1.4426950408889634
VMEM_BYTES = 56 << 20

f32 = jnp.float32
low = jnp.bfloat16


def dot(left, right):
    return lax.dot_general(left, right, (((1,), (0,)), ((), ())), preferred_element_type=f32)


def dot_t(left, right):
    return lax.dot_general(left, right, (((1,), (1,)), ((), ())), preferred_element_type=f32)


def dot_tt(left, right):
    return lax.dot_general(left, right, (((0,), (0,)), ((), ())), preferred_element_type=f32)


def gelu_both(inputs):
    ratio = 1.0 / (1.0 + (0.3275911 * root_half) * jnp.abs(inputs))
    bell = jnp.exp2((-0.5 * log2_e) * inputs * inputs)
    tail = ratio * (
        0.127414796
        + ratio * (-0.142248368 + ratio * (0.7107068705 + ratio * (-0.7265760135 + ratio * 0.5307027145)))
    )
    tail = tail * bell
    below = jnp.where(inputs >= 0.0, 1.0 - tail, tail)
    return inputs * below, below + inputs * bell * gauss_norm


def norm_rows(inputs):
    centred = inputs - jnp.mean(inputs, axis=-1, keepdims=True)
    inverse = lax.rsqrt(jnp.mean(centred * centred, axis=-1, keepdims=True) + epsilon)
    return centred * inverse, inverse


def norm_back(grad, gain, normed, inverse):
    scaled = grad * gain
    return inverse * (
        scaled
        - jnp.mean(scaled, axis=-1, keepdims=True)
        - normed * jnp.mean(scaled * normed, axis=-1, keepdims=True)
    )


def col_sum(inputs):
    return jnp.sum(inputs, axis=0, keepdims=True)


class Side:
    def __init__(self, side, own, other):
        self.side, self.own, self.other, self.shape = side, own, other, own.shape

    def copies(self, mine, own, other, held, sem):
        return [pltpu.make_async_copy(own if mine == self.side else other, held, sem)]


class Split:
    def __init__(self, own, other, groups, apart):
        self.own, self.other, self.groups, self.apart = own, other, groups, apart
        self.shape = (groups * apart, 2 * own.shape[1])

    def copies(self, mine, own, other, held, sem, parts=(0, 1)):
        size, half = self.own.shape[0] // self.groups, self.own.shape[1]
        found = []
        for which, ref in [((mine, own), (1 - mine, other))[n] for n in parts]:
            cols = slice(which * half, which * half + half)
            for n in range(self.groups):
                found.append(
                    pltpu.make_async_copy(
                        ref.at[n * size : n * size + size], held.at[n * self.apart : n * self.apart + size, cols], sem
                    )
                )
        return found


def call(body, name, steps, block, ins, outs, scratch=(), reverse=False, flops=0, grid=None):
    arrays, specs, kinds, weight_scratch = [], [], [], []
    at = (lambda i: steps - 1 - i) if reverse else (lambda i: i)
    for array, kind in ins:
        if kind in ("side", "split"):
            arrays += [array.own, array.other]
            specs += [pl.BlockSpec(memory_space=pl.ANY)] * 2
            weight_scratch.append(pltpu.VMEM(array.shape, array.own.dtype))
        elif kind == "rows":
            arrays.append(array)
            specs.append(pl.BlockSpec((block, array.shape[1]), lambda i: (at(i), 0)))
        elif kind == "clip":
            arrays.append(array)
            specs.append(pl.BlockSpec((None, block, array.shape[2]), lambda i: (lax.axis_index("section"), at(i), 0)))
        elif kind == "smem":
            arrays.append(array)
            specs.append(pl.BlockSpec(memory_space=pltpu.SMEM))
        else:
            arrays.append(array)
            specs.append(
                pl.BlockSpec(
                    array.shape,
                    lambda i, n=array.ndim: (0,) * n,
                    pipeline_mode=pl.Buffered(1),
                )
            )
        kinds.append((kind, array if kind in ("side", "split") else None))
    out_specs = [
        pl.BlockSpec((block, shape[1]), lambda i: (at(i), 0))
        if kind == "rows"
        else pl.BlockSpec(shape, lambda i, n=len(shape): (0,) * n)
        for shape, dtype, kind in outs
    ]
    n_in, n_out, n_weight = len(arrays), len(outs), len(weight_scratch)

    def kernel(*refs):
        in_refs, out_refs = refs[:n_in], refs[n_in : n_in + n_out]
        weights = refs[n_in + n_out : n_in + n_out + n_weight]
        extra = refs[n_in + n_out + n_weight :]
        given, r, w, loads = [], 0, 0, []
        for kind, array in kinds:
            if kind in ("side", "split"):
                loads.append((array, in_refs[r], in_refs[r + 1], weights[w]))
                given.append(weights[w])
                r, w = r + 2, w + 1
            else:
                given.append(in_refs[r])
                r += 1
        step = pl.program_id(0)
        if loads:
            sem = extra[-1]
            extra = extra[:-1]

            @pl.when(step == 0)
            def _():
                mine = lax.axis_index("section")
                for n, load in enumerate(loads):
                    for which in range(2):

                        @pl.when(mine == which)
                        def _(load=load, n=n, which=which):
                            array, own, other, held = load
                            for copy in array.copies(which, own, other, held, sem.at[n]):
                                copy.start()

                for n, (array, own, other, held) in enumerate(loads):
                    for copy in array.copies(0, own, other, held, sem.at[n]):
                        copy.wait()

        for ref, (shape, dtype, kind) in zip(out_refs, outs):
            if kind == "sums":

                @pl.when(step == 0)
                def _(ref=ref):
                    ref[...] = jnp.zeros(ref.shape, ref.dtype)

        body(step, given, out_refs, extra)

    scratch_shapes = weight_scratch + list(scratch)
    if weight_scratch:
        scratch_shapes.append(pltpu.SemaphoreType.DMA((n_weight,)))
    total = sum(a.size * a.dtype.itemsize for a in arrays) + sum(
        2 * s[0] * s[1] for s, d, k in outs
    )
    return pl.pallas_call(
        kernel,
        name=name,
        grid=(steps,),
        in_specs=specs,
        out_specs=out_specs,
        out_shape=[jax.ShapeDtypeStruct(shape, dtype) for shape, dtype, kind in outs],
        scratch_shapes=scratch_shapes,
        compiler_params=pltpu.CompilerParams(
            dimension_semantics=("arbitrary",), vmem_limit_bytes=VMEM_BYTES
        ),
        cost_estimate=pl.CostEstimate(flops=int(flops), bytes_accessed=int(total), transcendentals=0),
    )(*arrays)


def row(ref, n):
    return ref[n : n + 1, :].astype(f32)


def clear_pads(weight, bands):
    for n in range(3):
        weight[n * 128 + bands : n * 128 + 128, :] = jnp.zeros((128 - bands, weight.shape[1]), weight.dtype)


def write_halves(values, keep, send):
    half = values.shape[1] // 2
    mine = lax.axis_index("section")
    first, second = values[:, :half], values[:, half:]

    @pl.when(mine == 0)
    def _():
        keep[...] = first
        send[...] = second.astype(low)

    @pl.when(mine != 0)
    def _():
        keep[...] = second
        send[...] = first.astype(low)


def pair_cols(start, pair):
    return pl.ds(pl.multiple_of(start + pair * 128, 128), 128)


def seen(shape, key_axis):
    return lax.broadcasted_iota(jnp.int32, shape, key_axis) <= lax.broadcasted_iota(jnp.int32, shape, 1 - key_axis)


def attend_pair(query, key, value, causal):
    lane = lax.broadcasted_iota(jnp.int32, (1, 128), 1)
    mixed, logs = [], []
    for head in range(2):
        scores = dot_t(jnp.where(lane // 64 == head, query, jnp.zeros_like(query)), key)
        if causal:
            scores = jnp.where(seen(scores.shape, 1), scores, -1e30)
        top = jnp.max(scores, axis=1, keepdims=True) * log2_e
        exponent = jnp.exp2(scores * log2_e - top)
        total = jnp.sum(exponent, axis=1, keepdims=True)
        mixed.append(dot(exponent.astype(low), value) * (1.0 / total))
        logs.append(top + jnp.log2(total))
    both = jnp.where(lane == 0, logs[0], logs[1])
    return jnp.where(lane < 64, mixed[0], mixed[1]).astype(low), both.T[0:8, :]


def attend_pair_back(query, key, value, logs, grad, causal):
    lane = lax.broadcasted_iota(jnp.int32, (1, 128), 1)
    sub = lax.broadcasted_iota(jnp.int32, (128, 1), 0)
    turned = key.astype(f32).T.astype(low)
    found = []
    for head in range(2):
        part = jnp.where(lane // 64 == head, query, jnp.zeros_like(query))
        grad_part = jnp.where(lane // 64 == head, grad, jnp.zeros_like(grad))
        chance = jnp.exp2(dot_t(key, part) * log2_e - logs[head : head + 1, :])
        if causal:
            chance = jnp.where(seen(chance.shape, 0), chance, 0.0)
        product = chance * dot_t(value, grad_part)
        grad_scores = (product - chance * jnp.sum(product, axis=0, keepdims=True)).astype(low)
        found.append(
            (
                dot(jnp.where(sub // 64 == head, turned, jnp.zeros_like(turned)), grad_scores),
                dot(grad_scores, part),
                dot(chance.astype(low), grad_part),
            )
        )
    turned, key_grad, value_grad = (one + two for one, two in zip(*found))
    return turned.T * 0.125, key_grad, value_grad


def audio_feed(inputs, mixed, weight_out, smalls, ups, weight_up, weight_down, cross_a, cross_b, block):
    rows, width = inputs.shape
    hidden = ups.shape[1]

    def body(step, given, outs, extra):
        inputs, mixed, weight_out, smalls, ups, weight_up, weight_down, cross_a, cross_b = given
        middle_out, norm_out, hidden_out, slope_out, ending_out, memory_out, key_out, value_out = outs
        middle = inputs[...] + dot(mixed[...], weight_out[...]) + row(smalls, 8)
        middle_out[...] = middle
        normed, inverse = norm_rows(middle)
        rounded = (normed * row(smalls, 1) + row(smalls, 4)).astype(low)
        norm_out[...] = rounded
        ending = middle + row(smalls, 9)
        for part in range(hidden // 512):
            cols = slice(part * 512, part * 512 + 512)
            pre = dot(rounded, weight_up[:, cols]) + ups[:, cols].astype(f32)
            value, slope = gelu_both(pre)
            act = value.astype(low)
            hidden_out[:, cols] = act
            slope_out[:, cols] = slope.astype(low)
            ending += dot(act, weight_down[cols, :])
        ending_out[...] = ending
        normed, inverse = norm_rows(ending)
        memory = (normed * row(smalls, 2) + row(smalls, 5)).astype(low)
        memory_out[...] = memory
        key_out[...] = dot(memory, cross_a[...]).astype(low)
        value_out[...] = (dot(memory, cross_b[...]) + row(smalls, 11)).astype(low)

    wide, shape = (rows, hidden), (rows, width)
    return call(
        body, "audio_feed", rows // block, block,
        [(inputs, "rows"), (mixed, "rows"), (weight_out, "side"), (smalls, "full"), (ups, "full"),
         (weight_up, "side"), (weight_down, "side"), (cross_a, "side"), (cross_b, "side")],
        [(shape, f32, "rows"), (shape, low, "rows"), (wide, low, "rows"), (wide, low, "rows"),
         (shape, f32, "rows"), (shape, low, "rows"), (shape, low, "rows"), (shape, low, "rows")],
        flops=2 * rows * width * (3 * width + 2 * hidden),
    )


def text_start(inputs, weight, weight_out, smalls, cross_a):
    rows, width = inputs.shape[1:]

    def body(step, given, outs, extra):
        inputs, weight, weight_out, smalls, cross_a = given
        norm_out, joint, mixed, logs, middle_out, low_out, query_out = outs
        normed, inverse = norm_rows(inputs[...].astype(f32))
        rounded = (normed * row(smalls, 0) + row(smalls, 3)).astype(low)
        norm_out[...] = rounded
        joint[:, :width] = (dot(rounded, weight[:, :width]) + row(smalls, 6)).astype(low) * 0.125
        joint[:, width : 2 * width] = dot(rounded, weight[:, width : 2 * width]).astype(low)
        joint[:, 2 * width :] = (dot(rounded, weight[:, 2 * width :]) + row(smalls, 7)).astype(low)

        @pl.loop(0, HEADS // 2)
        def _(pair):
            cols = pair_cols(0, pair)
            mixed[:, cols], logs[pl.ds(pl.multiple_of(pair * 8, 8), 8), :] = attend_pair(
                joint[:, cols], joint[:, pair_cols(width, pair)], joint[:, pair_cols(2 * width, pair)], True
            )

        middle = inputs[...].astype(f32) + dot(mixed[...], weight_out[...]) + row(smalls, 8)
        middle_out[...] = middle
        normed, inverse = norm_rows(middle)
        rounded = (normed * row(smalls, 1) + row(smalls, 4)).astype(low)
        low_out[...] = rounded
        query_out[...] = (dot(rounded, cross_a[...]) + row(smalls, 10)).astype(low) * 0.125

    shape = (rows, width)
    return call(
        body, "text_start", 1, rows,
        [(inputs, "clip"), (weight, "side"), (weight_out, "side"), (smalls, "full"), (cross_a, "side")],
        [(shape, low, "rows"), ((rows, 3 * width), low, "rows"), (shape, low, "rows"), ((4 * HEADS, rows), f32, "whole"),
         (shape, f32, "rows"), (shape, low, "rows"), (shape, low, "rows")],
        flops=10 * rows * width * width,
    )


def text_cross(length, queries, keys, values, middle, cotangent, cross_b, smalls, ups, weight_up, weight_down):
    rows, width = middle.shape
    hidden = ups.shape[1]
    block, key_rows = rows, keys.shape[0]

    def body(step, given, outs, extra):
        length, queries, keys, values, middle, cotangent, cross_b, smalls, ups, weight_up, weight_down = given
        decoded_keep, decoded_send, norm_out, hidden_out, pre_out, cot_out, grad_out, grad_low, mixed, query_out, key_out, value_out, sums, wide_sums, cross_sums = outs
        logs, mixed_grad = extra

        @pl.loop(0, HEADS // 2)
        def _(pair):
            cols = pair_cols(0, pair)
            mixed[:, cols], logs[pl.ds(pl.multiple_of(pair * 8, 8), 8), :] = attend_pair(
                queries[:, cols], keys[:, cols], values[:, cols], False
            )

        after = middle[...] + dot(mixed[...], cross_b[...]) + row(smalls, 11)
        normed, inverse = norm_rows(after)
        rounded = (normed * row(smalls, 2) + row(smalls, 5)).astype(low)
        norm_out[...] = rounded
        at_row = lax.broadcasted_iota(jnp.int32, (block, 1), 0) + step * block
        valid = at_row < length[lax.axis_index("section")]
        grad = jnp.where(valid, cotangent[...].astype(f32), 0.0)
        cot = grad.astype(low)
        cot_out[...] = cot
        ending = after + row(smalls, 9)
        back = jnp.zeros((block, width), f32)
        for part in range(hidden // 512):
            cols = slice(part * 512, part * 512 + 512)
            pre = dot(rounded, weight_up[:, cols]) + ups[:, cols].astype(f32)
            value, slope = gelu_both(pre)
            act = value.astype(low)
            hidden_out[:, cols] = act
            ending += dot(act, weight_down[cols, :])
            grad_pre = dot_t(cot, weight_down[cols, :]) * slope
            wide_sums[0:1, cols] += col_sum(grad_pre)
            pre_low = grad_pre.astype(low)
            pre_out[:, cols] = pre_low
            back += dot_t(pre_low, weight_up[:, cols])
        write_halves(jnp.where(valid, ending, 0.0), decoded_keep, decoded_send)
        sums[0:1, :] += col_sum(back * normed)
        sums[1:2, :] += col_sum(back)
        sums[2:3, :] += col_sum(grad)
        grad = grad + norm_back(back, row(smalls, 2), normed, inverse)
        sums[3:4, :] += col_sum(grad)
        grad_out[...] = grad
        rounded = grad.astype(low)
        grad_low[...] = rounded
        mixed_grad[...] = dot_t(rounded, cross_b[...]).astype(low)

        @pl.loop(0, HEADS // 2)
        def _(pair):
            cols = pair_cols(0, pair)
            query_grad, key_grad, value_grad = attend_pair_back(
                queries[:, cols], keys[:, cols], values[:, cols], logs[pl.ds(pl.multiple_of(pair * 8, 8), 8), :],
                mixed_grad[:, cols], False,
            )
            query_out[:, cols] = query_grad.astype(low)
            key_out[:, cols] = key_grad.astype(low)
            value_grad = value_grad.astype(low)
            value_out[:, cols] = value_grad
            cross_sums[0:1, cols] = col_sum(query_grad)
            cross_sums[1:2, cols] = col_sum(value_grad.astype(f32))

    wide, shape = (rows, hidden), (rows, width)
    return call(
        body, "text_cross", 1, rows,
        [(length, "smem"), (queries, "rows"), (keys, "full"), (values, "full"), (middle, "rows"), (cotangent, "clip"), (cross_b, "side"),
         (smalls, "full"), (ups, "full"), (weight_up, "side"), (weight_down, "side")],
        [((rows, width // 2), f32, "rows"), ((rows, width // 2), low, "rows"), (shape, low, "rows"), (wide, low, "rows"),
         (wide, low, "rows"), (shape, low, "rows"), (shape, f32, "rows"), (shape, low, "rows"), (shape, low, "rows"), (shape, low, "rows"),
         ((key_rows, width), low, "whole"), ((key_rows, width), low, "whole"),
         ((8, width), f32, "sums"), ((8, hidden), f32, "sums"), ((8, width), f32, "sums")],
        scratch=[pltpu.VMEM((4 * HEADS, rows), f32), pltpu.VMEM(shape, low)],
        flops=2 * rows * width * (2 * width + 4 * hidden),
    )


def text_back(query_grad, middle, grad, joint, logs, inputs, smalls, cross_a, weight_out, weight):
    rows, width = middle.shape

    def body(step, given, outs, extra):
        query_grad, middle, grad, joint, logs, inputs, smalls, cross_a, weight_out, weight = given
        keep, send, low_out, query_out, key_out, value_out, cross_sums, attn_sums, first_sums = outs
        total, mixed_grad = extra
        back = dot_t(query_grad[...], cross_a[...])
        normed, inverse = norm_rows(middle[...])
        cross_sums[0:1, :] = col_sum(back * normed)
        cross_sums[1:2, :] = col_sum(back)
        total[...] = grad[...] + norm_back(back, row(smalls, 1), normed, inverse)
        cross_sums[2:3, :] = col_sum(total[...])
        rounded = total[...].astype(low)
        low_out[...] = rounded
        mixed_grad[...] = dot_t(rounded, weight_out[...]).astype(low)

        @pl.loop(0, HEADS // 2)
        def _(pair):
            cols = pair_cols(0, pair)
            query, key, value = attend_pair_back(
                joint[:, cols], joint[:, pair_cols(width, pair)], joint[:, pair_cols(2 * width, pair)],
                logs[pl.ds(pl.multiple_of(pair * 8, 8), 8), :], mixed_grad[:, cols], True,
            )
            query_out[:, cols] = query.astype(low)
            key_out[:, cols] = key.astype(low)
            value_out[:, cols] = value.astype(low)
            attn_sums[0:1, cols] = col_sum(query)
            attn_sums[1:2, cols] = col_sum(value)

        back = (
            dot_t(query_out[...], weight[:, :width])
            + dot_t(key_out[...], weight[:, width : 2 * width])
            + dot_t(value_out[...], weight[:, 2 * width :])
        )
        normed, inverse = norm_rows(inputs[...].astype(f32))
        first_sums[0:1, :] = col_sum(back * normed)
        first_sums[1:2, :] = col_sum(back)
        write_halves(total[...] + norm_back(back, row(smalls, 0), normed, inverse), keep, send)

    shape = (rows, width)
    return call(
        body, "text_back", 1, rows,
        [(query_grad, "rows"), (middle, "rows"), (grad, "rows"), (joint, "rows"), (logs, "full"), (inputs, "clip"),
         (smalls, "full"), (cross_a, "side"), (weight_out, "side"), (weight, "side")],
        [((rows, width // 2), f32, "rows"), ((rows, width // 2), low, "rows")] + [(shape, low, "rows")] * 4
        + [((8, width), f32, "sums")] * 3,
        scratch=[pltpu.VMEM(shape, f32), pltpu.VMEM(shape, low)],
        flops=14 * rows * width * width,
    )


def audio_feed_back(key_grad, value_grad, ending, middle, slope, smalls, cross_a, cross_b, weight_up, weight_down, weight_out, block):
    rows, width = ending.shape
    hidden = slope.shape[1]

    def body(step, given, outs, extra):
        key_grad, value_grad, ending, middle, slope, smalls, cross_a, cross_b, weight_up, weight_down, weight_out = given
        end_low, pre_out, grad_out, grad_low, mixed_out, sums, wide_sums = outs
        back = dot_t(key_grad[...], cross_a[...]) + dot_t(value_grad[...], cross_b[...])
        normed, inverse = norm_rows(ending[...])
        sums[0:1, :] += col_sum(back * normed)
        sums[1:2, :] += col_sum(back)
        grad = norm_back(back, row(smalls, 2), normed, inverse)
        sums[2:3, :] += col_sum(grad)
        rounded = grad.astype(low)
        end_low[...] = rounded
        back = jnp.zeros((block, width), f32)
        for part in range(hidden // 512):
            cols = slice(part * 512, part * 512 + 512)
            grad_pre = dot_t(rounded, weight_down[cols, :]) * slope[:, cols].astype(f32)
            wide_sums[0:1, cols] += col_sum(grad_pre)
            pre_low = grad_pre.astype(low)
            pre_out[:, cols] = pre_low
            back += dot_t(pre_low, weight_up[:, cols])
        normed, inverse = norm_rows(middle[...])
        sums[3:4, :] += col_sum(back * normed)
        sums[4:5, :] += col_sum(back)
        grad = grad + norm_back(back, row(smalls, 1), normed, inverse)
        sums[5:6, :] += col_sum(grad)
        grad_out[...] = grad
        rounded = grad.astype(low)
        grad_low[...] = rounded
        mixed_out[...] = dot_t(rounded, weight_out[...]).astype(low)

    wide, shape = (rows, hidden), (rows, width)
    return call(
        body, "audio_feed_back", rows // block, block,
        [(key_grad, "rows"), (value_grad, "rows"), (ending, "rows"), (middle, "rows"), (slope, "rows"), (smalls, "full"),
         (cross_a, "side"), (cross_b, "side"), (weight_up, "side"), (weight_down, "side"), (weight_out, "side")],
        [(shape, low, "rows"), (wide, low, "rows"), (shape, f32, "rows"), (shape, low, "rows"), (shape, low, "rows"),
         ((8, width), f32, "sums"), ((8, hidden), f32, "sums")],
        flops=2 * rows * width * (3 * width + 2 * hidden),
    )


def unpack(total, bands):
    width, half = total.shape[1], total.shape[1] // 2
    tiles = 14

    def kernel(total, joint, out, up, down, cross_a, cross_b, first, bias, second, gain, shift, wide, small, cross, held, found, in_sem, out_sem):
        def load(n):
            here = pl.ds(pl.multiple_of(n * width, width), width)
            return pltpu.make_async_copy(total.at[here], held.at[n], in_sem.at[n])

        def target(n):
            cols = lambda k: slice(k * width, k * width + width)
            if n < 4:
                return up.at[0, :, cols(n)]
            if n < 8:
                return down.at[0, cols(n - 4)]
            if n < 11:
                return (cross_a, cross_b, out)[n - 8].at[0]
            return joint.at[0, :, cols(n - 11)]

        def store(n):
            return pltpu.make_async_copy(found.at[n], target(n), out_sem.at[n])

        @pl.loop(0, tiles + 2)
        def _(n):
            load(n).start()

        @pl.loop(0, tiles)
        def _(n):
            load(n).wait()
            found[n] = held[n].astype(f32)
            for k in range(tiles):

                @pl.when(n == k)
                def _(k=k):
                    store(k).start()

        load(tiles).wait()
        load(tiles + 1).wait()
        tile = held.at[tiles]
        second[0] = tile[:, 0:half].astype(f32)
        second[1, half:width] = tile[0:half, half:width].astype(f32)
        second[2, 0:half] = tile[half:width, half:width].astype(f32)
        tile = held.at[tiles + 1]
        second[1, 0:half] = tile[0:half, 0:half].astype(f32)
        second[2, half:width] = tile[0:half, half:width].astype(f32)
        first[0] = tile[half : half + bands, 0:half].astype(f32)
        first[1, 0:64] = tile[half + 128 : half + 192, 0:half].astype(f32)
        first[1, 64:bands] = tile[half : half + bands - 64, half:width].astype(f32)
        first[2] = tile[half + 64 : half + 64 + bands, half:width].astype(f32)
        rows = tile[half + 192 : half + 224, :].astype(f32)
        for n in range(3):
            gain[n] = rows[n : n + 1]
            shift[n] = rows[3 + n : 4 + n]
        for n in range(6):
            small[n] = rows[6 + n : 7 + n]
        for n in range(4):
            wide[:, n * width : (n + 1) * width] = rows[12 + n : 13 + n]
        bias[...] = rows[16:17, 0:half]
        mine = lax.axis_index("section")
        cross[...] = jnp.where(mine == 0, rows[17:18, 0:half], rows[17:18, half:width])
        for n in range(tiles):
            store(n).wait()

    shapes = [
        (1, width, 3 * width), (1, width, width), (1, width, 4 * width), (1, 4 * width, width), (1, width, width), (1, width, width),
        (3, bands, half), (1, half), (3, width, half), (3, 1, width), (3, 1, width), (1, 4 * width), (6, 1, width), (1, half),
    ]
    return pl.pallas_call(
        kernel,
        name="unpack",
        in_specs=[pl.BlockSpec(memory_space=pl.ANY)],
        out_specs=[pl.BlockSpec(memory_space=pl.ANY)] * 6 + [pl.BlockSpec(memory_space=pltpu.VMEM)] * 8,
        out_shape=[jax.ShapeDtypeStruct(shape, f32) for shape in shapes],
        scratch_shapes=[
            pltpu.VMEM((tiles + 2, width, width), low), pltpu.VMEM((tiles, width, width), f32),
            pltpu.SemaphoreType.DMA((tiles + 2,)), pltpu.SemaphoreType.DMA((tiles,)),
        ],
        compiler_params=pltpu.CompilerParams(vmem_limit_bytes=VMEM_BYTES),
        cost_estimate=pl.CostEstimate(flops=0, bytes_accessed=6 * total.size, transcendentals=0),
    )(total)


def finish(parts, mel_keep, mel_got, spans, bands):
    count = len(parts)
    pair_rows = mel_keep.shape[0]
    frames = 2 * pair_rows

    def kernel(*refs):
        pairs, (keep_ref, got_ref), marks = refs[: 2 * count], refs[2 * count : 2 * count + 2], refs[2 * count + 2 : 2 * count + 6]
        outs, mel_out, laid = refs[2 * count + 6 : 3 * count + 6], refs[3 * count + 6], refs[3 * count + 7]
        mine = lax.axis_index("section")
        for n, out in enumerate(outs):
            out[mine] = pairs[2 * n][...]
            out[1 - mine] = pairs[2 * n + 1][...].astype(f32)
        band_at = lax.broadcasted_iota(jnp.int32, (bands, frames), 0)
        frame_at = lax.broadcasted_iota(jnp.int32, (bands, frames), 1) + mine * frames
        for clip, ref in ((mine, keep_ref), (1 - mine, got_ref)):
            for n in range(2):
                laid[pl.ds(n, pair_rows, stride=2), :] = ref[:, n * 128 : n * 128 + 128].astype(f32)
            start, span, band, width = (mark[clip] for mark in marks)
            keep = jnp.logical_and(
                jnp.logical_or(band_at < band, band_at >= band + width),
                jnp.logical_or(frame_at < start, frame_at >= start + span),
            )
            mel_out[clip] = jnp.where(keep, laid[...].T[0:bands, :], 0.0)

    def full(shape):
        return pl.BlockSpec(shape, lambda i, n=len(shape): (0,) * n)

    flat = [array for pair in parts for array in pair]
    shapes = [(2,) + keep.shape for keep, got in parts] + [(2, bands, frames)]
    return pl.pallas_call(
        kernel,
        name="finish",
        grid=(1,),
        in_specs=[full(array.shape) for array in flat + [mel_keep, mel_got]] + [pl.BlockSpec(memory_space=pltpu.SMEM)] * 4,
        out_specs=[full(shape) for shape in shapes],
        out_shape=[jax.ShapeDtypeStruct(shape, f32) for shape in shapes],
        scratch_shapes=[pltpu.VMEM((frames, 128), f32)],
        compiler_params=pltpu.CompilerParams(vmem_limit_bytes=VMEM_BYTES),
        cost_estimate=pl.CostEstimate(flops=0, bytes_accessed=sum(8 * a.size for a in flat), transcendentals=0),
    )(*flat, mel_keep, mel_got, *spans)


def begin(mel_input, spans, gain, shift, biases, up_bias, first_bias, first, second, joint_weight, weights, positions):
    frames, width = positions.shape
    bands, mel_frames = mel_input.shape[1:]
    lanes = width // 2
    hidden = up_bias.shape[1]
    block = 256
    blocks = frames // block
    sent = [second, joint_weight] + weights
    n_sent = len(sent)
    pieces = []
    for n, array in enumerate(sent):
        cuts = 2 if array.size >= 700000 else 1
        size = array.shape[0] // cuts
        pieces += [(n, c * size, size) for c in range(cuts)]
    n_pieces = len(pieces)
    flying = 2
    first_held = Split(first, first, 3, 128)
    second_held = Split(second, second, 3, width)
    n_any = n_sent + 3

    def kernel(*refs):
        mel_ref, positions_ref, first_ref = refs[:3]
        own = refs[3:n_any]
        times, time_spans, bands_from, band_spans = refs[n_any : n_any + 4]
        gain, shift, biases, up_bias, first_bias = refs[n_any + 4 : n_any + 9]
        outs = refs[n_any + 9 :]
        first_other = outs[0]
        other = outs[1 : 1 + n_sent]
        a_small, t_small, a_ups, t_ups = outs[1 + n_sent : 5 + n_sent]
        results = outs[5 + n_sent : 16 + n_sent]
        (
            taps, encoded, even_act, odd_act, even_slope, odd_slope, slope_second, norm, joint, mixed, logs,
            mel, turned, place, conv_first, conv_second, weight, carry, pack, pack_other,
            load_sem, weight_sem, out_sem, side_sem, near_sem, core_sem, sent_sem,
        ) = outs[16 + n_sent :]
        held = (taps, encoded, even_act, odd_act, even_slope, odd_slope, slope_second, norm, joint, mixed, logs)

        section, replica = lax.axis_index("section"), lax.axis_index("dp")
        side_peer = {"section": 1 - section}

        def flipped(value, bit):
            return value + bit - 2 * bit * ((value // bit) % 2)

        def peer(bit):
            return {"dp": flipped(replica, bit)}

        def remote(source, target, sent, sems, at, device):
            return pltpu.make_async_remote_copy(
                src_ref=source, dst_ref=target, send_sem=sent_sem.at[sent], recv_sem=sems.at[at],
                device_id=device, device_id_type=pl.DeviceIdType.MESH,
            )

        def part(p, q):
            n, start, size = pieces[p]
            return pl.ds(pl.multiple_of(start + q * (size // 4), 16), size // 4)

        def near(p):
            bit = 4 if p % 2 else 2
            quarter = replica % 2 + 2 * ((replica // bit) % 2)
            return bit, (quarter, flipped(quarter, 2))

        def side_copy(p):
            n = pieces[p][0]
            here = part(p, near(p)[1][0])
            return remote(own[n].at[here], other[n].at[here], n, side_sem, (p,), side_peer)

        def pass_on(p, q, sems, at, bit):
            n = pieces[p][0]
            here = other[n].at[part(p, q)]
            return remote(here, here, n, sems, at, peer(bit))

        def near_copies(p):
            bit, quarters = near(p)
            return [pass_on(p, quarters[0], near_sem, (p,), bit)]

        def core_copies(p):
            return [pass_on(p, q, core_sem, (b, p), 1) for b, q in enumerate(near(p)[1])]

        hops = (lambda p: [side_copy(p)], near_copies, core_copies)

        def advance(p, n):
            for copy in hops[n](p):
                copy.wait_recv()
            if n == 0 and p + flying < n_pieces:
                side_copy(p + flying).start()
            if n + 1 < len(hops):
                for copy in hops[n + 1](p):
                    copy.start()

        def tick(at):
            if at < 4:
                turn = [[(1, 0)], [(2, 0), (1, 1)], [(3, 0), (2, 1), (1, 2)], [(4, 0), (2, 2)]][at]
            else:
                turn = [(at + 1, 0), (at - 1, 1), (at - 2, 2)]
            for p, n in turn:
                if (3 if n else 1) <= p < n_pieces or at < 4:
                    advance(p, n)

        pack_copy = remote(pack, pack_other, n_sent, side_sem, (n_pieces,), side_peer)
        first_copy = remote(first_ref, first_other, n_sent + 1, side_sem, (n_pieces + 1,), side_peer)
        loads = [
            pltpu.make_async_copy(mel_ref.at[section], mel, load_sem.at[0]),
            pltpu.make_async_copy(positions_ref, place, load_sem.at[1]),
        ]

        def conv_copies(mine):
            return first_held.copies(mine, first_ref, first_other, conv_first, weight_sem.at[0]) + second_held.copies(
                mine, own[0], other[0], conv_second, weight_sem.at[1]
            )

        def weight_copy(mine):
            return pltpu.make_async_copy(own[1] if mine == 0 else other[1], weight, weight_sem.at[2])

        def keep(n):
            return pltpu.make_async_copy(held[n], results[n], out_sem.at[n])

        barrier = pltpu.get_barrier_semaphore()
        peers = [side_peer] + [peer(bit) for bit in (1, 2, 4)]
        for device in peers:
            pl.semaphore_signal(barrier, inc=1, device_id=device, device_id_type=pl.DeviceIdType.MESH)
        for copy in loads:
            copy.start()
        pack[0:3, :] = gain[...].astype(f32)
        pack[3:6, :] = shift[...].astype(f32)
        pack[6:12, :] = biases[...].astype(f32)
        for n in range(hidden // width):
            pack[12 + n : 13 + n, :] = up_bias[:, n * width : n * width + width].astype(f32)
        pack[16:17, 0:lanes] = first_bias[...].astype(f32).reshape(1, lanes)
        pack[16:17, lanes:width] = jnp.zeros((1, lanes), f32)
        pack[17:24, :] = jnp.zeros((7, width), f32)
        pl.semaphore_wait(barrier, len(peers))
        side_copy(0).start()
        first_copy.start()
        pack_copy.start()
        for p in range(1, flying):
            side_copy(p).start()

        turned[0:8, :] = jnp.zeros((8, 128), f32)
        turned[8 + mel_frames : 16 + mel_frames, :] = jnp.zeros((8, 128), f32)
        carry[...] = jnp.zeros(carry.shape, f32)
        clear_pads(conv_first, bands)
        for copy in loads:
            copy.wait()
        band_at = lax.broadcasted_iota(jnp.int32, (bands, block), 0)
        frame_at = lax.broadcasted_iota(jnp.int32, (bands, block), 1)
        time_from, band_from = times[section], bands_from[section]
        time_to, band_to = time_from + time_spans[section], band_from + band_spans[section]
        band_keep = jnp.logical_or(band_at < band_from, band_at >= band_to)
        for n in range(mel_frames // block):
            at = frame_at + n * block
            keep_here = jnp.logical_and(band_keep, jnp.logical_or(at < time_from, at >= time_to))
            values = jnp.where(keep_here, mel[:, n * block : n * block + block].astype(f32), 0.0)
            values = jnp.concatenate([values, jnp.zeros((128 - bands, block), f32)], axis=0)
            turned[8 + n * block : 8 + n * block + block, :] = values.T
        for n, start in enumerate((7, 8, 9, 10)):
            taps[:, n * 128 : n * 128 + 128] = turned[pl.ds(start, frames, stride=2), :].astype(low)
        keep(0).start()

        for n in range(len(hops)):
            advance(0, n)
        first_copy.wait_recv()
        pack_copy.wait_recv()
        for which in range(2):

            @pl.when(section == which)
            def _(which=which):
                for copy in conv_copies(which):
                    copy.start()

        first_section = section == 0
        a_small[...] = jnp.where(first_section, pack[...], pack_other[...])
        t_small[...] = jnp.where(first_section, pack_other[...], pack[...])
        for n in range(hidden // width):
            a_ups[:, n * width : n * width + width] = a_small[12 + n : 13 + n, :]
            t_ups[:, n * width : n * width + width] = t_small[12 + n : 13 + n, :]
        bias = jnp.concatenate([a_small[16:17, 0:lanes], t_small[16:17, 0:lanes]], axis=1)
        for copy in conv_copies(0):
            copy.wait()

        def stem_block(i):
            here = pl.ds(pl.multiple_of(i * block, block), block)
            value, slope = gelu_both(dot(taps[here, 0:384], conv_first[...]) + bias)
            even = value.astype(low)
            even_act[here] = even
            even_slope[here] = slope.astype(low)
            value, slope = gelu_both(dot(taps[here, 128:512], conv_first[...]) + bias)
            odd = value.astype(low)
            odd_act[here] = odd
            odd_slope[here] = slope.astype(low)
            prior = dot(odd, conv_second[0:width])
            at_row = lax.broadcasted_iota(jnp.int32, (block, width), 0)
            moved = jnp.where(at_row == 0, carry[0:1, :], pltpu.roll(prior, 1, 0))
            carry[0:1, :] = prior[block - 1 : block, :]
            pre = moved + dot(even, conv_second[width : 2 * width]) + dot(odd, conv_second[2 * width :]) + row(a_small, 10)
            value, slope = gelu_both(pre)
            slope_second[here] = slope.astype(low)
            encoded[here] = value + place[here].astype(f32)

        for i in range(blocks):
            stem_block(i)
            tick(i)
        for n in range(1, 7):
            keep(n).start()
        for which in range(2):

            @pl.when(section == which)
            def _(which=which):
                weight_copy(which).start()

        weight_copy(0).wait()

        def project_block(i):
            here = pl.ds(pl.multiple_of(i * block, block), block)
            normed, inverse = norm_rows(encoded[here])
            rounded = (normed * row(a_small, 0) + row(a_small, 3)).astype(low)
            norm[here] = rounded
            joint[here, 0:width] = (dot(rounded, weight[:, 0:width]) + row(a_small, 6)).astype(low) * 0.125
            joint[here, width : 2 * width] = dot(rounded, weight[:, width : 2 * width]).astype(low)
            joint[here, 2 * width :] = (dot(rounded, weight[:, 2 * width :]) + row(a_small, 7)).astype(low)

        for i in range(blocks):
            project_block(i)
        tick(blocks)
        keep(7).start()
        keep(8).start()

        def attention(pair):
            lane = lax.broadcasted_iota(jnp.int32, (1, 128), 1)

            def cols(start):
                return pl.ds(pl.multiple_of(start + pair * 128, 128), 128)

            key, value = joint[:, cols(width)], joint[:, cols(2 * width)]

            @pl.loop(0, blocks // 2)
            def _(i):
                here = pl.ds(pl.multiple_of(i * 2 * block, 2 * block), 2 * block)
                query = joint[here, cols(0)]
                found, log = [], []
                for head in range(2):
                    scores = dot_t(jnp.where(lane // 64 == head, query, jnp.zeros_like(query)), key)
                    top = jnp.max(scores, axis=1, keepdims=True) * log2_e
                    exponent = jnp.exp2(scores * log2_e - top)
                    total = jnp.sum(exponent, axis=1, keepdims=True)
                    found.append(dot(exponent.astype(low), value) * (1.0 / total))
                    log.append(top + jnp.log2(total))
                mixed[here, cols(0)] = jnp.where(lane < 64, found[0], found[1]).astype(low)
                both = jnp.where(lane == 0, log[0], log[1])
                logs[pl.ds(pl.multiple_of(pair * 8, 8), 8), here] = both.T[0:8, :]

        done = blocks + 1
        for pair in range(HEADS // 2):
            attention(pair)
            tick(done)
            done += 1
        while done < n_pieces + len(hops) - 1:
            tick(done)
            done += 1
        keep(9).start()
        keep(10).start()
        for n in range(n_sent):
            remote(own[n], other[n], n, side_sem, (0,), side_peer).wait_send()
        first_copy.wait_send()
        pack_copy.wait_send()
        for n in range(len(held)):
            keep(n).wait()

    def sems(*shape):
        return pltpu.SemaphoreType.DMA(shape)

    shape = (frames, width)
    kept = [(shape, low), (shape, f32)] + [(shape, low)] * 6 + [((frames, 3 * width), low), (shape, low), ((4 * HEADS, frames), f32)]
    everywhere, on_chip = pl.BlockSpec(memory_space=pl.ANY), pl.BlockSpec(memory_space=pltpu.VMEM)
    return pl.pallas_call(
        kernel,
        name="begin",
        in_specs=[everywhere] * n_any + [pl.BlockSpec(memory_space=pltpu.SMEM)] * 4 + [on_chip] * 5,
        out_specs=[everywhere] * (1 + n_sent) + [on_chip] * 4 + [everywhere] * len(kept),
        out_shape=[jax.ShapeDtypeStruct(a.shape, a.dtype) for a in [first] + sent]
        + [jax.ShapeDtypeStruct(s, f32) for s in ((24, width), (24, width), (1, hidden), (1, hidden))]
        + [jax.ShapeDtypeStruct(s, d) for s, d in kept],
        scratch_shapes=[pltpu.VMEM(s, d) for s, d in kept]
        + [
            pltpu.VMEM((bands, mel_frames), low), pltpu.VMEM((mel_frames + 16, 128), f32), pltpu.VMEM(shape, low),
            pltpu.VMEM((384, width), low), pltpu.VMEM((3 * width, width), low), pltpu.VMEM((width, 3 * width), low),
            pltpu.VMEM((8, width), f32), pltpu.VMEM((24, width), f32), pltpu.VMEM((24, width), f32),
            sems(2), sems(3), sems(len(kept)), sems(n_pieces + 2), sems(n_pieces), sems(2, n_pieces),
            sems(n_sent + 2),
        ],
        compiler_params=pltpu.CompilerParams(collective_id=1, has_side_effects=True, vmem_limit_bytes=VMEM_BYTES),
        cost_estimate=pl.CostEstimate(flops=10**10, bytes_accessed=10**8, transcendentals=0),
    )(mel_input, positions, first, *sent, *spans, gain, shift, biases, up_bias, first_bias)


def factors_of(size):
    found, rest = [], size // 2
    while rest > 1:
        radix = 2 if size <= 16 or rest % 4 else 4
        found.append(radix)
        rest //= radix
    return found


def finish_backward(audio, text, joint, logs, mixed_grad, grad, encoded, slopes, smalls, weight, second, first, acts, audio_sums, text_sums, bands):
    width, tile_rows = 512, 512
    half = tile_rows // 2
    lanes = width // 2
    frames, text_rows = joint.shape[0], text[0][0].shape[0]
    tiles = len(audio)
    count = tiles + 2
    early = 11
    flying = 3
    lag = 1
    rows = count * tile_rows
    block = 256
    blocks = frames // block
    replicas = lax.axis_size("dp")
    factors = factors_of(replicas)
    levels = len(factors)
    befores, sizes, scatters = [], [], []
    for radix in factors:
        before = sizes[-1] if sizes else half
        befores.append(before)
        scatters.append(before % (16 * radix) == 0)
        sizes.append(before // radix if scatters[-1] else before)

    arrays, places = [], {}

    def place(array):
        if id(array) not in places:
            places[id(array)] = len(arrays)
            arrays.append(array)
        return places[id(array)]

    def job(x, xc, y, yc):
        return (place(x), xc, y if isinstance(y, int) else (place(y),), yc)

    audio_jobs = [job(*one) for one in audio]
    text_jobs = [job(*one) for one in text]
    at_joint, at_logs, at_mixed, at_grad, at_encoded = [place(a) for a in (joint, logs, mixed_grad, grad, encoded)]
    at_slopes = [place(a) for a in slopes]
    odd_act, even_act, taps = acts
    at_odd, at_even, at_taps = place(odd_act), place(even_act), place(taps)
    at_weight = (place(weight.own), place(weight.other))
    at_second = (place(second.own), place(second.other))
    at_first = (place(first.own), place(first.other))
    n_any = len(arrays)
    n_chip = 1 + len(audio_sums) + len(text_sums)

    def kernel(*refs):
        given = refs[:n_any]
        smalls, *known = refs[n_any : n_any + n_chip]
        audio_sums, text_sums = known[:2], known[2:]
        out_ref, keep_ref, got_ref = refs[n_any + n_chip : n_any + n_chip + 3]
        refs = refs[n_any + n_chip + 3 :]
        (
            tile, core_recv, side_send, side_recv, work, final, x_audio, y_audio, x_text, y_text,
            joint, logs, mixed_grad, query_grad, key_grad, value_grad, key_acc, value_acc, key_turned, sums,
            encoded_in, grad_in, slope_in, weight, second, first, second_low, next_low, even_low, odd_low, taps_grad,
            carry, small_buf, mel_buf, mel_send,
            in_sem, load_sem, weight_sem, block_sem, keep_sem, core_sem, side_sem, back_sem, out_sem, mel_sem, sent_sem,
        ) = refs[:46]
        recvs = refs[46 : 46 + levels]
        rs_sems = refs[46 + levels : 46 + 2 * levels]
        ag_sems = refs[46 + 2 * levels :]
        own_grads = (query_grad, key_grad, value_grad)

        section, replica = lax.axis_index("section"), lax.axis_index("dp")
        core = replica % 2
        digits, strides, rest, stride = [], [], replica // 2, 2
        for radix in factors:
            digits.append(rest % radix)
            strides.append(stride)
            rest, stride = rest // radix, stride * radix
        core_peer = {"dp": replica + 1 - 2 * core}
        side_peer = {"section": 1 - section}

        def peer(level, distance):
            digit = (digits[level] + distance) % factors[level]
            return digit, {"dp": replica + (digit - digits[level]) * strides[level]}

        def remote(source, target, sent, sems, k, device):
            return pltpu.make_async_remote_copy(
                src_ref=source, dst_ref=target, send_sem=sent, recv_sem=sems.at[k],
                device_id=device, device_id_type=pl.DeviceIdType.MESH,
            )

        def rows_at(start, size):
            return pl.ds(pl.multiple_of(start, 16), size)

        def offset(level):
            found = 0
            for n in range(level):
                if scatters[n]:
                    found = found + digits[n] * sizes[n]
            return found

        def core_copy(k):
            return remote(
                tile.at[k % 2, :, rows_at((1 - core) * half, half)], core_recv.at[k % 4], core_sem.at[1, k], core_sem.at[0], k, core_peer
            )

        def side_copy(k):
            here = rows_at(k * half, half)
            return remote(side_send.at[here], side_recv.at[here], sent_sem.at[0], side_sem, k, side_peer)

        def scatter_copy(k, level, distance):
            digit, device = peer(level, distance)
            size = sizes[level]
            start = k * half + offset(level) + (digit * size if scatters[level] else 0)
            return remote(
                work.at[rows_at(start, size)], recvs[level].at[distance - 1, rows_at(k * size, size)],
                sent_sem.at[2 + 2 * level], rs_sems[level], k, device,
            )

        def scatter_wait(k, level):
            here = recvs[level].at[:, rows_at(k * sizes[level], sizes[level])]
            remote(here, here, sent_sem.at[0], rs_sems[level], k, side_peer).wait_recv()

        def gather_copy(k, level, distance):
            digit, device = peer(level, distance)
            here = final.at[rows_at(k * tile_rows + core * half + offset(level + 1), sizes[level])]
            return remote(here, here, sent_sem.at[3 + 2 * level], ag_sems[level], k, device)

        def gather_wait(k, level):
            here = recvs[level].at[:, rows_at(k * sizes[level], sizes[level])]
            remote(here, here, sent_sem.at[0], ag_sems[level], k, side_peer).wait_recv()

        def scatter_sent(level, start, size):
            here = recvs[level].at[:, rows_at(start, size)]
            remote(here, here, sent_sem.at[2 + 2 * level], rs_sems[level], 0, side_peer).wait_send()

        def all_sent():
            remote(side_send, side_recv, sent_sem.at[0], side_sem, 0, side_peer).wait_send()
            remote(side_send, side_recv, sent_sem.at[1], back_sem, 0, core_peer).wait_send()
            for level in range(levels):
                if scatters[level]:
                    scatter_sent(level, 0, count * sizes[level])
                    here = recvs[level]
                    remote(here, here, sent_sem.at[3 + 2 * level], ag_sems[level], 0, side_peer).wait_send()
            pltpu.make_async_copy(final, out_ref, out_sem).wait()

        def back_copy(k):
            here = final.at[rows_at(k * tile_rows + core * half, half)]
            return remote(here, here, sent_sem.at[1], back_sem, k, core_peer)

        def store(k):
            here = rows_at(k * tile_rows, tile_rows)
            return pltpu.make_async_copy(final.at[here], out_ref.at[here], out_sem)

        def mel_copy():
            return remote(mel_send, got_ref, mel_sem.at[1], mel_sem, 0, side_peer)

        def stage_core(k):
            core_copy(k).wait_recv()
            here, mine = rows_at(k * half, half), rows_at(core * half, half)
            slot, from_peer = k % 2, k % 4
            side_send[here] = tile[slot, 1 - section, mine] + core_recv[from_peer, 1 - section]

            @when(jnp.logical_or(k < flying, k == tiles))
            def _():
                side_copy(k).start()

            work[here] = tile[slot, section, mine] + core_recv[from_peer, section]

        scatter_levels = [n for n in range(levels) if scatters[n]]

        def next_exchange(k, level):
            if level + 1 < levels:
                for distance in range(1, factors[level + 1]):
                    scatter_copy(k, level + 1, distance).start()
            elif scatter_levels:
                for distance in range(1, factors[scatter_levels[-1]]):
                    gather_copy(k, scatter_levels[-1], distance).start()
            else:
                back_copy(k).start()

        def put(k, level, total):
            if level + 1 < levels:
                work[rows_at(k * half + offset(level + 1), total.shape[0])] = total.astype(low)
            else:
                start = k * tile_rows + core * half + offset(level + 1)
                final[rows_at(start, total.shape[0])] = total.astype(low)
            next_exchange(k, level)

        def stage_side(k):
            side_copy(k).wait_recv()
            later = k + flying

            @when(jnp.logical_and(later < count, later != tiles))
            def _():
                side_copy(later).start()

            here = rows_at(k * half, half)
            put(k, -1, work[here] + side_recv[here])

        def stage_scatter(k, level):
            size = sizes[level]
            scatter_wait(k, level)
            kind = f32 if factors[level] > 2 else low
            total = work[rows_at(k * half + offset(level + 1), size)].astype(kind)
            for distance in range(1, factors[level]):
                total += recvs[level][distance - 1, rows_at(k * size, size)].astype(kind)
            if not scatters[level]:
                scatter_sent(level, k * sizes[level], sizes[level])
            put(k, level, total)

        def stage_gather(k, level):
            gather_wait(k, level)
            if level != scatter_levels[0]:
                below = scatter_levels[scatter_levels.index(level) - 1]
                for distance in range(1, factors[below]):
                    gather_copy(k, below, distance).start()
            else:
                back_copy(k).start()

        def stage_back(k):
            back_copy(k).wait_recv()
            store(k).start()

        stages = [stage_side]
        stages += [functools.partial(stage_scatter, level=n) for n in range(levels)]
        stages += [functools.partial(stage_gather, level=n) for n in reversed(scatter_levels)]
        stages.append(stage_back)

        def tick(at):
            for n, stage in enumerate(stages):

                @pl.when(jnp.logical_and(at >= lag * n, at < count + lag * n))
                def _(n=n, stage=stage):
                    stage(at - lag * n)

        def when(cond):
            return pl.when(cond)

        def fetch_copies(job, x_buf, y_buf, slot, sems):
            x, xc, y, yc = job
            x_from = given[x].at[:, xc * width : (xc + 1) * width]
            y_from = own_grads[y] if isinstance(y, int) else given[y[0]].at[:, yc * width : (yc + 1) * width]
            return (
                pltpu.make_async_copy(x_from, x_buf.at[slot], sems.at[0, slot]),
                pltpu.make_async_copy(y_from, y_buf.at[slot], sems.at[1, slot]),
            )

        def fetch(k, first_k, last_k):
            for n in range(first_k, last_k):

                @when(k == n)
                def _(n=n):
                    for copy in fetch_copies(audio_jobs[n], x_audio, y_audio, n % 2, in_sem.at[0]):
                        copy.start()
                    for copy in fetch_copies(text_jobs[n], x_text, y_text, n % 2, in_sem.at[1]):
                        copy.start()

        def fetch_wait(k):
            slot = k % 2
            for copy in fetch_copies(audio_jobs[0], x_audio, y_audio, slot, in_sem.at[0]):
                copy.wait()
            for copy in fetch_copies(text_jobs[0], x_text, y_text, slot, in_sem.at[1]):
                copy.wait()

        def tile_grads(k, last_k, first_k):
            slot = k % 2

            @when(k + 1 < last_k)
            def _():
                fetch(k + 1, first_k, last_k)

            fetch_wait(k)

            @when(k >= 2)
            def _():
                core_copy(k - 2).wait_send()

            tile[slot, 0] = dot_tt(x_audio[slot], y_audio[slot]).astype(low)
            tile[slot, 1] = dot_tt(x_text[slot], y_text[slot]).astype(low)
            core_copy(k).start()

            @when(k > first_k)
            def _():
                stage_core(k - 1)

        attn_loads = [
            pltpu.make_async_copy(given[at_joint], joint, load_sem.at[0]),
            pltpu.make_async_copy(given[at_logs], logs, load_sem.at[1]),
            pltpu.make_async_copy(given[at_mixed], mixed_grad, load_sem.at[2]),
        ]

        def attention(step):
            pair, part_at = step // blocks, step % blocks
            lane = lax.broadcasted_iota(jnp.int32, (1, 128), 1)
            sub = lax.broadcasted_iota(jnp.int32, (128, 1), 0)

            def cols(start):
                return pl.ds(pl.multiple_of(start + pair * 128, 128), 128)

            here = rows_at(part_at * block, block)

            @when(part_at == 0)
            def _():
                key_acc[...] = jnp.zeros(key_acc.shape, f32)
                value_acc[...] = jnp.zeros(value_acc.shape, f32)
                key_turned[...] = joint[:, cols(width)].astype(f32).T.astype(low)

            query, key, value = joint[here, cols(0)], joint[:, cols(width)], joint[:, cols(2 * width)]
            grad = mixed_grad[here, cols(0)]
            log = logs[pl.ds(pl.multiple_of(pair * 8, 8), 8), pl.ds(pl.multiple_of(part_at * block, block), block)]
            turned = key_turned[...]
            found = []
            for head in range(2):
                part = jnp.where(lane // 64 == head, query, jnp.zeros_like(query))
                grad_part = jnp.where(lane // 64 == head, grad, jnp.zeros_like(grad))
                chance = jnp.exp2(dot_t(key, part) * log2_e - log[head : head + 1, :])
                product = chance * dot_t(value, grad_part)
                grad_scores = (product - chance * jnp.sum(product, axis=0, keepdims=True)).astype(low)
                found.append(
                    (
                        dot(chance.astype(low), grad_part),
                        dot(grad_scores, part),
                        dot(jnp.where(sub // 64 == head, turned, jnp.zeros_like(turned)), grad_scores),
                    )
                )
            value_acc[...] += found[0][0] + found[1][0]
            key_acc[...] += found[0][1] + found[1][1]
            query_turned = found[0][2] + found[1][2]
            grad_query = query_turned.T * 0.125
            query_grad[here, cols(0)] = grad_query.astype(low)
            sums[0:1, cols(0)] += col_sum(grad_query)

            @when(part_at == blocks - 1)
            def _():
                key_grad[:, cols(0)] = key_acc[...].astype(low)
                value_grad[:, cols(0)] = value_acc[...].astype(low)
                sums[1:2, cols(0)] = col_sum(value_acc[...])

        def weight_copies(mine):
            found = [pltpu.make_async_copy(given[at_weight[0 if mine == 0 else 1]], weight, weight_sem.at[0])]
            for n, (split, at, held) in enumerate(((second_side, at_second, second), (first_side, at_first, first))):
                found += split.copies(mine, given[at[0]], given[at[1]], held, weight_sem.at[1 + n])
            return found

        def block_copies(i, slot):
            here = rows_at(i * block, block)
            found = [
                pltpu.make_async_copy(given[at_encoded].at[here], encoded_in.at[slot], block_sem.at[0, slot]),
                pltpu.make_async_copy(given[at_grad].at[here], grad_in.at[slot], block_sem.at[1, slot]),
            ]
            for n in range(3):
                found.append(
                    pltpu.make_async_copy(given[at_slopes[n]].at[here], slope_in.at[slot, n], block_sem.at[2 + n, slot])
                )
            return found

        def stem_block(step):
            i = blocks - 1 - step
            slot = step % 2

            @when(step + 1 < blocks)
            def _():
                for copy in block_copies(i - 1, 1 - slot):
                    copy.start()

            for copy in block_copies(i, slot):
                copy.wait()
            here = rows_at(i * block, block)
            back = (
                dot_t(query_grad[here], weight[:, :width])
                + dot_t(key_grad[here], weight[:, width : 2 * width])
                + dot_t(value_grad[here], weight[:, 2 * width :])
            )
            normed, inverse = norm_rows(encoded_in[slot])
            sums[2:3, :] += col_sum(back * normed)
            sums[3:4, :] += col_sum(back)
            total = grad_in[slot] + norm_back(back, row(smalls, 0), normed, inverse)
            total = total * slope_in[slot, 0].astype(f32)
            sums[4:5, :] += col_sum(total)
            rounded = total.astype(low)
            second_low[here] = rounded
            at_row = lax.broadcasted_iota(jnp.int32, (block, width), 0)
            wide = rounded.astype(f32)
            moved = jnp.where(at_row == block - 1, carry[0:1, :], pltpu.roll(wide, block - 1, 0))
            carry[0:1, :] = wide[0:1, :]
            moved = moved.astype(low)
            next_low[here] = moved
            grad_even = dot_t(rounded, second[width : 2 * width]) * slope_in[slot, 1].astype(f32)
            grad_odd = (dot_t(rounded, second[2 * width :]) + dot_t(moved, second[0:width])) * slope_in[slot, 2].astype(f32)
            sums[5:6, :] += col_sum(grad_even) + col_sum(grad_odd)
            grad_even = grad_even.astype(low)
            grad_odd = grad_odd.astype(low)
            even_low[here] = grad_even
            odd_low[here] = grad_odd
            taps_even = dot_t(grad_even, first[...])
            taps_odd = dot_t(grad_odd, first[...])
            taps_grad[here, 0:128] = taps_even[:, 0:128]
            taps_grad[here, 128:256] = taps_even[:, 128:256] + taps_odd[:, 0:128]
            taps_grad[here, 256:384] = taps_even[:, 256:384] + taps_odd[:, 128:256]
            taps_grad[here, 384:512] = taps_odd[:, 256:384]

        def mel_rows():
            at_row = lax.broadcasted_iota(jnp.int32, (frames, 128), 0)
            before = jnp.where(at_row == 0, 0.0, pltpu.roll(taps_grad[:, 384:512], 1, 0))
            mel_buf[:, 0:128] = taps_grad[:, 128:256] + before
            after = jnp.where(at_row == frames - 1, 0.0, pltpu.roll(taps_grad[:, 0:128], frames - 1, 0))
            mel_buf[:, 128:256] = taps_grad[:, 256:384] + after
            mel_send[...] = mel_buf[rows_at((1 - section) * (frames // 2), frames // 2)].astype(low)

        def keep_copy():
            return pltpu.make_async_copy(mel_buf.at[rows_at(section * (frames // 2), frames // 2)], keep_ref, keep_sem)

        conv_jobs = [(at_odd, next_low), (at_even, second_low), (at_odd, second_low)]

        def conv_copies(n, slot):
            x, y = conv_jobs[n]
            return (
                pltpu.make_async_copy(given[x], x_audio.at[slot], in_sem.at[0, 0, slot]),
                pltpu.make_async_copy(y, y_audio.at[slot], in_sem.at[0, 1, slot]),
            )

        def tap_copies():
            return [
                pltpu.make_async_copy(given[at_taps].at[:, n * 128 : n * 128 + 384], x_audio.at[n, :, 0:384], in_sem.at[0, 0, n])
                for n in range(2)
            ]

        barrier = pltpu.get_barrier_semaphore()
        peers = [core_peer, side_peer]
        peers += [peer(n, d)[1] for n in range(levels) for d in range(1, factors[n])]
        for device in peers:
            pl.semaphore_signal(barrier, inc=1, device_id=device, device_id_type=pl.DeviceIdType.MESH)

        fetch(0, 0, 1)
        for copy in attn_loads:
            copy.start()
        for which in range(2):

            @when(section == which)
            def _(which=which):
                for copy in weight_copies(which):
                    copy.start()

        for copy in block_copies(blocks - 1, 0):
            copy.start()
        sums[...] = jnp.zeros(sums.shape, f32)
        carry[...] = jnp.zeros(carry.shape, f32)
        pl.semaphore_wait(barrier, len(peers))

        @pl.loop(0, early)
        def _(k):
            tile_grads(k, early, 0)

        stage_core(early - 1)
        for copy in attn_loads:
            copy.wait()

        @pl.loop(0, 4 * blocks)
        def _(step):
            attention(step)

            @when(jnp.logical_or(step < 3, step % 3 == 1))
            def _():
                tick(jnp.where(step < 3, step, 3 + (step - 4) // 3))

        fetch(early, early, early + 1)

        @pl.loop(early, tiles)
        def _(k):
            tile_grads(k, tiles, early)
            tick(k - early + 7)

        stage_core(tiles - 1)
        for copy in weight_copies(0):
            copy.wait()
        clear_pads(first, bands)

        @pl.loop(0, blocks)
        def _(step):
            stem_block(step)

            @when(step % 2 == 1)
            def _():
                tick(10 + step // 2)

        for copy in conv_copies(0, 0):
            copy.start()

        @pl.loop(0, 3)
        def _(n):
            slot = n % 2
            for which in range(1, 3):

                @when(n + 1 == which)
                def _(which=which):
                    for copy in conv_copies(which, which % 2):
                        copy.start()

            for copy in conv_copies(0, slot):
                copy.wait()
            joint[0:tile_rows, pl.ds(pl.multiple_of(n * width, width), width)] = dot_tt(x_audio[slot], y_audio[slot]).astype(low)

        for copy in tap_copies():
            copy.start()
        core_copy(tiles - 2).wait_send()
        slot = tiles % 2

        def conv_part(tap, start, s):
            cols = slice(tap * width + s * lanes, tap * width + s * lanes + lanes)
            return joint[start : start + half, cols]

        for s in range(2):
            tile[slot, s, 0:half, 0:lanes] = conv_part(0, 0, s)
            tile[slot, s, half:tile_rows, 0:lanes] = conv_part(0, half, s)
            tile[slot, s, 0:half, lanes:width] = conv_part(1, half, s)
            tile[slot, s, half:tile_rows, lanes:width] = conv_part(2, 0, s)
        core_copy(tiles).start()
        for copy in tap_copies():
            copy.wait()
        first_grad = (
            dot_tt(x_audio[0, :, 0:384], even_low[...]) + dot_tt(x_audio[1, :, 0:384], odd_low[...])
        ).astype(low)
        stage_core(tiles)
        core_copy(tiles - 1).wait_send()
        slot = 1 - slot
        feed, wide_feed = audio_sums
        text_feed_sums, text_wide, text_cross, cross_sums, text_attn, text_first = text_sums
        small_buf[...] = jnp.zeros(small_buf.shape, f32)
        text_rows_from = (
            (text_first, 0), (text_cross, 0), (text_feed_sums, 0), (text_first, 1), (text_cross, 1), (text_feed_sums, 1),
            (text_attn, 0), (text_attn, 1), (text_cross, 2), (text_feed_sums, 2), (cross_sums, 0), (text_feed_sums, 3),
        )
        for at, (ref, n) in enumerate(text_rows_from):
            small_buf[1, at : at + 1, :] = ref[n : n + 1, :]
        for at, ref, n in (
            (1, feed, 3), (2, feed, 0), (4, feed, 4), (5, feed, 1), (8, feed, 5), (9, feed, 2), (11, cross_sums, 1),
        ):
            small_buf[0, at : at + 1, :] = ref[n : n + 1, :]
        for n in range(4):
            cols = slice(n * width, n * width + width)
            small_buf[0, 12 + n : 13 + n, :] = wide_feed[0:1, cols]
            small_buf[1, 12 + n : 13 + n, :] = text_wide[0:1, cols]
        for s in range(2):
            small_buf[s, 17:18, :] = text_feed_sums[3:4, :]
        small_buf[0, 6:8, :] = sums[0:2, :]
        small_buf[0, 0:1, :] = sums[2:3, :]
        small_buf[0, 3:4, :] = sums[3:4, :]
        small_buf[0, 10:11, :] = sums[4:5, :]
        small_buf[0, 16:17, 0:lanes] = sums[5:6, 0:lanes]
        small_buf[1, 16:17, 0:lanes] = sums[5:6, lanes:width]
        for s in range(2):
            cols = slice(s * lanes, s * lanes + lanes)
            tile[slot, s, 0:half, 0:lanes] = conv_part(1, 0, s)
            tile[slot, s, 0:half, lanes:width] = conv_part(2, half, s)
            tile[slot, s, half : half + 192, 0:lanes] = first_grad[0:192, cols]
            tile[slot, s, half : half + 192, lanes:width] = first_grad[192:384, cols]
            tile[slot, s, half + 192 : half + 224, :] = small_buf[s].astype(low)
            tile[slot, s, half + 224 : tile_rows, :] = jnp.zeros((32, width), low)
        core_copy(tiles + 1).start()
        mel_rows()
        keep_copy().start()
        stage_core(tiles + 1)
        mel_copy().start()

        @pl.loop(12, count + lag * (len(stages) - 1))
        def _(at):
            tick(at)

        keep_copy().wait()
        mel_copy().wait()
        for k in (count - 2, count - 1):
            core_copy(k).wait_send()

        all_sent()

    second_side, first_side = second, first

    def sems(*shape):
        return pltpu.SemaphoreType.DMA(shape)

    def vmem(*shape, dtype=low):
        return pltpu.VMEM(shape, dtype)

    whole = (frames, width)
    return pl.pallas_call(
        kernel,
        name="finish_backward",
        in_specs=[pl.BlockSpec(memory_space=pl.ANY)] * n_any + [pl.BlockSpec(memory_space=pltpu.VMEM)] * n_chip,
        out_specs=[pl.BlockSpec(memory_space=pl.ANY)] * 3,
        out_shape=[
            jax.ShapeDtypeStruct((rows, width), low),
            jax.ShapeDtypeStruct((frames // 2, 256), f32),
            jax.ShapeDtypeStruct((frames // 2, 256), low),
        ],
        scratch_shapes=[
            vmem(2, 2, tile_rows, width), vmem(4, 2, half, width), vmem(count * half, width), vmem(count * half, width),
            vmem(count * half, width), vmem(rows, width),
            vmem(2, *whole), vmem(2, *whole), vmem(2, text_rows, width), vmem(2, text_rows, width),
            vmem(frames, 3 * width), vmem(32, frames, dtype=f32), vmem(*whole), vmem(*whole), vmem(*whole), vmem(*whole),
            vmem(frames, 128, dtype=f32), vmem(frames, 128, dtype=f32), vmem(128, frames), vmem(8, width, dtype=f32),
            vmem(2, block, width, dtype=f32), vmem(2, block, width, dtype=f32), vmem(2, 3, block, width),
            vmem(width, 3 * width), vmem(*second.shape), vmem(*first.shape),
            vmem(*whole), vmem(*whole), vmem(*whole), vmem(*whole), vmem(*whole, dtype=f32),
            vmem(8, width, dtype=f32), vmem(2, 32, width, dtype=f32),
            vmem(frames, 256, dtype=f32), vmem(frames // 2, 256),
            sems(2, 2, 2), sems(3), sems(3), sems(5, 2), pltpu.SemaphoreType.DMA, sems(2, count), sems(count), sems(count),
            pltpu.SemaphoreType.DMA, sems(2), sems(2 + 2 * levels),
            *[vmem(r - 1, count * s, width) for r, s in zip(factors, sizes)],
            *[sems(count) for r in factors],
            *[sems(count) for r in factors],
        ],
        compiler_params=pltpu.CompilerParams(
            collective_id=0, has_side_effects=True, vmem_limit_bytes=63 << 20
        ),
        cost_estimate=pl.CostEstimate(flops=10**11, bytes_accessed=10**8, transcendentals=0),
    )(*arrays, smalls, *audio_sums, *text_sums)


def shards(
    mel_input,
    time_start,
    time_width,
    freq_start,
    freq_width,
    text_len,
    text_embed,
    cotangent,
    positions,
    conv_first,
    conv_first_bias,
    conv_second,
    norm_gain,
    norm_shift,
    attn_in,
    attn_out,
    mlp_up,
    mlp_down,
    up_bias,
    small_bias,
    cross_first,
    cross_second,
):
    frames, width = positions.shape
    bands, mel_frames = mel_input.shape[1], mel_input.shape[2]
    audio_block = frames // 2
    swap_pairs = [(0, 1), (1, 0)]

    def partner(array):
        return lax.ppermute(array, "section", swap_pairs)

    first_own = conv_first.reshape(3 * bands, -1)
    second_own = conv_second.reshape(3 * width, -1)
    owns = [w[0] for w in (attn_in, attn_out, mlp_up, mlp_down, cross_first, cross_second)]
    (
        first_other, second_other, *others, a_small, t_small, a_ups, t_ups,
        taps, encoded, even_act, odd_act, even_slope, odd_slope, slope_second, a_norm, a_joint, a_mixed, a_logs,
    ) = begin(
        mel_input, (time_start, time_width, freq_start, freq_width), norm_gain[0], norm_shift[0], small_bias[0], up_bias,
        conv_first_bias, first_own, second_own, owns[0], owns[1:], positions,
    )
    a_in, a_out, a_up, a_down, a_cross_a, a_cross_b = [Side(0, o, p) for o, p in zip(owns, others)]
    t_in, t_out, t_up, t_down, t_cross_a, t_cross_b = [Side(1, o, p) for o, p in zip(owns, others)]
    first_all = Split(first_own, first_other, 3, 128)
    second_all = Split(second_own, second_other, 3, width)

    a_middle, a_feed_norm, a_hidden, a_slope, a_ending, memory, memory_keys, memory_values = audio_feed(
        encoded, a_mixed, a_out, a_small, a_ups, a_up, a_down, a_cross_a, a_cross_b, audio_block
    )

    t_norm, t_joint, t_mixed, t_logs, t_middle, cross_low, cross_query = text_start(
        text_embed, t_in, t_out, t_small, t_cross_a
    )
    (
        decoded_keep, decoded_send, t_feed_norm, t_hidden, t_pre, cot_low, after_grad, after_low, c_mixed,
        query_grad, key_grad, value_grad, feed_sums, feed_wide, c_sums,
    ) = text_cross(
        text_len, cross_query, memory_keys, memory_values, t_middle, cotangent, t_cross_b, t_small, t_ups, t_up, t_down
    )
    text_keep, text_send, middle_low, tq_grad, tk_grad, tv_grad, cross_sums, t_sums, text_sums = text_back(
        query_grad, t_middle, after_grad, t_joint, t_logs, text_embed, t_small, t_cross_a, t_out, t_in
    )
    decoded_got, text_got = partner(decoded_send), partner(text_send)
    end_low, a_pre, a_grad, a_grad_low, a_mixed_grad, a_feed_sums, a_feed_wide = audio_feed_back(
        key_grad, value_grad, a_ending, a_middle, a_slope, a_small, a_cross_a, a_cross_b, a_up, a_down, a_out, audio_block
    )

    audio = [(a_feed_norm, 0, a_pre, n) for n in range(4)] + [(a_hidden, n, end_low, 0) for n in range(4)]
    audio += [(memory, 0, key_grad, 0), (memory, 0, value_grad, 0), (a_mixed, 0, a_grad_low, 0)]
    audio += [(a_norm, 0, n, 0) for n in range(3)]
    text = [(t_feed_norm, 0, t_pre, n) for n in range(4)] + [(t_hidden, n, cot_low, 0) for n in range(4)]
    text += [(cross_low, 0, query_grad, 0), (c_mixed, 0, after_low, 0), (t_mixed, 0, middle_low, 0)]
    text += [(t_norm, 0, part, 0) for part in (tq_grad, tk_grad, tv_grad)]
    a_feed_sums, decoded_got, text_got = lax.optimization_barrier((a_feed_sums, decoded_got, text_got))
    total, mel_keep, mel_got = finish_backward(
        audio, text, a_joint, a_logs, a_mixed_grad, a_grad, encoded, (slope_second, even_slope, odd_slope), a_small, a_in,
        second_all, first_all, (odd_act, even_act, taps), (a_feed_sums, a_feed_wide),
        (feed_sums, feed_wide, cross_sums, c_sums, t_sums, text_sums), bands,
    )

    decoded, text_grad, mel_out = finish(
        [(decoded_keep, decoded_got), (text_keep, text_got)], mel_keep, mel_got,
        (time_start, time_width, freq_start, freq_width), bands,
    )
    joint, out, up, down, cross_a, cross_b, first, bias, second, gain, shift, wide, small, cross = unpack(total, bands)
    gain, shift, small = (jnp.transpose(rows, (1, 0, 2)) for rows in (gain, shift, small))
    return (
        decoded, text_grad, mel_out, first, bias[0], second, gain, shift, joint, out, up, down, wide, small, cross_a, cross_b,
        cross[0],
    )


def solution(mesh):
    return jax.shard_map(
        shards,
        mesh=mesh,
        in_specs=(
            P("dp", None, None),
            P("dp"),
            P("dp"),
            P("dp"),
            P("dp"),
            P("dp"),
            P("dp", None, None),
            P("dp", None, None),
            P(),
            P(None, None, "section"),
            P("section"),
            P(None, None, "section"),
            P("section", None, None),
            P("section", None, None),
            P("section", None, None),
            P("section", None, None),
            P("section", None, None),
            P("section", None, None),
            P("section", None),
            P("section", None, None),
            P("section", None, None),
            P("section", None, None),
        ),
        out_specs=(
            P("dp", None, "section"),
            P("dp", None, "section"),
            P("dp", None, "section"),
            P(None, None, "section"),
            P("section"),
            P(None, None, "section"),
            P("section", None, None),
            P("section", None, None),
            P("section", None, None),
            P("section", None, None),
            P("section", None, None),
            P("section", None, None),
            P("section", None),
            P("section", None, None),
            P("section", None, None),
            P("section", None, None),
            P("section"),
        ),
        check_vma=False,
    )
```
